32 devices in a mesh: dp: 16 (over z, x, core), mp: 2 (over y).
Axes of the slice: x: 2, y: 2, z: 4, core: 2. Of those that a mesh axis runs over, the one named last changes fastest.
Arguments:
- tokens: bfloat16 [4, 384, 15, 1024], P(None, 'dp'), may hold values from -6 to 6
- cotangent: bfloat16 [4, 384, 15, 1024], P(None, 'dp'), may hold values from -6 to 6
- domain_ids: int32 [4, 384], P(None, 'dp'), may hold values from 0 to 6
- domain_counts: int32 [7], replicated, may hold values from 32 to 2047
- w_query: bfloat16 [1024, 1024], P('dp', 'mp'), may hold values from -0.25 to 0.25
- w_key: bfloat16 [1024, 1024], P('dp', 'mp'), may hold values from -0.25 to 0.25
- w_value: bfloat16 [1024, 1024], P('dp', 'mp'), may hold values from -0.1875 to 0.1875
- w_out: bfloat16 [1024, 1024], P('dp', 'mp'), may hold values from -0.375 to 0.375
- w_up: bfloat16 [1024, 2048], P('dp', 'mp'), may hold values from -0.1875 to 0.1875
- w_down: bfloat16 [1024, 2048], P('dp', 'mp'), may hold values from -0.125 to 0.125
- gain_attn: bfloat16 [1024], P('dp'), may hold values from 0.5 to 1.5
- shift_attn: bfloat16 [1024], P('dp'), may hold values from -3 to 3
- gain_ffn: bfloat16 [1024], P('dp'), may hold values from 0.5 to 1.5
- shift_ffn: bfloat16 [1024], P('dp'), may hold values from -3 to 3
Outputs:
- block_out: bfloat16 [4, 384, 15, 1024], P(None, 'dp')
- grad_tokens: float32 [4, 384, 15, 1024], P(None, 'dp')
- grad_query: float32 [1024, 1024], P('dp', 'mp')
- grad_key: float32 [1024, 1024], P('dp', 'mp')
- grad_value: float32 [1024, 1024], P('dp', 'mp')
- grad_out: float32 [1024, 1024], P('dp', 'mp')
- grad_up: float32 [1024, 2048], P('dp', 'mp')
- grad_down: float32 [1024, 2048], P('dp', 'mp')
- grad_gain_attn: float32 [1024], P('dp')
- grad_shift_attn: float32 [1024], P('dp')
- grad_gain_ffn: float32 [1024], P('dp')
- grad_shift_ffn: float32 [1024], P('dp')
The draws below stay inside these ranges and needn't reach their ends.
All inputs are finite; a program needn't handle non-finite values.
Results may differ from the reference program's by a relative error of at most 0.013.
Values may be sent and summed in bfloat16 or wider, within the bound.
A program may use at most 192 MiB of HBM per device.

```python
import math
import jax
import jax.numpy as jnp
import numpy as np
from jax import lax

D = 1024
H = 8
HD = 128
FF = 2048
PATCHES = 15
MB = 4
DOMAINS = 7
SER_DEV = 24
SERIES = 384
N_DP = 16


def plant(values, stream_key, low, largest):
    spot = [jax.random.randint(jax.random.fold_in(stream_key, axis), (), 0, length) for axis, length in enumerate(values.shape)]
    longest = values.shape.index(max(values.shape))
    next_to = spot[:longest] + [(spot[longest] + 1) % values.shape[longest]] + spot[longest + 1:]
    return values.at[tuple(spot)].set(low).at[tuple(next_to)].set(largest)


def levels(own_key, shape, cuts, smallest, high):
    factor_of, own = 1.0, jax.random.fold_in(own_key, 6)
    for axis_at, shards_of in cuts:
        draws = jnp.exp(jax.random.uniform(jax.random.fold_in(own, axis_at), (shards_of,), jnp.float32, smallest / len(cuts), high / len(cuts)))
        factor_of = factor_of * jnp.repeat(draws, shape[axis_at] // shards_of).reshape([-1 if axis == axis_at else 1 for axis in range(len(shape))])
    return factor_of


def cumulative_ranks(number_of, lean):
    portions = [(1 << 20) // math.isqrt(standing ** lean) + 1 for standing in range(1, number_of + 1)]
    scale = 1 + sum(portions) // (1 << 30)
    return np.cumsum(np.array([max(1, weight // scale) for weight in portions]))


def skewed_ids(key, shape, count, skew):
    table = cumulative_ranks(count, skew)
    pick = jax.random.randint(jax.random.fold_in(key, 1), shape, 0, int(table[count - 1]))
    grade = jnp.searchsorted(jnp.asarray(table, jnp.int32), pick, side="right")
    return jax.random.permutation(jax.random.fold_in(key, 2), count)[grade].astype(jnp.int32)


def bell_draw(rng, extent, width, bound, split=(), dtype=jnp.bfloat16):
    loudness = levels(rng, extent, split, -0.22, 0.18) if split else 1.0
    entries = jax.random.normal(rng, extent, jnp.float32) * width * loudness
    return jnp.minimum(jnp.maximum(entries, -bound), bound).astype(dtype)


def setup_inputs(seed: int = 0) -> dict:
    keys = jax.random.split(jax.random.key(seed), 15)
    tokens = bell_draw(keys[0], (MB, SERIES, PATCHES, D), 1.0, 6.0, ((1, 16),))
    cotangent = bell_draw(keys[1], (MB, SERIES, PATCHES, D), 1.0, 6.0, ((1, 16),))
    domain_ids = plant(skewed_ids(keys[2], (MB, SERIES), DOMAINS, 2), jax.random.fold_in(keys[2], 3), 0, DOMAINS - 1).astype(jnp.int32)
    domain_counts = plant(jax.random.randint(keys[3], (DOMAINS,), 32, 2048), jax.random.fold_in(keys[3], 1), 32, 2047).astype(jnp.int32)
    w_query = bell_draw(keys[4], (D, H * HD), (D // 2) ** -0.5, 0.25, ((0, 16), (1, 2)))
    w_key = bell_draw(keys[5], (D, H * HD), (D // 2) ** -0.5, 0.25, ((0, 16), (1, 2)))
    w_value = bell_draw(keys[6], (D, H * HD), D ** -0.5, 0.1875, ((0, 16), (1, 2)))
    w_out = bell_draw(keys[7], (D, H * HD), (H * HD // 4) ** -0.5, 0.375, ((0, 16), (1, 2)))
    w_up = bell_draw(keys[8], (D, FF), D ** -0.5, 0.1875, ((0, 16), (1, 2)))
    w_down = bell_draw(keys[9], (D, FF), FF ** -0.5, 0.125, ((0, 16), (1, 2)))
    gain_attn = jnp.clip(1.0 + 0.1 * jax.random.normal(keys[10], (D,), jnp.float32), 0.5, 1.5).astype(jnp.bfloat16)
    shift_attn = bell_draw(keys[11], (D,), 0.5, 3.0, ((0, 16),))
    gain_ffn = jnp.clip(1.0 + 0.1 * jax.random.normal(keys[12], (D,), jnp.float32), 0.5, 1.5).astype(jnp.bfloat16)
    shift_ffn = bell_draw(keys[13], (D,), 0.5, 3.0, ((0, 16),))
    return {"tokens": tokens, "cotangent": cotangent, "domain_ids": domain_ids, "domain_counts": domain_counts, "w_query": w_query, "w_key": w_key, "w_value": w_value, "w_out": w_out, "w_up": w_up, "w_down": w_down, "gain_attn": gain_attn, "shift_attn": shift_attn, "gain_ffn": gain_ffn, "shift_ffn": shift_ffn}


eps = 1e-05
highest = lax.Precision.HIGHEST

@jax.custom_vjp
def low(v):
    return lax.optimization_barrier(v.astype(jnp.bfloat16)).astype(jnp.float32)

@jax.custom_vjp
def low_back(v):
    return v

def low_keep(v):
    return (low(v), None)

def low_pass(kept, grad):
    return (grad,)

def back_keep(v):
    return (v, None)

def back_low(kept, grad):
    return (low(grad),)
low.defvjp(low_keep, low_pass)
low_back.defvjp(back_keep, back_low)

def round_both(values):
    return low(low_back(values))

def layer_norm(values, gain, shift):
    center = values - lax.optimization_barrier(jnp.mean(values, axis=-1, keepdims=True))
    second = lax.optimization_barrier(jnp.mean(center * center, axis=-1, keepdims=True))
    return center * lax.rsqrt(second + eps) * gain + shift

def block_forward(tensors, inputs):
    w_query, w_key, w_value, w_out, w_up, w_down, gain_attn, shift_attn, gain_ffn, shift_ffn = tensors
    series = inputs.shape[0]
    normed = low(layer_norm(inputs, gain_attn, shift_attn))
    queries = round_both(jnp.einsum('spd,de->spe', normed, w_query, precision=highest)).reshape(series, PATCHES, H, HD)
    keys_round = round_both(jnp.einsum('spd,de->spe', normed, w_key, precision=highest)).reshape(series, PATCHES, H, HD)
    values_round = round_both(jnp.einsum('spd,de->spe', normed, w_value, precision=highest)).reshape(series, PATCHES, H, HD)
    scores = low_back(jnp.einsum('sihd,sjhd->shij', queries, keys_round, precision=highest) * HD ** (-0.5))
    causal = jnp.arange(PATCHES)[:, None] >= jnp.arange(PATCHES)[None, :]
    scores = jnp.where(causal, scores, -1e+30)
    attention = low(jax.nn.softmax(scores, axis=-1))
    mixture = round_both(jnp.einsum('shij,sjhd->sihd', attention, values_round, precision=highest).reshape(series, PATCHES, H * HD))
    attended = low_back(jnp.einsum('spe,de->spd', mixture, w_out, precision=highest))
    residual = inputs + attended
    normed_two = low(layer_norm(residual, gain_ffn, shift_ffn))
    hidden = low_back(jnp.einsum('spd,df->spf', normed_two, w_up, precision=highest))
    active = low(jax.nn.gelu(hidden, approximate=False))
    ffn_out = low_back(jnp.einsum('spf,df->spd', active, w_down, precision=highest))
    return residual + ffn_out

def reference(tokens, cotangent, domain_ids, domain_counts, w_query, w_key, w_value, w_out, w_up, w_down, gain_attn, shift_attn, gain_ffn, shift_ffn):
    tensors = tuple((array.astype(jnp.float32) for array in (w_query, w_key, w_value, w_out, w_up, w_down, gain_attn, shift_attn, gain_ffn, shift_ffn)))
    counts_real = domain_counts.astype(jnp.float32)
    mean_count = jnp.mean(counts_real)
    series_weight = 2.0 * mean_count / (mean_count + counts_real[domain_ids])
    groups = MB * N_DP
    inputs = tokens.astype(jnp.float32).reshape(groups, SER_DEV, PATCHES, D)
    weighted = (cotangent.astype(jnp.float32) * series_weight[:, :, None, None]).reshape(groups, SER_DEV, PATCHES, D)

    def group_step(totals, pair):
        group_in, group_grad = pair
        result, pull = jax.vjp(block_forward, tensors, group_in)
        tensor_grads, input_grad = pull(group_grad)
        totals = tuple((total + grad for total, grad in zip(totals, tensor_grads)))
        return (totals, (result.astype(jnp.bfloat16), input_grad))
    zeros_init = tuple((jnp.zeros_like(tensor) for tensor in tensors))
    totals, (results, input_grads) = lax.scan(group_step, zeros_init, (inputs, weighted))
    return (results.reshape(tokens.shape), input_grads.reshape(tokens.shape), totals[0], totals[1], totals[2], totals[3], totals[4], totals[5], totals[6], totals[7], totals[8], totals[9])
```

```python
import functools

import jax
import jax.numpy as jnp
from jax import lax
from jax.experimental import pallas as pl
from jax.experimental.pallas import tpu as pltpu
from jax.sharding import PartitionSpec as P

BF = jnp.bfloat16
F32 = jnp.float32
HD = 128
SEG = 512
TILE = 128
PAD = 16
EPS = 1e-05
MESH = pl.DeviceIdType.MESH
VMEM_LIMIT = 62 * 1024 * 1024

Q, K, V, O, U0, U1, D0, D1 = range(8)
UPS = (U0, U1)
DOWNS = (D0, D1)
ORDERS = ("zxy", "zyx", "xyz", "zxy", "zyx", "xyz", "zxy", "zyx")


def nn(a, b):
    return lax.dot_general(a, b, (((1,), (0,)), ((), ())), preferred_element_type=F32)


def nt(a, b):
    return lax.dot_general(a, b, (((1,), (1,)), ((), ())), preferred_element_type=F32)


def flat(value):
    return value.reshape(-1, value.shape[-1])


def norm_stats(values):
    mean = jnp.mean(values, axis=-1, keepdims=True)
    center = values - mean
    inverse = lax.rsqrt(jnp.mean(center * center, axis=-1, keepdims=True) + EPS)
    return center * inverse, inverse


def norm_pull(grad, values, gain):
    normal, inverse = norm_stats(values)
    scaled = grad * gain
    first = jnp.mean(scaled, axis=-1, keepdims=True)
    second = jnp.mean(scaled * normal, axis=-1, keepdims=True)
    return inverse * (scaled - first - normal * second), normal


def fold_rows(values):
    rows, width = values.shape
    return jnp.sum(values.reshape(rows // 8, 8, width), axis=0)


def score_mask():
    row = lax.broadcasted_iota(jnp.int32, (TILE, TILE), 0)
    col = lax.broadcasted_iota(jnp.int32, (TILE, TILE), 1)
    return (row // PAD == col // PAD) & (col <= row)


def row_loop(rows, body, step=TILE):
    def once(index, carry):
        body(pl.ds(pl.multiple_of(index * step, step), step), index)
        return carry

    lax.fori_loop(0, rows // step, once, 0)


def half_loop(count, body):
    def once(index, carry):
        body(index)
        return carry

    lax.fori_loop(0, count, once, 0)


def half(index):
    return pl.ds(pl.multiple_of(index * SEG, SEG), SEG)


def norm_in(x, normed, gain, shift):
    def block(rows, _):
        normal, _inv = norm_stats(x[rows, :].astype(F32))
        normed[rows, :] = (normal * gain + shift).astype(BF)

    row_loop(x.shape[0], block)


def project(source, weights, seg, target):
    def one(m):
        target[:, half(m)] = nn(source[...], flat(weights[seg, m])).astype(BF)

    half_loop(weights.shape[1], one)


def attend(queries, keys, values, probs, mixture):
    mask = score_mask()
    scale = HD ** (-0.5)

    def group(rows, index):
        for head in range(queries.shape[1] // HD):
            cols = slice(head * HD, (head + 1) * HD)
            scores = nt(queries[rows, cols], keys[rows, cols]) * scale
            scores = jnp.where(mask, scores, -1e30)
            powers = jnp.exp(scores - jnp.max(scores, axis=-1, keepdims=True))
            share = powers * (1.0 / jnp.sum(powers, axis=-1, keepdims=True))
            probs[index, head] = share
            mixture[rows, cols] = nn(share.astype(BF), values[rows, cols]).astype(BF)

    row_loop(queries.shape[0], group)


def attend_back(queries, keys, values, probs, grad_mix, grad_q, grad_k, grad_v):
    scale = HD ** (-0.5)

    def group(rows, index):
        for head in range(queries.shape[1] // HD):
            cols = slice(head * HD, (head + 1) * HD)
            share = probs[index, head]
            grad = grad_mix[rows, cols]
            grad_share = nt(grad, values[rows, cols])
            grad_v[rows, cols] = nn(share.T.astype(BF), grad).astype(BF)
            inner = jnp.sum(grad_share * share, axis=-1, keepdims=True)
            grad_scores = share * (grad_share - inner)
            low = grad_scores.astype(BF)
            grad_q[rows, cols] = (nn(low, keys[rows, cols]) * scale).astype(BF)
            turned = grad_scores.T.astype(BF)
            grad_k[rows, cols] = (nn(turned, queries[rows, cols]) * scale).astype(BF)

    row_loop(queries.shape[0], group)


def back_through(source, weights, seg, total, fresh):
    def one(m):
        total[...] += nt(source(m), flat(weights[seg, m]))

    if fresh:
        total[...] = nt(source(0), flat(weights[seg, 0]))
        for m in range(1, weights.shape[1]):
            total[...] += nt(source(m), flat(weights[seg, m]))
    else:
        half_loop(weights.shape[1], one)


def feed_up(normed_two, weights, which, active, slope):
    def one(m):
        hidden = nn(normed_two[...], flat(weights[UPS[which], m]))
        bell = 0.5 + 0.5 * lax.erf(hidden * (0.5**0.5))
        active[which, m] = (hidden * bell).astype(BF)
        density = jnp.exp(-0.5 * hidden * hidden) * 0.3989422804014327
        slope[which, m] = bell + hidden * density

    half_loop(weights.shape[1], one)


def turn(source, target):
    def block(rows, _):
        target[:, rows] = source[rows, :].T

    row_loop(source.shape[0], block)


def weight_grad(turned, right, target, seg):
    def one(m):
        product = nn(turned[...], right(m)).astype(BF)
        target[seg, m] = product.reshape(target.shape[2:])

    half_loop(target.shape[1], one)


class Place:
    def __init__(self, shape):
        self.nz, self.nx, self.ny = shape
        index = lax.axis_index("dp")
        self.core = lax.rem(index, 2)
        chip = lax.div(index, 2)
        self.at = {"z": lax.div(chip, self.nx), "x": lax.rem(chip, self.nx), "y": lax.axis_index("mp")}
        self.count = {"z": self.nz, "x": self.nx, "y": self.ny}

    def device(self, core=None, **moved):
        at = {**self.at, **moved}
        core = self.core if core is None else core
        return ((at["z"] * self.nx + at["x"]) * 2 + core, at["y"])

    def partner(self):
        return self.device(core=1 - self.core)

    def neighbour(self, dim, step):
        return self.device(**{dim: self.at[dim] + step})

    def barrier(self, dims):
        semaphore = pltpu.get_barrier_semaphore()
        pl.semaphore_signal(semaphore, inc=1, device_id=self.partner(), device_id_type=MESH)
        peers = 1
        for dim in dims:
            for step in (1, -1):
                there = self.at[dim] + step
                valid = (there >= 0) & (there < self.count[dim])
                peers = peers + valid.astype(jnp.int32)

                @pl.when(valid)
                def _(dim=dim, step=step):
                    other = self.neighbour(dim, step)
                    pl.semaphore_signal(semaphore, inc=1, device_id=other, device_id_type=MESH)

        pl.semaphore_wait(semaphore, peers)


def link_slots(count, dims):
    return sum(2 * (count[dim] - 1) for dim in dims)


class Gather:
    def __init__(self, place, buffer, axes, order, sems):
        self.place, self.buffer, self.axes, self.order = place, buffer, axes, order
        self.send, self.recv, self.pass_send, self.pass_recv = sems
        self.rounds = [(dim, t) for dim in order for t in range(place.count[dim] - 1)]
        self.slots = {}
        for dim, t in self.rounds:
            for way in (1, -1):
                self.slots[dim, t, way] = len(self.slots)

    def block(self, dim, position, core):
        done = self.order[: self.order.index(dim)] if dim else ""
        index = []
        for axis in self.axes:
            if axis == dim:
                index.append(position)
            elif axis in done:
                index.append(pl.ds(0, self.place.count[axis]))
            else:
                index.append(self.place.at[axis])
        return self.buffer.at[tuple(index) + (core,)]

    def link(self, dim, t, way, position, device):
        block = self.block(dim, position, self.place.core)
        slot = self.slots[dim, t, way]
        return pltpu.make_async_remote_copy(
            block, block, self.send.at[slot], self.recv.at[slot], device_id=device, device_id_type=MESH
        )

    def hand(self, slot, dim, position, core):
        block = self.block(dim, position, core)
        return pltpu.make_async_remote_copy(
            block,
            block,
            self.pass_send.at[slot],
            self.pass_recv.at[slot],
            device_id=self.place.partner(),
            device_id_type=MESH,
        )

    def sends(self, dim, t):
        here, count = self.place.at[dim], self.place.count[dim]
        yield 1, here - t, (here - t >= 0) & (here < count - 1)
        yield -1, here + t, (here + t < count) & (here > 0)

    def arrivals(self, dim, t):
        here, count = self.place.at[dim], self.place.count[dim]
        yield 1, here - 1 - t, here - 1 - t >= 0
        yield -1, here + 1 + t, here + 1 + t < count

    def start(self):
        self.hand(len(self.slots), "", None, self.place.core).start()
        self.send_round(0)

    def send_round(self, number):
        dim, t = self.rounds[number]
        for way, position, valid in self.sends(dim, t):

            @pl.when(valid)
            def _(way=way, position=position):
                self.link(dim, t, way, position, self.place.neighbour(dim, way)).start()

    def advance(self, number):
        dim, t = self.rounds[number - 1]
        for way, position, valid in self.arrivals(dim, t):

            @pl.when(valid)
            def _(way=way, position=position):
                self.link(dim, t, way, position, self.place.partner()).wait_recv()
                self.hand(self.slots[dim, t, way], dim, position, self.place.core).start()

        if number < len(self.rounds):
            self.send_round(number)

    def finish(self):
        other = 1 - self.place.core
        self.hand(len(self.slots), "", None, other).wait_recv()
        for dim, t in self.rounds:
            for way, position, valid in self.arrivals(dim, t):

                @pl.when(valid)
                def _(dim=dim, t=t, way=way, position=position):
                    self.hand(self.slots[dim, t, way], dim, position, other).wait_recv()

    def drain(self):
        self.hand(len(self.slots), "", None, self.place.core).wait_send()
        for dim, t in self.rounds:
            for way, position, valid in self.sends(dim, t):

                @pl.when(valid)
                def _(dim=dim, t=t, way=way, position=position):
                    self.link(dim, t, way, position, self.place.partner()).wait_send()

            for way, position, valid in self.arrivals(dim, t):

                @pl.when(valid)
                def _(dim=dim, t=t, way=way, position=position):
                    self.hand(self.slots[dim, t, way], dim, position, self.place.core).wait_send()


class Scatter:
    def __init__(self, place, mine, axes, order, inbox, hand_box, sems, both=False):
        self.place, self.mine, self.axes, self.order, self.both = place, mine, axes, order, both
        self.inbox, self.hand_box = inbox, hand_box
        self.send, self.recv = sems
        self.rounds = [(dim, t) for dim in order for t in range(place.count[dim] - 1)]
        self.slots = {}
        for dim, t in self.rounds:
            for way in (1, -1):
                self.slots[dim, t, way] = len(self.slots) + 1

    def own(self, index):
        return index + ((() if self.both else (self.place.core,)))

    def hand(self):
        whole = tuple(pl.ds(0, self.place.count[axis]) for axis in self.axes)
        source = self.mine.at[whole] if self.both else self.mine.at[whole + (1 - self.place.core,)]
        return pltpu.make_async_remote_copy(
            source, self.hand_box, self.send.at[0], self.recv.at[0], device_id=self.place.partner(), device_id_type=MESH
        )

    def start(self):
        self.hand().start()

    def take_hand(self):
        self.hand().wait_recv()
        first = self.place.count[self.axes[0]]
        rest = tuple(pl.ds(0, self.place.count[axis]) for axis in self.axes[1:])
        if self.both:
            self.hand().wait_send()
            self.mine[...] = self.mine[...] + self.hand_box[...]
        else:
            for p in range(first):
                for r in range(self.place.count[self.axes[1]]):
                    index = (p, r) + rest[1:]
                    here = self.mine[index + (self.place.core,)].astype(F32)
                    there = self.hand_box[index].astype(F32)
                    self.mine[index + (self.place.core,)] = (here + there).astype(self.mine.dtype)
        self.send_round(0)

    def block(self, dim, position):
        done = self.order[: self.order.index(dim)]
        index = []
        for axis in self.axes:
            if axis == dim:
                index.append(position)
            elif axis in done:
                index.append(self.place.at[axis])
            else:
                index.append(pl.ds(0, self.place.count[axis]))
        return self.own(tuple(index))

    def link(self, dim, t, way, position, device):
        slot = self.slots[dim, t, way]
        return pltpu.make_async_remote_copy(
            self.mine.at[self.block(dim, position)],
            self.inbox[slot],
            self.send.at[slot],
            self.recv.at[slot],
            device_id=device,
            device_id_type=MESH,
        )

    def sends(self, dim, t):
        here, count = self.place.at[dim], self.place.count[dim]
        yield 1, count - 1 - t + here, (t >= here) & (here < count - 1)
        back = count - 1 - here
        yield -1, t - back, (t >= back) & (here > 0)

    def arrivals(self, dim, t):
        here, count = self.place.at[dim], self.place.count[dim]
        yield 1, count - 2 - t + here, (t >= here - 1) & (here > 0)
        back = count - 1 - here
        yield -1, t + 1 - back, (t >= back - 1) & (here < count - 1)

    def send_round(self, number):
        dim, t = self.rounds[number]
        for way, position, valid in self.sends(dim, t):

            @pl.when(valid)
            def _(way=way, position=position):
                self.link(dim, t, way, position, self.place.neighbour(dim, way)).start()

    def advance(self, number):
        dim, t = self.rounds[number - 1]
        for way, position, valid in self.arrivals(dim, t):

            @pl.when(valid)
            def _(way=way, position=position):
                self.link(dim, t, way, position, self.place.partner()).wait_recv()
                index = self.block(dim, position)
                total = self.mine[index].astype(F32) + self.inbox[self.slots[dim, t, way]][...].astype(F32)
                self.mine[index] = total.astype(self.mine.dtype)

        if number < len(self.rounds):
            self.send_round(number)

    def result(self):
        return self.mine[self.own(tuple(self.place.at[axis] for axis in self.axes))]

    def drain(self):
        if not self.both:
            self.hand().wait_send()
        for dim, t in self.rounds:
            for way, position, valid in self.sends(dim, t):

                @pl.when(valid)
                def _(dim=dim, t=t, way=way, position=position):
                    self.link(dim, t, way, position, self.place.partner()).wait_send()


def inbox_shapes(count, axes, order, block):
    shapes, left = [], dict(count)
    for dim in order:
        left.pop(dim)
        for _ in range(2 * (count[dim] - 1)):
            shapes.append(tuple(count[axis] for axis in axes if axis in left) + block)
    return shapes


def read_vectors(vectors, tiles):
    nz, nx = tiles.shape[:2]
    pieces = []
    for z in range(nz):
        for x in range(nx):
            pieces.append(tiles[z, x, 0].astype(F32) + tiles[z, x, 1].astype(F32))
    vectors[...] = jnp.concatenate(pieces, axis=1)[:8]


def forward_stages(x, vectors, g, nrm, q, k, v, probs, mix, res, nrm2, active, slope, block_out):
    gain, shift = vectors[0:1, :], vectors[1:2, :]
    gain_two, shift_two = vectors[2:3, :], vectors[3:4, :]
    norm_in(x, nrm, gain, shift)
    for seg, target in ((Q, q), (K, k), (V, v)):
        project(nrm, g, seg, target)
    attend(q, k, v, probs, mix)
    back_through(lambda m: mix[:, half(m)], g, O, res, True)

    def second(rows, _):
        total = res[rows, :] + x[rows, :].astype(F32)
        res[rows, :] = total
        normal, _inv = norm_stats(total)
        nrm2[rows, :] = (normal * gain_two + shift_two).astype(BF)

    row_loop(x.shape[0], second)
    for which in range(2):
        feed_up(nrm2, g, which, active, slope)


def forward_tail(g, res, active, block_out, total):
    for which in range(2):
        back_through(lambda m, which=which: active[which, m], g, DOWNS[which], total, which == 0)

    def last(rows, _):
        block_out[rows, :] = (res[rows, :] + total[rows, :]).astype(BF)

    row_loop(res.shape[0], last)


def forward_kernel(x, vectors, g, nrm, q, k, v, probs, mix, res, nrm2, active, slope, block_out, total):
    forward_stages(x, vectors, g, nrm, q, k, v, probs, mix, res, nrm2, active, slope, block_out)
    forward_tail(g, res, active, block_out, total)


def gather_kernel(shape, shards, tile, g_out, vectors, g, tiles, send, recv, pass_send, pass_recv, local):
    place = Place(shape)
    segs = shards.shape[0]
    mine = []
    for seg in range(segs):
        spot = g.at[seg, place.at["y"], place.at["z"], place.at["x"], place.core]
        copy = pltpu.make_async_copy(shards.at[seg], spot, local.at[seg])
        copy.start()
        mine.append(copy)
    spot = tiles.at[place.at["z"], place.at["x"], place.core]
    copy = pltpu.make_async_copy(tile, spot, local.at[segs])
    copy.start()
    mine.append(copy)
    place.barrier("zxy")
    runs = []
    for seg in range(segs):
        sems = tuple(sem.at[seg] for sem in (send, recv, pass_send, pass_recv))
        runs.append(Gather(place, g.at[seg], "yzx", ORDERS[seg], sems))
    sems = tuple(sem.at[segs] for sem in (send, recv, pass_send, pass_recv))
    runs.append(Gather(place, tiles, "zx", "zx", sems))
    order = [segs] + list(range(segs))
    for index in order:
        mine[index].wait()
        runs[index].start()
    deepest = max(len(run.rounds) for run in runs)
    for number in range(1, deepest + 1):
        for index in order:
            if number <= len(runs[index].rounds):
                runs[index].advance(number)
    for index in order:
        runs[index].finish()
    copy = pltpu.make_async_copy(g, g_out, local.at[segs + 1])
    copy.start()
    read_vectors(vectors, tiles)
    for index in order:
        runs[index].drain()
    copy.wait()


def fetch(source, target, sems, segs):
    copies = []
    for index, seg in enumerate(segs):
        copy = pltpu.make_async_copy(source.at[seg], target.at[index], sems.at[index])
        copy.start()
        copies.append(copy)
    return copies


def feed_back_kernel(cot, row_weight, vectors, g_all, active, slope, nrm2, res, dw, gres, vec, g, gl, glt, gh, n2t, gn2, sems):
    copies = fetch(g_all, g, sems, DOWNS + UPS)
    gain_two = vectors[2:3, :]

    def first(rows, _):
        gl[rows, :] = (cot[rows, :].astype(F32) * row_weight[rows, :]).astype(BF)

    row_loop(cot.shape[0], first)
    turn(gl, glt)
    turn(nrm2, n2t)
    for which in range(2):
        copies[which].wait()

        def one(m, which=which):
            pulled = nn(gl[...], flat(g[which, m]))
            gh[which, m] = (pulled * slope[which, m]).astype(BF)

        half_loop(g.shape[1], one)
        weight_grad(glt, lambda m, which=which: active[which, m], dw, 2 + which)
    for which in range(2):
        copies[2 + which].wait()
        weight_grad(n2t, lambda m, which=which: gh[which, m], dw, which)
        back_through(lambda m, which=which: gh[which, m], g, 2 + which, gn2, which == 0)
    vec[...] = jnp.zeros_like(vec)

    def last(rows, _):
        grad = gn2[rows, :]
        pulled, normal = norm_pull(grad, res[rows, :], gain_two)
        vec[0] += fold_rows(grad * normal)
        vec[1] += fold_rows(grad)
        gres[rows, :] = cot[rows, :].astype(F32) * row_weight[rows, :] + pulled

    row_loop(cot.shape[0], last)


def attn_back_kernel(
    gres, x, vectors, g_all, mix, probs, q, k, v, nrm, dw, gtok, vec, g, gal, galt, gm, gq, gk, gv, nrmt, gn, sems
):
    copies = fetch(g_all, g, sems, (O, Q, K, V))
    gain = vectors[0:1, :]

    def first(rows, _):
        gal[rows, :] = gres[rows, :].astype(BF)

    row_loop(x.shape[0], first)
    turn(gal, galt)
    turn(nrm, nrmt)
    copies[0].wait()
    project(gal, g, 0, gm)
    weight_grad(galt, lambda m: mix[:, half(m)], dw, 3)
    attend_back(q, k, v, probs, gm, gq, gk, gv)
    for seg, grad in ((0, gq), (1, gk), (2, gv)):
        copies[1 + seg].wait()
        weight_grad(nrmt, lambda m, grad=grad: grad[:, half(m)], dw, seg)
        back_through(lambda m, grad=grad: grad[:, half(m)], g, 1 + seg, gn, seg == 0)
    vec[...] = jnp.zeros_like(vec)

    def last(rows, _):
        grad = gn[rows, :]
        pulled, normal = norm_pull(grad, x[rows, :].astype(F32), gain)
        vec[0] += fold_rows(grad * normal)
        vec[1] += fold_rows(grad)
        gtok[rows, :] = gres[rows, :] + pulled

    row_loop(x.shape[0], last)


def vector_tiles(tiles, vec_a, vec_f):
    tiles[...] = jnp.zeros_like(tiles)
    nz, nx = tiles.shape[:2]
    for line, (source, part) in enumerate(((vec_a, 0), (vec_a, 1), (vec_f, 0), (vec_f, 1))):
        row = jnp.sum(source[part], axis=0, keepdims=True)
        for z in range(nz):
            for x in range(nx):
                chip = z * nx + x
                tiles[z, x, line : line + 1, :] = row[:, chip * 128 : (chip + 1) * 128]


def scatter_kernel(shape, plan, dw_a, dw_f, vec_a, vec_f, *refs):
    outs, vec_out = refs[:6], refs[6]
    dw, tiles, hands, vec_hand, ybox, local, send, recv, ysem = refs[7:16]
    boxes = refs[16:]
    place = Place(shape)
    loads = []
    for seg in (D0, D1, U0, U1, O, Q, K, V):
        source = dw_a.at[seg] if seg < 4 else dw_f.at[seg - 4]
        copy = pltpu.make_async_copy(source, dw.at[seg], local.at[seg])
        copy.start()
        loads.append((seg, copy))
    vector_tiles(tiles, vec_a, vec_f)
    place.barrier("zxy")
    segs = dw.shape[0]
    runs, start = {}, 0
    for seg in range(segs + 1):
        order = ORDERS[seg][::-1] if seg < segs else "zx"
        sems = (send.at[seg], recv.at[seg])
        if seg < segs:
            run = Scatter(place, dw.at[seg], "yzx", order, {}, hands.at[seg], sems)
        else:
            run = Scatter(place, tiles, "zx", "zx", {}, vec_hand, sems, both=True)
        for slot in range(1, len(run.slots) + 1):
            run.inbox[slot] = boxes[start + slot - 1]
        start += len(run.slots)
        runs[seg] = run
    runs[segs].start()
    line = [segs]
    for seg, copy in loads:
        copy.wait()
        runs[seg].start()
        line.append(seg)
    for index in line:
        runs[index].take_hand()
    deepest = max(len(run.rounds) for run in runs.values())
    for number in range(1, deepest + 1):
        for index in line:
            if number <= len(runs[index].rounds):
                runs[index].advance(number)
    here = tiles.at[place.at["z"], place.at["x"]]
    other = place.device(y=1 - place.at["y"])
    copy = pltpu.make_async_remote_copy(here, ybox, ysem.at[0], ysem.at[1], device_id=other, device_id_type=MESH)
    copy.start()
    for seg in range(4):
        outs[seg][...] = runs[seg].result().astype(F32)
    for which in range(2):
        outs[4][:, which * SEG : (which + 1) * SEG] = runs[UPS[which]].result().astype(F32)
        outs[5][:, which * SEG : (which + 1) * SEG] = runs[DOWNS[which]].result().astype(F32)
    copy.wait()
    vec_out[...] = tiles[place.at["z"], place.at["x"]] + ybox[...]
    for index in line:
        runs[index].drain()


def shape_of(shape, dtype):
    return jax.ShapeDtypeStruct(shape, dtype)


IN_VMEM = pl.BlockSpec(memory_space=pltpu.VMEM)
ANYWHERE = pl.BlockSpec(memory_space=pl.ANY)


def call(body, outs, ins, out_specs, scratch, name, collective=None):
    params = {"vmem_limit_bytes": VMEM_LIMIT}
    if collective is not None:
        params.update(collective_id=collective, has_side_effects=True)
    return pl.pallas_call(
        body,
        out_shape=outs,
        in_specs=ins,
        out_specs=out_specs,
        scratch_shapes=scratch,
        compiler_params=pltpu.CompilerParams(**params),
        name=name,
    )


def gather_weights(shape, shards, tile):
    nz, nx, ny = shape
    segs, rows, cols = shards.shape
    full = (segs, ny, nz, nx, 2, rows, cols)
    count = {"z": nz, "x": nx, "y": ny}
    slots = link_slots(count, "zxy")
    dma = pltpu.SemaphoreType.DMA
    scratch = [
        pltpu.VMEM(full, BF),
        pltpu.VMEM((nz, nx, 2) + tile.shape, BF),
        dma((segs + 1, slots)),
        dma((segs + 1, slots)),
        dma((segs + 1, slots + 1)),
        dma((segs + 1, slots + 1)),
        dma((segs + 2,)),
    ]
    outs = (shape_of(full, BF), shape_of((8, nz * nx * 128), F32))
    return call(
        functools.partial(gather_kernel, shape), outs, [IN_VMEM] * 2, (ANYWHERE, IN_VMEM), scratch, "gather_weights", 0
    )(shards, tile)


def forward(x, vectors, g):
    rows, width = x.shape
    heads, groups = width // HD, rows // TILE
    wide = (2, g.shape[1], rows, SEG)
    low = shape_of((rows, width), BF)
    outs = (
        low,
        low,
        low,
        low,
        shape_of((groups, heads, TILE, TILE), F32),
        low,
        shape_of((rows, width), F32),
        low,
        shape_of(wide, BF),
        shape_of(wide, F32),
        low,
    )
    scratch = [pltpu.VMEM((rows, width), F32)]
    return call(forward_kernel, outs, [IN_VMEM] * 3, (IN_VMEM,) * len(outs), scratch, "forward")(x, vectors, g)


def feed_back(cot, row_weight, vectors, g, active, slope, nrm2, res):
    rows, width = cot.shape
    part = (4,) + g.shape[1:]
    outs = (shape_of(part, BF), shape_of((rows, width), F32), shape_of((2, 8, width), F32))
    low = pltpu.VMEM((rows, width), BF)
    scratch = [
        pltpu.VMEM(part, BF),
        low,
        pltpu.VMEM((width, rows), BF),
        pltpu.VMEM(active.shape, BF),
        pltpu.VMEM((width, rows), BF),
        pltpu.VMEM((rows, width), F32),
        pltpu.SemaphoreType.DMA((4,)),
    ]
    ins = [IN_VMEM] * 8
    ins[3] = ANYWHERE
    return call(feed_back_kernel, outs, ins, (IN_VMEM,) * 3, scratch, "feed_back")(
        cot, row_weight, vectors, g, active, slope, nrm2, res
    )


def attn_back(gres, x, vectors, g, mix, probs, q, k, v, nrm):
    rows, width = x.shape
    part = (4,) + g.shape[1:]
    outs = (shape_of(part, BF), shape_of((rows, width), F32), shape_of((2, 8, width), F32))
    low = pltpu.VMEM((rows, width), BF)
    turned = pltpu.VMEM((width, rows), BF)
    scratch = [
        pltpu.VMEM(part, BF),
        low,
        turned,
        low,
        low,
        low,
        low,
        turned,
        pltpu.VMEM((rows, width), F32),
        pltpu.SemaphoreType.DMA((4,)),
    ]
    ins = [IN_VMEM] * 10
    ins[3] = ANYWHERE
    return call(attn_back_kernel, outs, ins, (IN_VMEM,) * 3, scratch, "attn_back")(
        gres, x, vectors, g, mix, probs, q, k, v, nrm
    )


def scatter_grads(shape, dw_a, dw_f, vec_a, vec_f):
    nz, nx, ny = shape
    rows, cols = dw_a.shape[-2:]
    segs = 8
    count = {"z": nz, "x": nx, "y": ny}
    slots = link_slots(count, "zxy")
    dma = pltpu.SemaphoreType.DMA
    full = (segs,) + dw_a.shape[1:]
    scratch = [
        pltpu.VMEM(full, BF),
        pltpu.VMEM((nz, nx, 8, 128), F32),
        pltpu.VMEM((segs, ny, nz, nx, rows, cols), BF),
        pltpu.VMEM((nz, nx, 8, 128), F32),
        pltpu.VMEM((8, 128), F32),
        dma((segs,)),
        dma((segs + 1, slots + 1)),
        dma((segs + 1, slots + 1)),
        dma((2,)),
    ]
    for seg in range(segs):
        scratch += [pltpu.VMEM(s, BF) for s in inbox_shapes(count, "yzx", ORDERS[seg][::-1], (rows, cols))]
    scratch += [pltpu.VMEM(s, F32) for s in inbox_shapes({"z": nz, "x": nx}, "zx", "zx", (8, 128))]
    small, large = shape_of((rows, cols), F32), shape_of((rows, 2 * cols), F32)
    outs = (small, small, small, small, large, large, shape_of((8, 128), F32))
    return call(
        functools.partial(scatter_kernel, shape, None),
        outs,
        [ANYWHERE, ANYWHERE, IN_VMEM, IN_VMEM],
        (IN_VMEM,) * 7,
        scratch,
        "scatter_grads",
        1,
    )(dw_a, dw_f, vec_a, vec_f)


def chip_grid(chips):
    nx = 1
    while (nx * 2) ** 2 <= chips:
        nx *= 2
    return chips // nx, nx


def body(counts_of, tokens, cotangent, domain_ids, domain_counts, *params):
    weights, norms = params[:6], params[6:]
    n_dp, n_mp = counts_of
    micro = tokens.shape[0] // n_mp
    y = lax.axis_index("mp")
    dp = lax.axis_index("dp")

    def mine(array):
        return lax.dynamic_slice_in_dim(array, y * micro, micro, 0)

    counts_real = domain_counts.astype(F32)
    mean_count = jnp.mean(counts_real)
    kinds = jnp.arange(counts_real.shape[0], dtype=jnp.int32)
    ids = mine(domain_ids)
    matches = (ids[:, :, None] == kinds).astype(F32)
    series_counts = jnp.sum(matches * counts_real, axis=-1)
    series_weight = 2.0 * mean_count / (mean_count + series_counts)
    series, patches, width = ids.shape[1], tokens.shape[2], tokens.shape[3]
    rows = micro * series * PAD
    row_weight = jnp.broadcast_to(series_weight[:, :, None], (micro, series, PAD)).reshape(rows, 1)

    def padded(array):
        return jnp.pad(mine(array), ((0, 0), (0, 0), (0, PAD - patches), (0, 0))).reshape(rows, width)

    x, cot = padded(tokens), padded(cotangent)
    wq, wk, wv, wo, wu, wd = weights
    shards = jnp.stack((wq, wk, wv, wo, wu[:, :SEG], wu[:, SEG:], wd[:, :SEG], wd[:, SEG:]))
    linked = shards.shape[1] % 16 == 0 and n_dp % 4 == 0 and shards.shape[1] * n_dp == width
    share = width // n_dp
    if linked:
        shape = chip_grid(n_dp // 2) + (n_mp,)
        core = lax.rem(dp, 2)
        tile = jnp.stack(norms)
        tile = jnp.where(core == 0, jnp.pad(tile, ((0, 12), (0, share))), jnp.pad(tile, ((0, 12), (share, 0))))
        g, vectors = gather_weights(shape, shards, tile)
    else:
        g = lax.all_gather(lax.all_gather(shards, "dp", axis=1, tiled=True), "mp", axis=1)
        vectors = lax.all_gather(jnp.stack(norms), "dp", axis=1, tiled=True).astype(F32)
        vectors = jnp.pad(vectors, ((0, 4), (0, 0)))
    nrm, q, k, v, probs, mix, res, nrm2, active, slope, block_out = forward(x, vectors, g)
    dw_f, gres, vec_f = feed_back(cot, row_weight, vectors, g, active, slope, nrm2, res)
    dw_a, gtok, vec_a = attn_back(gres, x, vectors, g, mix, probs, q, k, v, nrm)
    if linked:
        grads = scatter_grads(shape, dw_a, dw_f, vec_a, vec_f)
        grads, vec = list(grads[:6]), grads[6]
        vec = lax.dynamic_slice(vec, (0, core * share), (4, share))
    else:
        dw = jnp.concatenate((dw_a, dw_f)).astype(F32)
        dw = lax.psum_scatter(lax.psum_scatter(dw, "mp", scatter_dimension=1), "dp", scatter_dimension=1, tiled=True)
        grads = [dw[0], dw[1], dw[2], dw[3]]
        grads += [jnp.concatenate((dw[a], dw[b]), axis=1) for a, b in (UPS, DOWNS)]
        vec = jnp.concatenate((jnp.sum(vec_a, axis=1), jnp.sum(vec_f, axis=1)))
        vec = lax.psum_scatter(lax.psum(vec, "mp"), "dp", scatter_dimension=1, tiled=True)

    def both_halves(array):
        own = array.reshape(micro, series, PAD, width)[:, :, :patches]
        whole = jnp.zeros((micro * n_mp,) + own.shape[1:], own.dtype)
        whole = lax.dynamic_update_slice_in_dim(whole, own, y * micro, 0)
        piece, at = own, y
        for _ in range(n_mp - 1):
            piece = lax.ppermute(piece, "mp", [(i, (i + 1) % n_mp) for i in range(n_mp)])
            at = lax.rem(at + n_mp - 1, n_mp)
            whole = lax.dynamic_update_slice_in_dim(whole, piece, at * micro, 0)
        return whole

    out = both_halves(block_out)
    grad_tokens = both_halves(gtok)
    return (out, grad_tokens, *grads, vec[0], vec[1], vec[2], vec[3])


def solution(mesh):
    rows, matrix, vector = P(None, "dp", None, None), P("dp", "mp"), P("dp")
    in_specs = (rows, rows, P(None, "dp"), P()) + (matrix,) * 6 + (vector,) * 4
    out_specs = (rows, rows) + (matrix,) * 6 + (vector,) * 4
    run = functools.partial(body, (mesh.shape["dp"], mesh.shape["mp"]))
    return jax.shard_map(run, mesh=mesh, in_specs=in_specs, out_specs=out_specs, check_vma=False)
```

```python
import functools

import jax
import jax.numpy as jnp
from jax import lax
from jax.experimental import pallas as pl
from jax.experimental.pallas import tpu as pltpu
from jax.sharding import PartitionSpec as P

BF = jnp.bfloat16
F32 = jnp.float32
HD = 128
SEG = 512
TILE = 128
PAD = 16
EPS = 1e-05
MESH = pl.DeviceIdType.MESH
VMEM_LIMIT = 62 * 1024 * 1024

Q, K, V, O, U0, U1, D0, D1 = range(8)
UPS = (U0, U1)
DOWNS = (D0, D1)
ORDERS = ("zxy", "zyx", "xyz", "zxy", "zyx", "xyz", "zxy", "zyx")
BACK_ORDERS = ("xzy", "xyz", "zxy", "xzy", "yxz", "xzy", "yxz", "xzy")


def nn(a, b):
    return lax.dot_general(a, b, (((1,), (0,)), ((), ())), preferred_element_type=F32)


def nt(a, b):
    return lax.dot_general(a, b, (((1,), (1,)), ((), ())), preferred_element_type=F32)


def flat(value):
    return value.reshape(-1, value.shape[-1])


def norm_stats(values):
    mean = jnp.mean(values, axis=-1, keepdims=True)
    center = values - mean
    inverse = lax.rsqrt(jnp.mean(center * center, axis=-1, keepdims=True) + EPS)
    return center * inverse, inverse


def norm_pull(grad, values, gain):
    normal, inverse = norm_stats(values)
    scaled = grad * gain
    first = jnp.mean(scaled, axis=-1, keepdims=True)
    second = jnp.mean(scaled * normal, axis=-1, keepdims=True)
    return inverse * (scaled - first - normal * second), normal


def fold_rows(values):
    rows, width = values.shape
    return jnp.sum(values.reshape(rows // 8, 8, width), axis=0)


def score_mask():
    row = lax.broadcasted_iota(jnp.int32, (TILE, TILE), 0)
    col = lax.broadcasted_iota(jnp.int32, (TILE, TILE), 1)
    return (row // PAD == col // PAD) & (col <= row)


def row_loop(rows, body, step=TILE):
    def once(index, carry):
        body(pl.ds(pl.multiple_of(index * step, step), step), index)
        return carry

    lax.fori_loop(0, rows // step, once, 0)


def half_loop(count, body):
    def once(index, carry):
        body(index)
        return carry

    lax.fori_loop(0, count, once, 0)


def half(index):
    return pl.ds(pl.multiple_of(index * SEG, SEG), SEG)


def norm_in(x, normed, gain, shift):
    def block(rows, _):
        normal, _inv = norm_stats(x[rows, :].astype(F32))
        normed[rows, :] = (normal * gain + shift).astype(BF)

    row_loop(x.shape[0], block)


def project(source, weights, seg, target):
    def one(m):
        target[:, half(m)] = nn(source[...], flat(weights[seg, m])).astype(BF)

    half_loop(weights.shape[1], one)


def attend(queries, keys, values, probs, mixture):
    mask = score_mask()
    scale = HD ** (-0.5)

    def group(rows, index):
        for head in range(queries.shape[1] // HD):
            cols = slice(head * HD, (head + 1) * HD)
            scores = nt(queries[rows, cols], keys[rows, cols]) * scale
            scores = jnp.where(mask, scores, -1e30)
            powers = jnp.exp(scores - jnp.max(scores, axis=-1, keepdims=True))
            share = powers * (1.0 / jnp.sum(powers, axis=-1, keepdims=True))
            probs[index, head] = share
            mixture[rows, cols] = nn(share.astype(BF), values[rows, cols]).astype(BF)

    row_loop(queries.shape[0], group)


def attend_back(queries, keys, values, probs, grad_mix, grad_q, grad_k, grad_v):
    scale = HD ** (-0.5)

    def group(rows, index):
        for head in range(queries.shape[1] // HD):
            cols = slice(head * HD, (head + 1) * HD)
            share = probs[index, head]
            grad = grad_mix[rows, cols]
            grad_share = nt(grad, values[rows, cols])
            grad_v[rows, cols] = nn(share.T.astype(BF), grad).astype(BF)
            inner = jnp.sum(grad_share * share, axis=-1, keepdims=True)
            grad_scores = share * (grad_share - inner)
            low = grad_scores.astype(BF)
            grad_q[rows, cols] = (nn(low, keys[rows, cols]) * scale).astype(BF)
            turned = grad_scores.T.astype(BF)
            grad_k[rows, cols] = (nn(turned, queries[rows, cols]) * scale).astype(BF)

    row_loop(queries.shape[0], group)


def back_through(source, weights, seg, total, fresh):
    def one(m):
        total[...] += nt(source(m), flat(weights[seg, m]))

    if fresh:
        total[...] = nt(source(0), flat(weights[seg, 0]))
        for m in range(1, weights.shape[1]):
            total[...] += nt(source(m), flat(weights[seg, m]))
    else:
        half_loop(weights.shape[1], one)


def feed_up(normed_two, weights, which, active, slope):
    def one(m):
        hidden = nn(normed_two[...], flat(weights[UPS[which], m]))
        bell = 0.5 + 0.5 * lax.erf(hidden * (0.5**0.5))
        active[which, m] = (hidden * bell).astype(BF)
        density = jnp.exp(-0.5 * hidden * hidden) * 0.3989422804014327
        slope[which, m] = bell + hidden * density

    half_loop(weights.shape[1], one)


def turn(source, target):
    def block(rows, _):
        target[:, rows] = source[rows, :].T

    row_loop(source.shape[0], block)


def weight_grad(turned, right, target, seg):
    def one(m):
        product = nn(turned[...], right(m)).astype(BF)
        target[seg, m] = product.reshape(target.shape[2:])

    half_loop(target.shape[1], one)


class Place:
    def __init__(self, shape):
        self.nz, self.nx, self.ny = shape
        index = lax.axis_index("dp")
        self.core = lax.rem(index, 2)
        chip = lax.div(index, 2)
        self.at = {"z": lax.div(chip, self.nx), "x": lax.rem(chip, self.nx), "y": lax.axis_index("mp")}
        self.count = {"z": self.nz, "x": self.nx, "y": self.ny}

    def device(self, core=None, **moved):
        at = {**self.at, **moved}
        core = self.core if core is None else core
        return ((at["z"] * self.nx + at["x"]) * 2 + core, at["y"])

    def partner(self):
        return self.device(core=1 - self.core)

    def neighbour(self, dim, step):
        return self.device(**{dim: self.at[dim] + step})

    def barrier(self, dims):
        semaphore = pltpu.get_barrier_semaphore()
        pl.semaphore_signal(semaphore, inc=1, device_id=self.partner(), device_id_type=MESH)
        peers = 1
        for dim in dims:
            for step in (1, -1):
                there = self.at[dim] + step
                valid = (there >= 0) & (there < self.count[dim])
                peers = peers + valid.astype(jnp.int32)

                @pl.when(valid)
                def _(dim=dim, step=step):
                    other = self.neighbour(dim, step)
                    pl.semaphore_signal(semaphore, inc=1, device_id=other, device_id_type=MESH)

        pl.semaphore_wait(semaphore, peers)


def link_slots(count, dims):
    return sum(2 * (count[dim] - 1) for dim in dims)


class Gather:
    def __init__(self, place, buffer, axes, order, sems):
        self.place, self.buffer, self.axes, self.order = place, buffer, axes, order
        self.send, self.recv, self.pass_send, self.pass_recv = sems
        self.rounds = [(dim, t) for dim in order for t in range(place.count[dim] - 1)]
        self.slots = {}
        for dim, t in self.rounds:
            for way in (1, -1):
                self.slots[dim, t, way] = len(self.slots)

    def block(self, dim, position, core):
        done = self.order[: self.order.index(dim)] if dim else ""
        index = []
        for axis in self.axes:
            if axis == dim:
                index.append(position)
            elif axis in done:
                index.append(pl.ds(0, self.place.count[axis]))
            else:
                index.append(self.place.at[axis])
        return self.buffer.at[tuple(index) + (core,)]

    def link(self, dim, t, way, position, device):
        block = self.block(dim, position, self.place.core)
        slot = self.slots[dim, t, way]
        return pltpu.make_async_remote_copy(
            block, block, self.send.at[slot], self.recv.at[slot], device_id=device, device_id_type=MESH
        )

    def hand(self, slot, dim, position, core):
        block = self.block(dim, position, core)
        return pltpu.make_async_remote_copy(
            block,
            block,
            self.pass_send.at[slot],
            self.pass_recv.at[slot],
            device_id=self.place.partner(),
            device_id_type=MESH,
        )

    def sends(self, dim, t):
        here, count = self.place.at[dim], self.place.count[dim]
        yield 1, here - t, (here - t >= 0) & (here < count - 1)
        yield -1, here + t, (here + t < count) & (here > 0)

    def arrivals(self, dim, t):
        here, count = self.place.at[dim], self.place.count[dim]
        yield 1, here - 1 - t, here - 1 - t >= 0
        yield -1, here + 1 + t, here + 1 + t < count

    def start(self):
        self.hand(len(self.slots), "", None, self.place.core).start()
        self.send_round(0)

    def send_round(self, number):
        dim, t = self.rounds[number]
        for way, position, valid in self.sends(dim, t):

            @pl.when(valid)
            def _(way=way, position=position):
                self.link(dim, t, way, position, self.place.neighbour(dim, way)).start()

    def advance(self, number):
        dim, t = self.rounds[number - 1]
        for way, position, valid in self.arrivals(dim, t):

            @pl.when(valid)
            def _(way=way, position=position):
                self.link(dim, t, way, position, self.place.partner()).wait_recv()
                self.hand(self.slots[dim, t, way], dim, position, self.place.core).start()

        if number < len(self.rounds):
            self.send_round(number)

    def finish(self):
        other = 1 - self.place.core
        self.hand(len(self.slots), "", None, other).wait_recv()
        for dim, t in self.rounds:
            for way, position, valid in self.arrivals(dim, t):

                @pl.when(valid)
                def _(dim=dim, t=t, way=way, position=position):
                    self.hand(self.slots[dim, t, way], dim, position, other).wait_recv()

    def drain(self):
        self.hand(len(self.slots), "", None, self.place.core).wait_send()
        for dim, t in self.rounds:
            for way, position, valid in self.sends(dim, t):

                @pl.when(valid)
                def _(dim=dim, t=t, way=way, position=position):
                    self.link(dim, t, way, position, self.place.partner()).wait_send()

            for way, position, valid in self.arrivals(dim, t):

                @pl.when(valid)
                def _(dim=dim, t=t, way=way, position=position):
                    self.hand(self.slots[dim, t, way], dim, position, self.place.core).wait_send()


class Scatter:
    def __init__(self, place, mine, axes, order, inbox, hand_box, sems, both=False):
        self.place, self.mine, self.axes, self.order, self.both = place, mine, axes, order, both
        self.inbox, self.hand_box = inbox, hand_box
        self.send, self.recv = sems
        self.rounds = [(dim, t) for dim in order for t in range(place.count[dim] - 1)]
        self.slots = {}
        for dim, t in self.rounds:
            for way in (1, -1):
                self.slots[dim, t, way] = len(self.slots) + 1

    def own(self, index):
        return index + ((() if self.both else (self.place.core,)))

    def hand(self):
        whole = tuple(pl.ds(0, self.place.count[axis]) for axis in self.axes)
        source = self.mine.at[whole] if self.both else self.mine.at[whole + (1 - self.place.core,)]
        return pltpu.make_async_remote_copy(
            source, self.hand_box, self.send.at[0], self.recv.at[0], device_id=self.place.partner(), device_id_type=MESH
        )

    def start(self):
        self.hand().start()

    def take_hand(self):
        self.hand().wait_recv()
        first = self.place.count[self.axes[0]]
        rest = tuple(pl.ds(0, self.place.count[axis]) for axis in self.axes[1:])
        if self.both:
            self.hand().wait_send()
            self.mine[...] = self.mine[...] + self.hand_box[...]
        else:
            for p in range(first):
                for r in range(self.place.count[self.axes[1]]):
                    index = (p, r) + rest[1:]
                    here = self.mine[index + (self.place.core,)].astype(F32)
                    there = self.hand_box[index].astype(F32)
                    self.mine[index + (self.place.core,)] = (here + there).astype(self.mine.dtype)
        self.send_round(0)

    def block(self, dim, position):
        done = self.order[: self.order.index(dim)]
        index = []
        for axis in self.axes:
            if axis == dim:
                index.append(position)
            elif axis in done:
                index.append(self.place.at[axis])
            else:
                index.append(pl.ds(0, self.place.count[axis]))
        return self.own(tuple(index))

    def link(self, dim, t, way, position, device):
        slot = self.slots[dim, t, way]
        return pltpu.make_async_remote_copy(
            self.mine.at[self.block(dim, position)],
            self.inbox[slot],
            self.send.at[slot],
            self.recv.at[slot],
            device_id=device,
            device_id_type=MESH,
        )

    def sends(self, dim, t):
        here, count = self.place.at[dim], self.place.count[dim]
        yield 1, count - 1 - t + here, (t >= here) & (here < count - 1)
        back = count - 1 - here
        yield -1, t - back, (t >= back) & (here > 0)

    def arrivals(self, dim, t):
        here, count = self.place.at[dim], self.place.count[dim]
        yield 1, count - 2 - t + here, (t >= here - 1) & (here > 0)
        back = count - 1 - here
        yield -1, t + 1 - back, (t >= back - 1) & (here < count - 1)

    def send_round(self, number):
        dim, t = self.rounds[number]
        for way, position, valid in self.sends(dim, t):

            @pl.when(valid)
            def _(way=way, position=position):
                self.link(dim, t, way, position, self.place.neighbour(dim, way)).start()

    def advance(self, number):
        dim, t = self.rounds[number - 1]
        for way, position, valid in self.arrivals(dim, t):

            @pl.when(valid)
            def _(way=way, position=position):
                self.link(dim, t, way, position, self.place.partner()).wait_recv()
                index = self.block(dim, position)
                total = self.mine[index].astype(F32) + self.inbox[self.slots[dim, t, way]][...].astype(F32)
                self.mine[index] = total.astype(self.mine.dtype)

        if number < len(self.rounds):
            self.send_round(number)

    def result(self):
        return self.mine[self.own(tuple(self.place.at[axis] for axis in self.axes))]

    def drain(self):
        if not self.both:
            self.hand().wait_send()
        for dim, t in self.rounds:
            for way, position, valid in self.sends(dim, t):

                @pl.when(valid)
                def _(dim=dim, t=t, way=way, position=position):
                    self.link(dim, t, way, position, self.place.partner()).wait_send()


def inbox_shapes(count, axes, order, block):
    shapes, left = [], dict(count)
    for dim in order:
        left.pop(dim)
        for _ in range(2 * (count[dim] - 1)):
            shapes.append(tuple(count[axis] for axis in axes if axis in left) + block)
    return shapes


def read_vectors(vectors, tiles):
    nz, nx = tiles.shape[:2]
    pieces = []
    for z in range(nz):
        for x in range(nx):
            pieces.append(tiles[z, x, 0].astype(F32) + tiles[z, x, 1].astype(F32))
    vectors[...] = jnp.concatenate(pieces, axis=1)[:8]


def forward_stages(x, vectors, g, nrm, q, k, v, probs, mix, res, nrm2, active, slope, block_out):
    gain, shift = vectors[0:1, :], vectors[1:2, :]
    gain_two, shift_two = vectors[2:3, :], vectors[3:4, :]
    norm_in(x, nrm, gain, shift)
    for seg, target in ((Q, q), (K, k), (V, v)):
        project(nrm, g, seg, target)
    attend(q, k, v, probs, mix)
    back_through(lambda m: mix[:, half(m)], g, O, res, True)

    def second(rows, _):
        total = res[rows, :] + x[rows, :].astype(F32)
        res[rows, :] = total
        normal, _inv = norm_stats(total)
        nrm2[rows, :] = (normal * gain_two + shift_two).astype(BF)

    row_loop(x.shape[0], second)
    for which in range(2):
        feed_up(nrm2, g, which, active, slope)


def forward_tail(g, res, active, block_out, total):
    for which in range(2):
        back_through(lambda m, which=which: active[which, m], g, DOWNS[which], total, which == 0)

    def last(rows, _):
        block_out[rows, :] = (res[rows, :] + total[rows, :]).astype(BF)

    row_loop(res.shape[0], last)


def forward_kernel(x, vectors, g, nrm, q, k, v, probs, mix, res, nrm2, active, slope, block_out, total):
    forward_stages(x, vectors, g, nrm, q, k, v, probs, mix, res, nrm2, active, slope, block_out)
    forward_tail(g, res, active, block_out, total)


def gather_kernel(shape, shards, tile, g_out, vectors, g, tiles, send, recv, pass_send, pass_recv, local):
    place = Place(shape)
    segs = shards.shape[0]
    mine = []
    for seg in range(segs):
        spot = g.at[seg, place.at["y"], place.at["z"], place.at["x"], place.core]
        copy = pltpu.make_async_copy(shards.at[seg], spot, local.at[seg])
        copy.start()
        mine.append(copy)
    spot = tiles.at[place.at["z"], place.at["x"], place.core]
    copy = pltpu.make_async_copy(tile, spot, local.at[segs])
    copy.start()
    mine.append(copy)
    place.barrier("zxy")
    runs = []
    for seg in range(segs):
        sems = tuple(sem.at[seg] for sem in (send, recv, pass_send, pass_recv))
        runs.append(Gather(place, g.at[seg], "yzx", ORDERS[seg], sems))
    sems = tuple(sem.at[segs] for sem in (send, recv, pass_send, pass_recv))
    runs.append(Gather(place, tiles, "zx", "zx", sems))
    order = [segs] + list(range(segs))
    for index in order:
        mine[index].wait()
        runs[index].start()
    deepest = max(len(run.rounds) for run in runs)
    for number in range(1, deepest + 1):
        for index in order:
            if number <= len(runs[index].rounds):
                runs[index].advance(number)
    for index in order:
        runs[index].finish()
    copy = pltpu.make_async_copy(g, g_out, local.at[segs + 1])
    copy.start()
    read_vectors(vectors, tiles)
    for index in order:
        runs[index].drain()
    copy.wait()


def fetch(source, target, sems, segs):
    copies = []
    for index, seg in enumerate(segs):
        copy = pltpu.make_async_copy(source.at[seg], target.at[index], sems.at[index])
        copy.start()
        copies.append(copy)
    return copies


def feed_back_kernel(cot, row_weight, vectors, g_all, active, slope, nrm2, res, dw, gres, vec, g, gl, glt, gh, n2t, gn2, sems):
    copies = fetch(g_all, g, sems, DOWNS + UPS)
    gain_two = vectors[2:3, :]

    def first(rows, _):
        gl[rows, :] = (cot[rows, :].astype(F32) * row_weight[rows, :]).astype(BF)

    row_loop(cot.shape[0], first)
    turn(gl, glt)
    turn(nrm2, n2t)
    for which in range(2):
        copies[which].wait()

        def one(m, which=which):
            pulled = nn(gl[...], flat(g[which, m]))
            gh[which, m] = (pulled * slope[which, m]).astype(BF)

        half_loop(g.shape[1], one)
        weight_grad(glt, lambda m, which=which: active[which, m], dw, 2 + which)
    for which in range(2):
        copies[2 + which].wait()
        weight_grad(n2t, lambda m, which=which: gh[which, m], dw, which)
        back_through(lambda m, which=which: gh[which, m], g, 2 + which, gn2, which == 0)
    vec[...] = jnp.zeros_like(vec)

    def last(rows, _):
        grad = gn2[rows, :]
        pulled, normal = norm_pull(grad, res[rows, :], gain_two)
        vec[0] += fold_rows(grad * normal)
        vec[1] += fold_rows(grad)
        gres[rows, :] = cot[rows, :].astype(F32) * row_weight[rows, :] + pulled

    row_loop(cot.shape[0], last)


def attn_back_kernel(
    gres, x, vectors, g_all, mix, probs, q, k, v, nrm, dw, gtok, gtok_low, vec, g, gal, galt, gm, gq, gk, gv, nrmt, gn, sems
):
    copies = fetch(g_all, g, sems, (O, Q, K, V))
    gain = vectors[0:1, :]

    def first(rows, _):
        gal[rows, :] = gres[rows, :].astype(BF)

    row_loop(x.shape[0], first)
    turn(gal, galt)
    turn(nrm, nrmt)
    copies[0].wait()
    project(gal, g, 0, gm)
    weight_grad(galt, lambda m: mix[:, half(m)], dw, 3)
    attend_back(q, k, v, probs, gm, gq, gk, gv)
    for seg, grad in ((0, gq), (1, gk), (2, gv)):
        copies[1 + seg].wait()
        weight_grad(nrmt, lambda m, grad=grad: grad[:, half(m)], dw, seg)
        back_through(lambda m, grad=grad: grad[:, half(m)], g, 1 + seg, gn, seg == 0)
    vec[...] = jnp.zeros_like(vec)

    def last(rows, _):
        grad = gn[rows, :]
        pulled, normal = norm_pull(grad, x[rows, :].astype(F32), gain)
        vec[0] += fold_rows(grad * normal)
        vec[1] += fold_rows(grad)
        total = gres[rows, :] + pulled
        gtok[rows, :] = total
        gtok_low[rows, :] = total.astype(BF)

    row_loop(x.shape[0], last)


def vector_tiles(tiles, vec_a, vec_f):
    tiles[...] = jnp.zeros_like(tiles)
    nz, nx = tiles.shape[:2]
    for line, (source, part) in enumerate(((vec_a, 0), (vec_a, 1), (vec_f, 0), (vec_f, 1))):
        row = jnp.sum(source[part], axis=0, keepdims=True)
        for z in range(nz):
            for x in range(nx):
                chip = z * nx + x
                tiles[z, x, line : line + 1, :] = row[:, chip * 128 : (chip + 1) * 128]


def scatter_kernel(shape, plan, dw_a, dw_f, vec_a, vec_f, *refs):
    outs, vec_out = refs[:6], refs[6]
    dw, tiles, hands, vec_hand, ybox, local, send, recv, ysem = refs[7:16]
    boxes = refs[16:]
    place = Place(shape)
    loads = []
    for seg in (D0, D1, U0, U1, O, Q, K, V):
        source = dw_a.at[seg] if seg < 4 else dw_f.at[seg - 4]
        copy = pltpu.make_async_copy(source, dw.at[seg], local.at[seg])
        copy.start()
        loads.append((seg, copy))
    vector_tiles(tiles, vec_a, vec_f)
    place.barrier("zxy")
    segs = dw.shape[0]
    runs, start = {}, 0
    for seg in range(segs + 1):
        order = BACK_ORDERS[seg] if seg < segs else "zx"
        sems = (send.at[seg], recv.at[seg])
        if seg < segs:
            run = Scatter(place, dw.at[seg], "yzx", order, {}, hands.at[seg], sems)
        else:
            run = Scatter(place, tiles, "zx", "zx", {}, vec_hand, sems, both=True)
        for slot in range(1, len(run.slots) + 1):
            run.inbox[slot] = boxes[start + slot - 1]
        start += len(run.slots)
        runs[seg] = run
    runs[segs].start()
    line = [segs]
    for seg, copy in loads:
        copy.wait()
        runs[seg].start()
        line.append(seg)
    for index in line:
        runs[index].take_hand()
    deepest = max(len(run.rounds) for run in runs.values())
    for number in range(1, deepest + 1):
        for index in line:
            if number <= len(runs[index].rounds):
                runs[index].advance(number)
    here = tiles.at[place.at["z"], place.at["x"]]
    other = place.device(y=1 - place.at["y"])
    copy = pltpu.make_async_remote_copy(here, ybox, ysem.at[0], ysem.at[1], device_id=other, device_id_type=MESH)
    copy.start()
    for seg in range(4):
        outs[seg][...] = runs[seg].result().astype(F32)
    for which in range(2):
        outs[4][:, which * SEG : (which + 1) * SEG] = runs[UPS[which]].result().astype(F32)
        outs[5][:, which * SEG : (which + 1) * SEG] = runs[DOWNS[which]].result().astype(F32)
    copy.wait()
    vec_out[...] = tiles[place.at["z"], place.at["x"]] + ybox[...]
    for index in line:
        runs[index].drain()


def shape_of(shape, dtype):
    return jax.ShapeDtypeStruct(shape, dtype)


IN_VMEM = pl.BlockSpec(memory_space=pltpu.VMEM)
ANYWHERE = pl.BlockSpec(memory_space=pl.ANY)


def call(body, outs, ins, out_specs, scratch, name, collective=None):
    params = {"vmem_limit_bytes": VMEM_LIMIT}
    if collective is not None:
        params.update(collective_id=collective, has_side_effects=True)
    return pl.pallas_call(
        body,
        out_shape=outs,
        in_specs=ins,
        out_specs=out_specs,
        scratch_shapes=scratch,
        compiler_params=pltpu.CompilerParams(**params),
        name=name,
    )


def gather_weights(shape, shards, tile):
    nz, nx, ny = shape
    segs, rows, cols = shards.shape
    full = (segs, ny, nz, nx, 2, rows, cols)
    count = {"z": nz, "x": nx, "y": ny}
    slots = link_slots(count, "zxy")
    dma = pltpu.SemaphoreType.DMA
    scratch = [
        pltpu.VMEM(full, BF),
        pltpu.VMEM((nz, nx, 2) + tile.shape, BF),
        dma((segs + 1, slots)),
        dma((segs + 1, slots)),
        dma((segs + 1, slots + 1)),
        dma((segs + 1, slots + 1)),
        dma((segs + 2,)),
    ]
    outs = (shape_of(full, BF), shape_of((8, nz * nx * 128), F32))
    return call(
        functools.partial(gather_kernel, shape), outs, [IN_VMEM] * 2, (ANYWHERE, IN_VMEM), scratch, "gather_weights", 0
    )(shards, tile)


def forward(x, vectors, g):
    rows, width = x.shape
    heads, groups = width // HD, rows // TILE
    wide = (2, g.shape[1], rows, SEG)
    low = shape_of((rows, width), BF)
    outs = (
        low,
        low,
        low,
        low,
        shape_of((groups, heads, TILE, TILE), F32),
        low,
        shape_of((rows, width), F32),
        low,
        shape_of(wide, BF),
        shape_of(wide, F32),
        low,
    )
    scratch = [pltpu.VMEM((rows, width), F32)]
    return call(forward_kernel, outs, [IN_VMEM] * 3, (IN_VMEM,) * len(outs), scratch, "forward")(x, vectors, g)


def feed_back(cot, row_weight, vectors, g, active, slope, nrm2, res):
    rows, width = cot.shape
    part = (4,) + g.shape[1:]
    outs = (shape_of(part, BF), shape_of((rows, width), F32), shape_of((2, 8, width), F32))
    low = pltpu.VMEM((rows, width), BF)
    scratch = [
        pltpu.VMEM(part, BF),
        low,
        pltpu.VMEM((width, rows), BF),
        pltpu.VMEM(active.shape, BF),
        pltpu.VMEM((width, rows), BF),
        pltpu.VMEM((rows, width), F32),
        pltpu.SemaphoreType.DMA((4,)),
    ]
    ins = [IN_VMEM] * 8
    ins[3] = ANYWHERE
    return call(feed_back_kernel, outs, ins, (IN_VMEM,) * 3, scratch, "feed_back")(
        cot, row_weight, vectors, g, active, slope, nrm2, res
    )


def attn_back(gres, x, vectors, g, mix, probs, q, k, v, nrm):
    rows, width = x.shape
    part = (4,) + g.shape[1:]
    outs = (shape_of(part, BF), shape_of((rows, width), F32), shape_of((rows, width), BF), shape_of((2, 8, width), F32))
    low = pltpu.VMEM((rows, width), BF)
    turned = pltpu.VMEM((width, rows), BF)
    scratch = [
        pltpu.VMEM(part, BF),
        low,
        turned,
        low,
        low,
        low,
        low,
        turned,
        pltpu.VMEM((rows, width), F32),
        pltpu.SemaphoreType.DMA((4,)),
    ]
    ins = [IN_VMEM] * 10
    ins[3] = ANYWHERE
    return call(attn_back_kernel, outs, ins, (IN_VMEM,) * 4, scratch, "attn_back")(
        gres, x, vectors, g, mix, probs, q, k, v, nrm
    )


def scatter_grads(shape, dw_a, dw_f, vec_a, vec_f):
    nz, nx, ny = shape
    rows, cols = dw_a.shape[-2:]
    segs = 8
    count = {"z": nz, "x": nx, "y": ny}
    slots = link_slots(count, "zxy")
    dma = pltpu.SemaphoreType.DMA
    full = (segs,) + dw_a.shape[1:]
    scratch = [
        pltpu.VMEM(full, BF),
        pltpu.VMEM((nz, nx, 8, 128), F32),
        pltpu.VMEM((segs, ny, nz, nx, rows, cols), BF),
        pltpu.VMEM((nz, nx, 8, 128), F32),
        pltpu.VMEM((8, 128), F32),
        dma((segs,)),
        dma((segs + 1, slots + 1)),
        dma((segs + 1, slots + 1)),
        dma((2,)),
    ]
    for seg in range(segs):
        scratch += [pltpu.VMEM(s, BF) for s in inbox_shapes(count, "yzx", BACK_ORDERS[seg], (rows, cols))]
    scratch += [pltpu.VMEM(s, F32) for s in inbox_shapes({"z": nz, "x": nx}, "zx", "zx", (8, 128))]
    small, large = shape_of((rows, cols), F32), shape_of((rows, 2 * cols), F32)
    outs = (small, small, small, small, large, large, shape_of((8, 128), F32))
    return call(
        functools.partial(scatter_kernel, shape, None),
        outs,
        [ANYWHERE, ANYWHERE, IN_VMEM, IN_VMEM],
        (IN_VMEM,) * 7,
        scratch,
        "scatter_grads",
        1,
    )(dw_a, dw_f, vec_a, vec_f)


def chip_grid(chips):
    nx = 1
    while (nx * 2) ** 2 <= chips:
        nx *= 2
    return chips // nx, nx


def body(counts_of, tokens, cotangent, domain_ids, domain_counts, *params):
    weights, norms = params[:6], params[6:]
    n_dp, n_mp = counts_of
    micro = tokens.shape[0] // n_mp
    y = lax.axis_index("mp")
    dp = lax.axis_index("dp")

    def mine(array):
        return lax.dynamic_slice_in_dim(array, y * micro, micro, 0)

    counts_real = domain_counts.astype(F32)
    mean_count = jnp.mean(counts_real)
    kinds = jnp.arange(counts_real.shape[0], dtype=jnp.int32)
    ids = mine(domain_ids)
    matches = (ids[:, :, None] == kinds).astype(F32)
    series_counts = jnp.sum(matches * counts_real, axis=-1)
    series_weight = 2.0 * mean_count / (mean_count + series_counts)
    series, patches, width = ids.shape[1], tokens.shape[2], tokens.shape[3]
    rows = micro * series * PAD
    row_weight = jnp.broadcast_to(series_weight[:, :, None], (micro, series, PAD)).reshape(rows, 1)

    def padded(array):
        return jnp.pad(mine(array), ((0, 0), (0, 0), (0, PAD - patches), (0, 0))).reshape(rows, width)

    x, cot = padded(tokens), padded(cotangent)
    wq, wk, wv, wo, wu, wd = weights
    shards = jnp.stack((wq, wk, wv, wo, wu[:, :SEG], wu[:, SEG:], wd[:, :SEG], wd[:, SEG:]))
    linked = shards.shape[1] % 16 == 0 and n_dp % 4 == 0 and shards.shape[1] * n_dp == width
    share = width // n_dp
    if linked:
        shape = chip_grid(n_dp // 2) + (n_mp,)
        core = lax.rem(dp, 2)
        tile = jnp.stack(norms)
        tile = jnp.where(core == 0, jnp.pad(tile, ((0, 12), (0, share))), jnp.pad(tile, ((0, 12), (share, 0))))
        g, vectors = gather_weights(shape, shards, tile)
    else:
        g = lax.all_gather(lax.all_gather(shards, "dp", axis=1, tiled=True), "mp", axis=1)
        vectors = lax.all_gather(jnp.stack(norms), "dp", axis=1, tiled=True).astype(F32)
        vectors = jnp.pad(vectors, ((0, 4), (0, 0)))
    nrm, q, k, v, probs, mix, res, nrm2, active, slope, block_out = forward(x, vectors, g)
    dw_f, gres, vec_f = feed_back(cot, row_weight, vectors, g, active, slope, nrm2, res)
    dw_a, gtok, gtok_low, vec_a = attn_back(gres, x, vectors, g, mix, probs, q, k, v, nrm)
    if linked:
        grads = scatter_grads(shape, dw_a, dw_f, vec_a, vec_f)
        grads, vec = list(grads[:6]), grads[6]
        vec = lax.dynamic_slice(vec, (0, core * share), (4, share))
    else:
        dw = jnp.concatenate((dw_a, dw_f)).astype(F32)
        dw = lax.psum_scatter(lax.psum_scatter(dw, "mp", scatter_dimension=1), "dp", scatter_dimension=1, tiled=True)
        grads = [dw[0], dw[1], dw[2], dw[3]]
        grads += [jnp.concatenate((dw[a], dw[b]), axis=1) for a, b in (UPS, DOWNS)]
        vec = jnp.concatenate((jnp.sum(vec_a, axis=1), jnp.sum(vec_f, axis=1)))
        vec = lax.psum_scatter(lax.psum(vec, "mp"), "dp", scatter_dimension=1, tiled=True)

    def both_halves(array, low):
        own = array.reshape(micro, series, PAD, width)[:, :, :patches]
        whole = jnp.zeros((micro * n_mp,) + own.shape[1:], own.dtype)
        whole = lax.dynamic_update_slice_in_dim(whole, own, y * micro, 0)
        piece, at = low.reshape(micro, series, PAD, width)[:, :, :patches], y
        for _ in range(n_mp - 1):
            piece = lax.ppermute(piece, "mp", [(i, (i + 1) % n_mp) for i in range(n_mp)])
            at = lax.rem(at + n_mp - 1, n_mp)
            whole = lax.dynamic_update_slice_in_dim(whole, piece.astype(own.dtype), at * micro, 0)
        return whole

    out = both_halves(block_out, block_out)
    grad_tokens = both_halves(gtok, gtok_low)
    return (out, grad_tokens, *grads, vec[0], vec[1], vec[2], vec[3])


def solution(mesh):
    rows, matrix, vector = P(None, "dp", None, None), P("dp", "mp"), P("dp")
    in_specs = (rows, rows, P(None, "dp"), P()) + (matrix,) * 6 + (vector,) * 4
    out_specs = (rows, rows) + (matrix,) * 6 + (vector,) * 4
    run = functools.partial(body, (mesh.shape["dp"], mesh.shape["mp"]))
    return jax.shard_map(run, mesh=mesh, in_specs=in_specs, out_specs=out_specs, check_vma=False)
```

```python
import functools

import jax
import jax.numpy as jnp
from jax import lax
from jax.experimental import pallas as pl
from jax.experimental.pallas import tpu as pltpu
from jax.sharding import PartitionSpec as P

BF = jnp.bfloat16
F32 = jnp.float32
HD = 128
SEG = 512
TILE = 128
PAD = 16
EPS = 1e-05
MESH = pl.DeviceIdType.MESH
VMEM_LIMIT = 62 * 1024 * 1024

Q, K, V, O, U0, U1, D0, D1 = range(8)
UPS = (U0, U1)
DOWNS = (D0, D1)
ORDERS = ("zxy", "zyx", "xyz", "zxy", "zyx", "xyz", "zxy", "zyx")
BACK_ORDERS = ("xzy", "xyz", "zxy", "xzy", "yxz", "xzy", "yxz", "xzy")


def nn(a, b):
    return lax.dot_general(a, b, (((1,), (0,)), ((), ())), preferred_element_type=F32)


def nt(a, b):
    return lax.dot_general(a, b, (((1,), (1,)), ((), ())), preferred_element_type=F32)


def flat(value):
    return value.reshape(-1, value.shape[-1])


def norm_stats(values):
    mean = jnp.mean(values, axis=-1, keepdims=True)
    center = values - mean
    inverse = lax.rsqrt(jnp.mean(center * center, axis=-1, keepdims=True) + EPS)
    return center * inverse, inverse


def norm_pull(grad, values, gain):
    normal, inverse = norm_stats(values)
    scaled = grad * gain
    first = jnp.mean(scaled, axis=-1, keepdims=True)
    second = jnp.mean(scaled * normal, axis=-1, keepdims=True)
    return inverse * (scaled - first - normal * second), normal


def fold_rows(values):
    rows, width = values.shape
    return jnp.sum(values.reshape(rows // 8, 8, width), axis=0)


def score_mask():
    row = lax.broadcasted_iota(jnp.int32, (TILE, TILE), 0)
    col = lax.broadcasted_iota(jnp.int32, (TILE, TILE), 1)
    return (row // PAD == col // PAD) & (col <= row)


def row_loop(rows, body, first=0):
    def once(index, carry):
        body(pl.ds(pl.multiple_of(index * TILE, TILE), TILE), index)
        return carry

    lax.fori_loop(first, first + rows // TILE, once, 0)


def half_loop(count, body):
    def once(index, carry):
        body(index)
        return carry

    lax.fori_loop(0, count, once, 0)


def half(index):
    return pl.ds(pl.multiple_of(index * SEG, SEG), SEG)


def spread_rows(patches, series):
    row = lax.broadcasted_iota(jnp.int32, (series * PAD, patches * series), 0)
    col = lax.broadcasted_iota(jnp.int32, (series * PAD, patches * series), 1)
    hit = (lax.rem(row, PAD) * series + lax.div(row, PAD) == col) & (lax.rem(row, PAD) < patches)
    return jnp.where(hit, 1.0, 0.0).astype(BF)


def gather_rows(patches, series):
    row = lax.broadcasted_iota(jnp.int32, (patches * series, series * PAD), 0)
    col = lax.broadcasted_iota(jnp.int32, (patches * series, series * PAD), 1)
    return jnp.where(lax.rem(row, series) * PAD + lax.div(row, series) == col, 1.0, 0.0).astype(BF)


def to_rows(raw, target):
    micro, patches, series, _ = raw.shape
    matrix = spread_rows(patches, series)
    for part in range(micro):
        target[part * series * PAD : (part + 1) * series * PAD, :] = nn(matrix, flat(raw[part])).astype(BF)


def from_rows(source, raw):
    micro, patches, series, width = raw.shape
    matrix = gather_rows(patches, series)
    for part in range(micro):
        rows = source[part * series * PAD : (part + 1) * series * PAD, :]
        raw[part] = nn(matrix, rows).astype(raw.dtype).reshape(patches, series, width)


def norm_in(x, normed, gain, shift):
    def block(rows, _):
        normal, _inv = norm_stats(x[rows, :].astype(F32))
        normed[rows, :] = (normal * gain + shift).astype(BF)

    row_loop(x.shape[0], block)


def project(source, weights, seg, target):
    def one(m):
        target[:, half(m)] = nn(source[...], flat(weights[seg, m])).astype(BF)

    half_loop(weights.shape[1], one)


def attend(queries, keys, values, probs, mixture, first, count):
    mask = score_mask()
    scale = HD ** (-0.5)

    def group(rows, index):
        for head in range(queries.shape[1] // HD):
            cols = slice(head * HD, (head + 1) * HD)
            scores = nt(queries[rows, cols], keys[rows, cols]) * scale
            scores = jnp.where(mask, scores, -1e30)
            powers = jnp.exp(scores - jnp.max(scores, axis=-1, keepdims=True))
            share = powers * (1.0 / jnp.sum(powers, axis=-1, keepdims=True))
            probs[index, head] = share
            mixture[rows, cols] = nn(share.astype(BF), values[rows, cols]).astype(BF)

    row_loop(count * TILE, group, first)


def attend_back(queries, keys, values, probs, grad_mix, grad_q, grad_k, grad_v):
    scale = HD ** (-0.5)

    def group(rows, index):
        for head in range(queries.shape[1] // HD):
            cols = slice(head * HD, (head + 1) * HD)
            share = probs[index, head]
            grad = grad_mix[rows, cols]
            grad_share = nt(grad, values[rows, cols])
            grad_v[rows, cols] = nn(share.T.astype(BF), grad).astype(BF)
            inner = jnp.sum(grad_share * share, axis=-1, keepdims=True)
            grad_scores = share * (grad_share - inner)
            low = grad_scores.astype(BF)
            grad_q[rows, cols] = (nn(low, keys[rows, cols]) * scale).astype(BF)
            turned = grad_scores.T.astype(BF)
            grad_k[rows, cols] = (nn(turned, queries[rows, cols]) * scale).astype(BF)

    row_loop(queries.shape[0], group)


def back_through(source, weights, seg, total, fresh):
    def one(m):
        total[...] += nt(source(m), flat(weights[seg, m]))

    if fresh:
        total[...] = nt(source(0), flat(weights[seg, 0]))
        for m in range(1, weights.shape[1]):
            total[...] += nt(source(m), flat(weights[seg, m]))
    else:
        half_loop(weights.shape[1], one)


def feed_up(normed_two, weights, which, active, slope):
    def one(m):
        hidden = nn(normed_two[...], flat(weights[UPS[which], m]))
        bell = 0.5 + 0.5 * lax.erf(hidden * (0.5**0.5))
        active[which, m] = (hidden * bell).astype(BF)
        density = jnp.exp(-0.5 * hidden * hidden) * 0.3989422804014327
        slope[which, m] = bell + hidden * density

    half_loop(weights.shape[1], one)


def turn(source, target):
    def block(rows, _):
        target[:, rows] = source[rows, :].T

    row_loop(source.shape[0], block)


def weight_grad(turned, right, target, seg):
    def one(m):
        product = nn(turned[...], right(m)).astype(BF)
        target[seg, m] = product.reshape(target.shape[2:])

    half_loop(target.shape[1], one)


class Place:
    def __init__(self, shape):
        self.nz, self.nx, self.ny = shape
        index = lax.axis_index("dp")
        self.core = lax.rem(index, 2)
        chip = lax.div(index, 2)
        self.at = {"z": lax.div(chip, self.nx), "x": lax.rem(chip, self.nx), "y": lax.axis_index("mp")}
        self.count = {"z": self.nz, "x": self.nx, "y": self.ny}

    def device(self, core=None, **moved):
        at = {**self.at, **moved}
        core = self.core if core is None else core
        return ((at["z"] * self.nx + at["x"]) * 2 + core, at["y"])

    def partner(self):
        return self.device(core=1 - self.core)

    def neighbour(self, dim, step):
        return self.device(**{dim: self.at[dim] + step})

    def barrier(self, dims):
        semaphore = pltpu.get_barrier_semaphore()
        pl.semaphore_signal(semaphore, inc=1, device_id=self.partner(), device_id_type=MESH)
        peers = 1
        for dim in dims:
            for step in (1, -1):
                there = self.at[dim] + step
                valid = (there >= 0) & (there < self.count[dim])
                peers = peers + valid.astype(jnp.int32)

                @pl.when(valid)
                def _(dim=dim, step=step):
                    other = self.neighbour(dim, step)
                    pl.semaphore_signal(semaphore, inc=1, device_id=other, device_id_type=MESH)

        pl.semaphore_wait(semaphore, peers)


def link_slots(count, dims):
    return sum(2 * (count[dim] - 1) for dim in dims)


class Gather:
    def __init__(self, place, buffer, axes, order, sems):
        self.place, self.buffer, self.axes, self.order = place, buffer, axes, order
        self.send, self.recv, self.pass_send, self.pass_recv = sems
        self.rounds = [(dim, t) for dim in order for t in range(place.count[dim] - 1)]
        self.slots = {}
        for dim, t in self.rounds:
            for way in (1, -1):
                self.slots[dim, t, way] = len(self.slots)

    def block(self, dim, position, core):
        done = self.order[: self.order.index(dim)] if dim else ""
        index = []
        for axis in self.axes:
            if axis == dim:
                index.append(position)
            elif axis in done:
                index.append(pl.ds(0, self.place.count[axis]))
            else:
                index.append(self.place.at[axis])
        return self.buffer.at[tuple(index) + (core,)]

    def link(self, dim, t, way, position, device):
        block = self.block(dim, position, self.place.core)
        slot = self.slots[dim, t, way]
        return pltpu.make_async_remote_copy(
            block, block, self.send.at[slot], self.recv.at[slot], device_id=device, device_id_type=MESH
        )

    def hand(self, slot, dim, position, core):
        block = self.block(dim, position, core)
        return pltpu.make_async_remote_copy(
            block,
            block,
            self.pass_send.at[slot],
            self.pass_recv.at[slot],
            device_id=self.place.partner(),
            device_id_type=MESH,
        )

    def sends(self, dim, t):
        here, count = self.place.at[dim], self.place.count[dim]
        yield 1, here - t, (here - t >= 0) & (here < count - 1)
        yield -1, here + t, (here + t < count) & (here > 0)

    def arrivals(self, dim, t):
        here, count = self.place.at[dim], self.place.count[dim]
        yield 1, here - 1 - t, here - 1 - t >= 0
        yield -1, here + 1 + t, here + 1 + t < count

    def start(self):
        self.hand(len(self.slots), "", None, self.place.core).start()
        self.send_round(0)

    def send_round(self, number):
        dim, t = self.rounds[number]
        for way, position, valid in self.sends(dim, t):

            @pl.when(valid)
            def _(way=way, position=position):
                self.link(dim, t, way, position, self.place.neighbour(dim, way)).start()

    def advance(self, number):
        dim, t = self.rounds[number - 1]
        for way, position, valid in self.arrivals(dim, t):

            @pl.when(valid)
            def _(way=way, position=position):
                self.link(dim, t, way, position, self.place.partner()).wait_recv()
                self.hand(self.slots[dim, t, way], dim, position, self.place.core).start()

        if number < len(self.rounds):
            self.send_round(number)

    def finish(self):
        other = 1 - self.place.core
        self.hand(len(self.slots), "", None, other).wait_recv()
        for dim, t in self.rounds:
            for way, position, valid in self.arrivals(dim, t):

                @pl.when(valid)
                def _(dim=dim, t=t, way=way, position=position):
                    self.hand(self.slots[dim, t, way], dim, position, other).wait_recv()

    def drain(self):
        self.hand(len(self.slots), "", None, self.place.core).wait_send()
        for dim, t in self.rounds:
            for way, position, valid in self.sends(dim, t):

                @pl.when(valid)
                def _(dim=dim, t=t, way=way, position=position):
                    self.link(dim, t, way, position, self.place.partner()).wait_send()

            for way, position, valid in self.arrivals(dim, t):

                @pl.when(valid)
                def _(dim=dim, t=t, way=way, position=position):
                    self.hand(self.slots[dim, t, way], dim, position, self.place.core).wait_send()


class Scatter:
    def __init__(self, place, mine, axes, order, inbox, hand_box, sems, both=False):
        self.place, self.mine, self.axes, self.order, self.both = place, mine, axes, order, both
        self.inbox, self.hand_box = inbox, hand_box
        self.send, self.recv = sems
        self.rounds = [(dim, t) for dim in order for t in range(place.count[dim] - 1)]
        self.slots = {}
        for dim, t in self.rounds:
            for way in (1, -1):
                self.slots[dim, t, way] = len(self.slots) + 1

    def own(self, index):
        return index + ((() if self.both else (self.place.core,)))

    def hand(self):
        whole = tuple(pl.ds(0, self.place.count[axis]) for axis in self.axes)
        source = self.mine.at[whole] if self.both else self.mine.at[whole + (1 - self.place.core,)]
        return pltpu.make_async_remote_copy(
            source, self.hand_box, self.send.at[0], self.recv.at[0], device_id=self.place.partner(), device_id_type=MESH
        )

    def start(self):
        self.hand().start()

    def take_hand(self):
        self.hand().wait_recv()
        first = self.place.count[self.axes[0]]
        rest = tuple(pl.ds(0, self.place.count[axis]) for axis in self.axes[1:])
        if self.both:
            self.hand().wait_send()
            self.mine[...] = self.mine[...] + self.hand_box[...]
        else:
            for p in range(first):
                for r in range(self.place.count[self.axes[1]]):
                    index = (p, r) + rest[1:]
                    here = self.mine[index + (self.place.core,)].astype(F32)
                    there = self.hand_box[index].astype(F32)
                    self.mine[index + (self.place.core,)] = (here + there).astype(self.mine.dtype)
        self.send_round(0)

    def block(self, dim, position):
        done = self.order[: self.order.index(dim)]
        index = []
        for axis in self.axes:
            if axis == dim:
                index.append(position)
            elif axis in done:
                index.append(self.place.at[axis])
            else:
                index.append(pl.ds(0, self.place.count[axis]))
        return self.own(tuple(index))

    def link(self, dim, t, way, position, device):
        slot = self.slots[dim, t, way]
        return pltpu.make_async_remote_copy(
            self.mine.at[self.block(dim, position)],
            self.inbox[slot],
            self.send.at[slot],
            self.recv.at[slot],
            device_id=device,
            device_id_type=MESH,
        )

    def sends(self, dim, t):
        here, count = self.place.at[dim], self.place.count[dim]
        yield 1, count - 1 - t + here, (t >= here) & (here < count - 1)
        back = count - 1 - here
        yield -1, t - back, (t >= back) & (here > 0)

    def arrivals(self, dim, t):
        here, count = self.place.at[dim], self.place.count[dim]
        yield 1, count - 2 - t + here, (t >= here - 1) & (here > 0)
        back = count - 1 - here
        yield -1, t + 1 - back, (t >= back - 1) & (here < count - 1)

    def send_round(self, number):
        dim, t = self.rounds[number]
        for way, position, valid in self.sends(dim, t):

            @pl.when(valid)
            def _(way=way, position=position):
                self.link(dim, t, way, position, self.place.neighbour(dim, way)).start()

    def advance(self, number):
        dim, t = self.rounds[number - 1]
        for way, position, valid in self.arrivals(dim, t):

            @pl.when(valid)
            def _(way=way, position=position):
                self.link(dim, t, way, position, self.place.partner()).wait_recv()
                index = self.block(dim, position)
                total = self.mine[index].astype(F32) + self.inbox[self.slots[dim, t, way]][...].astype(F32)
                self.mine[index] = total.astype(self.mine.dtype)

        if number < len(self.rounds):
            self.send_round(number)

    def result(self):
        return self.mine[self.own(tuple(self.place.at[axis] for axis in self.axes))]

    def drain(self):
        if not self.both:
            self.hand().wait_send()
        for dim, t in self.rounds:
            for way, position, valid in self.sends(dim, t):

                @pl.when(valid)
                def _(dim=dim, t=t, way=way, position=position):
                    self.link(dim, t, way, position, self.place.partner()).wait_send()


def inbox_shapes(count, axes, order, block):
    shapes, left = [], dict(count)
    for dim in order:
        left.pop(dim)
        for _ in range(2 * (count[dim] - 1)):
            shapes.append(tuple(count[axis] for axis in axes if axis in left) + block)
    return shapes


class Mover:
    def __init__(self, sems):
        self.sems, self.used, self.open = sems, 0, []

    def start(self, source, target):
        copy = pltpu.make_async_copy(source, target, self.sems.at[self.used])
        self.used += 1
        copy.start()
        return copy

    def save(self, source, target):
        self.open.append(self.start(source, target))

    def close(self):
        for copy in self.open:
            copy.wait()


def read_vectors(vectors, tiles):
    nz, nx = tiles.shape[:2]
    pieces = [tiles[z, x, 0] + tiles[z, x, 1] for z in range(nz) for x in range(nx)]
    vectors[...] = jnp.concatenate(pieces, axis=1)


def column_parts(weights):
    wq, wk, wv, wo, wu, wd = weights
    left, right = pl.ds(0, SEG), pl.ds(SEG, SEG)
    return [wq, wk, wv, wo, wu.at[:, left], wu.at[:, right], wd.at[:, left], wd.at[:, right]]


FWD_OUT = ("x", "nrm", "q", "k", "v", "probs", "mix", "res", "nrm2", "active", "slope", "out")


def forward_kernel(shape, micro, tokens, *refs):
    if shape:
        weights, norms, refs = refs[:6], refs[6:10], refs[10:]
        g_out, vectors = refs[:2]
        saved = dict(zip(FWD_OUT, refs[2:14]))
        refs = refs[14:]
    else:
        g_in, vectors = refs[:2]
        saved = dict(zip(FWD_OUT, refs[2:14]))
        refs = refs[14:]
    here = dict(zip(FWD_OUT, refs[:12]))
    raw, low, total, g, sems = refs[12:17]
    mover = Mover(sems)
    y = lax.axis_index("mp")
    take = mover.start(tokens.at[pl.ds(y * micro, micro)], raw)
    x, nrm, q, k, v = (here[name] for name in ("x", "nrm", "q", "k", "v"))
    probs, mix, res, nrm2 = (here[name] for name in ("probs", "mix", "res", "nrm2"))
    active, slope, out = (here[name] for name in ("active", "slope", "out"))

    def keep(*names):
        for name in names:
            mover.save(here[name], saved[name])

    if shape:
        tiles, send, recv, pass_send, pass_recv = refs[17:]
        place = Place(shape)
        spot = (place.at["y"], place.at["z"], place.at["x"], place.core)
        mine = [mover.start(part, g.at[(seg,) + spot]) for seg, part in enumerate(column_parts(weights))]
        tile = (place.at["z"], place.at["x"], place.core)
        tiles[tile] = jnp.zeros(tiles.shape[3:], F32)
        share = norms[0].shape[1]
        for line, norm in enumerate(norms):
            value = norm[...].astype(F32)
            for core in range(2):

                @pl.when(place.core == core)
                def _(line=line, value=value, core=core):
                    tiles[tile + (slice(line, line + 1), slice(core * share, (core + 1) * share))] = value

        place.barrier("zxy")
        pick = lambda seg: tuple(sem.at[seg] for sem in (send, recv, pass_send, pass_recv))
        runs = [Gather(place, g.at[seg], "yzx", ORDERS[seg], pick(seg)) for seg in range(8)]
        runs.append(Gather(place, tiles, "zx", "zx", pick(8)))

        def begin(*segs):
            for seg in segs:
                if seg < 8:
                    mine[seg].wait()
                runs[seg].start()

        def step(number, *segs):
            for seg in segs:
                if number <= len(runs[seg].rounds):
                    runs[seg].advance(number)

        def have(*segs):
            for seg in segs:
                runs[seg].finish()
                if seg < 8:
                    mover.save(g.at[seg], g_out.at[seg])

        def drain():
            for run in runs:
                run.drain()

        depth = len(runs[0].rounds)
    else:
        loads = [mover.start(g_in.at[seg], g.at[seg]) for seg in range(8)]
        begin = step = lambda *args: None
        depth = 5

        def have(*segs):
            for seg in segs:
                if seg < 8:
                    loads[seg].wait()

        def drain():
            pass

    early, middle, late = (Q, K, V), (O, U0, U1), (D0, D1)
    begin(8, *early)
    take.wait()
    to_rows(raw, x)
    keep("x")
    for number in range(1, depth + 1):
        step(number, 8, *early)
        if number == 2:
            begin(*middle)
        if number > 3:
            step(number - 3, *middle)
    have(8)
    if shape:
        read_vectors(vectors, tiles)
    gain, shift = vectors[0:1, :], vectors[1:2, :]
    gain_two, shift_two = vectors[2:3, :], vectors[3:4, :]
    norm_in(x, nrm, gain, shift)
    keep("nrm")
    begin(*late)
    have(Q)
    project(nrm, g, Q, q)
    step(depth - 2, *middle)
    have(K)
    project(nrm, g, K, k)
    step(1, *late)
    have(V)
    project(nrm, g, V, v)
    keep("q", "k", "v")
    step(depth - 1, *middle)
    step(2, *late)
    groups = x.shape[0] // TILE // 2
    for part in range(2):
        attend(q, k, v, probs, mix, part * groups, groups)
        if part == 0:
            step(depth, *middle)
        step(3 + part, *late)
    keep("probs", "mix")
    have(O)
    back_through(lambda m: mix[:, half(m)], g, O, res, True)

    def second(rows, _):
        sums = res[rows, :] + x[rows, :].astype(F32)
        res[rows, :] = sums
        normal, _inv = norm_stats(sums)
        nrm2[rows, :] = (normal * gain_two + shift_two).astype(BF)

    row_loop(x.shape[0], second)
    keep("res", "nrm2")
    step(5, *late)
    have(U0)
    feed_up(nrm2, g, 0, active, slope)
    have(U1)
    feed_up(nrm2, g, 1, active, slope)
    keep("active", "slope")
    for which in range(2):
        have(DOWNS[which])
        back_through(lambda m, which=which: active[which, m], g, DOWNS[which], total, which == 0)

    def last(rows, _):
        low[rows, :] = (res[rows, :] + total[rows, :]).astype(BF)

    row_loop(x.shape[0], last)
    from_rows(low, out)
    keep("out")
    drain()
    mover.close()


def row_weights(ids, counts, y, micro, target):
    series = ids.shape[1]
    sums = counts[0]
    for kind in range(1, counts.shape[0]):
        sums = sums + counts[kind]
    mean = jnp.full((PAD, 1), sums.astype(F32), F32) / counts.shape[0]

    def one(index, carry):
        kind = ids[y * micro + lax.div(index, series), lax.rem(index, series)]
        count = counts[kind].astype(F32)
        target[pl.ds(pl.multiple_of(index * PAD, PAD), PAD), :] = 2.0 * mean / (mean + count)
        return carry

    lax.fori_loop(0, micro * series, one, 0)


def feed_back_kernel(micro, cotangent, ids, counts, vectors, g_in, active_in, slope_in, nrm2_in, res_in, *refs):
    dw_out, gres_out, vec = refs[:3]
    raw, cot, weight, active, slope, nrm2, res, g, dw, gl, glt, gh, n2t, gn2, gres, sems = refs[3:]
    mover = Mover(sems)
    y = lax.axis_index("mp")
    loads = {"raw": mover.start(cotangent.at[pl.ds(y * micro, micro)], raw)}
    for which in range(2):
        loads["d", which] = mover.start(g_in.at[DOWNS[which]], g.at[2 + which])
        loads["slope", which] = mover.start(slope_in.at[which], slope.at[which])
        loads["active", which] = mover.start(active_in.at[which], active.at[which])
    loads["nrm2"] = mover.start(nrm2_in, nrm2)
    for which in range(2):
        loads["u", which] = mover.start(g_in.at[UPS[which]], g.at[which])
    loads["res"] = mover.start(res_in, res)
    row_weights(ids, counts, y, micro, weight)
    gain_two = vectors[2:3, :]
    loads["raw"].wait()
    to_rows(raw, cot)

    def first(rows, _):
        gl[rows, :] = (cot[rows, :].astype(F32) * weight[rows, :]).astype(BF)

    row_loop(cot.shape[0], first)
    turn(gl, glt)
    for which in range(2):
        loads["d", which].wait()
        loads["slope", which].wait()
        loads["active", which].wait()
        weight_grad(glt, lambda m, which=which: active[which, m], dw, 2 + which)
        mover.save(dw.at[2 + which], dw_out.at[2 + which])

        def one(m, which=which):
            pulled = nn(gl[...], flat(g[2 + which, m]))
            gh[which, m] = (pulled * slope[which, m]).astype(BF)

        half_loop(g.shape[1], one)
    loads["nrm2"].wait()
    turn(nrm2, n2t)
    for which in range(2):
        loads["u", which].wait()
        weight_grad(n2t, lambda m, which=which: gh[which, m], dw, which)
        mover.save(dw.at[which], dw_out.at[which])
        back_through(lambda m, which=which: gh[which, m], g, which, gn2, which == 0)
    loads["res"].wait()
    vec[...] = jnp.zeros_like(vec)

    def last(rows, _):
        grad = gn2[rows, :]
        pulled, normal = norm_pull(grad, res[rows, :], gain_two)
        vec[0] += fold_rows(grad * normal)
        vec[1] += fold_rows(grad)
        gres[rows, :] = cot[rows, :].astype(F32) * weight[rows, :] + pulled

    row_loop(cot.shape[0], last)
    mover.save(gres, gres_out)
    mover.close()


BACK_IN = ("gres", "mix", "nrm", "q", "k", "v", "probs", "x")


def attn_back_kernel(vectors, g_in, *refs):
    given = dict(zip(BACK_IN, refs[:8]))
    dw_out, out, vec = refs[8:11]
    here = dict(zip(BACK_IN, refs[11:19]))
    g, dw, gal, galt, gm, gq, gk, gv, nrmt, gn, raw, sems = refs[19:]
    mover = Mover(sems)
    loads = {"gres": mover.start(given["gres"], here["gres"]), O: mover.start(g_in.at[O], g.at[O])}
    for name in BACK_IN[1:]:
        loads[name] = mover.start(given[name], here[name])
    for seg in (Q, K, V):
        loads[seg] = mover.start(g_in.at[seg], g.at[seg])
    gres, mix, nrm, q, k, v, probs, x = (here[name] for name in BACK_IN)
    gain = vectors[0:1, :]
    loads["gres"].wait()

    def first(rows, _):
        gal[rows, :] = gres[rows, :].astype(BF)

    row_loop(gal.shape[0], first)
    turn(gal, galt)
    loads[O].wait()
    loads["mix"].wait()
    weight_grad(galt, lambda m: mix[:, half(m)], dw, O)
    mover.save(dw.at[O], dw_out.at[O])
    project(gal, g, O, gm)
    loads["nrm"].wait()
    turn(nrm, nrmt)
    for name in ("q", "k", "v", "probs"):
        loads[name].wait()
    attend_back(q, k, v, probs, gm, gq, gk, gv)
    for seg, grad in ((Q, gq), (K, gk), (V, gv)):
        loads[seg].wait()
        weight_grad(nrmt, lambda m, grad=grad: grad[:, half(m)], dw, seg)
        mover.save(dw.at[seg], dw_out.at[seg])
        back_through(lambda m, grad=grad: grad[:, half(m)], g, seg, gn, seg == Q)
    loads["x"].wait()
    vec[...] = jnp.zeros_like(vec)

    def last(rows, _):
        grad = gn[rows, :]
        pulled, normal = norm_pull(grad, x[rows, :].astype(F32), gain)
        vec[0] += fold_rows(grad * normal)
        vec[1] += fold_rows(grad)
        gal[rows, :] = (gres[rows, :] + pulled).astype(BF)

    row_loop(gal.shape[0], last)
    from_rows(gal, raw)
    mover.save(raw, out)
    mover.close()


def vector_tiles(tiles, vec_a, vec_f):
    tiles[...] = jnp.zeros_like(tiles)
    nz, nx = tiles.shape[:2]
    for line, (source, part) in enumerate(((vec_a, 0), (vec_a, 1), (vec_f, 0), (vec_f, 1))):
        row = jnp.sum(source[part], axis=0, keepdims=True)
        for z in range(nz):
            for x in range(nx):
                chip = z * nx + x
                tiles[z, x, line : line + 1, :] = row[:, chip * 128 : (chip + 1) * 128]


def scatter_kernel(shape, dw_a, dw_f, vec_a, vec_f, low_out, low_tokens, *refs):
    outs, vec_out, pairs = refs[:6], refs[6], refs[7:9]
    dw, tiles, hands, vec_hand, ybox, halves, local, send, recv, ysem = refs[9:19]
    boxes = refs[19:]
    place = Place(shape)
    y = place.at["y"]
    micro = halves.shape[1]
    mover = Mover(local)
    sides = [mover.start(source, halves.at[index]) for index, source in enumerate((low_tokens, low_out))]
    loads = []
    for seg in (D0, D1, U0, U1, O, Q, K, V):
        source = dw_a.at[seg] if seg < 4 else dw_f.at[seg - 4]
        loads.append((seg, mover.start(source, dw.at[seg])))
    vector_tiles(tiles, vec_a, vec_f)
    place.barrier("zxy")
    other = place.device(y=1 - y)
    swaps = []
    for index, copy in enumerate(sides):
        copy.wait()
        target = pairs[1 - index].at[pl.ds(y * micro, micro)]
        swap = pltpu.make_async_remote_copy(
            halves.at[index],
            target,
            ysem.at[2 + 2 * index],
            ysem.at[3 + 2 * index],
            device_id=other,
            device_id_type=MESH,
        )
        mover.save(halves.at[index], target)
        swaps.append(swap)
    segs = dw.shape[0]
    runs, start = {}, 0
    for seg in range(segs + 1):
        order = BACK_ORDERS[seg] if seg < segs else "zx"
        sems = (send.at[seg], recv.at[seg])
        if seg < segs:
            run = Scatter(place, dw.at[seg], "yzx", order, {}, hands.at[seg], sems)
        else:
            run = Scatter(place, tiles, "zx", "zx", {}, vec_hand, sems, both=True)
        for slot in range(1, len(run.slots) + 1):
            run.inbox[slot] = boxes[start + slot - 1]
        start += len(run.slots)
        runs[seg] = run
    runs[segs].start()
    line = [segs]
    for seg, copy in loads:
        copy.wait()
        runs[seg].start()
        line.append(seg)
    for index in line:
        runs[index].take_hand()
    for swap in swaps:
        swap.start()
    deepest = max(len(run.rounds) for run in runs.values())
    for number in range(1, deepest + 1):
        for index in line:
            if number <= len(runs[index].rounds):
                runs[index].advance(number)
    here = tiles.at[place.at["z"], place.at["x"]]
    copy = pltpu.make_async_remote_copy(here, ybox, ysem.at[0], ysem.at[1], device_id=other, device_id_type=MESH)
    copy.start()
    for seg in range(4):
        outs[seg][...] = runs[seg].result().astype(F32)
    for which in range(2):
        outs[4][:, which * SEG : (which + 1) * SEG] = runs[UPS[which]].result().astype(F32)
        outs[5][:, which * SEG : (which + 1) * SEG] = runs[DOWNS[which]].result().astype(F32)
    copy.wait()
    vec_out[...] = tiles[place.at["z"], place.at["x"]] + ybox[...]
    for index in line:
        runs[index].drain()
    for swap in swaps:
        swap.wait()
    mover.close()


def shape_of(shape, dtype):
    return jax.ShapeDtypeStruct(shape, dtype)


IN_VMEM = pl.BlockSpec(memory_space=pltpu.VMEM)
IN_SMEM = pl.BlockSpec(memory_space=pltpu.SMEM)
ANYWHERE = pl.BlockSpec(memory_space=pl.ANY)
DMA = pltpu.SemaphoreType.DMA


def call(body, outs, ins, out_specs, scratch, name, collective=None):
    params = {"vmem_limit_bytes": VMEM_LIMIT}
    if collective is not None:
        params.update(collective_id=collective, has_side_effects=True)
    return pl.pallas_call(
        body,
        out_shape=outs,
        in_specs=ins,
        out_specs=out_specs,
        scratch_shapes=scratch,
        compiler_params=pltpu.CompilerParams(**params),
        name=name,
    )


def vmem(like):
    return pltpu.VMEM(like.shape, like.dtype)


def forward(shape, micro, tokens, weights, norms, g_in=None, vectors_in=None):
    _, patches, series, width = tokens.shape
    rows, heads = micro * series * PAD, width // HD
    groups = rows // TILE
    full = g_in.shape if shape is None else (8, shape[2], shape[0], shape[1], 2, weights[0].shape[0], SEG)
    low, high = shape_of((rows, width), BF), shape_of((rows, width), F32)
    wide = (2, full[1], rows, SEG)
    raw = shape_of((micro, patches, series, width), BF)
    kinds = {name: low for name in FWD_OUT}
    kinds.update(
        probs=shape_of((groups, heads, TILE, TILE), F32),
        res=high,
        active=shape_of(wide, BF),
        slope=shape_of(wide, F32),
        out=raw,
    )
    saved = tuple(kinds[name] for name in FWD_OUT)
    scratch = [vmem(kind) for kind in saved] + [vmem(raw), vmem(low), vmem(high), pltpu.VMEM(full, BF), DMA((64,))]
    if shape is None:
        results = call(
            functools.partial(forward_kernel, None, micro),
            saved,
            [ANYWHERE, ANYWHERE, IN_VMEM],
            (ANYWHERE,) * 12,
            scratch,
            "forward",
        )(tokens, g_in, vectors_in)
        return g_in, vectors_in, dict(zip(FWD_OUT, results))
    count = dict(zip("zxy", shape))
    slots = link_slots(count, "zxy")
    scratch += [pltpu.VMEM(shape[:2] + (2, 8, 128), F32)]
    scratch += [DMA((9, slots)), DMA((9, slots)), DMA((9, slots + 1)), DMA((9, slots + 1))]
    results = call(
        functools.partial(forward_kernel, shape, micro),
        (shape_of(full, BF), shape_of((8, width), F32)) + saved,
        [ANYWHERE] * 7 + [IN_VMEM] * 4,
        (ANYWHERE, IN_VMEM) + (ANYWHERE,) * 12,
        scratch,
        "forward",
        0,
    )(tokens, *weights, *norms)
    return results[0], results[1], dict(zip(FWD_OUT, results[2:]))


def feed_back(micro, cotangent, ids, counts, vectors, g, kept):
    _, patches, series, width = cotangent.shape
    low, high = kept["x"], kept["res"]
    rows = low.shape[0]
    part = shape_of((4,) + g.shape[1:], BF)
    turned = pltpu.VMEM((width, rows), BF)
    scratch = [
        pltpu.VMEM((micro, patches, series, width), BF),
        vmem(low),
        pltpu.VMEM((rows, 1), F32),
        vmem(kept["active"]),
        vmem(kept["slope"]),
        vmem(low),
        vmem(high),
        vmem(part),
        vmem(part),
        vmem(low),
        turned,
        vmem(kept["active"]),
        turned,
        vmem(high),
        vmem(high),
        DMA((32,)),
    ]
    return call(
        functools.partial(feed_back_kernel, micro),
        (part, shape_of(high.shape, F32), shape_of((2, 8, width), F32)),
        [ANYWHERE, IN_SMEM, IN_SMEM, IN_VMEM] + [ANYWHERE] * 5,
        (ANYWHERE, ANYWHERE, IN_VMEM),
        scratch,
        "feed_back",
    )(cotangent, ids, counts, vectors, g, kept["active"], kept["slope"], kept["nrm2"], kept["res"])


def attn_back(vectors, g, kept):
    low, high = kept["x"], kept["res"]
    rows, width = low.shape
    part = shape_of((4,) + g.shape[1:], BF)
    raw = kept["out"]
    turned = pltpu.VMEM((width, rows), BF)
    scratch = [vmem(kept[name]) for name in BACK_IN]
    scratch += [vmem(part), vmem(part), vmem(low), turned, vmem(low), vmem(low), vmem(low), vmem(low), turned]
    scratch += [vmem(high), vmem(raw), DMA((32,))]
    return call(
        attn_back_kernel,
        (part, shape_of(raw.shape, BF), shape_of((2, 8, width), F32)),
        [IN_VMEM] + [ANYWHERE] * 9,
        (ANYWHERE, ANYWHERE, IN_VMEM),
        scratch,
        "attn_back",
    )(vectors, g, *(kept[name] for name in BACK_IN))


def scatter_grads(shape, dw_a, dw_f, vec_a, vec_f, low_out, low_tokens):
    nz, nx, ny = shape
    rows, cols = dw_a.shape[-2:]
    segs = 8
    count = {"z": nz, "x": nx, "y": ny}
    slots = link_slots(count, "zxy")
    full = (segs,) + dw_a.shape[1:]
    scratch = [
        pltpu.VMEM(full, BF),
        pltpu.VMEM((nz, nx, 8, 128), F32),
        pltpu.VMEM((segs, ny, nz, nx, rows, cols), BF),
        pltpu.VMEM((nz, nx, 8, 128), F32),
        pltpu.VMEM((8, 128), F32),
        pltpu.VMEM((2,) + low_out.shape, BF),
        DMA((16,)),
        DMA((segs + 1, slots + 1)),
        DMA((segs + 1, slots + 1)),
        DMA((6,)),
    ]
    for seg in range(segs):
        scratch += [pltpu.VMEM(s, BF) for s in inbox_shapes(count, "yzx", BACK_ORDERS[seg], (rows, cols))]
    scratch += [pltpu.VMEM(s, F32) for s in inbox_shapes({"z": nz, "x": nx}, "zx", "zx", (8, 128))]
    small, large = shape_of((rows, cols), F32), shape_of((rows, 2 * cols), F32)
    pair = shape_of((ny * low_out.shape[0],) + low_out.shape[1:], BF)
    outs = (small, small, small, small, large, large, shape_of((8, 128), F32), pair, pair)
    return call(
        functools.partial(scatter_kernel, shape),
        outs,
        [ANYWHERE, ANYWHERE, IN_VMEM, IN_VMEM, ANYWHERE, ANYWHERE],
        (IN_VMEM,) * 7 + (ANYWHERE,) * 2,
        scratch,
        "scatter_grads",
        1,
    )(dw_a, dw_f, vec_a, vec_f, low_out, low_tokens)


def chip_grid(chips):
    nx = 1
    while (nx * 2) ** 2 <= chips:
        nx *= 2
    return chips // nx, nx


def body(counts_of, tokens, cotangent, domain_ids, domain_counts, *params):
    weights, norms = params[:6], params[6:]
    n_dp, n_mp = counts_of
    micro = tokens.shape[0] // n_mp
    width = tokens.shape[3]
    share = width // n_dp
    y = lax.axis_index("mp")
    linked = n_mp == 2 and share * 2 == TILE
    flip = lambda array: jnp.transpose(array, (0, 2, 1, 3))
    x, cot = flip(tokens), flip(cotangent)
    if linked:
        shape = chip_grid(n_dp // 2) + (n_mp,)
        g, vectors, kept = forward(shape, micro, x, weights, [norm.reshape(1, -1) for norm in norms])
    else:
        shards = jnp.stack(
            weights[:4] + tuple(w[:, i * SEG : (i + 1) * SEG] for w in weights[4:] for i in range(2))
        )
        g = lax.all_gather(lax.all_gather(shards, "dp", axis=1, tiled=True), "mp", axis=1)
        vectors = lax.all_gather(jnp.stack(norms), "dp", axis=1, tiled=True).astype(F32)
        vectors = jnp.pad(vectors, ((0, 4), (0, 0)))
        g, vectors, kept = forward(None, micro, x, None, None, g, vectors)
    dw_f, gres, vec_f = feed_back(micro, cot, domain_ids, domain_counts, vectors, g, kept)
    dw_a, low_tokens, vec_a = attn_back(vectors, g, {**kept, "gres": gres})
    if linked:
        results = scatter_grads(shape, dw_a, dw_f, vec_a, vec_f, kept["out"], low_tokens)
        grads, vec, out, grad_tokens = results[:6], results[6], results[7], results[8]
        core = lax.rem(lax.axis_index("dp"), 2)
        vec = lax.dynamic_slice(vec, (0, core * share), (4, share))
    else:
        dw = jnp.concatenate((dw_a, dw_f)).astype(F32)
        dw = lax.psum_scatter(lax.psum_scatter(dw, "mp", scatter_dimension=1), "dp", scatter_dimension=1, tiled=True)
        grads = [dw[0], dw[1], dw[2], dw[3]]
        grads += [jnp.concatenate((dw[a], dw[b]), axis=1) for a, b in (UPS, DOWNS)]
        vec = jnp.concatenate((jnp.sum(vec_a, axis=1), jnp.sum(vec_f, axis=1)))
        vec = lax.psum_scatter(lax.psum(vec, "mp"), "dp", scatter_dimension=1, tiled=True)
        out = lax.all_gather(kept["out"], "mp", axis=0, tiled=True)
        grad_tokens = lax.all_gather(low_tokens, "mp", axis=0, tiled=True)
    return (flip(out), flip(grad_tokens.astype(F32)), *grads, vec[0], vec[1], vec[2], vec[3])


def solution(mesh):
    rows, matrix, vector = P(None, "dp", None, None), P("dp", "mp"), P("dp")
    in_specs = (rows, rows, P(None, "dp"), P()) + (matrix,) * 6 + (vector,) * 4
    out_specs = (rows, rows) + (matrix,) * 6 + (vector,) * 4
    run = functools.partial(body, (mesh.shape["dp"], mesh.shape["mp"]))
    return jax.shard_map(run, mesh=mesh, in_specs=in_specs, out_specs=out_specs, check_vma=False)
```

```python
import functools

import jax
import jax.numpy as jnp
from jax import lax
from jax.experimental import pallas as pl
from jax.experimental.pallas import tpu as pltpu
from jax.sharding import PartitionSpec as P

BF = jnp.bfloat16
F32 = jnp.float32
HD = 128
SEG = 512
TILE = 128
PAD = 16
EPS = 1e-05
MESH = pl.DeviceIdType.MESH
VMEM_LIMIT = 62 * 1024 * 1024

Q, K, V, O, U0, U1, D0, D1 = range(8)
UPS = (U0, U1)
DOWNS = (D0, D1)
ORDERS = ("zxy", "zyx", "xyz", "yzx", "zxy", "zxy", "yxz", "yzx")
BACK_ORDERS = ("yxz", "xzy", "xzy", "yxz", "yzx", "zxy", "zxy", "xyz")

FORWARD_PLAN = (
    0, 8, 1, 2, 7, 5, 0, 8, 2, 1, 5, 0, 4, 6, 0, 1, 5, 3, -1, 5, 1, 2, 6, 0,
    8, 4, 3, 8, 2, 4, 1, 8, 5, 3, 3, 2, 0, 4, 7, -1, 1, 6, -1, -1, 3, 2, 4, 5,
    -1, 7, -1, -1, -1, 7, 3, 4, -1, 7, 6, -1, -1, 6, -1, -1, 7, 6, -1, -1, -1, -1,
)
FEED_PLAN = (
    -1, -1, 2, -1, 0, -1, -1, 1, 0, 2, 2, 1, -1, -1, -1, 0, -1, -1, 1, 2, 0, -1, -1, 1,
    0, 1, 0, 1, 0, 1,
)
ATTN_PLAN = (
    0, -1, -1, -1, 2, -1, -1, 1, 2, -1, 0, -1, 1, -1, -1, 3, -1, 4, 1, -1, 3, 2, -1, -1,
    1, 4, -1, 5, -1, 7, 2, 6, 0, 5, 7, 7, 6, 6, 0, 2, 4, 4, 0, 3, 4, 7, 5, 6,
    5, 3, 6, 2, 0, 1, 3, 4, 5, 1, 3, 6, 0, 5, 2, 1, 3, 4, 5,
)
GRADS_FIRST = 3


def nn(a, b):
    return lax.dot_general(a, b, (((1,), (0,)), ((), ())), preferred_element_type=F32)


def nt(a, b):
    return lax.dot_general(a, b, (((1,), (1,)), ((), ())), preferred_element_type=F32)


def flat(value):
    return value.reshape(-1, value.shape[-1])


def norm_stats(values):
    mean = jnp.mean(values, axis=-1, keepdims=True)
    center = values - mean
    inverse = lax.rsqrt(jnp.mean(center * center, axis=-1, keepdims=True) + EPS)
    return center * inverse, inverse


def norm_pull(grad, values, gain):
    normal, inverse = norm_stats(values)
    scaled = grad * gain
    first = jnp.mean(scaled, axis=-1, keepdims=True)
    second = jnp.mean(scaled * normal, axis=-1, keepdims=True)
    return inverse * (scaled - first - normal * second), normal


def fold_rows(values):
    rows, width = values.shape
    return jnp.sum(values.reshape(rows // 8, 8, width), axis=0)


def score_mask():
    row = lax.broadcasted_iota(jnp.int32, (TILE, TILE), 0)
    col = lax.broadcasted_iota(jnp.int32, (TILE, TILE), 1)
    return (row // PAD == col // PAD) & (col <= row)


def row_loop(rows, body, first=0):
    def once(index, carry):
        body(pl.ds(pl.multiple_of(index * TILE, TILE), TILE), index)
        return carry

    lax.fori_loop(first, first + rows // TILE, once, 0)


def half_loop(count, body):
    def once(index, carry):
        body(index)
        return carry

    lax.fori_loop(0, count, once, 0)


def half(index):
    return pl.ds(pl.multiple_of(index * SEG, SEG), SEG)


def spread_rows(patches, series):
    row = lax.broadcasted_iota(jnp.int32, (series * PAD, patches * series), 0)
    col = lax.broadcasted_iota(jnp.int32, (series * PAD, patches * series), 1)
    hit = (lax.rem(row, PAD) * series + lax.div(row, PAD) == col) & (lax.rem(row, PAD) < patches)
    return jnp.where(hit, 1.0, 0.0).astype(BF)


def gather_rows(patches, series):
    row = lax.broadcasted_iota(jnp.int32, (patches * series, series * PAD), 0)
    col = lax.broadcasted_iota(jnp.int32, (patches * series, series * PAD), 1)
    return jnp.where(lax.rem(row, series) * PAD + lax.div(row, series) == col, 1.0, 0.0).astype(BF)


def to_rows(raw, target):
    micro, patches, series, _ = raw.shape
    matrix = spread_rows(patches, series)
    for part in range(micro):
        target[part * series * PAD : (part + 1) * series * PAD, :] = nn(matrix, flat(raw[part])).astype(BF)


def from_rows(source, raw):
    micro, patches, series, width = raw.shape
    matrix = gather_rows(patches, series)
    for part in range(micro):
        rows = source[part * series * PAD : (part + 1) * series * PAD, :]
        raw[part] = nn(matrix, rows).astype(raw.dtype).reshape(patches, series, width)


def norm_in(x, normed, gain, shift):
    def block(rows, _):
        normal, _inv = norm_stats(x[rows, :].astype(F32))
        normed[rows, :] = (normal * gain + shift).astype(BF)

    row_loop(x.shape[0], block)


def project(source, weights, seg, target):
    def one(m):
        target[:, half(m)] = nn(source[...], flat(weights[seg, m])).astype(BF)

    half_loop(weights.shape[1], one)


def attend(queries, keys, values, probs, mixture, first, count):
    mask = score_mask()
    scale = HD ** (-0.5)

    def group(rows, index):
        for head in range(queries.shape[1] // HD):
            cols = slice(head * HD, (head + 1) * HD)
            scores = nt(queries[rows, cols], keys[rows, cols]) * scale
            scores = jnp.where(mask, scores, -1e30)
            powers = jnp.exp(scores - jnp.max(scores, axis=-1, keepdims=True))
            share = powers * (1.0 / jnp.sum(powers, axis=-1, keepdims=True))
            probs[rows, cols] = share
            mixture[rows, cols] = nn(share.astype(BF), values[rows, cols]).astype(BF)

    row_loop(count * TILE, group, first)


def attend_back(queries, keys, values, probs, grad_mix, grad_q, grad_k, grad_v, first, count):
    scale = HD ** (-0.5)

    def group(rows, index):
        for head in range(queries.shape[1] // HD):
            cols = slice(head * HD, (head + 1) * HD)
            share = probs[rows, cols]
            grad = grad_mix[rows, cols]
            grad_share = nt(grad, values[rows, cols])
            grad_v[rows, cols] = nn(share.T.astype(BF), grad).astype(BF)
            inner = jnp.sum(grad_share * share, axis=-1, keepdims=True)
            grad_scores = share * (grad_share - inner)
            low = grad_scores.astype(BF)
            grad_q[rows, cols] = (nn(low, keys[rows, cols]) * scale).astype(BF)
            turned = grad_scores.T.astype(BF)
            grad_k[rows, cols] = (nn(turned, queries[rows, cols]) * scale).astype(BF)

    row_loop(count * TILE, group, first)


def back_through(source, weights, seg, total):
    def one(m):
        total[...] += nt(source(m), flat(weights[seg, m]))

    half_loop(weights.shape[1], one)


def feed_up(normed_two, weights, which, m, active, slope):
    hidden = nn(normed_two[...], flat(weights[UPS[which], m]))
    bell = 0.5 + 0.5 * lax.erf(hidden * (0.5**0.5))
    active[which, m] = (hidden * bell).astype(BF)
    density = jnp.exp(-0.5 * hidden * hidden) * 0.3989422804014327
    slope[which, m] = bell + hidden * density


def turn(source, target):
    def block(rows, _):
        target[:, rows] = source[rows, :].T

    row_loop(source.shape[0], block)


def weight_grad(turned, right, target, seg):
    def one(m):
        product = nn(turned[...], right(m)).astype(BF)
        target[seg, m] = product.reshape(target.shape[2:])

    half_loop(target.shape[1], one)


class Place:
    def __init__(self, shape):
        self.nz, self.nx, self.ny = shape
        index = lax.axis_index("dp")
        self.core = lax.rem(index, 2)
        chip = lax.div(index, 2)
        self.at = {"z": lax.div(chip, self.nx), "x": lax.rem(chip, self.nx), "y": lax.axis_index("mp")}
        self.count = {"z": self.nz, "x": self.nx, "y": self.ny}

    def device(self, core=None, **moved):
        at = {**self.at, **moved}
        core = self.core if core is None else core
        return ((at["z"] * self.nx + at["x"]) * 2 + core, at["y"])

    def partner(self):
        return self.device(core=1 - self.core)

    def neighbour(self, dim, step):
        return self.device(**{dim: self.at[dim] + step})

    def barrier(self, dims):
        semaphore = pltpu.get_barrier_semaphore()
        pl.semaphore_signal(semaphore, inc=1, device_id=self.partner(), device_id_type=MESH)
        peers = 1
        for dim in dims:
            for step in (1, -1):
                there = self.at[dim] + step
                valid = (there >= 0) & (there < self.count[dim])
                peers = peers + valid.astype(jnp.int32)

                @pl.when(valid)
                def _(dim=dim, step=step):
                    other = self.neighbour(dim, step)
                    pl.semaphore_signal(semaphore, inc=1, device_id=other, device_id_type=MESH)

        pl.semaphore_wait(semaphore, peers)


def link_slots(count, dims):
    return sum(2 * (count[dim] - 1) for dim in dims)


class Gather:
    def __init__(self, place, buffer, axes, order, sems):
        self.place, self.buffer, self.axes, self.order = place, buffer, axes, order
        self.send, self.recv, self.pass_send, self.pass_recv = sems
        self.rounds = [(dim, t) for dim in order for t in range(place.count[dim] - 1)]
        self.slots = {}
        for dim, t in self.rounds:
            for way in (1, -1):
                self.slots[dim, t, way] = len(self.slots)

    def block(self, dim, position, core):
        done = self.order[: self.order.index(dim)] if dim else ""
        index = []
        for axis in self.axes:
            if axis == dim:
                index.append(position)
            elif axis in done:
                index.append(pl.ds(0, self.place.count[axis]))
            else:
                index.append(self.place.at[axis])
        return self.buffer.at[tuple(index) + (core,)]

    def link(self, dim, t, way, position, device):
        block = self.block(dim, position, self.place.core)
        slot = self.slots[dim, t, way]
        return pltpu.make_async_remote_copy(
            block, block, self.send.at[slot], self.recv.at[slot], device_id=device, device_id_type=MESH
        )

    def hand(self, slot, dim, position, core):
        block = self.block(dim, position, core)
        return pltpu.make_async_remote_copy(
            block,
            block,
            self.pass_send.at[slot],
            self.pass_recv.at[slot],
            device_id=self.place.partner(),
            device_id_type=MESH,
        )

    def sends(self, dim, t):
        here, count = self.place.at[dim], self.place.count[dim]
        yield 1, here - t, (here - t >= 0) & (here < count - 1)
        yield -1, here + t, (here + t < count) & (here > 0)

    def arrivals(self, dim, t):
        here, count = self.place.at[dim], self.place.count[dim]
        yield 1, here - 1 - t, here - 1 - t >= 0
        yield -1, here + 1 + t, here + 1 + t < count

    def start(self):
        self.hand(len(self.slots), "", None, self.place.core).start()
        self.send_round(0)

    def send_round(self, number):
        dim, t = self.rounds[number]
        for way, position, valid in self.sends(dim, t):

            @pl.when(valid)
            def _(way=way, position=position):
                self.link(dim, t, way, position, self.place.neighbour(dim, way)).start()

    def advance(self, number):
        dim, t = self.rounds[number - 1]
        for way, position, valid in self.arrivals(dim, t):

            @pl.when(valid)
            def _(way=way, position=position):
                self.link(dim, t, way, position, self.place.partner()).wait_recv()
                self.hand(self.slots[dim, t, way], dim, position, self.place.core).start()

        if number < len(self.rounds):
            self.send_round(number)

    def steps(self):
        return [self.start] + [functools.partial(self.advance, n + 1) for n in range(len(self.rounds))]

    def finish(self):
        other = 1 - self.place.core
        self.hand(len(self.slots), "", None, other).wait_recv()
        for dim, t in self.rounds:
            for way, position, valid in self.arrivals(dim, t):

                @pl.when(valid)
                def _(dim=dim, t=t, way=way, position=position):
                    self.hand(self.slots[dim, t, way], dim, position, other).wait_recv()

    def drain(self):
        self.hand(len(self.slots), "", None, self.place.core).wait_send()
        for dim, t in self.rounds:
            for way, position, valid in self.sends(dim, t):

                @pl.when(valid)
                def _(dim=dim, t=t, way=way, position=position):
                    self.link(dim, t, way, position, self.place.partner()).wait_send()

            for way, position, valid in self.arrivals(dim, t):

                @pl.when(valid)
                def _(dim=dim, t=t, way=way, position=position):
                    self.hand(self.slots[dim, t, way], dim, position, self.place.core).wait_send()


class Scatter:
    def __init__(self, place, mine, axes, order, inbox, hand_box, sems, both=False):
        self.place, self.mine, self.axes, self.order, self.both = place, mine, axes, order, both
        self.inbox, self.hand_box = inbox, hand_box
        self.send, self.recv = sems
        self.rounds = [(dim, t) for dim in order for t in range(place.count[dim] - 1)]
        self.slots = {}
        for dim, t in self.rounds:
            for way in (1, -1):
                self.slots[dim, t, way] = len(self.slots) + 1

    def own(self, index):
        return index + ((() if self.both else (self.place.core,)))

    def hand(self):
        whole = tuple(pl.ds(0, self.place.count[axis]) for axis in self.axes)
        source = self.mine.at[whole] if self.both else self.mine.at[whole + (1 - self.place.core,)]
        return pltpu.make_async_remote_copy(
            source, self.hand_box, self.send.at[0], self.recv.at[0], device_id=self.place.partner(), device_id_type=MESH
        )

    def start(self):
        self.hand().start()

    def take_hand(self):
        self.hand().wait_recv()
        first = self.place.count[self.axes[0]]
        rest = tuple(pl.ds(0, self.place.count[axis]) for axis in self.axes[1:])
        if self.both:
            self.hand().wait_send()
            self.mine[...] = self.mine[...] + self.hand_box[...]
        else:
            for p in range(first):
                for r in range(self.place.count[self.axes[1]]):
                    index = (p, r) + rest[1:]
                    here = self.mine[index + (self.place.core,)].astype(F32)
                    there = self.hand_box[index].astype(F32)
                    self.mine[index + (self.place.core,)] = (here + there).astype(self.mine.dtype)
        self.send_round(0)

    def block(self, dim, position):
        done = self.order[: self.order.index(dim)]
        index = []
        for axis in self.axes:
            if axis == dim:
                index.append(position)
            elif axis in done:
                index.append(self.place.at[axis])
            else:
                index.append(pl.ds(0, self.place.count[axis]))
        return self.own(tuple(index))

    def link(self, dim, t, way, position, device):
        slot = self.slots[dim, t, way]
        return pltpu.make_async_remote_copy(
            self.mine.at[self.block(dim, position)],
            self.inbox[slot],
            self.send.at[slot],
            self.recv.at[slot],
            device_id=device,
            device_id_type=MESH,
        )

    def sends(self, dim, t):
        here, count = self.place.at[dim], self.place.count[dim]
        yield 1, count - 1 - t + here, (t >= here) & (here < count - 1)
        back = count - 1 - here
        yield -1, t - back, (t >= back) & (here > 0)

    def arrivals(self, dim, t):
        here, count = self.place.at[dim], self.place.count[dim]
        yield 1, count - 2 - t + here, (t >= here - 1) & (here > 0)
        back = count - 1 - here
        yield -1, t + 1 - back, (t >= back - 1) & (here < count - 1)

    def send_round(self, number):
        dim, t = self.rounds[number]
        for way, position, valid in self.sends(dim, t):

            @pl.when(valid)
            def _(way=way, position=position):
                self.link(dim, t, way, position, self.place.neighbour(dim, way)).start()

    def advance(self, number):
        dim, t = self.rounds[number - 1]
        for way, position, valid in self.arrivals(dim, t):

            @pl.when(valid)
            def _(way=way, position=position):
                self.link(dim, t, way, position, self.place.partner()).wait_recv()
                index = self.block(dim, position)
                total = self.mine[index].astype(F32) + self.inbox[self.slots[dim, t, way]][...].astype(F32)
                self.mine[index] = total.astype(self.mine.dtype)

        if number < len(self.rounds):
            self.send_round(number)

    def steps(self):
        later = [functools.partial(self.advance, n + 1) for n in range(len(self.rounds))]
        return [self.start, self.take_hand] + later

    def result(self):
        return self.mine[self.own(tuple(self.place.at[axis] for axis in self.axes))]

    def drain(self):
        if not self.both:
            self.hand().wait_send()
        for dim, t in self.rounds:
            for way, position, valid in self.sends(dim, t):

                @pl.when(valid)
                def _(dim=dim, t=t, way=way, position=position):
                    self.link(dim, t, way, position, self.place.partner()).wait_send()


def inbox_shapes(count, axes, order, block):
    shapes, slots, left = [], {}, dict(count)
    for dim in order:
        left.pop(dim)
        for t in range(count[dim] - 1):
            for way in (1, -1):
                if way == 1 or count[dim] > 2:
                    shapes.append(tuple(count[axis] for axis in axes if axis in left) + block)
                slots[dim, t, way] = len(shapes) - 1
    return shapes, slots


def open_inbox(run, count, axes, order, block, boxes):
    shapes, slots = inbox_shapes(count, axes, order, block)
    for key, slot in run.slots.items():
        run.inbox[slot] = boxes[slots[key]]
    del boxes[: len(shapes)]


def play(plan, comm, pieces):
    for token in plan:
        if token < 0:
            pieces.pop(0)()
        elif comm:
            comm[token].pop(0)()
    assert not pieces and not any(comm.values())


class Mover:
    def __init__(self, sems):
        self.sems, self.used, self.open = sems, 0, []

    def start(self, source, target):
        copy = pltpu.make_async_copy(source, target, self.sems.at[self.used])
        self.used += 1
        copy.start()
        return copy

    def save(self, source, target):
        self.open.append(self.start(source, target))

    def close(self):
        for copy in self.open:
            copy.wait()


def read_vectors(vectors, tiles):
    nz, nx = tiles.shape[:2]
    pieces = [tiles[z, x, 0] + tiles[z, x, 1] for z in range(nz) for x in range(nx)]
    vectors[...] = jnp.concatenate(pieces, axis=1)


def column_parts(weights):
    wq, wk, wv, wo, wu, wd = weights
    left, right = pl.ds(0, SEG), pl.ds(SEG, SEG)
    return [wq, wk, wv, wo, wu.at[:, left], wu.at[:, right], wd.at[:, left], wd.at[:, right]]


def fill_tile(place, tiles, norms):
    tile = (place.at["z"], place.at["x"], place.core)
    tiles[tile] = jnp.zeros(tiles.shape[3:], F32)
    share = norms[0].shape[1]
    for line, norm in enumerate(norms):
        value = norm[...].astype(F32)
        for core in range(2):

            @pl.when(place.core == core)
            def _(line=line, value=value, core=core):
                tiles[tile + (slice(line, line + 1), slice(core * share, (core + 1) * share))] = value


FWD_OUT = ("x", "nrm", "q", "k", "v", "probs", "mix", "res", "nrm2", "active", "slope", "out")


def forward_kernel(shape, micro, tokens, *refs):
    if shape:
        weights, norms, g_out, refs = refs[:6], refs[6:10], refs[10], refs[11:]
    else:
        g_in, vectors_in, refs = refs[0], refs[1], refs[2:]
    if shape:
        vectors, refs = refs[0], refs[1:]
    else:
        vectors = vectors_in
    saved = dict(zip(FWD_OUT, refs[:12]))
    here = dict(zip(FWD_OUT, refs[12:24]))
    raw, low, total, g, sems = refs[24:29]
    mover = Mover(sems)
    y = lax.axis_index("mp")
    take = mover.start(tokens.at[pl.ds(y * micro, micro)], raw)
    x, nrm, q, k, v, probs, mix, res, nrm2, active, slope, out = (here[name] for name in FWD_OUT)

    def keep(*names):
        for name in names:
            mover.save(here[name], saved[name])

    comm = {}
    if shape:
        tiles, send, recv, pass_send, pass_recv = refs[29:]
        place = Place(shape)
        spot = (place.at["y"], place.at["z"], place.at["x"], place.core)
        mine = [mover.start(part, g.at[(seg,) + spot]) for seg, part in enumerate(column_parts(weights))]
        fill_tile(place, tiles, norms)
        place.barrier("zxy")
        pick = lambda seg: tuple(sem.at[seg] for sem in (send, recv, pass_send, pass_recv))
        runs = [Gather(place, g.at[seg], "yzx", ORDERS[seg], pick(seg)) for seg in range(8)]
        runs.append(Gather(place, tiles, "zx", "zx", pick(8)))
        comm = {seg: run.steps() for seg, run in enumerate(runs)}
        for seg in range(8):
            comm[seg][0] = lambda seg=seg: (mine[seg].wait(), runs[seg].start())

        def have(seg):
            runs[seg].finish()
            if seg < 8:
                mover.save(g.at[seg], g_out.at[seg])
            else:
                read_vectors(vectors, tiles)

    else:
        loads = [mover.start(g_in.at[seg], g.at[seg]) for seg in range(8)]

        def have(seg):
            if seg < 8:
                loads[seg].wait()

    def spread():
        take.wait()
        to_rows(raw, x)
        keep("x")

    def norm_one():
        have(8)
        norm_in(x, nrm, vectors[0:1, :], vectors[1:2, :])
        keep("nrm")

    def head_part(seg, target, name):
        have(seg)
        project(nrm, g, seg, target)
        keep(name)

    groups = x.shape[0] // TILE
    third = groups // 3

    def mixing(part):
        attend(q, k, v, probs, mix, part * third, third)
        if part == 2:
            keep("probs", "mix")

    def project_out():
        have(O)
        res[...] = x[...].astype(F32)
        back_through(lambda m: mix[:, half(m)], g, O, res)
        keep("res")

    def norm_two():
        gain, shift = vectors[2:3, :], vectors[3:4, :]

        def block(rows, _):
            normal, _inv = norm_stats(res[rows, :])
            nrm2[rows, :] = (normal * gain + shift).astype(BF)

        row_loop(x.shape[0], block)
        keep("nrm2")

    def up(which, m):
        if m == 0:
            have(UPS[which])
        feed_up(nrm2, g, which, m, active, slope)
        mover.save(active.at[which, m], saved["active"].at[which, m])
        mover.save(slope.at[which, m], saved["slope"].at[which, m])

    def down(which):
        have(DOWNS[which])
        if which == 0:
            total[...] = res[...]
        back_through(lambda m: active[which, m], g, DOWNS[which], total)

    def last():
        low[...] = total[...].astype(BF)
        from_rows(low, out)
        keep("out")

    pieces = [spread, norm_one]
    pieces += [functools.partial(head_part, *args) for args in ((Q, q, "q"), (K, k, "k"), (V, v, "v"))]
    pieces += [functools.partial(mixing, part) for part in range(3)] + [project_out, norm_two]
    pieces += [functools.partial(up, which, m) for which in range(2) for m in range(2)]
    pieces += [functools.partial(down, which) for which in range(2)] + [last]
    play(FORWARD_PLAN, comm, pieces)
    if shape:
        for run in runs:
            run.drain()
    mover.close()


def row_weights(ids, counts, y, micro, target):
    series = ids.shape[1]
    sums = counts[0]
    for kind in range(1, counts.shape[0]):
        sums = sums + counts[kind]
    mean = jnp.full((PAD, 1), sums.astype(F32), F32) / counts.shape[0]

    def one(index, carry):
        kind = ids[y * micro + lax.div(index, series), lax.rem(index, series)]
        count = counts[kind].astype(F32)
        target[pl.ds(pl.multiple_of(index * PAD, PAD), PAD), :] = 2.0 * mean / (mean + count)
        return carry

    lax.fori_loop(0, micro * series, one, 0)


class Swap:
    def __init__(self, place, mover, sems, ready, source, target):
        self.mover, self.source, self.ready = mover, source, ready
        y, (micro, patches) = place.at["y"], source.shape[:2]
        cut = patches // 2 + 1
        self.spot = target.at[pl.ds(y * micro, micro)]
        self.copies = []
        for part in range(micro):
            for piece in (pl.ds(0, cut), pl.ds(cut, patches - cut)):
                slot = 2 * len(self.copies)
                self.copies.append(
                    pltpu.make_async_remote_copy(
                        source.at[part, piece],
                        target.at[y * micro + part, piece],
                        sems.at[slot],
                        sems.at[slot + 1],
                        device_id=place.device(y=1 - y),
                        device_id_type=MESH,
                    )
                )

    def start(self):
        self.ready()
        self.copies[0].start()
        self.mover.save(self.source, self.spot)

    def steps(self):
        return [self.start] + [copy.start for copy in self.copies[1:]]

    def wait(self):
        for copy in self.copies:
            copy.wait()


def feed_back_kernel(
    shape, micro, cotangent, ids, counts, vectors, g_in, active_in, slope_in, nrm2_in, res_in, out_in, *refs
):
    if shape:
        dw_out, gres_out, vec, pair, grad_down, refs = refs[:5] + (refs[5:],)
    else:
        dw_out, gres_out, vec, refs = refs[:3] + (refs[3:],)
    raw, cot, weight, active, slope, nrm2, res, g, dw, gl, glt, gh, n2t, gn2, gres, sems = refs[:16]
    mover = Mover(sems)
    y = lax.axis_index("mp")
    loads = {"raw": mover.start(cotangent.at[pl.ds(y * micro, micro)], raw)}
    for which in range(2):
        loads["active", which] = mover.start(active_in.at[which], active.at[which])
        loads["d", which] = mover.start(g_in.at[DOWNS[which]], g.at[2 + which])
        loads["slope", which] = mover.start(slope_in.at[which], slope.at[which])
    loads["nrm2"] = mover.start(nrm2_in, nrm2)
    for which in range(2):
        loads["u", which] = mover.start(g_in.at[UPS[which]], g.at[which])
    loads["res"] = mover.start(res_in, res)
    comm = {}
    if shape:
        half_out, hands, send, recv, ysem = refs[16:21]
        boxes = list(refs[21:])
        side = mover.start(out_in, half_out)
        place = Place(shape)
        place.barrier("zxy")
        runs = []
        for which in range(2):
            order = BACK_ORDERS[DOWNS[which]]
            run = Scatter(
                place, dw.at[2 + which], "yzx", order, {}, hands.at[which], (send.at[which], recv.at[which])
            )
            open_inbox(run, place.count, "yzx", order, dw.shape[-2:], boxes)
            runs.append(run)
        swap = Swap(place, mover, ysem, side.wait, half_out, pair)
        comm = {0: runs[0].steps(), 1: runs[1].steps(), 2: swap.steps()}
    row_weights(ids, counts, y, micro, weight)

    def spread():
        loads["raw"].wait()
        to_rows(raw, cot)

    def first():
        def block(rows, _):
            gl[rows, :] = (cot[rows, :].astype(F32) * weight[rows, :]).astype(BF)

        row_loop(cot.shape[0], block)
        turn(gl, glt)

    def down_grad(which):
        loads["active", which].wait()
        weight_grad(glt, lambda m: active[which, m], dw, 2 + which)
        if not shape:
            mover.save(dw.at[2 + which], dw_out.at[2 + which])

    def hidden_grad(which):
        loads["d", which].wait()
        loads["slope", which].wait()

        def one(m):
            pulled = nn(gl[...], flat(g[2 + which, m]))
            gh[which, m] = (pulled * slope[which, m]).astype(BF)

        half_loop(g.shape[1], one)

    def turn_two():
        loads["nrm2"].wait()
        turn(nrm2, n2t)
        gn2[...] = jnp.zeros_like(gn2)

    def up_grad(which):
        weight_grad(n2t, lambda m: gh[which, m], dw, which)
        mover.save(dw.at[which], dw_out.at[which])

    def norm_grad(which):
        loads["u", which].wait()
        back_through(lambda m: gh[which, m], g, which, gn2)

    def last():
        loads["res"].wait()
        gain = vectors[2:3, :]
        vec[...] = jnp.zeros_like(vec)

        def block(rows, _):
            grad = gn2[rows, :]
            pulled, normal = norm_pull(grad, res[rows, :], gain)
            vec[0] += fold_rows(grad * normal)
            vec[1] += fold_rows(grad)
            gres[rows, :] = cot[rows, :].astype(F32) * weight[rows, :] + pulled

        row_loop(cot.shape[0], block)
        mover.save(gres, gres_out)

    pieces = [spread, first]
    for which in range(2):
        pieces += [functools.partial(down_grad, which), functools.partial(hidden_grad, which)]
    pieces.append(turn_two)
    for which in range(2):
        pieces += [functools.partial(up_grad, which), functools.partial(norm_grad, which)]
    pieces.append(last)
    play(FEED_PLAN, comm, pieces)
    if shape:
        for which in range(2):
            grad_down[:, which * SEG : (which + 1) * SEG] = runs[which].result().astype(F32)
            runs[which].drain()
        swap.wait()
    mover.close()


def vector_tiles(tiles, vec_a, vec_f):
    tiles[...] = jnp.zeros_like(tiles)
    nz, nx = tiles.shape[:2]
    for line, (source, part) in enumerate(((vec_a, 0), (vec_a, 1), (vec_f, 0), (vec_f, 1))):
        row = jnp.sum(source[part], axis=0, keepdims=True)
        for z in range(nz):
            for x in range(nx):
                chip = z * nx + x
                tiles[z, x, line : line + 1, :] = row[:, chip * 128 : (chip + 1) * 128]


BACK_IN = ("gres", "mix", "nrm", "q", "k", "v", "probs")
SHARED = (U0, U1, O, Q, K, V)


def attn_back_kernel(shape, vectors, vec_f, g_in, dw_up, x_in, *refs):
    given = dict(zip(BACK_IN, refs[:7]))
    refs = refs[7:]
    if shape:
        pair, grads, vec_out, refs = refs[0], refs[1:6], refs[6], refs[7:]
    else:
        dw_out, out, vec, refs = refs[0], refs[1], refs[2], refs[3:]
    here = dict(zip(BACK_IN, refs[:7]))
    g, dw, gal, turned, gm, gq, gk, gv, raw, sems = refs[7:17]
    mover = Mover(sems)
    loads = {"gres": mover.start(given["gres"], here["gres"]), "mix": mover.start(given["mix"], here["mix"])}
    comm = {}
    if shape:
        ups, tiles, hands, vec_hand, ybox, vec, send, recv, ysem = refs[17:26]
        boxes = list(refs[26:])
        for which in range(2):
            loads["dw", which] = mover.start(dw_up.at[which], ups.at[which])
    loads[O] = mover.start(g_in.at[O], g.at[O])
    for name in BACK_IN[2:]:
        loads[name] = mover.start(given[name], here[name])
    for seg in (Q, K, V):
        loads[seg] = mover.start(g_in.at[seg], g.at[seg])
    gres, mix, nrm, q, k, v, probs = (here[name] for name in BACK_IN)
    x, gn = mix, probs
    if shape:
        place = Place(shape)
        place.barrier("zxy")
        runs = []
        for spot, seg in enumerate(SHARED):
            source = ups.at[spot] if spot < 2 else dw.at[seg]
            order = BACK_ORDERS[seg]
            run = Scatter(place, source, "yzx", order, {}, hands.at[spot], (send.at[spot], recv.at[spot]))
            open_inbox(run, place.count, "yzx", order, dw.shape[-2:], boxes)
            runs.append(run)
        run = Scatter(place, tiles, "zx", "zx", {}, vec_hand, (send.at[6], recv.at[6]), both=True)
        open_inbox(run, {"z": place.nz, "x": place.nx}, "zx", "zx", (8, 128), boxes)
        runs.append(run)
        swap = Swap(place, mover, ysem, lambda: None, raw, pair)
        comm = {spot: run.steps() for spot, run in enumerate(runs)}
        comm[7] = swap.steps()
        for which in range(2):
            comm[which][0] = lambda which=which: (loads["dw", which].wait(), runs[which].start())

    def first():
        loads["gres"].wait()

        def block(rows, _):
            gal[rows, :] = gres[rows, :].astype(BF)

        row_loop(gal.shape[0], block)

    def out_grad():
        loads["mix"].wait()
        weight_grad(turned, lambda m: mix[:, half(m)], dw, O)
        if not shape:
            mover.save(dw.at[O], dw_out.at[O])

    def mix_grad():
        loads["x"] = mover.start(x_in, x)
        loads[O].wait()
        project(gal, g, O, gm)

    def turn_normed():
        loads["nrm"].wait()
        turn(nrm, turned)

    groups = gal.shape[0] // TILE
    third = groups // 3

    def mixing(part):
        if part == 0:
            for name in ("q", "k", "v", "probs"):
                loads[name].wait()
        attend_back(q, k, v, probs, gm, gq, gk, gv, part * third, third)

    def head_grad(seg, grad):
        weight_grad(turned, lambda m: grad[:, half(m)], dw, seg)
        if not shape:
            mover.save(dw.at[seg], dw_out.at[seg])

    def norm_grad(seg, grad):
        if seg == Q:
            gn[...] = jnp.zeros_like(gn)
        loads[seg].wait()
        back_through(lambda m: grad[:, half(m)], g, seg, gn)

    def last():
        loads["x"].wait()
        gain = vectors[0:1, :]
        vec[...] = jnp.zeros_like(vec)

        def block(rows, _):
            grad = gn[rows, :]
            pulled, normal = norm_pull(grad, x[rows, :].astype(F32), gain)
            vec[0] += fold_rows(grad * normal)
            vec[1] += fold_rows(grad)
            gal[rows, :] = (gres[rows, :] + pulled).astype(BF)

        row_loop(gal.shape[0], block)
        from_rows(gal, raw)
        if shape:
            vector_tiles(tiles, vec, vec_f)
        else:
            mover.save(raw, out)

    heads = ((Q, gq), (K, gk), (V, gv))
    pieces = [first, lambda: turn(gal, turned), out_grad, mix_grad, turn_normed]
    pieces += [functools.partial(mixing, part) for part in range(3)]
    pieces += [functools.partial(head_grad, *pair_of) for pair_of in heads[:GRADS_FIRST]]
    pieces += [functools.partial(norm_grad, *pair_of) for pair_of in heads] + [last]
    pieces += [functools.partial(head_grad, *pair_of) for pair_of in heads[GRADS_FIRST:]]
    play(ATTN_PLAN, comm, pieces)
    if shape:
        here_tile = tiles.at[place.at["z"], place.at["x"]]
        copy = pltpu.make_async_remote_copy(
            here_tile, ybox, ysem.at[8], ysem.at[9], device_id=place.device(y=1 - place.at["y"]), device_id_type=MESH
        )
        copy.start()
        for spot, seg in enumerate(SHARED[2:]):
            grads[(3, 0, 1, 2)[spot]][...] = runs[2 + spot].result().astype(F32)
        for which in range(2):
            grads[4][:, which * SEG : (which + 1) * SEG] = runs[which].result().astype(F32)
        for run in runs:
            run.drain()
        copy.wait()
        vec_out[...] = tiles[place.at["z"], place.at["x"]] + ybox[...]
        swap.wait()
    mover.close()


def shape_of(shape, dtype):
    return jax.ShapeDtypeStruct(shape, dtype)


IN_VMEM = pl.BlockSpec(memory_space=pltpu.VMEM)
IN_SMEM = pl.BlockSpec(memory_space=pltpu.SMEM)
ANYWHERE = pl.BlockSpec(memory_space=pl.ANY)
DMA = pltpu.SemaphoreType.DMA


def call(body, outs, ins, out_specs, scratch, name, collective=None):
    params = {"vmem_limit_bytes": VMEM_LIMIT}
    if collective is not None:
        params.update(collective_id=collective, has_side_effects=True)
    return pl.pallas_call(
        body,
        out_shape=outs,
        in_specs=ins,
        out_specs=out_specs,
        scratch_shapes=scratch,
        compiler_params=pltpu.CompilerParams(**params),
        name=name,
    )


def vmem(like):
    return pltpu.VMEM(like.shape, like.dtype)


def forward(shape, micro, tokens, weights, norms, g_in=None, vectors_in=None):
    _, patches, series, width = tokens.shape
    rows = micro * series * PAD
    full = g_in.shape if shape is None else (8, shape[2], shape[0], shape[1], 2, weights[0].shape[0], SEG)
    low, high = shape_of((rows, width), BF), shape_of((rows, width), F32)
    wide = (2, full[1], rows, SEG)
    raw = shape_of((micro, patches, series, width), BF)
    kinds = {name: low for name in FWD_OUT}
    kinds.update(
        probs=high,
        res=high,
        active=shape_of(wide, BF),
        slope=shape_of(wide, F32),
        out=raw,
    )
    saved = tuple(kinds[name] for name in FWD_OUT)
    scratch = [vmem(kind) for kind in saved] + [vmem(raw), vmem(low), vmem(high), pltpu.VMEM(full, BF), DMA((64,))]
    if shape is None:
        results = call(
            functools.partial(forward_kernel, None, micro),
            saved,
            [ANYWHERE, ANYWHERE, IN_VMEM],
            (ANYWHERE,) * 12,
            scratch,
            "forward",
        )(tokens, g_in, vectors_in)
        return g_in, vectors_in, dict(zip(FWD_OUT, results))
    count = dict(zip("zxy", shape))
    slots = link_slots(count, "zxy")
    scratch += [pltpu.VMEM(shape[:2] + (2, 8, 128), F32)]
    scratch += [DMA((9, slots)), DMA((9, slots)), DMA((9, slots + 1)), DMA((9, slots + 1))]
    results = call(
        functools.partial(forward_kernel, shape, micro),
        (shape_of(full, BF), shape_of((8, width), F32)) + saved,
        [ANYWHERE] * 7 + [IN_VMEM] * 4,
        (ANYWHERE, IN_VMEM) + (ANYWHERE,) * 12,
        scratch,
        "forward",
        0,
    )(tokens, *weights, *norms)
    return results[0], results[1], dict(zip(FWD_OUT, results[2:]))


def scatter_scratch(segs, part, count, orders):
    rows, cols = part.shape[-2:]
    slots = link_slots(count, "zxy") + 1
    boxes = []
    for order in orders:
        boxes += [pltpu.VMEM(s, BF) for s in inbox_shapes(count, "yzx", order, (rows, cols))[0]]
    hands = pltpu.VMEM((len(orders),) + part.shape[1:4] + (rows, cols), BF)
    return hands, [DMA((segs, slots)), DMA((segs, slots))], boxes


def pair_of(raw, ny):
    return shape_of((ny * raw.shape[0],) + raw.shape[1:], BF)


def feed_back(shape, micro, cotangent, ids, counts, vectors, g, kept):
    _, patches, series, width = cotangent.shape
    low, high, raw = kept["x"], kept["res"], kept["out"]
    rows = low.shape[0]
    part = shape_of((4,) + g.shape[1:], BF)
    turned = pltpu.VMEM((width, rows), BF)
    scratch = [
        vmem(raw),
        vmem(low),
        pltpu.VMEM((rows, 1), F32),
        vmem(kept["active"]),
        vmem(kept["slope"]),
        vmem(low),
        vmem(high),
        vmem(part),
        vmem(part),
        vmem(low),
        turned,
        vmem(kept["active"]),
        turned,
        vmem(high),
        vmem(high),
        DMA((32,)),
    ]
    given = (g, kept["active"], kept["slope"], kept["nrm2"], kept["res"], raw)
    outs = [part, shape_of(high.shape, F32), shape_of((2, 8, width), F32)]
    specs = [ANYWHERE, ANYWHERE, IN_VMEM]
    if shape:
        count = dict(zip("zxy", shape))
        hands, sems, boxes = scatter_scratch(2, part, count, [BACK_ORDERS[seg] for seg in DOWNS])
        scratch += [vmem(raw), hands] + sems + [DMA((8,))] + boxes
        outs += [pair_of(raw, shape[2]), shape_of((part.shape[-2], 2 * SEG), F32)]
        specs += [ANYWHERE, IN_VMEM]
    return call(
        functools.partial(feed_back_kernel, shape, micro),
        tuple(outs),
        [ANYWHERE, IN_SMEM, IN_SMEM, IN_VMEM] + [ANYWHERE] * 6,
        tuple(specs),
        scratch,
        "feed_back",
        1 if shape else None,
    )(cotangent, ids, counts, vectors, *given)


def attn_back(shape, vectors, vec_f, g, dw_up, kept):
    low, high, raw = kept["x"], kept["res"], kept["out"]
    rows, width = low.shape
    part = shape_of((4,) + g.shape[1:], BF)
    turned = pltpu.VMEM((width, rows), BF)
    scratch = [vmem(kept[name]) for name in BACK_IN]
    scratch += [vmem(part), vmem(part), vmem(low), turned, vmem(low), vmem(low), vmem(low), vmem(low), vmem(raw)]
    scratch += [DMA((32,))]
    vec = shape_of((2, 8, width), F32)
    if shape:
        nz, nx, ny = shape
        count = dict(zip("zxy", shape))
        share = part.shape[-2]
        small, large = shape_of((share, SEG), F32), shape_of((share, 2 * SEG), F32)
        outs = [pair_of(raw, ny)] + [small] * 4 + [large, shape_of((8, 128), F32)]
        specs = [ANYWHERE] + [IN_VMEM] * 6
        hands, sems, boxes = scatter_scratch(7, part, count, [BACK_ORDERS[seg] for seg in SHARED])
        tiles = pltpu.VMEM((nz, nx, 8, 128), F32)
        scratch += [pltpu.VMEM((2,) + part.shape[1:], BF), tiles, hands, tiles, pltpu.VMEM((8, 128), F32), vmem(vec)]
        scratch += sems + [DMA((10,))] + boxes
        scratch += [pltpu.VMEM(s, F32) for s in inbox_shapes({"z": nz, "x": nx}, "zx", "zx", (8, 128))[0]]
    else:
        outs, specs = [part, raw, vec], [ANYWHERE, ANYWHERE, IN_VMEM]
        outs[1] = shape_of(raw.shape, BF)
    return call(
        functools.partial(attn_back_kernel, shape),
        tuple(outs),
        [IN_VMEM] * 2 + [ANYWHERE] * 10,
        tuple(specs),
        scratch,
        "attn_back",
        2 if shape else None,
    )(vectors, vec_f, g, dw_up, kept["x"], *(kept[name] for name in BACK_IN))


def chip_grid(chips):
    nx = 1
    while (nx * 2) ** 2 <= chips:
        nx *= 2
    return chips // nx, nx


def body(counts_of, tokens, cotangent, domain_ids, domain_counts, *params):
    weights, norms = params[:6], params[6:]
    n_dp, n_mp = counts_of
    micro = tokens.shape[0] // n_mp
    width = tokens.shape[3]
    share = width // n_dp
    y = lax.axis_index("mp")
    linked = n_mp == 2 and share * 2 == TILE
    flip = lambda array: jnp.transpose(array, (0, 2, 1, 3))
    x, cot = flip(tokens), flip(cotangent)
    if linked:
        shape = chip_grid(n_dp // 2) + (n_mp,)
        g, vectors, kept = forward(shape, micro, x, weights, [norm.reshape(1, -1) for norm in norms])
    else:
        shards = jnp.stack(
            weights[:4] + tuple(w[:, i * SEG : (i + 1) * SEG] for w in weights[4:] for i in range(2))
        )
        g = lax.all_gather(lax.all_gather(shards, "dp", axis=1, tiled=True), "mp", axis=1)
        vectors = lax.all_gather(jnp.stack(norms), "dp", axis=1, tiled=True).astype(F32)
        vectors = jnp.pad(vectors, ((0, 4), (0, 0)))
        g, vectors, kept = forward(None, micro, x, None, None, g, vectors)
    shape = shape if linked else None
    results = feed_back(shape, micro, cot, domain_ids, domain_counts, vectors, g, kept)
    dw_f, gres, vec_f = results[:3]
    kept = {**kept, "gres": gres}
    if linked:
        out, grad_down = results[3:]
        grad_tokens, *grads, vec = attn_back(shape, vectors, vec_f, g, dw_f, kept)
        grads.append(grad_down)
        core = lax.rem(lax.axis_index("dp"), 2)
        vec = lax.dynamic_slice(vec, (0, core * share), (4, share))
    else:
        dw_a, low_tokens, vec_a = attn_back(shape, vectors, vec_f, g, dw_f, kept)
        dw = jnp.concatenate((dw_a, dw_f)).astype(F32)
        dw = lax.psum_scatter(lax.psum_scatter(dw, "mp", scatter_dimension=1), "dp", scatter_dimension=1, tiled=True)
        grads = [dw[0], dw[1], dw[2], dw[3]]
        grads += [jnp.concatenate((dw[a], dw[b]), axis=1) for a, b in (UPS, DOWNS)]
        vec = jnp.concatenate((jnp.sum(vec_a, axis=1), jnp.sum(vec_f, axis=1)))
        vec = lax.psum_scatter(lax.psum(vec, "mp"), "dp", scatter_dimension=1, tiled=True)
        out = lax.all_gather(kept["out"], "mp", axis=0, tiled=True)
        grad_tokens = lax.all_gather(low_tokens, "mp", axis=0, tiled=True)
    return (flip(out), flip(grad_tokens.astype(F32)), *grads, vec[0], vec[1], vec[2], vec[3])


def solution(mesh):
    rows, matrix, vector = P(None, "dp", None, None), P("dp", "mp"), P("dp")
    in_specs = (rows, rows, P(None, "dp"), P()) + (matrix,) * 6 + (vector,) * 4
    out_specs = (rows, rows) + (matrix,) * 6 + (vector,) * 4
    run = functools.partial(body, (mesh.shape["dp"], mesh.shape["mp"]))
    return jax.shard_map(run, mesh=mesh, in_specs=in_specs, out_specs=out_specs, check_vma=False)
```

```python
import functools

import jax
import jax.numpy as jnp
from jax import lax
from jax.experimental import pallas as pl
from jax.experimental.pallas import tpu as pltpu
from jax.sharding import PartitionSpec as P

BF = jnp.bfloat16
F32 = jnp.float32
HD = 128
SEG = 512
TILE = 128
PAD = 16
EPS = 1e-05
MESH = pl.DeviceIdType.MESH
VMEM_LIMIT = 62 * 1024 * 1024

Q, K, V, O, U0, U1, D0, D1 = range(8)
UPS = (U0, U1)
DOWNS = (D0, D1)
ORDERS = ("zyx", "xyz", "zxy", "zyx", "zxy", "yxz", "zyx", "yxz")
BACK_ORDERS = ("xzy", "xzy", "yxz", "zxy", "yzx", "xyz", "zxy", "xyz")

FORWARD_PLAN = (
    2, 1, 8, 4, 5, 6, 2, 8, 0, -1, 2, 4, 2, 0, 1, 3, 0, 4, 6, 3, 7, 8, 1, 5,
    0, 2, 8, 4, 0, 3, 3, 1, 8, -1, 6, 6, 1, 5, -1, 7, 2, 4, 0, 3, 1, -1, -1, 5,
    -1, -1, 7, -1, 3, 6, 5, -1, -1, 7, 4, -1, -1, 5, -1, 6, 7, -1, -1, 7, -1, -1, -1,
)
FEED_PLAN = (
    2, -1, 0, -1, -1, 1, 2, 0, 1, -1, 2, -1, 0, -1, -1, -1, 0, 1, -1, 2, -1, 0, 1, -1,
    1, 0, -1, 1, -1, 0, 1,
)
ATTN_PLAN = (
    0, 2, -1, 1, -1, 1, 0, -1, -1, 2, -1, 3, -1, 1, -1, 5, 2, 3, -1, 5, 0, -1, -1, 2,
    -1, 7, 4, 3, 6, 6, 1, 7, 4, 6, 5, 7, 0, 2, 1, 1, 7, 3, 3, 0, 4, 4, 6, 5,
    2, 4, 0, 5, 1, 6, 4, 3, 5, 0, 4, 2, 6, 5, 3,
)
GRADS_FIRST = 3


def nn(a, b):
    return lax.dot_general(a, b, (((1,), (0,)), ((), ())), preferred_element_type=F32)


def nt(a, b):
    return lax.dot_general(a, b, (((1,), (1,)), ((), ())), preferred_element_type=F32)


def flat(value):
    return value.reshape(-1, value.shape[-1])


def norm_stats(values):
    mean = jnp.mean(values, axis=-1, keepdims=True)
    center = values - mean
    inverse = lax.rsqrt(jnp.mean(center * center, axis=-1, keepdims=True) + EPS)
    return center * inverse, inverse


def norm_pull(grad, values, gain):
    normal, inverse = norm_stats(values)
    scaled = grad * gain
    first = jnp.mean(scaled, axis=-1, keepdims=True)
    second = jnp.mean(scaled * normal, axis=-1, keepdims=True)
    return inverse * (scaled - first - normal * second), normal


def fold_rows(values):
    rows, width = values.shape
    return jnp.sum(values.reshape(rows // 8, 8, width), axis=0)


def score_mask():
    row = lax.broadcasted_iota(jnp.int32, (TILE, TILE), 0)
    col = lax.broadcasted_iota(jnp.int32, (TILE, TILE), 1)
    return (row // PAD == col // PAD) & (col <= row)


def row_loop(rows, body, first=0):
    def once(index, carry):
        index = first + index
        body(pl.ds(pl.multiple_of(index * TILE, TILE), TILE), index)
        return carry

    lax.fori_loop(0, rows // TILE, once, 0)


def half_loop(count, body):
    def once(index, carry):
        body(index)
        return carry

    lax.fori_loop(0, count, once, 0)


def half(index):
    return pl.ds(pl.multiple_of(index * SEG, SEG), SEG)


def spread_rows(patches, series):
    row = lax.broadcasted_iota(jnp.int32, (series * PAD, patches * series), 0)
    col = lax.broadcasted_iota(jnp.int32, (series * PAD, patches * series), 1)
    hit = (lax.rem(row, PAD) * series + lax.div(row, PAD) == col) & (lax.rem(row, PAD) < patches)
    return jnp.where(hit, 1.0, 0.0).astype(BF)


def gather_rows(patches, series):
    row = lax.broadcasted_iota(jnp.int32, (patches * series, series * PAD), 0)
    col = lax.broadcasted_iota(jnp.int32, (patches * series, series * PAD), 1)
    return jnp.where(lax.rem(row, series) * PAD + lax.div(row, series) == col, 1.0, 0.0).astype(BF)


def to_rows(raw, target):
    micro, patches, series, _ = raw.shape
    matrix = spread_rows(patches, series)
    for part in range(micro):
        target[part * series * PAD : (part + 1) * series * PAD, :] = nn(matrix, flat(raw[part])).astype(BF)


def from_rows(source, raw):
    micro, patches, series, width = raw.shape
    matrix = gather_rows(patches, series)
    for part in range(micro):
        rows = source[part * series * PAD : (part + 1) * series * PAD, :]
        raw[part] = nn(matrix, rows).astype(raw.dtype).reshape(patches, series, width)


def norm_in(x, normed, gain, shift):
    def block(rows, _):
        normal, _inv = norm_stats(x[rows, :].astype(F32))
        normed[rows, :] = (normal * gain + shift).astype(BF)

    row_loop(x.shape[0], block)


def project(source, weights, seg, target):
    def one(m):
        target[:, half(m)] = nn(source[...], flat(weights[seg, m])).astype(BF)

    half_loop(weights.shape[1], one)


def attend(queries, keys, values, probs, mixture, first, count):
    mask = score_mask()
    scale = HD ** (-0.5)

    def group(rows, index):
        for head in range(queries.shape[1] // HD):
            cols = slice(head * HD, (head + 1) * HD)
            scores = nt(queries[rows, cols], keys[rows, cols]) * scale
            scores = jnp.where(mask, scores, -1e30)
            powers = jnp.exp(scores - jnp.max(scores, axis=-1, keepdims=True))
            share = powers * (1.0 / jnp.sum(powers, axis=-1, keepdims=True))
            probs[rows, cols] = share
            mixture[rows, cols] = nn(share.astype(BF), values[rows, cols]).astype(BF)

    row_loop(count * TILE, group, first)


def attend_back(queries, keys, values, probs, grad_mix, grad_q, grad_k, grad_v, first, count):
    scale = HD ** (-0.5)

    def group(rows, index):
        for head in range(queries.shape[1] // HD):
            cols = slice(head * HD, (head + 1) * HD)
            share = probs[rows, cols]
            grad = grad_mix[rows, cols]
            grad_share = nt(grad, values[rows, cols])
            grad_v[rows, cols] = nn(share.T.astype(BF), grad).astype(BF)
            inner = jnp.sum(grad_share * share, axis=-1, keepdims=True)
            grad_scores = share * (grad_share - inner)
            low = grad_scores.astype(BF)
            grad_q[rows, cols] = (nn(low, keys[rows, cols]) * scale).astype(BF)
            turned = grad_scores.T.astype(BF)
            grad_k[rows, cols] = (nn(turned, queries[rows, cols]) * scale).astype(BF)

    row_loop(count * TILE, group, first)


def back_through(source, weights, seg, total):
    def one(m):
        total[...] += nt(source(m), flat(weights[seg, m]))

    half_loop(weights.shape[1], one)


def feed_up(normed_two, weights, which, m, active, slope):
    hidden = nn(normed_two[...], flat(weights[UPS[which], m]))
    bell = 0.5 + 0.5 * lax.erf(hidden * (0.5**0.5))
    active[which, m] = (hidden * bell).astype(BF)
    density = jnp.exp(-0.5 * hidden * hidden) * 0.3989422804014327
    slope[which, m] = bell + hidden * density


def turn(source, target):
    def block(rows, _):
        target[:, rows] = source[rows, :].T

    row_loop(source.shape[0], block)


def weight_grad(turned, right, target, seg):
    def one(m):
        product = nn(turned[...], right(m)).astype(BF)
        target[seg, m] = product.reshape(target.shape[2:])

    half_loop(target.shape[1], one)


class Place:
    def __init__(self, shape):
        self.nz, self.nx, self.ny = shape
        index = lax.axis_index("dp")
        self.core = lax.rem(index, 2)
        chip = lax.div(index, 2)
        self.at = {"z": lax.div(chip, self.nx), "x": lax.rem(chip, self.nx), "y": lax.axis_index("mp")}
        self.count = {"z": self.nz, "x": self.nx, "y": self.ny}

    def device(self, core=None, **moved):
        at = {**self.at, **moved}
        core = self.core if core is None else core
        return ((at["z"] * self.nx + at["x"]) * 2 + core, at["y"])

    def partner(self):
        return self.device(core=1 - self.core)

    def neighbour(self, dim, step):
        return self.device(**{dim: self.at[dim] + step})

    def barrier(self, dims):
        semaphore = pltpu.get_barrier_semaphore()
        pl.semaphore_signal(semaphore, inc=1, device_id=self.partner(), device_id_type=MESH)
        peers = 1
        for dim in dims:
            for step in (1, -1):
                there = self.at[dim] + step
                valid = (there >= 0) & (there < self.count[dim])
                peers = peers + valid.astype(jnp.int32)

                @pl.when(valid)
                def _(dim=dim, step=step):
                    other = self.neighbour(dim, step)
                    pl.semaphore_signal(semaphore, inc=1, device_id=other, device_id_type=MESH)

        pl.semaphore_wait(semaphore, peers)


def link_slots(count, dims):
    return sum(2 * (count[dim] - 1) for dim in dims)


class Gather:
    def __init__(self, place, buffer, axes, order, sems):
        self.place, self.buffer, self.axes, self.order = place, buffer, axes, order
        self.send, self.recv, self.pass_send, self.pass_recv = sems
        self.rounds = [(dim, t) for dim in order for t in range(place.count[dim] - 1)]
        self.slots = {}
        for dim, t in self.rounds:
            for way in (1, -1):
                self.slots[dim, t, way] = len(self.slots)

    def block(self, dim, position, core):
        done = self.order[: self.order.index(dim)] if dim else ""
        index = []
        for axis in self.axes:
            if axis == dim:
                index.append(position)
            elif axis in done:
                index.append(pl.ds(0, self.place.count[axis]))
            else:
                index.append(self.place.at[axis])
        return self.buffer.at[tuple(index) + (core,)]

    def link(self, dim, t, way, position, device):
        block = self.block(dim, position, self.place.core)
        slot = self.slots[dim, t, way]
        return pltpu.make_async_remote_copy(
            block, block, self.send.at[slot], self.recv.at[slot], device_id=device, device_id_type=MESH
        )

    def hand(self, slot, dim, position, core):
        block = self.block(dim, position, core)
        return pltpu.make_async_remote_copy(
            block,
            block,
            self.pass_send.at[slot],
            self.pass_recv.at[slot],
            device_id=self.place.partner(),
            device_id_type=MESH,
        )

    def sends(self, dim, t):
        here, count = self.place.at[dim], self.place.count[dim]
        yield 1, here - t, (here - t >= 0) & (here < count - 1)
        yield -1, here + t, (here + t < count) & (here > 0)

    def arrivals(self, dim, t):
        here, count = self.place.at[dim], self.place.count[dim]
        yield 1, here - 1 - t, here - 1 - t >= 0
        yield -1, here + 1 + t, here + 1 + t < count

    def start(self):
        self.hand(len(self.slots), "", None, self.place.core).start()
        self.send_round(0)

    def send_round(self, number):
        dim, t = self.rounds[number]
        for way, position, valid in self.sends(dim, t):

            @pl.when(valid)
            def _(way=way, position=position):
                self.link(dim, t, way, position, self.place.neighbour(dim, way)).start()

    def advance(self, number):
        dim, t = self.rounds[number - 1]
        for way, position, valid in self.arrivals(dim, t):

            @pl.when(valid)
            def _(way=way, position=position):
                self.link(dim, t, way, position, self.place.partner()).wait_recv()
                self.hand(self.slots[dim, t, way], dim, position, self.place.core).start()

        if number < len(self.rounds):
            self.send_round(number)

    def steps(self):
        return [self.start] + [functools.partial(self.advance, n + 1) for n in range(len(self.rounds))]

    def finish(self):
        other = 1 - self.place.core
        self.hand(len(self.slots), "", None, other).wait_recv()
        for dim, t in self.rounds:
            for way, position, valid in self.arrivals(dim, t):

                @pl.when(valid)
                def _(dim=dim, t=t, way=way, position=position):
                    self.hand(self.slots[dim, t, way], dim, position, other).wait_recv()

    def drain(self):
        self.hand(len(self.slots), "", None, self.place.core).wait_send()
        for dim, t in self.rounds:
            for way, position, valid in self.sends(dim, t):

                @pl.when(valid)
                def _(dim=dim, t=t, way=way, position=position):
                    self.link(dim, t, way, position, self.place.partner()).wait_send()

            for way, position, valid in self.arrivals(dim, t):

                @pl.when(valid)
                def _(dim=dim, t=t, way=way, position=position):
                    self.hand(self.slots[dim, t, way], dim, position, self.place.core).wait_send()


class Scatter:
    def __init__(self, place, mine, axes, order, inbox, hand_box, sems, both=False):
        self.place, self.mine, self.axes, self.order, self.both = place, mine, axes, order, both
        self.inbox, self.hand_box = inbox, hand_box
        self.send, self.recv = sems
        self.rounds = [(dim, t) for dim in order for t in range(place.count[dim] - 1)]
        self.slots = {}
        for dim, t in self.rounds:
            for way in (1, -1):
                self.slots[dim, t, way] = len(self.slots) + 1

    def own(self, index):
        return index + ((() if self.both else (self.place.core,)))

    def hand(self):
        whole = tuple(pl.ds(0, self.place.count[axis]) for axis in self.axes)
        source = self.mine.at[whole] if self.both else self.mine.at[whole + (1 - self.place.core,)]
        return pltpu.make_async_remote_copy(
            source, self.hand_box, self.send.at[0], self.recv.at[0], device_id=self.place.partner(), device_id_type=MESH
        )

    def start(self):
        self.hand().start()

    def take_hand(self):
        self.hand().wait_recv()
        first = self.place.count[self.axes[0]]
        rest = tuple(pl.ds(0, self.place.count[axis]) for axis in self.axes[1:])
        if self.both:
            self.hand().wait_send()
            self.mine[...] = self.mine[...] + self.hand_box[...]
        else:
            for p in range(first):
                for r in range(self.place.count[self.axes[1]]):
                    index = (p, r) + rest[1:]
                    here = self.mine[index + (self.place.core,)].astype(F32)
                    there = self.hand_box[index].astype(F32)
                    self.mine[index + (self.place.core,)] = (here + there).astype(self.mine.dtype)
        self.send_round(0)

    def block(self, dim, position):
        done = self.order[: self.order.index(dim)]
        index = []
        for axis in self.axes:
            if axis == dim:
                index.append(position)
            elif axis in done:
                index.append(self.place.at[axis])
            else:
                index.append(pl.ds(0, self.place.count[axis]))
        return self.own(tuple(index))

    def link(self, dim, t, way, position, device):
        slot = self.slots[dim, t, way]
        return pltpu.make_async_remote_copy(
            self.mine.at[self.block(dim, position)],
            self.inbox[slot],
            self.send.at[slot],
            self.recv.at[slot],
            device_id=device,
            device_id_type=MESH,
        )

    def sends(self, dim, t):
        here, count = self.place.at[dim], self.place.count[dim]
        yield 1, count - 1 - t + here, (t >= here) & (here < count - 1)
        back = count - 1 - here
        yield -1, t - back, (t >= back) & (here > 0)

    def arrivals(self, dim, t):
        here, count = self.place.at[dim], self.place.count[dim]
        yield 1, count - 2 - t + here, (t >= here - 1) & (here > 0)
        back = count - 1 - here
        yield -1, t + 1 - back, (t >= back - 1) & (here < count - 1)

    def send_round(self, number):
        dim, t = self.rounds[number]
        for way, position, valid in self.sends(dim, t):

            @pl.when(valid)
            def _(way=way, position=position):
                self.link(dim, t, way, position, self.place.neighbour(dim, way)).start()

    def advance(self, number):
        dim, t = self.rounds[number - 1]
        for way, position, valid in self.arrivals(dim, t):

            @pl.when(valid)
            def _(way=way, position=position):
                self.link(dim, t, way, position, self.place.partner()).wait_recv()
                index = self.block(dim, position)
                total = self.mine[index].astype(F32) + self.inbox[self.slots[dim, t, way]][...].astype(F32)
                self.mine[index] = total.astype(self.mine.dtype)

        if number < len(self.rounds):
            self.send_round(number)

    def steps(self):
        later = [functools.partial(self.advance, n + 1) for n in range(len(self.rounds))]
        return [self.start, self.take_hand] + later

    def result(self):
        return self.mine[self.own(tuple(self.place.at[axis] for axis in self.axes))]

    def drain(self):
        if not self.both:
            self.hand().wait_send()
        for dim, t in self.rounds:
            for way, position, valid in self.sends(dim, t):

                @pl.when(valid)
                def _(dim=dim, t=t, way=way, position=position):
                    self.link(dim, t, way, position, self.place.partner()).wait_send()


def inbox_shapes(count, axes, order, block):
    shapes, slots, left = [], {}, dict(count)
    for dim in order:
        left.pop(dim)
        for t in range(count[dim] - 1):
            for way in (1, -1):
                if way == 1 or count[dim] > 2:
                    shapes.append(tuple(count[axis] for axis in axes if axis in left) + block)
                slots[dim, t, way] = len(shapes) - 1
    return shapes, slots


def open_inbox(run, count, axes, order, block, boxes):
    shapes, slots = inbox_shapes(count, axes, order, block)
    for key, slot in run.slots.items():
        run.inbox[slot] = boxes[slots[key]]
    del boxes[: len(shapes)]


def play(plan, comm, pieces):
    plan = list(plan)
    while plan:
        token = plan.pop(0)
        if token >= 0:
            if comm:
                comm[token].pop(0)()
        elif callable(pieces[0]):
            pieces.pop(0)()
        else:
            count, piece = pieces.pop(0)
            between = [[] for _ in range(count - 1)]
            for spot in range(count - 1):
                while plan[0] >= 0:
                    token = plan.pop(0)
                    if comm:
                        between[spot].append(comm[token].pop(0))
                plan.pop(0)

            def once(index, carry, piece=piece, between=between):
                piece(index)
                for spot, steps in enumerate(between):
                    if steps:

                        @pl.when(index == spot)
                        def _(steps=steps):
                            for step in steps:
                                step()

                return carry

            lax.fori_loop(0, count, once, 0)
    assert not pieces and not any(comm.values())


class Mover:
    def __init__(self, sems):
        self.sems, self.used, self.open = sems, 0, []

    def start(self, source, target):
        copy = pltpu.make_async_copy(source, target, self.sems.at[self.used])
        self.used += 1
        copy.start()
        return copy

    def save(self, source, target):
        self.open.append(self.start(source, target))

    def close(self):
        for copy in self.open:
            copy.wait()


def read_vectors(vectors, tiles):
    nz, nx = tiles.shape[:2]
    pieces = [tiles[z, x, 0] + tiles[z, x, 1] for z in range(nz) for x in range(nx)]
    vectors[...] = jnp.concatenate(pieces, axis=1)


def column_parts(weights):
    wq, wk, wv, wo, wu, wd = weights
    left, right = pl.ds(0, SEG), pl.ds(SEG, SEG)
    return [wq, wk, wv, wo, wu.at[:, left], wu.at[:, right], wd.at[:, left], wd.at[:, right]]


def fill_tile(place, tiles, norms):
    tile = (place.at["z"], place.at["x"], place.core)
    tiles[tile] = jnp.zeros(tiles.shape[3:], F32)
    share = norms[0].shape[1]
    for line, norm in enumerate(norms):
        value = norm[...].astype(F32)
        for core in range(2):

            @pl.when(place.core == core)
            def _(line=line, value=value, core=core):
                tiles[tile + (slice(line, line + 1), slice(core * share, (core + 1) * share))] = value


FWD_OUT = (
    "x", "q", "k", "v", "probs", "mix", "res", "nrm2", "active", "slope", "out", "cot", "gl", "glt", "weight",
    "nrmt",
)
KEPT = len(FWD_OUT)


def forward_kernel(shape, micro, tokens, cotangent, ids, counts, *refs):
    if shape:
        weights, norms, g_out, refs = refs[:6], refs[6:10], refs[10], refs[11:]
    else:
        g_in, vectors_in, refs = refs[0], refs[1], refs[2:]
    if shape:
        vectors, refs = refs[0], refs[1:]
    else:
        vectors = vectors_in
    saved = dict(zip(FWD_OUT, refs[:KEPT]))
    here = dict(zip(FWD_OUT, refs[KEPT : 2 * KEPT]))
    refs = refs[2 * KEPT :]
    raw, nrm, low, total, g, sems = refs[:6]
    mover = Mover(sems)
    y = lax.axis_index("mp")
    take = mover.start(tokens.at[pl.ds(y * micro, micro)], raw)
    x, q, k, v, probs, mix, res, nrm2, active, slope, out, cot, gl, glt, weight, nrmt = (
        here[name] for name in FWD_OUT
    )

    def keep(*names):
        for name in names:
            mover.save(here[name], saved[name])

    comm = {}
    if shape:
        tiles, send, recv, pass_send, pass_recv = refs[6:]
        place = Place(shape)
        spot = (place.at["y"], place.at["z"], place.at["x"], place.core)
        mine = [mover.start(part, g.at[(seg,) + spot]) for seg, part in enumerate(column_parts(weights))]
        fill_tile(place, tiles, norms)
        place.barrier("zxy")
        pick = lambda seg: tuple(sem.at[seg] for sem in (send, recv, pass_send, pass_recv))
        runs = [Gather(place, g.at[seg], "yzx", ORDERS[seg], pick(seg)) for seg in range(8)]
        runs.append(Gather(place, tiles, "zx", "zx", pick(8)))
        comm = {seg: run.steps() for seg, run in enumerate(runs)}
        for seg in range(8):
            comm[seg][0] = lambda seg=seg: (mine[seg].wait(), runs[seg].start())

        def have(seg):
            runs[seg].finish()
            if seg < 8:
                mover.save(g.at[seg], g_out.at[seg])
            else:
                read_vectors(vectors, tiles)

    else:
        loads = [mover.start(g_in.at[seg], g.at[seg]) for seg in range(8)]

        def have(seg):
            if seg < 8:
                loads[seg].wait()

    def spread():
        take.wait()
        to_rows(raw, x)
        keep("x")
        loads_cot.append(mover.start(cotangent.at[pl.ds(y * micro, micro)], raw))
        row_weights(ids, counts, y, micro, weight)

    loads_cot = []

    def weigh():
        loads_cot[0].wait()
        to_rows(raw, cot)

        def block(rows, _):
            gl[rows, :] = (cot[rows, :].astype(F32) * weight[rows, :]).astype(BF)

        row_loop(cot.shape[0], block)
        turn(gl, glt)
        keep("cot", "gl", "glt", "weight")

    def norm_one():
        have(8)
        norm_in(x, nrm, vectors[0:1, :], vectors[1:2, :])
        turn(nrm, nrmt)
        keep("nrmt")

    def head_part(seg, target, name):
        have(seg)
        project(nrm, g, seg, target)
        keep(name)

    third = x.shape[0] // TILE // 3

    def mixing(part):
        attend(q, k, v, probs, mix, part * third, third)

    def project_out():
        keep("probs", "mix")
        have(O)
        res[...] = x[...].astype(F32)
        back_through(lambda m: mix[:, half(m)], g, O, res)
        keep("res")

    def norm_two():
        gain, shift = vectors[2:3, :], vectors[3:4, :]

        def block(rows, _):
            normal, _inv = norm_stats(res[rows, :])
            nrm2[rows, :] = (normal * gain + shift).astype(BF)

        row_loop(x.shape[0], block)
        keep("nrm2")

    def up(which, m):
        if m == 0:
            have(UPS[which])
        feed_up(nrm2, g, which, m, active, slope)
        mover.save(active.at[which, m], saved["active"].at[which, m])
        mover.save(slope.at[which, m], saved["slope"].at[which, m])

    def down(which):
        have(DOWNS[which])
        if which == 0:
            total[...] = res[...]
        back_through(lambda m: active[which, m], g, DOWNS[which], total)

    def last():
        low[...] = total[...].astype(BF)
        from_rows(low, out)
        keep("out")

    pieces = [spread, weigh, norm_one]
    pieces += [functools.partial(head_part, *args) for args in ((Q, q, "q"), (K, k, "k"), (V, v, "v"))]
    pieces += [(3, mixing), project_out, norm_two]
    pieces += [functools.partial(up, which, m) for which in range(2) for m in range(2)]
    pieces += [functools.partial(down, which) for which in range(2)] + [last]
    play(FORWARD_PLAN, comm, pieces)
    if shape:
        for run in runs:
            run.drain()
    mover.close()


def row_weights(ids, counts, y, micro, target):
    series = ids.shape[1]
    sums = counts[0]
    for kind in range(1, counts.shape[0]):
        sums = sums + counts[kind]
    mean = jnp.full((PAD, 1), sums.astype(F32), F32) / counts.shape[0]

    def one(index, carry):
        kind = ids[y * micro + lax.div(index, series), lax.rem(index, series)]
        count = counts[kind].astype(F32)
        target[pl.ds(pl.multiple_of(index * PAD, PAD), PAD), :] = 2.0 * mean / (mean + count)
        return carry

    lax.fori_loop(0, micro * series, one, 0)


class Swap:
    def __init__(self, place, mover, sems, ready, source, target):
        self.mover, self.source, self.ready = mover, source, ready
        y, (micro, patches) = place.at["y"], source.shape[:2]
        cut = patches // 2 + 1
        self.spot = target.at[pl.ds(y * micro, micro)]
        self.copies = []
        for part in range(micro):
            for piece in (pl.ds(0, cut), pl.ds(cut, patches - cut)):
                slot = 2 * len(self.copies)
                self.copies.append(
                    pltpu.make_async_remote_copy(
                        source.at[part, piece],
                        target.at[y * micro + part, piece],
                        sems.at[slot],
                        sems.at[slot + 1],
                        device_id=place.device(y=1 - y),
                        device_id_type=MESH,
                    )
                )

    def start(self):
        self.ready()
        self.copies[0].start()
        self.mover.save(self.source, self.spot)

    def steps(self):
        return [self.start] + [copy.start for copy in self.copies[1:]]

    def wait(self):
        for copy in self.copies:
            copy.wait()


def feed_back_kernel(shape, vectors, g_in, active_in, slope_in, nrm2_in, res_in, out_in, cot_in, gl_in, glt_in, weight_in, mix_in, *refs):
    if shape:
        dw_out, gres_out, gm_out, vec, pair, grad_down, refs = refs[:6] + (refs[6:],)
    else:
        dw_out, gres_out, gm_out, vec, refs = refs[:4] + (refs[4:],)
    cot, weight, active, slope, nrm2, res, g, dw, gl, glt, gh, n2t, gn2, gres, mix, gm, sems = refs[:17]
    mover = Mover(sems)
    loads = {"glt": mover.start(glt_in, glt), ("active", 0): mover.start(active_in.at[0], active.at[0])}
    loads["gl"] = mover.start(gl_in, gl)
    for which in range(2):
        if which == 1:
            loads["active", which] = mover.start(active_in.at[which], active.at[which])
        loads["d", which] = mover.start(g_in.at[DOWNS[which]], g.at[2 + which])
        loads["slope", which] = mover.start(slope_in.at[which], slope.at[which])
    loads["nrm2"] = mover.start(nrm2_in, nrm2)
    for which in range(2):
        loads["u", which] = mover.start(g_in.at[UPS[which]], g.at[which])
    loads["res"] = mover.start(res_in, res)
    loads["cot"] = mover.start(cot_in, cot)
    loads["mix"] = mover.start(mix_in, mix)
    loads["o"] = mover.start(g_in.at[O], g.at[4])
    loads["weight"] = mover.start(weight_in, weight)
    comm = {}
    if shape:
        half_out, hands, send, recv, ysem = refs[17:22]
        boxes = list(refs[22:])
        side = mover.start(out_in, half_out)
        place = Place(shape)
        place.barrier("zxy")
        runs = []
        for which in range(2):
            order = BACK_ORDERS[DOWNS[which]]
            run = Scatter(
                place, dw.at[2 + which], "yzx", order, {}, hands.at[which], (send.at[which], recv.at[which])
            )
            open_inbox(run, place.count, "yzx", order, dw.shape[-2:], boxes)
            runs.append(run)
        swap = Swap(place, mover, ysem, side.wait, half_out, pair)
        comm = {0: runs[0].steps(), 1: runs[1].steps(), 2: swap.steps()}

    def down_grad(which):
        if which == 0:
            loads["glt"].wait()
        loads["active", which].wait()
        weight_grad(glt, lambda m: active[which, m], dw, 2 + which)
        if not shape:
            mover.save(dw.at[2 + which], dw_out.at[2 + which])

    def hidden_grad(which):
        if which == 0:
            loads["gl"].wait()
        loads["d", which].wait()
        loads["slope", which].wait()

        def one(m):
            pulled = nn(gl[...], flat(g[2 + which, m]))
            gh[which, m] = (pulled * slope[which, m]).astype(BF)

        half_loop(g.shape[1], one)

    def turn_two():
        loads["nrm2"].wait()
        turn(nrm2, n2t)
        gn2[...] = jnp.zeros_like(gn2)

    def up_grad(which):
        weight_grad(n2t, lambda m: gh[which, m], dw, which)
        mover.save(dw.at[which], dw_out.at[which])

    def norm_grad(which):
        loads["u", which].wait()
        back_through(lambda m: gh[which, m], g, which, gn2)

    def last():
        for name in ("res", "cot", "weight"):
            loads[name].wait()
        gain = vectors[2:3, :]
        vec[...] = jnp.zeros_like(vec)

        def block(rows, _):
            grad = gn2[rows, :]
            pulled, normal = norm_pull(grad, res[rows, :], gain)
            vec[0] += fold_rows(grad * normal)
            vec[1] += fold_rows(grad)
            total = cot[rows, :].astype(F32) * weight[rows, :] + pulled
            gres[rows, :] = total
            gl[rows, :] = total.astype(BF)

        row_loop(cot.shape[0], block)
        mover.save(gres, gres_out)

    def mix_grad():
        loads["o"].wait()
        project(gl, g, 4, gm)
        mover.save(gm, gm_out)

    def out_grad():
        loads["mix"].wait()
        weight_grad(glt, lambda m: mix[:, half(m)], dw, 4)
        mover.save(dw.at[4], dw_out.at[4])

    pieces = []
    for which in range(2):
        pieces += [functools.partial(down_grad, which), functools.partial(hidden_grad, which)]
    pieces.append(turn_two)
    for which in range(2):
        pieces += [functools.partial(up_grad, which), functools.partial(norm_grad, which)]
    pieces += [last, mix_grad, lambda: turn(gl, glt), out_grad]
    play(FEED_PLAN, comm, pieces)
    if shape:
        for which in range(2):
            grad_down[:, which * SEG : (which + 1) * SEG] = runs[which].result().astype(F32)
            runs[which].drain()
        swap.wait()
    mover.close()


def vector_tiles(tiles, vec_a, vec_f):
    tiles[...] = jnp.zeros_like(tiles)
    nz, nx = tiles.shape[:2]
    for line, (source, part) in enumerate(((vec_a, 0), (vec_a, 1), (vec_f, 0), (vec_f, 1))):
        row = jnp.sum(source[part], axis=0, keepdims=True)
        for z in range(nz):
            for x in range(nx):
                chip = z * nx + x
                tiles[z, x, line : line + 1, :] = row[:, chip * 128 : (chip + 1) * 128]


BACK_IN = ("gm", "q", "k", "v", "probs", "nrmt", "gres", "x")
SHARED = (U0, U1, O, Q, K, V)
KEPT_GRADS = (0, 1, 4)


def attn_back_kernel(shape, vectors, vec_f, g_in, dw_in, *refs):
    given = dict(zip(BACK_IN, refs[:8]))
    refs = refs[8:]
    if shape:
        pair, grads, vec_out, refs = refs[0], refs[1:6], refs[6], refs[7:]
    else:
        dw_out, out, vec, refs = refs[0], refs[1], refs[2], refs[3:]
    here = dict(zip(BACK_IN, refs[:8]))
    g, dw, gal, gq, gk, gv, raw, sems = refs[8:16]
    mover = Mover(sems)
    loads, comm = {}, {}
    if shape:
        held, tiles, hands, vec_hand, ybox, vec, send, recv, ysem = refs[16:25]
        boxes = list(refs[25:])
        for spot, part in enumerate(KEPT_GRADS):
            loads["dw", spot] = mover.start(dw_in.at[part], held.at[spot])
    for name in BACK_IN:
        loads[name] = mover.start(given[name], here[name])
    for seg in (Q, K, V):
        loads[seg] = mover.start(g_in.at[seg], g.at[seg])
    gm, q, k, v, probs, nrmt, gres, x = (here[name] for name in BACK_IN)
    gn = probs
    if shape:
        place = Place(shape)
        place.barrier("zxy")
        runs = []
        for spot, seg in enumerate(SHARED):
            source = held.at[spot] if spot < 3 else dw.at[seg]
            order = BACK_ORDERS[seg]
            run = Scatter(place, source, "yzx", order, {}, hands.at[spot], (send.at[spot], recv.at[spot]))
            open_inbox(run, place.count, "yzx", order, dw.shape[-2:], boxes)
            runs.append(run)
        run = Scatter(place, tiles, "zx", "zx", {}, vec_hand, (send.at[6], recv.at[6]), both=True)
        open_inbox(run, {"z": place.nz, "x": place.nx}, "zx", "zx", (8, 128), boxes)
        runs.append(run)
        swap = Swap(place, mover, ysem, lambda: None, raw, pair)
        comm = {spot: run.steps() for spot, run in enumerate(runs)}
        comm[7] = swap.steps()
        for spot in range(3):
            comm[spot][0] = lambda spot=spot: (loads["dw", spot].wait(), runs[spot].start())

    third = gal.shape[0] // TILE // 3

    def ready():
        for name in BACK_IN[:6]:
            loads[name].wait()

    def mixing(part):
        attend_back(q, k, v, probs, gm, gq, gk, gv, part * third, third)

    def head_grad(seg, grad):
        weight_grad(nrmt, lambda m: grad[:, half(m)], dw, seg)
        if not shape:
            mover.save(dw.at[seg], dw_out.at[seg])

    def norm_grad(seg, grad):
        if seg == Q:
            gn[...] = jnp.zeros_like(gn)
        loads[seg].wait()
        back_through(lambda m: grad[:, half(m)], g, seg, gn)

    def last():
        loads["gres"].wait()
        loads["x"].wait()
        gain = vectors[0:1, :]
        vec[...] = jnp.zeros_like(vec)

        def block(rows, _):
            grad = gn[rows, :]
            pulled, normal = norm_pull(grad, x[rows, :].astype(F32), gain)
            vec[0] += fold_rows(grad * normal)
            vec[1] += fold_rows(grad)
            gal[rows, :] = (gres[rows, :] + pulled).astype(BF)

        row_loop(gal.shape[0], block)
        from_rows(gal, raw)
        if shape:
            vector_tiles(tiles, vec, vec_f)
        else:
            mover.save(raw, out)

    heads = ((Q, gq), (K, gk), (V, gv))
    pieces = [ready, (3, mixing)]
    pieces += [functools.partial(head_grad, *pair_of) for pair_of in heads[:GRADS_FIRST]]
    pieces += [functools.partial(norm_grad, *pair_of) for pair_of in heads] + [last]
    pieces += [functools.partial(head_grad, *pair_of) for pair_of in heads[GRADS_FIRST:]]
    play(ATTN_PLAN, comm, pieces)
    if shape:
        here_tile = tiles.at[place.at["z"], place.at["x"]]
        copy = pltpu.make_async_remote_copy(
            here_tile, ybox, ysem.at[8], ysem.at[9], device_id=place.device(y=1 - place.at["y"]), device_id_type=MESH
        )
        copy.start()
        for spot, seg in enumerate(SHARED[2:]):
            grads[(3, 0, 1, 2)[spot]][...] = runs[2 + spot].result().astype(F32)
        for which in range(2):
            grads[4][:, which * SEG : (which + 1) * SEG] = runs[which].result().astype(F32)
        for run in runs:
            run.drain()
        copy.wait()
        vec_out[...] = tiles[place.at["z"], place.at["x"]] + ybox[...]
        swap.wait()
    mover.close()


def shape_of(shape, dtype):
    return jax.ShapeDtypeStruct(shape, dtype)


IN_VMEM = pl.BlockSpec(memory_space=pltpu.VMEM)
IN_SMEM = pl.BlockSpec(memory_space=pltpu.SMEM)
ANYWHERE = pl.BlockSpec(memory_space=pl.ANY)
DMA = pltpu.SemaphoreType.DMA


def call(body, outs, ins, out_specs, scratch, name, collective=None):
    params = {"vmem_limit_bytes": VMEM_LIMIT}
    if collective is not None:
        params.update(collective_id=collective, has_side_effects=True)
    return pl.pallas_call(
        body,
        out_shape=outs,
        in_specs=ins,
        out_specs=out_specs,
        scratch_shapes=scratch,
        compiler_params=pltpu.CompilerParams(**params),
        name=name,
    )


def vmem(like):
    return pltpu.VMEM(like.shape, like.dtype)


def forward(shape, micro, tokens, cotangent, ids, counts, weights, norms, g_in=None, vectors_in=None):
    _, patches, series, width = tokens.shape
    rows = micro * series * PAD
    full = g_in.shape if shape is None else (8, shape[2], shape[0], shape[1], 2, weights[0].shape[0], SEG)
    low, high = shape_of((rows, width), BF), shape_of((rows, width), F32)
    wide = (2, full[1], rows, SEG)
    raw = shape_of((micro, patches, series, width), BF)
    kinds = {name: low for name in FWD_OUT}
    kinds.update(
        probs=high,
        res=high,
        active=shape_of(wide, BF),
        slope=shape_of(wide, F32),
        out=raw,
        glt=shape_of((width, rows), BF),
        nrmt=shape_of((width, rows), BF),
        weight=shape_of((rows, 1), F32),
    )
    saved = tuple(kinds[name] for name in FWD_OUT)
    scratch = [vmem(kind) for kind in saved] + [vmem(raw), vmem(low), vmem(low), vmem(high), pltpu.VMEM(full, BF), DMA((64,))]
    if shape is None:
        results = call(
            functools.partial(forward_kernel, None, micro),
            saved,
            [ANYWHERE, ANYWHERE, IN_SMEM, IN_SMEM, ANYWHERE, IN_VMEM],
            (ANYWHERE,) * KEPT,
            scratch,
            "forward",
        )(tokens, cotangent, ids, counts, g_in, vectors_in)
        return g_in, vectors_in, dict(zip(FWD_OUT, results))
    count = dict(zip("zxy", shape))
    slots = link_slots(count, "zxy")
    scratch += [pltpu.VMEM(shape[:2] + (2, 8, 128), F32)]
    scratch += [DMA((9, slots)), DMA((9, slots)), DMA((9, slots + 1)), DMA((9, slots + 1))]
    results = call(
        functools.partial(forward_kernel, shape, micro),
        (shape_of(full, BF), shape_of((8, width), F32)) + saved,
        [ANYWHERE, ANYWHERE, IN_SMEM, IN_SMEM] + [ANYWHERE] * 6 + [IN_VMEM] * 4,
        (ANYWHERE, IN_VMEM) + (ANYWHERE,) * KEPT,
        scratch,
        "forward",
        0,
    )(tokens, cotangent, ids, counts, *weights, *norms)
    return results[0], results[1], dict(zip(FWD_OUT, results[2:]))


def scatter_scratch(segs, part, count, orders):
    rows, cols = part.shape[-2:]
    slots = link_slots(count, "zxy") + 1
    boxes = []
    for order in orders:
        boxes += [pltpu.VMEM(s, BF) for s in inbox_shapes(count, "yzx", order, (rows, cols))[0]]
    hands = pltpu.VMEM((len(orders),) + part.shape[1:4] + (rows, cols), BF)
    return hands, [DMA((segs, slots)), DMA((segs, slots))], boxes


def pair_of(raw, ny):
    return shape_of((ny * raw.shape[0],) + raw.shape[1:], BF)


def feed_back(shape, vectors, g, kept):
    low, high, raw = kept["x"], kept["res"], kept["out"]
    rows, width = low.shape
    part = shape_of((5,) + g.shape[1:], BF)
    turned = pltpu.VMEM((width, rows), BF)
    scratch = [
        vmem(low),
        pltpu.VMEM((rows, 1), F32),
        vmem(kept["active"]),
        vmem(kept["slope"]),
        vmem(low),
        vmem(high),
        vmem(part),
        vmem(part),
        vmem(low),
        turned,
        vmem(kept["active"]),
        turned,
        vmem(high),
        vmem(high),
        vmem(low),
        vmem(low),
        DMA((32,)),
    ]
    given = [g] + [kept[name] for name in ("active", "slope", "nrm2", "res", "out", "cot", "gl", "glt", "weight", "mix")]
    outs = [part, shape_of(high.shape, F32), shape_of(low.shape, BF), shape_of((2, 8, width), F32)]
    specs = [ANYWHERE, ANYWHERE, ANYWHERE, IN_VMEM]
    if shape:
        count = dict(zip("zxy", shape))
        hands, sems, boxes = scatter_scratch(2, part, count, [BACK_ORDERS[seg] for seg in DOWNS])
        scratch += [vmem(raw), hands] + sems + [DMA((8,))] + boxes
        outs += [pair_of(raw, shape[2]), shape_of((part.shape[-2], 2 * SEG), F32)]
        specs += [ANYWHERE, IN_VMEM]
    return call(
        functools.partial(feed_back_kernel, shape),
        tuple(outs),
        [IN_VMEM] + [ANYWHERE] * 11,
        tuple(specs),
        scratch,
        "feed_back",
        1 if shape else None,
    )(vectors, *given)


def attn_back(shape, vectors, vec_f, g, dw_in, kept):
    low, raw = kept["x"], kept["out"]
    width = low.shape[1]
    part = shape_of((3,) + g.shape[1:], BF)
    scratch = [vmem(kept[name]) for name in BACK_IN]
    scratch += [vmem(part), vmem(part), vmem(low), vmem(low), vmem(low), vmem(low), vmem(raw), DMA((32,))]
    vec = shape_of((2, 8, width), F32)
    if shape:
        nz, nx, ny = shape
        count = dict(zip("zxy", shape))
        share = part.shape[-2]
        small, large = shape_of((share, SEG), F32), shape_of((share, 2 * SEG), F32)
        outs = [pair_of(raw, ny)] + [small] * 4 + [large, shape_of((8, 128), F32)]
        specs = [ANYWHERE] + [IN_VMEM] * 6
        hands, sems, boxes = scatter_scratch(7, part, count, [BACK_ORDERS[seg] for seg in SHARED])
        tiles = pltpu.VMEM((nz, nx, 8, 128), F32)
        scratch += [vmem(part), tiles, hands, tiles, pltpu.VMEM((8, 128), F32), vmem(vec)]
        scratch += sems + [DMA((10,))] + boxes
        scratch += [pltpu.VMEM(s, F32) for s in inbox_shapes({"z": nz, "x": nx}, "zx", "zx", (8, 128))[0]]
    else:
        outs, specs = [part, raw, vec], [ANYWHERE, ANYWHERE, IN_VMEM]
        outs[1] = shape_of(raw.shape, BF)
    return call(
        functools.partial(attn_back_kernel, shape),
        tuple(outs),
        [IN_VMEM] * 2 + [ANYWHERE] * 10,
        tuple(specs),
        scratch,
        "attn_back",
        2 if shape else None,
    )(vectors, vec_f, g, dw_in, *(kept[name] for name in BACK_IN))


def chip_grid(chips):
    nx = 1
    while (nx * 2) ** 2 <= chips:
        nx *= 2
    return chips // nx, nx


def body(counts_of, tokens, cotangent, domain_ids, domain_counts, *params):
    weights, norms = params[:6], params[6:]
    n_dp, n_mp = counts_of
    micro = tokens.shape[0] // n_mp
    width = tokens.shape[3]
    share = width // n_dp
    y = lax.axis_index("mp")
    linked = n_mp == 2 and share * 2 == TILE
    flip = lambda array: jnp.transpose(array, (0, 2, 1, 3))
    x, cot = flip(tokens), flip(cotangent)
    if linked:
        shape = chip_grid(n_dp // 2) + (n_mp,)
        g, vectors, kept = forward(shape, micro, x, cot, domain_ids, domain_counts, weights, [norm.reshape(1, -1) for norm in norms])
    else:
        shards = jnp.stack(
            weights[:4] + tuple(w[:, i * SEG : (i + 1) * SEG] for w in weights[4:] for i in range(2))
        )
        g = lax.all_gather(lax.all_gather(shards, "dp", axis=1, tiled=True), "mp", axis=1)
        vectors = lax.all_gather(jnp.stack(norms), "dp", axis=1, tiled=True).astype(F32)
        vectors = jnp.pad(vectors, ((0, 4), (0, 0)))
        g, vectors, kept = forward(None, micro, x, cot, domain_ids, domain_counts, None, None, g, vectors)
    shape = shape if linked else None
    results = feed_back(shape, vectors, g, kept)
    dw_f, gres, gm, vec_f = results[:4]
    kept = {**kept, "gres": gres, "gm": gm}
    if linked:
        out, grad_down = results[4:]
        grad_tokens, *grads, vec = attn_back(shape, vectors, vec_f, g, dw_f, kept)
        grads.append(grad_down)
        core = lax.rem(lax.axis_index("dp"), 2)
        vec = lax.dynamic_slice(vec, (0, core * share), (4, share))
    else:
        dw_a, low_tokens, vec_a = attn_back(shape, vectors, vec_f, g, dw_f, kept)
        dw = jnp.concatenate((dw_a, dw_f[4:], dw_f[:4])).astype(F32)
        dw = lax.psum_scatter(lax.psum_scatter(dw, "mp", scatter_dimension=1), "dp", scatter_dimension=1, tiled=True)
        grads = [dw[0], dw[1], dw[2], dw[3]]
        grads += [jnp.concatenate((dw[a], dw[b]), axis=1) for a, b in (UPS, DOWNS)]
        vec = jnp.concatenate((jnp.sum(vec_a, axis=1), jnp.sum(vec_f, axis=1)))
        vec = lax.psum_scatter(lax.psum(vec, "mp"), "dp", scatter_dimension=1, tiled=True)
        out = lax.all_gather(kept["out"], "mp", axis=0, tiled=True)
        grad_tokens = lax.all_gather(low_tokens, "mp", axis=0, tiled=True)
    return (flip(out), flip(grad_tokens.astype(F32)), *grads, vec[0], vec[1], vec[2], vec[3])


def solution(mesh):
    rows, matrix, vector = P(None, "dp", None, None), P("dp", "mp"), P("dp")
    in_specs = (rows, rows, P(None, "dp"), P()) + (matrix,) * 6 + (vector,) * 4
    out_specs = (rows, rows) + (matrix,) * 6 + (vector,) * 4
    run = functools.partial(body, (mesh.shape["dp"], mesh.shape["mp"]))
    return jax.shard_map(run, mesh=mesh, in_specs=in_specs, out_specs=out_specs, check_vma=False)
```

```python
import functools

import jax
import jax.numpy as jnp
from jax import lax
from jax.experimental import pallas as pl
from jax.experimental.pallas import tpu as pltpu
from jax.sharding import PartitionSpec as P

BF = jnp.bfloat16
F32 = jnp.float32
HD = 128
SEG = 512
TILE = 128
PAD = 16
EPS = 1e-05
MESH = pl.DeviceIdType.MESH
VMEM_LIMIT = 62 * 1024 * 1024

Q, K, V, O, U0, U1, D0, D1 = range(8)
UPS = (U0, U1)
DOWNS = (D0, D1)
ORDERS = ("zyx", "xyz", "zxy", "zyx", "zxy", "yxz", "zxy", "zyx")
BACK_ORDERS = ("yxz", "xzy", "xzy", "xzy", "zxy", "yzx", "zxy", "xyz")

FORWARD_PLAN = (
    0, 8, 1, 2, 3, 8, 0, 5, 1, 2, -1, 5, 8, 4, 0, 0, 2, 3, 2, 6, 4, 8, 3, 1,
    4, 3, 0, -1, 2, 8, 1, 4, -1, 1, 0, 3, 6, -1, 7, 2, 1, 4, 6, 5, -1, -1, -1, 6,
    7, -1, 7, 3, 5, 7, -1, -1, 6, 4, -1, 7, 5, -1, 5, -1, -1, 6, -1, 7, -1, -1, -1,
)
FEED_PLAN = (
    2, -1, 0, -1, -1, 1, 0, 2, 2, 1, -1, -1, 0, -1, -1, -1, 0, 1, -1, 2, -1, 0, 1, -1,
    1, -1, 0, 1, -1, 0, 1,
)
ATTN_PLAN = (
    -1, 2, 1, 0, -1, 0, 2, 1, -1, -1, -1, -1, 3, 0, -1, 4, 3, 1, -1, 5, 4, 0, -1, 7,
    1, 2, 7, 5, 1, -1, 2, 2, 8, 3, 4, -1, 4, 6, 8, 4, 6, 1, 5, 3, 6, 5, 2, 6,
    3, 0, 5, 6, 3, 4, 0, 6, 5, 4, 0, 1, 3, 2, 5,
)
GRADS_FIRST = 1


def nn(a, b):
    return lax.dot_general(a, b, (((1,), (0,)), ((), ())), preferred_element_type=F32)


def nt(a, b):
    return lax.dot_general(a, b, (((1,), (1,)), ((), ())), preferred_element_type=F32)


def flat(value):
    return value.reshape(-1, value.shape[-1])


def norm_stats(values):
    mean = jnp.mean(values, axis=-1, keepdims=True)
    center = values - mean
    inverse = lax.rsqrt(jnp.mean(center * center, axis=-1, keepdims=True) + EPS)
    return center * inverse, inverse


def norm_pull(grad, values, gain):
    normal, inverse = norm_stats(values)
    scaled = grad * gain
    first = jnp.mean(scaled, axis=-1, keepdims=True)
    second = jnp.mean(scaled * normal, axis=-1, keepdims=True)
    return inverse * (scaled - first - normal * second), normal


def fold_rows(values):
    rows, width = values.shape
    return jnp.sum(values.reshape(rows // 8, 8, width), axis=0)


def score_mask():
    row = lax.broadcasted_iota(jnp.int32, (TILE, TILE), 0)
    col = lax.broadcasted_iota(jnp.int32, (TILE, TILE), 1)
    return (row // PAD == col // PAD) & (col <= row)


def row_loop(rows, body, first=0):
    def once(index, carry):
        index = first + index
        body(pl.ds(pl.multiple_of(index * TILE, TILE), TILE), index)
        return carry

    lax.fori_loop(0, rows // TILE, once, 0)


def half_loop(count, body):
    def once(index, carry):
        body(index)
        return carry

    lax.fori_loop(0, count, once, 0)


def half(index):
    return pl.ds(pl.multiple_of(index * SEG, SEG), SEG)


def spread_rows(patches, series):
    row = lax.broadcasted_iota(jnp.int32, (series * PAD, patches * series), 0)
    col = lax.broadcasted_iota(jnp.int32, (series * PAD, patches * series), 1)
    hit = (lax.rem(row, PAD) * series + lax.div(row, PAD) == col) & (lax.rem(row, PAD) < patches)
    return jnp.where(hit, 1.0, 0.0).astype(BF)


def gather_rows(patches, series):
    row = lax.broadcasted_iota(jnp.int32, (patches * series, series * PAD), 0)
    col = lax.broadcasted_iota(jnp.int32, (patches * series, series * PAD), 1)
    return jnp.where(lax.rem(row, series) * PAD + lax.div(row, series) == col, 1.0, 0.0).astype(BF)


def to_rows(raw, target):
    micro, patches, series, _ = raw.shape
    matrix = spread_rows(patches, series)
    for part in range(micro):
        target[part * series * PAD : (part + 1) * series * PAD, :] = nn(matrix, flat(raw[part])).astype(BF)


def from_rows(source, raw):
    micro, patches, series, width = raw.shape
    matrix = gather_rows(patches, series)
    for part in range(micro):
        rows = source[part * series * PAD : (part + 1) * series * PAD, :]
        raw[part] = nn(matrix, rows).astype(raw.dtype).reshape(patches, series, width)


def norm_in(x, normed, gain, shift):
    def block(rows, _):
        normal, _inv = norm_stats(x[rows, :].astype(F32))
        normed[rows, :] = (normal * gain + shift).astype(BF)

    row_loop(x.shape[0], block)


def project(source, weights, seg, target):
    def one(m):
        target[:, half(m)] = nn(source[...], flat(weights[seg, m])).astype(BF)

    half_loop(weights.shape[1], one)


def attend(queries, keys, values, probs, mixture, first, count):
    mask = score_mask()
    scale = HD ** (-0.5)

    def group(rows, index):
        for head in range(queries.shape[1] // HD):
            cols = slice(head * HD, (head + 1) * HD)
            scores = nt(queries[rows, cols], keys[rows, cols]) * scale
            scores = jnp.where(mask, scores, -1e30)
            powers = jnp.exp(scores - jnp.max(scores, axis=-1, keepdims=True))
            share = powers * (1.0 / jnp.sum(powers, axis=-1, keepdims=True))
            probs[rows, cols] = share
            mixture[rows, cols] = nn(share.astype(BF), values[rows, cols]).astype(BF)

    row_loop(count * TILE, group, first)


def attend_back(queries, keys, values, probs, grad_mix, grad_q, grad_k, grad_v, first, count):
    scale = HD ** (-0.5)

    def group(rows, index):
        for head in range(queries.shape[1] // HD):
            cols = slice(head * HD, (head + 1) * HD)
            share = probs[rows, cols]
            grad = grad_mix[rows, cols]
            grad_share = nt(grad, values[rows, cols])
            grad_v[rows, cols] = nn(share.T.astype(BF), grad).astype(BF)
            inner = jnp.sum(grad_share * share, axis=-1, keepdims=True)
            grad_scores = share * (grad_share - inner)
            low = grad_scores.astype(BF)
            grad_q[rows, cols] = (nn(low, keys[rows, cols]) * scale).astype(BF)
            turned = grad_scores.T.astype(BF)
            grad_k[rows, cols] = (nn(turned, queries[rows, cols]) * scale).astype(BF)

    row_loop(count * TILE, group, first)


def back_through(source, weights, seg, total):
    def one(m):
        total[...] += nt(source(m), flat(weights[seg, m]))

    half_loop(weights.shape[1], one)


def feed_up(normed_two, weights, which, m, active, slope):
    hidden = nn(normed_two[...], flat(weights[UPS[which], m]))
    bell = 0.5 + 0.5 * lax.erf(hidden * (0.5**0.5))
    active[which, m] = (hidden * bell).astype(BF)
    density = jnp.exp(-0.5 * hidden * hidden) * 0.3989422804014327
    slope[which, m] = bell + hidden * density


def turn(source, target):
    def block(rows, _):
        target[:, rows] = source[rows, :].T

    row_loop(source.shape[0], block)


def weight_grad(turned, right, target, seg):
    def one(m):
        product = nn(turned[...], right(m)).astype(BF)
        target[seg, m] = product.reshape(target.shape[2:])

    half_loop(target.shape[1], one)


class Place:
    def __init__(self, shape):
        self.nz, self.nx, self.ny = shape
        index = lax.axis_index("dp")
        self.core = lax.rem(index, 2)
        chip = lax.div(index, 2)
        self.at = {"z": lax.div(chip, self.nx), "x": lax.rem(chip, self.nx), "y": lax.axis_index("mp")}
        self.count = {"z": self.nz, "x": self.nx, "y": self.ny}

    def device(self, core=None, **moved):
        at = {**self.at, **moved}
        core = self.core if core is None else core
        return ((at["z"] * self.nx + at["x"]) * 2 + core, at["y"])

    def partner(self):
        return self.device(core=1 - self.core)

    def neighbour(self, dim, step):
        return self.device(**{dim: self.at[dim] + step})

    def barrier(self, dims):
        semaphore = pltpu.get_barrier_semaphore()
        pl.semaphore_signal(semaphore, inc=1, device_id=self.partner(), device_id_type=MESH)
        peers = 1
        for dim in dims:
            for step in (1, -1):
                there = self.at[dim] + step
                valid = (there >= 0) & (there < self.count[dim])
                peers = peers + valid.astype(jnp.int32)

                @pl.when(valid)
                def _(dim=dim, step=step):
                    other = self.neighbour(dim, step)
                    pl.semaphore_signal(semaphore, inc=1, device_id=other, device_id_type=MESH)

        pl.semaphore_wait(semaphore, peers)


def link_slots(count, dims):
    return sum(2 * (count[dim] - 1) for dim in dims)


class Gather:
    def __init__(self, place, buffer, axes, order, sems):
        self.place, self.buffer, self.axes, self.order = place, buffer, axes, order
        self.send, self.recv, self.pass_send, self.pass_recv = sems
        self.rounds = [(dim, t) for dim in order for t in range(place.count[dim] - 1)]
        self.slots = {}
        for dim, t in self.rounds:
            for way in (1, -1):
                self.slots[dim, t, way] = len(self.slots)

    def block(self, dim, position, core):
        done = self.order[: self.order.index(dim)] if dim else ""
        index = []
        for axis in self.axes:
            if axis == dim:
                index.append(position)
            elif axis in done:
                index.append(pl.ds(0, self.place.count[axis]))
            else:
                index.append(self.place.at[axis])
        return self.buffer.at[tuple(index) + (core,)]

    def link(self, dim, t, way, position, device):
        block = self.block(dim, position, self.place.core)
        slot = self.slots[dim, t, way]
        return pltpu.make_async_remote_copy(
            block, block, self.send.at[slot], self.recv.at[slot], device_id=device, device_id_type=MESH
        )

    def hand(self, slot, dim, position, core):
        block = self.block(dim, position, core)
        return pltpu.make_async_remote_copy(
            block,
            block,
            self.pass_send.at[slot],
            self.pass_recv.at[slot],
            device_id=self.place.partner(),
            device_id_type=MESH,
        )

    def sends(self, dim, t):
        here, count = self.place.at[dim], self.place.count[dim]
        yield 1, here - t, (here - t >= 0) & (here < count - 1)
        yield -1, here + t, (here + t < count) & (here > 0)

    def arrivals(self, dim, t):
        here, count = self.place.at[dim], self.place.count[dim]
        yield 1, here - 1 - t, here - 1 - t >= 0
        yield -1, here + 1 + t, here + 1 + t < count

    def start(self):
        self.hand(len(self.slots), "", None, self.place.core).start()
        self.send_round(0)

    def send_round(self, number):
        dim, t = self.rounds[number]
        for way, position, valid in self.sends(dim, t):

            @pl.when(valid)
            def _(way=way, position=position):
                self.link(dim, t, way, position, self.place.neighbour(dim, way)).start()

    def advance(self, number):
        dim, t = self.rounds[number - 1]
        for way, position, valid in self.arrivals(dim, t):

            @pl.when(valid)
            def _(way=way, position=position):
                self.link(dim, t, way, position, self.place.partner()).wait_recv()
                self.hand(self.slots[dim, t, way], dim, position, self.place.core).start()

        if number < len(self.rounds):
            self.send_round(number)

    def steps(self):
        return [self.start] + [functools.partial(self.advance, n + 1) for n in range(len(self.rounds))]

    def finish(self):
        other = 1 - self.place.core
        self.hand(len(self.slots), "", None, other).wait_recv()
        for dim, t in self.rounds:
            for way, position, valid in self.arrivals(dim, t):

                @pl.when(valid)
                def _(dim=dim, t=t, way=way, position=position):
                    self.hand(self.slots[dim, t, way], dim, position, other).wait_recv()

    def drain(self):
        self.hand(len(self.slots), "", None, self.place.core).wait_send()
        for dim, t in self.rounds:
            for way, position, valid in self.sends(dim, t):

                @pl.when(valid)
                def _(dim=dim, t=t, way=way, position=position):
                    self.link(dim, t, way, position, self.place.partner()).wait_send()

            for way, position, valid in self.arrivals(dim, t):

                @pl.when(valid)
                def _(dim=dim, t=t, way=way, position=position):
                    self.hand(self.slots[dim, t, way], dim, position, self.place.core).wait_send()


class Scatter:
    def __init__(self, place, mine, axes, order, inbox, hand_box, sems, both=False):
        self.place, self.mine, self.axes, self.order, self.both = place, mine, axes, order, both
        self.inbox, self.hand_box = inbox, hand_box
        self.send, self.recv = sems
        self.rounds = [(dim, t) for dim in order for t in range(place.count[dim] - 1)]
        self.slots = {}
        for dim, t in self.rounds:
            for way in (1, -1):
                self.slots[dim, t, way] = len(self.slots) + 1

    def own(self, index):
        return index + ((() if self.both else (self.place.core,)))

    def hand(self):
        whole = tuple(pl.ds(0, self.place.count[axis]) for axis in self.axes)
        source = self.mine.at[whole] if self.both else self.mine.at[whole + (1 - self.place.core,)]
        return pltpu.make_async_remote_copy(
            source, self.hand_box, self.send.at[0], self.recv.at[0], device_id=self.place.partner(), device_id_type=MESH
        )

    def start(self):
        self.hand().start()

    def take_hand(self):
        self.hand().wait_recv()
        first = self.place.count[self.axes[0]]
        rest = tuple(pl.ds(0, self.place.count[axis]) for axis in self.axes[1:])
        if self.both:
            self.hand().wait_send()
            self.mine[...] = self.mine[...] + self.hand_box[...]
        else:
            for p in range(first):
                for r in range(self.place.count[self.axes[1]]):
                    index = (p, r) + rest[1:]
                    here = self.mine[index + (self.place.core,)].astype(F32)
                    there = self.hand_box[index].astype(F32)
                    self.mine[index + (self.place.core,)] = (here + there).astype(self.mine.dtype)
        self.send_round(0)

    def block(self, dim, position):
        done = self.order[: self.order.index(dim)]
        index = []
        for axis in self.axes:
            if axis == dim:
                index.append(position)
            elif axis in done:
                index.append(self.place.at[axis])
            else:
                index.append(pl.ds(0, self.place.count[axis]))
        return self.own(tuple(index))

    def link(self, dim, t, way, position, device):
        slot = self.slots[dim, t, way]
        return pltpu.make_async_remote_copy(
            self.mine.at[self.block(dim, position)],
            self.inbox[slot],
            self.send.at[slot],
            self.recv.at[slot],
            device_id=device,
            device_id_type=MESH,
        )

    def sends(self, dim, t):
        here, count = self.place.at[dim], self.place.count[dim]
        yield 1, count - 1 - t + here, (t >= here) & (here < count - 1)
        back = count - 1 - here
        yield -1, t - back, (t >= back) & (here > 0)

    def arrivals(self, dim, t):
        here, count = self.place.at[dim], self.place.count[dim]
        yield 1, count - 2 - t + here, (t >= here - 1) & (here > 0)
        back = count - 1 - here
        yield -1, t + 1 - back, (t >= back - 1) & (here < count - 1)

    def send_round(self, number):
        dim, t = self.rounds[number]
        for way, position, valid in self.sends(dim, t):

            @pl.when(valid)
            def _(way=way, position=position):
                self.link(dim, t, way, position, self.place.neighbour(dim, way)).start()

    def advance(self, number):
        dim, t = self.rounds[number - 1]
        for way, position, valid in self.arrivals(dim, t):

            @pl.when(valid)
            def _(way=way, position=position):
                self.link(dim, t, way, position, self.place.partner()).wait_recv()
                index = self.block(dim, position)
                total = self.mine[index].astype(F32) + self.inbox[self.slots[dim, t, way]][...].astype(F32)
                self.mine[index] = total.astype(self.mine.dtype)

        if number < len(self.rounds):
            self.send_round(number)

    def steps(self):
        later = [functools.partial(self.advance, n + 1) for n in range(len(self.rounds))]
        return [self.start, self.take_hand] + later

    def result(self):
        return self.mine[self.own(tuple(self.place.at[axis] for axis in self.axes))]

    def drain(self):
        if not self.both:
            self.hand().wait_send()
        for dim, t in self.rounds:
            for way, position, valid in self.sends(dim, t):

                @pl.when(valid)
                def _(dim=dim, t=t, way=way, position=position):
                    self.link(dim, t, way, position, self.place.partner()).wait_send()


def inbox_shapes(count, axes, order, block):
    shapes, slots, left = [], {}, dict(count)
    for dim in order:
        left.pop(dim)
        for t in range(count[dim] - 1):
            for way in (1, -1):
                if way == 1 or count[dim] > 2:
                    shapes.append(tuple(count[axis] for axis in axes if axis in left) + block)
                slots[dim, t, way] = len(shapes) - 1
    return shapes, slots


def open_inbox(run, count, axes, order, block, boxes):
    shapes, slots = inbox_shapes(count, axes, order, block)
    for key, slot in run.slots.items():
        run.inbox[slot] = boxes[slots[key]]
    del boxes[: len(shapes)]


def play(plan, comm, pieces):
    plan = list(plan)
    while plan:
        token = plan.pop(0)
        if token >= 0:
            if comm:
                comm[token].pop(0)()
        elif callable(pieces[0]):
            pieces.pop(0)()
        else:
            count, piece = pieces.pop(0)
            between = [[] for _ in range(count - 1)]
            for spot in range(count - 1):
                while plan[0] >= 0:
                    token = plan.pop(0)
                    if comm:
                        between[spot].append(comm[token].pop(0))
                plan.pop(0)

            def once(index, carry, piece=piece, between=between):
                piece(index)
                for spot, steps in enumerate(between):
                    if steps:

                        @pl.when(index == spot)
                        def _(steps=steps):
                            for step in steps:
                                step()

                return carry

            lax.fori_loop(0, count, once, 0)
    assert not pieces and not any(comm.values())


class Mover:
    def __init__(self, sems):
        self.sems, self.used, self.open = sems, 0, []

    def start(self, source, target):
        copy = pltpu.make_async_copy(source, target, self.sems.at[self.used])
        self.used += 1
        copy.start()
        return copy

    def save(self, source, target):
        self.open.append(self.start(source, target))

    def close(self):
        for copy in self.open:
            copy.wait()


def read_vectors(vectors, tiles):
    nz, nx = tiles.shape[:2]
    pieces = [tiles[z, x, 0] + tiles[z, x, 1] for z in range(nz) for x in range(nx)]
    vectors[...] = jnp.concatenate(pieces, axis=1)


def column_parts(weights):
    wq, wk, wv, wo, wu, wd = weights
    left, right = pl.ds(0, SEG), pl.ds(SEG, SEG)
    return [wq, wk, wv, wo, wu.at[:, left], wu.at[:, right], wd.at[:, left], wd.at[:, right]]


def fill_tile(place, tiles, norms):
    tile = (place.at["z"], place.at["x"], place.core)
    tiles[tile] = jnp.zeros(tiles.shape[3:], F32)
    share = norms[0].shape[1]
    for line, norm in enumerate(norms):
        value = norm[...].astype(F32)
        for core in range(2):

            @pl.when(place.core == core)
            def _(line=line, value=value, core=core):
                tiles[tile + (slice(line, line + 1), slice(core * share, (core + 1) * share))] = value


FWD_OUT = (
    "x", "q", "k", "v", "probs", "mix", "res", "nrm2", "active", "slope", "out", "cot", "gl", "glt", "weight",
    "nrmt",
)
KEPT = len(FWD_OUT)


def forward_kernel(shape, micro, tokens, cotangent, ids, counts, *refs):
    if shape:
        weights, norms, g_out, refs = refs[:6], refs[6:10], refs[10], refs[11:]
    else:
        g_in, vectors_in, refs = refs[0], refs[1], refs[2:]
    if shape:
        vectors, refs = refs[0], refs[1:]
    else:
        vectors = vectors_in
    saved = dict(zip(FWD_OUT, refs[:KEPT]))
    here = dict(zip(FWD_OUT, refs[KEPT : 2 * KEPT]))
    refs = refs[2 * KEPT :]
    raw, nrm, low, total, g, sems = refs[:6]
    mover = Mover(sems)
    y = lax.axis_index("mp")
    take = mover.start(tokens.at[pl.ds(y * micro, micro)], raw)
    x, q, k, v, probs, mix, res, nrm2, active, slope, out, cot, gl, glt, weight, nrmt = (
        here[name] for name in FWD_OUT
    )

    def keep(*names):
        for name in names:
            mover.save(here[name], saved[name])

    comm = {}
    if shape:
        tiles, send, recv, pass_send, pass_recv = refs[6:]
        place = Place(shape)
        spot = (place.at["y"], place.at["z"], place.at["x"], place.core)
        mine = [mover.start(part, g.at[(seg,) + spot]) for seg, part in enumerate(column_parts(weights))]
        fill_tile(place, tiles, norms)
        place.barrier("zxy")
        pick = lambda seg: tuple(sem.at[seg] for sem in (send, recv, pass_send, pass_recv))
        runs = [Gather(place, g.at[seg], "yzx", ORDERS[seg], pick(seg)) for seg in range(8)]
        runs.append(Gather(place, tiles, "zx", "zx", pick(8)))
        comm = {seg: run.steps() for seg, run in enumerate(runs)}
        for seg in range(8):
            comm[seg][0] = lambda seg=seg: (mine[seg].wait(), runs[seg].start())

        def have(seg):
            runs[seg].finish()
            if seg < 8:
                mover.save(g.at[seg], g_out.at[seg])
            else:
                read_vectors(vectors, tiles)

    else:
        loads = [mover.start(g_in.at[seg], g.at[seg]) for seg in range(8)]

        def have(seg):
            if seg < 8:
                loads[seg].wait()

    def spread():
        take.wait()
        to_rows(raw, x)
        keep("x")
        loads_cot.append(mover.start(cotangent.at[pl.ds(y * micro, micro)], raw))
        row_weights(ids, counts, y, micro, weight)

    loads_cot = []

    def weigh():
        loads_cot[0].wait()
        to_rows(raw, cot)

        def block(rows, _):
            gl[rows, :] = (cot[rows, :].astype(F32) * weight[rows, :]).astype(BF)

        row_loop(cot.shape[0], block)
        turn(gl, glt)
        keep("cot", "gl", "glt", "weight")

    def norm_one():
        have(8)
        norm_in(x, nrm, vectors[0:1, :], vectors[1:2, :])
        turn(nrm, nrmt)
        keep("nrmt")

    def head_part(seg, target, name):
        have(seg)
        project(nrm, g, seg, target)
        keep(name)

    third = x.shape[0] // TILE // 3

    def mixing(part):
        attend(q, k, v, probs, mix, part * third, third)

    def project_out():
        keep("probs", "mix")
        have(O)
        res[...] = x[...].astype(F32)
        back_through(lambda m: mix[:, half(m)], g, O, res)
        keep("res")

    def norm_two():
        gain, shift = vectors[2:3, :], vectors[3:4, :]

        def block(rows, _):
            normal, _inv = norm_stats(res[rows, :])
            nrm2[rows, :] = (normal * gain + shift).astype(BF)

        row_loop(x.shape[0], block)
        keep("nrm2")

    def up(which, m):
        if m == 0:
            have(UPS[which])
        feed_up(nrm2, g, which, m, active, slope)
        mover.save(active.at[which, m], saved["active"].at[which, m])
        mover.save(slope.at[which, m], saved["slope"].at[which, m])

    def down(which):
        have(DOWNS[which])
        if which == 0:
            total[...] = res[...]
        back_through(lambda m: active[which, m], g, DOWNS[which], total)

    def last():
        low[...] = total[...].astype(BF)
        from_rows(low, out)
        keep("out")

    pieces = [spread, weigh, norm_one]
    pieces += [functools.partial(head_part, *args) for args in ((Q, q, "q"), (K, k, "k"), (V, v, "v"))]
    pieces += [(3, mixing), project_out, norm_two]
    pieces += [functools.partial(up, which, m) for which in range(2) for m in range(2)]
    pieces += [functools.partial(down, which) for which in range(2)] + [last]
    play(FORWARD_PLAN, comm, pieces)
    if shape:
        for run in runs:
            run.drain()
    mover.close()


def row_weights(ids, counts, y, micro, target):
    series = ids.shape[1]
    sums = counts[0]
    for kind in range(1, counts.shape[0]):
        sums = sums + counts[kind]
    mean = jnp.full((PAD, 1), sums.astype(F32), F32) / counts.shape[0]

    def one(index, carry):
        kind = ids[y * micro + lax.div(index, series), lax.rem(index, series)]
        count = counts[kind].astype(F32)
        target[pl.ds(pl.multiple_of(index * PAD, PAD), PAD), :] = 2.0 * mean / (mean + count)
        return carry

    lax.fori_loop(0, micro * series, one, 0)


class Swap:
    def __init__(self, place, mover, sems, ready, source, target):
        self.mover, self.source, self.ready = mover, source, ready
        y, (micro, patches) = place.at["y"], source.shape[:2]
        cut = patches // 2 + 1
        self.spots = [target.at[y * micro + part] for part in range(micro)]
        self.copies = []
        for part in range(micro):
            for piece in (pl.ds(0, cut), pl.ds(cut, patches - cut)):
                slot = 2 * len(self.copies)
                self.copies.append(
                    pltpu.make_async_remote_copy(
                        source.at[part, piece],
                        target.at[y * micro + part, piece],
                        sems.at[slot],
                        sems.at[slot + 1],
                        device_id=place.device(y=1 - y),
                        device_id_type=MESH,
                    )
                )

    def start(self, part):
        if part == 0:
            self.ready()
        self.copies[2 * part].start()
        self.mover.save(self.source.at[part], self.spots[part])

    def steps(self, part):
        return [functools.partial(self.start, part), self.copies[2 * part + 1].start]

    def wait(self):
        for copy in self.copies:
            copy.wait()


def feed_back_kernel(shape, vectors, g_in, active_in, slope_in, nrm2_in, res_in, out_in, cot_in, gl_in, glt_in, weight_in, mix_in, *refs):
    if shape:
        dw_out, gres_out, gm_out, vec, pair, grad_down, refs = refs[:6] + (refs[6:],)
    else:
        dw_out, gres_out, gm_out, vec, refs = refs[:4] + (refs[4:],)
    cot, weight, active, slope, nrm2, res, g, dw, gl, glt, gh, n2t, gn2, gres, mix, gm, sems = refs[:17]
    mover = Mover(sems)
    if shape:
        half_out, hands, send, recv, ysem = refs[17:22]
        boxes = list(refs[22:])
        side = mover.start(out_in, half_out)
    loads = {"glt": mover.start(glt_in, glt), ("active", 0): mover.start(active_in.at[0], active.at[0])}
    loads["gl"] = mover.start(gl_in, gl)
    for which in range(2):
        if which == 1:
            loads["active", which] = mover.start(active_in.at[which], active.at[which])
        loads["d", which] = mover.start(g_in.at[DOWNS[which]], g.at[2 + which])
        loads["slope", which] = mover.start(slope_in.at[which], slope.at[which])
    loads["nrm2"] = mover.start(nrm2_in, nrm2)
    for which in range(2):
        loads["u", which] = mover.start(g_in.at[UPS[which]], g.at[which])
    loads["res"] = mover.start(res_in, res)
    loads["cot"] = mover.start(cot_in, cot)
    loads["mix"] = mover.start(mix_in, mix)
    loads["o"] = mover.start(g_in.at[O], g.at[4])
    loads["weight"] = mover.start(weight_in, weight)
    comm = {}
    if shape:
        place = Place(shape)
        place.barrier("zxy")
        runs = []
        for which in range(2):
            order = BACK_ORDERS[DOWNS[which]]
            run = Scatter(
                place, dw.at[2 + which], "yzx", order, {}, hands.at[which], (send.at[which], recv.at[which])
            )
            open_inbox(run, place.count, "yzx", order, dw.shape[-2:], boxes)
            runs.append(run)
        swap = Swap(place, mover, ysem, side.wait, half_out, pair)
        comm = {0: runs[0].steps(), 1: runs[1].steps(), 2: swap.steps(0) + swap.steps(1)}

    def down_grad(which):
        if which == 0:
            loads["glt"].wait()
        loads["active", which].wait()
        weight_grad(glt, lambda m: active[which, m], dw, 2 + which)
        if not shape:
            mover.save(dw.at[2 + which], dw_out.at[2 + which])

    def hidden_grad(which):
        if which == 0:
            loads["gl"].wait()
        loads["d", which].wait()
        loads["slope", which].wait()

        def one(m):
            pulled = nn(gl[...], flat(g[2 + which, m]))
            gh[which, m] = (pulled * slope[which, m]).astype(BF)

        half_loop(g.shape[1], one)

    def turn_two():
        loads["nrm2"].wait()
        turn(nrm2, n2t)
        gn2[...] = jnp.zeros_like(gn2)

    def up_grad(which):
        weight_grad(n2t, lambda m: gh[which, m], dw, which)
        mover.save(dw.at[which], dw_out.at[which])

    def norm_grad(which):
        loads["u", which].wait()
        back_through(lambda m: gh[which, m], g, which, gn2)

    def last():
        for name in ("res", "cot", "weight"):
            loads[name].wait()
        gain = vectors[2:3, :]
        vec[...] = jnp.zeros_like(vec)

        def block(rows, _):
            grad = gn2[rows, :]
            pulled, normal = norm_pull(grad, res[rows, :], gain)
            vec[0] += fold_rows(grad * normal)
            vec[1] += fold_rows(grad)
            total = cot[rows, :].astype(F32) * weight[rows, :] + pulled
            gres[rows, :] = total
            gl[rows, :] = total.astype(BF)

        row_loop(cot.shape[0], block)
        mover.save(gres, gres_out)

    def mix_grad():
        loads["o"].wait()
        project(gl, g, 4, gm)
        mover.save(gm, gm_out)

    def out_grad():
        loads["mix"].wait()
        weight_grad(glt, lambda m: mix[:, half(m)], dw, 4)
        mover.save(dw.at[4], dw_out.at[4])

    pieces = []
    for which in range(2):
        pieces += [functools.partial(down_grad, which), functools.partial(hidden_grad, which)]
    pieces.append(turn_two)
    for which in range(2):
        pieces += [functools.partial(up_grad, which), functools.partial(norm_grad, which)]
    pieces += [last, mix_grad, lambda: turn(gl, glt), out_grad]
    play(FEED_PLAN, comm, pieces)
    if shape:
        for which in range(2):
            grad_down[:, which * SEG : (which + 1) * SEG] = runs[which].result().astype(F32)
            runs[which].drain()
        swap.wait()
    mover.close()


def vector_tiles(tiles, vec_a, vec_f):
    tiles[...] = jnp.zeros_like(tiles)
    nz, nx = tiles.shape[:2]
    for line, (source, part) in enumerate(((vec_a, 0), (vec_a, 1), (vec_f, 0), (vec_f, 1))):
        row = jnp.sum(source[part], axis=0, keepdims=True)
        for z in range(nz):
            for x in range(nx):
                chip = z * nx + x
                tiles[z, x, line : line + 1, :] = row[:, chip * 128 : (chip + 1) * 128]


BACK_IN = ("gm", "q", "k", "v", "probs", "nrmt", "gres", "x")
SHARED = (U0, U1, O, Q, K, V)
KEPT_GRADS = (0, 1, 4)


def attn_back_kernel(shape, vectors, vec_f, g_in, dw_in, *refs):
    given = dict(zip(BACK_IN, refs[:8]))
    refs = refs[8:]
    if shape:
        pair, grads, vec_out, refs = refs[0], refs[1:6], refs[6], refs[7:]
    else:
        dw_out, out, vec, refs = refs[0], refs[1], refs[2], refs[3:]
    here = dict(zip(BACK_IN, refs[:8]))
    g, dw, gal, pulls, raw, sems = refs[8:14]
    mover = Mover(sems)
    loads, comm = {}, {}
    if shape:
        held, tiles, hands, vec_hand, ybox, vec, send, recv, ysem = refs[14:23]
        boxes = list(refs[23:])

    def fetch_held(*spots):
        for spot in spots:
            if shape:
                loads["dw", spot] = mover.start(dw_in.at[KEPT_GRADS[spot]], held.at[spot])

    fetch_held(0)
    for name in BACK_IN[:5]:
        loads[name] = mover.start(given[name], here[name])
    fetch_held(1, 2)
    for name in BACK_IN[5:]:
        loads[name] = mover.start(given[name], here[name])
    for seg in (Q, K, V):
        loads[seg] = mover.start(g_in.at[seg], g.at[seg])
    gm, q, k, v, probs, nrmt, gres, x = (here[name] for name in BACK_IN)
    gn = probs
    if shape:
        place = Place(shape)
        place.barrier("zxy")
        runs = []
        for spot, seg in enumerate(SHARED):
            source = held.at[spot] if spot < 3 else dw.at[seg]
            order = BACK_ORDERS[seg]
            run = Scatter(place, source, "yzx", order, {}, hands.at[spot], (send.at[spot], recv.at[spot]))
            open_inbox(run, place.count, "yzx", order, dw.shape[-2:], boxes)
            runs.append(run)
        run = Scatter(place, tiles, "zx", "zx", {}, vec_hand, (send.at[6], recv.at[6]), both=True)
        open_inbox(run, {"z": place.nz, "x": place.nx}, "zx", "zx", (8, 128), boxes)
        runs.append(run)
        swap = Swap(place, mover, ysem, lambda: None, raw, pair)
        comm = {spot: run.steps() for spot, run in enumerate(runs)}
        comm[7], comm[8] = swap.steps(0), swap.steps(1)
        for spot in range(3):
            comm[spot][0] = lambda spot=spot: (loads["dw", spot].wait(), runs[spot].start())

    third = gal.shape[0] // TILE // 3
    micro = raw.shape[0]
    share = gal.shape[0] // micro

    def ready():
        for name in BACK_IN[:5]:
            loads[name].wait()
        vec[...] = jnp.zeros_like(vec)

    def mixing(part):
        attend_back(q, k, v, probs, gm, pulls.at[0], pulls.at[1], pulls.at[2], part * third, third)

    def head_grad(seg):
        weight_grad(nrmt, lambda m: pulls[seg, :, half(m)], dw, seg)

    def token_grad(part):
        rows_of = pl.ds(part * share, share)
        gn[rows_of, :] = jnp.zeros((share, gn.shape[1]), F32)
        if part == 0:
            for name in (Q, K, V, "gres", "x"):
                loads[name].wait()

        def one(index, carry):
            seg, m = lax.div(index, 2), lax.rem(index, 2)
            gn[rows_of, :] += nt(pulls[seg, rows_of, half(m)], flat(g[seg, m]))
            return carry

        lax.fori_loop(0, 6, one, 0)
        gain = vectors[0:1, :]

        def block(rows, _):
            grad = gn[rows, :]
            pulled, normal = norm_pull(grad, x[rows, :].astype(F32), gain)
            vec[0] += fold_rows(grad * normal)
            vec[1] += fold_rows(grad)
            gal[rows, :] = (gres[rows, :] + pulled).astype(BF)

        row_loop(share, block, part * share // TILE)
        patches, series, width = raw.shape[1:]
        turned = nn(gather_rows(patches, series), gal[rows_of, :]).astype(raw.dtype)
        raw[part] = turned.reshape(patches, series, width)

    def spread_vectors():
        if shape:
            vector_tiles(tiles, vec, vec_f)

    def before_heads():
        loads["nrmt"].wait()

    pieces = [ready, (3, mixing), before_heads]
    parts = [functools.partial(token_grad, part) for part in range(micro)]
    heads = [(3, head_grad)]
    pieces += heads + parts if GRADS_FIRST else parts + heads
    pieces.insert(len(pieces) - (0 if GRADS_FIRST else 1), spread_vectors)
    play(ATTN_PLAN, comm, pieces)
    if not shape:
        mover.save(raw, out)
        for seg in (Q, K, V):
            mover.save(dw.at[seg], dw_out.at[seg])
    if shape:
        here_tile = tiles.at[place.at["z"], place.at["x"]]
        copy = pltpu.make_async_remote_copy(
            here_tile, ybox, ysem.at[8], ysem.at[9], device_id=place.device(y=1 - place.at["y"]), device_id_type=MESH
        )
        copy.start()
        for spot, seg in enumerate(SHARED[2:]):
            grads[(3, 0, 1, 2)[spot]][...] = runs[2 + spot].result().astype(F32)
        for which in range(2):
            grads[4][:, which * SEG : (which + 1) * SEG] = runs[which].result().astype(F32)
        for run in runs:
            run.drain()
        copy.wait()
        vec_out[...] = tiles[place.at["z"], place.at["x"]] + ybox[...]
        swap.wait()
    mover.close()


def shape_of(shape, dtype):
    return jax.ShapeDtypeStruct(shape, dtype)


IN_VMEM = pl.BlockSpec(memory_space=pltpu.VMEM)
IN_SMEM = pl.BlockSpec(memory_space=pltpu.SMEM)
ANYWHERE = pl.BlockSpec(memory_space=pl.ANY)
DMA = pltpu.SemaphoreType.DMA


def call(body, outs, ins, out_specs, scratch, name, collective=None):
    params = {"vmem_limit_bytes": VMEM_LIMIT}
    if collective is not None:
        params.update(collective_id=collective, has_side_effects=True)
    return pl.pallas_call(
        body,
        out_shape=outs,
        in_specs=ins,
        out_specs=out_specs,
        scratch_shapes=scratch,
        compiler_params=pltpu.CompilerParams(**params),
        name=name,
    )


def vmem(like):
    return pltpu.VMEM(like.shape, like.dtype)


def forward(shape, micro, tokens, cotangent, ids, counts, weights, norms, g_in=None, vectors_in=None):
    _, patches, series, width = tokens.shape
    rows = micro * series * PAD
    full = g_in.shape if shape is None else (8, shape[2], shape[0], shape[1], 2, weights[0].shape[0], SEG)
    low, high = shape_of((rows, width), BF), shape_of((rows, width), F32)
    wide = (2, full[1], rows, SEG)
    raw = shape_of((micro, patches, series, width), BF)
    kinds = {name: low for name in FWD_OUT}
    kinds.update(
        probs=high,
        res=high,
        active=shape_of(wide, BF),
        slope=shape_of(wide, F32),
        out=raw,
        glt=shape_of((width, rows), BF),
        nrmt=shape_of((width, rows), BF),
        weight=shape_of((rows, 1), F32),
    )
    saved = tuple(kinds[name] for name in FWD_OUT)
    scratch = [vmem(kind) for kind in saved] + [vmem(raw), vmem(low), vmem(low), vmem(high), pltpu.VMEM(full, BF), DMA((64,))]
    if shape is None:
        results = call(
            functools.partial(forward_kernel, None, micro),
            saved,
            [ANYWHERE, ANYWHERE, IN_SMEM, IN_SMEM, ANYWHERE, IN_VMEM],
            (ANYWHERE,) * KEPT,
            scratch,
            "forward",
        )(tokens, cotangent, ids, counts, g_in, vectors_in)
        return g_in, vectors_in, dict(zip(FWD_OUT, results))
    count = dict(zip("zxy", shape))
    slots = link_slots(count, "zxy")
    scratch += [pltpu.VMEM(shape[:2] + (2, 8, 128), F32)]
    scratch += [DMA((9, slots)), DMA((9, slots)), DMA((9, slots + 1)), DMA((9, slots + 1))]
    results = call(
        functools.partial(forward_kernel, shape, micro),
        (shape_of(full, BF), shape_of((8, width), F32)) + saved,
        [ANYWHERE, ANYWHERE, IN_SMEM, IN_SMEM] + [ANYWHERE] * 6 + [IN_VMEM] * 4,
        (ANYWHERE, IN_VMEM) + (ANYWHERE,) * KEPT,
        scratch,
        "forward",
        0,
    )(tokens, cotangent, ids, counts, *weights, *norms)
    return results[0], results[1], dict(zip(FWD_OUT, results[2:]))


def scatter_scratch(segs, part, count, orders):
    rows, cols = part.shape[-2:]
    slots = link_slots(count, "zxy") + 1
    boxes = []
    for order in orders:
        boxes += [pltpu.VMEM(s, BF) for s in inbox_shapes(count, "yzx", order, (rows, cols))[0]]
    hands = pltpu.VMEM((len(orders),) + part.shape[1:4] + (rows, cols), BF)
    return hands, [DMA((segs, slots)), DMA((segs, slots))], boxes


def pair_of(raw, ny):
    return shape_of((ny * raw.shape[0],) + raw.shape[1:], BF)


def feed_back(shape, vectors, g, kept):
    low, high, raw = kept["x"], kept["res"], kept["out"]
    rows, width = low.shape
    part = shape_of((5,) + g.shape[1:], BF)
    turned = pltpu.VMEM((width, rows), BF)
    scratch = [
        vmem(low),
        pltpu.VMEM((rows, 1), F32),
        vmem(kept["active"]),
        vmem(kept["slope"]),
        vmem(low),
        vmem(high),
        vmem(part),
        vmem(part),
        vmem(low),
        turned,
        vmem(kept["active"]),
        turned,
        vmem(high),
        vmem(high),
        vmem(low),
        vmem(low),
        DMA((32,)),
    ]
    given = [g] + [kept[name] for name in ("active", "slope", "nrm2", "res", "out", "cot", "gl", "glt", "weight", "mix")]
    outs = [part, shape_of(high.shape, F32), shape_of(low.shape, BF), shape_of((2, 8, width), F32)]
    specs = [ANYWHERE, ANYWHERE, ANYWHERE, IN_VMEM]
    if shape:
        count = dict(zip("zxy", shape))
        hands, sems, boxes = scatter_scratch(2, part, count, [BACK_ORDERS[seg] for seg in DOWNS])
        scratch += [vmem(raw), hands] + sems + [DMA((8,))] + boxes
        outs += [pair_of(raw, shape[2]), shape_of((part.shape[-2], 2 * SEG), F32)]
        specs += [ANYWHERE, IN_VMEM]
    return call(
        functools.partial(feed_back_kernel, shape),
        tuple(outs),
        [IN_VMEM] + [ANYWHERE] * 11,
        tuple(specs),
        scratch,
        "feed_back",
        1 if shape else None,
    )(vectors, *given)


def attn_back(shape, vectors, vec_f, g, dw_in, kept):
    low, raw = kept["x"], kept["out"]
    width = low.shape[1]
    part = shape_of((3,) + g.shape[1:], BF)
    scratch = [vmem(kept[name]) for name in BACK_IN]
    scratch += [vmem(part), vmem(part), vmem(low), pltpu.VMEM((3,) + low.shape, BF), vmem(raw), DMA((32,))]
    vec = shape_of((2, 8, width), F32)
    if shape:
        nz, nx, ny = shape
        count = dict(zip("zxy", shape))
        share = part.shape[-2]
        small, large = shape_of((share, SEG), F32), shape_of((share, 2 * SEG), F32)
        outs = [pair_of(raw, ny)] + [small] * 4 + [large, shape_of((8, 128), F32)]
        specs = [ANYWHERE] + [IN_VMEM] * 6
        hands, sems, boxes = scatter_scratch(7, part, count, [BACK_ORDERS[seg] for seg in SHARED])
        tiles = pltpu.VMEM((nz, nx, 8, 128), F32)
        scratch += [vmem(part), tiles, hands, tiles, pltpu.VMEM((8, 128), F32), vmem(vec)]
        scratch += sems + [DMA((10,))] + boxes
        scratch += [pltpu.VMEM(s, F32) for s in inbox_shapes({"z": nz, "x": nx}, "zx", "zx", (8, 128))[0]]
    else:
        outs, specs = [part, raw, vec], [ANYWHERE, ANYWHERE, IN_VMEM]
        outs[1] = shape_of(raw.shape, BF)
    return call(
        functools.partial(attn_back_kernel, shape),
        tuple(outs),
        [IN_VMEM] * 2 + [ANYWHERE] * 10,
        tuple(specs),
        scratch,
        "attn_back",
        2 if shape else None,
    )(vectors, vec_f, g, dw_in, *(kept[name] for name in BACK_IN))


def chip_grid(chips):
    nx = 1
    while (nx * 2) ** 2 <= chips:
        nx *= 2
    return chips // nx, nx


def body(counts_of, tokens, cotangent, domain_ids, domain_counts, *params):
    weights, norms = params[:6], params[6:]
    n_dp, n_mp = counts_of
    micro = tokens.shape[0] // n_mp
    width = tokens.shape[3]
    share = width // n_dp
    y = lax.axis_index("mp")
    linked = n_mp == 2 and share * 2 == TILE
    flip = lambda array: jnp.transpose(array, (0, 2, 1, 3))
    x, cot = flip(tokens), flip(cotangent)
    if linked:
        shape = chip_grid(n_dp // 2) + (n_mp,)
        g, vectors, kept = forward(shape, micro, x, cot, domain_ids, domain_counts, weights, [norm.reshape(1, -1) for norm in norms])
    else:
        shards = jnp.stack(
            weights[:4] + tuple(w[:, i * SEG : (i + 1) * SEG] for w in weights[4:] for i in range(2))
        )
        g = lax.all_gather(lax.all_gather(shards, "dp", axis=1, tiled=True), "mp", axis=1)
        vectors = lax.all_gather(jnp.stack(norms), "dp", axis=1, tiled=True).astype(F32)
        vectors = jnp.pad(vectors, ((0, 4), (0, 0)))
        g, vectors, kept = forward(None, micro, x, cot, domain_ids, domain_counts, None, None, g, vectors)
    shape = shape if linked else None
    results = feed_back(shape, vectors, g, kept)
    dw_f, gres, gm, vec_f = results[:4]
    kept = {**kept, "gres": gres, "gm": gm}
    if linked:
        out, grad_down = results[4:]
        grad_tokens, *grads, vec = attn_back(shape, vectors, vec_f, g, dw_f, kept)
        grads.append(grad_down)
        core = lax.rem(lax.axis_index("dp"), 2)
        vec = lax.dynamic_slice(vec, (0, core * share), (4, share))
    else:
        dw_a, low_tokens, vec_a = attn_back(shape, vectors, vec_f, g, dw_f, kept)
        dw = jnp.concatenate((dw_a, dw_f[4:], dw_f[:4])).astype(F32)
        dw = lax.psum_scatter(lax.psum_scatter(dw, "mp", scatter_dimension=1), "dp", scatter_dimension=1, tiled=True)
        grads = [dw[0], dw[1], dw[2], dw[3]]
        grads += [jnp.concatenate((dw[a], dw[b]), axis=1) for a, b in (UPS, DOWNS)]
        vec = jnp.concatenate((jnp.sum(vec_a, axis=1), jnp.sum(vec_f, axis=1)))
        vec = lax.psum_scatter(lax.psum(vec, "mp"), "dp", scatter_dimension=1, tiled=True)
        out = lax.all_gather(kept["out"], "mp", axis=0, tiled=True)
        grad_tokens = lax.all_gather(low_tokens, "mp", axis=0, tiled=True)
    return (flip(out), flip(grad_tokens.astype(F32)), *grads, vec[0], vec[1], vec[2], vec[3])


def solution(mesh):
    rows, matrix, vector = P(None, "dp", None, None), P("dp", "mp"), P("dp")
    in_specs = (rows, rows, P(None, "dp"), P()) + (matrix,) * 6 + (vector,) * 4
    out_specs = (rows, rows) + (matrix,) * 6 + (vector,) * 4
    run = functools.partial(body, (mesh.shape["dp"], mesh.shape["mp"]))
    return jax.shard_map(run, mesh=mesh, in_specs=in_specs, out_specs=out_specs, check_vma=False)
```

```python
import functools

import jax
import jax.numpy as jnp
from jax import lax
from jax.experimental import pallas as pl
from jax.experimental.pallas import tpu as pltpu
from jax.sharding import PartitionSpec as P

BF = jnp.bfloat16
F32 = jnp.float32
HD = 128
SEG = 512
TILE = 128
PAD = 16
EPS = 1e-05
MESH = pl.DeviceIdType.MESH
VMEM_LIMIT = 62 * 1024 * 1024

Q, K, V, O, U0, U1, D0, D1 = range(8)
UPS = (U0, U1)
DOWNS = (D0, D1)
ORDERS = ("zyx", "zxy", "zxy", "yzx", "xyz", "zxy", "zyx", "xyz")
BACK_ORDERS = ("yxz", "xzy", "xzy", "zxy", "xzy", "yxz", "zxy", "xyz")

FORWARD_PLAN = (
    2, 1, 8, 4, 0, 3, 4, 2, 7, 8, -1, 0, 2, 7, 8, 1, 2, 0, 6, 0, 1, 5, 3, 1,
    2, 8, 5, 4, 0, 5, 8, 6, -1, 6, 3, 1, 5, 3, 3, 0, 4, -1, 2, 6, -1, 4, 1, 5,
    7, -1, -1, 6, -1, 4, 3, -1, 7, -1, -1, -1, -1, 5, 7, -1, -1, 6, -1, 7, -1, -1, -1,
)
FEED_PLAN = (
    2, -1, 0, -1, -1, 1, 0, 2, 2, 1, -1, -1, -1, 0, -1, -1, 1, 2, 0, -1, -1, -1, 1, 0,
    1, -1, 0, 1, -1, 0, 1,
)
ATTN_PLAN = (
    0, 1, -1, 1, 0, -1, 2, -1, -1, -1, -1, 3, 2, -1, 4, 3, -1, 2, 4, 0, 5, -1, 7, 0,
    5, 1, 0, 7, 3, 2, 4, -1, 8, -1, 0, 4, 5, 5, 8, 6, 6, 1, 4, 6, 5, 2, 6, 4,
    3, 1, 5, 6, 3, 1, 2, 6, 3, 5, 1, 4, 0, 3, 2,
)
GRADS_FIRST = 1


def nn(a, b):
    return lax.dot_general(a, b, (((1,), (0,)), ((), ())), preferred_element_type=F32)


def nt(a, b):
    return lax.dot_general(a, b, (((1,), (1,)), ((), ())), preferred_element_type=F32)


def flat(value):
    return value.reshape(-1, value.shape[-1])


def norm_stats(values):
    mean = jnp.mean(values, axis=-1, keepdims=True)
    center = values - mean
    inverse = lax.rsqrt(jnp.mean(center * center, axis=-1, keepdims=True) + EPS)
    return center * inverse, inverse


def norm_pull(grad, values, gain):
    normal, inverse = norm_stats(values)
    scaled = grad * gain
    first = jnp.mean(scaled, axis=-1, keepdims=True)
    second = jnp.mean(scaled * normal, axis=-1, keepdims=True)
    return inverse * (scaled - first - normal * second), normal


def fold_rows(values):
    rows, width = values.shape
    return jnp.sum(values.reshape(rows // 8, 8, width), axis=0)


def score_mask():
    key = lax.broadcasted_iota(jnp.int32, (TILE, TILE), 0)
    query = lax.broadcasted_iota(jnp.int32, (TILE, TILE), 1)
    return (query // PAD == key // PAD) & (key <= query)


def row_loop(rows, body, first=0):
    def once(index, carry):
        index = first + index
        body(pl.ds(pl.multiple_of(index * TILE, TILE), TILE), index)
        return carry

    lax.fori_loop(0, rows // TILE, once, 0)


def half_loop(count, body):
    def once(index, carry):
        body(index)
        return carry

    lax.fori_loop(0, count, once, 0)


def half(index):
    return pl.ds(pl.multiple_of(index * SEG, SEG), SEG)


def spread_rows(patches, series):
    row = lax.broadcasted_iota(jnp.int32, (series * PAD, patches * series), 0)
    col = lax.broadcasted_iota(jnp.int32, (series * PAD, patches * series), 1)
    hit = (lax.rem(row, PAD) * series + lax.div(row, PAD) == col) & (lax.rem(row, PAD) < patches)
    return jnp.where(hit, 1.0, 0.0).astype(BF)


def gather_rows(patches, series):
    row = lax.broadcasted_iota(jnp.int32, (patches * series, series * PAD), 0)
    col = lax.broadcasted_iota(jnp.int32, (patches * series, series * PAD), 1)
    return jnp.where(lax.rem(row, series) * PAD + lax.div(row, series) == col, 1.0, 0.0).astype(BF)


def to_rows(raw, target):
    micro, patches, series, _ = raw.shape
    matrix = spread_rows(patches, series)
    for part in range(micro):
        target[part * series * PAD : (part + 1) * series * PAD, :] = nn(matrix, flat(raw[part])).astype(BF)


def from_rows(source, raw):
    micro, patches, series, width = raw.shape
    matrix = gather_rows(patches, series)
    for part in range(micro):
        rows = source[part * series * PAD : (part + 1) * series * PAD, :]
        raw[part] = nn(matrix, rows).astype(raw.dtype).reshape(patches, series, width)


def norm_in(x, normed, gain, shift):
    def block(rows, _):
        normal, _inv = norm_stats(x[rows, :].astype(F32))
        normed[rows, :] = (normal * gain + shift).astype(BF)

    row_loop(x.shape[0], block)


def project(source, weights, seg, target):
    def one(m):
        target[:, half(m)] = nn(source[...], flat(weights[seg, m])).astype(BF)

    half_loop(weights.shape[1], one)


def attend(queries, keys, values, probs, mixture, first, count):
    mask = score_mask()
    scale = HD ** (-0.5)
    columns = [slice(at, at + HD) for at in range(0, queries.shape[1], HD)]

    def group(rows, _):
        scores = [nt(keys[rows, cols], queries[rows, cols]) * scale for cols in columns]
        scores = [jnp.where(mask, score, -1e30) for score in scores]
        peaks = [jnp.max(score, axis=0, keepdims=True) for score in scores]
        powers = [jnp.exp(score - peak) for score, peak in zip(scores, peaks)]
        inverses = [1.0 / jnp.sum(power, axis=0, keepdims=True) for power in powers]
        shares = [power * inverse for power, inverse in zip(powers, inverses)]
        for cols, share in zip(columns, shares):
            probs[rows, cols] = share
        mixed = [nn(share.astype(BF).T, values[rows, cols]) for share, cols in zip(shares, columns)]
        for cols, part in zip(columns, mixed):
            mixture[rows, cols] = part.astype(BF)

    row_loop(count * TILE, group, first)


def attend_back(queries, keys, values, probs, grad_mix, grad_q, grad_k, grad_v, first, count):
    scale = HD ** (-0.5)
    columns = [slice(at, at + HD) for at in range(0, queries.shape[1], HD)]

    def group(rows, _):
        shares = [probs[rows, cols] for cols in columns]
        grads = [grad_mix[rows, cols] for cols in columns]
        pulls = [nt(values[rows, cols], grad) for cols, grad in zip(columns, grads)]
        back_v = [nn(share.astype(BF), grad) for share, grad in zip(shares, grads)]
        inner = [jnp.sum(pull * share, axis=0, keepdims=True) for pull, share in zip(pulls, shares)]
        lows = [(share * (pull - mean)).astype(BF) for share, pull, mean in zip(shares, pulls, inner)]
        back_k = [nn(low, queries[rows, cols]) * scale for low, cols in zip(lows, columns)]
        back_q = [nn(low.T, keys[rows, cols]) * scale for low, cols in zip(lows, columns)]
        for cols, one, two, three in zip(columns, back_q, back_k, back_v):
            grad_q[rows, cols] = one.astype(BF)
            grad_k[rows, cols] = two.astype(BF)
            grad_v[rows, cols] = three.astype(BF)

    row_loop(count * TILE, group, first)


def back_through(source, weights, seg, total):
    def one(m):
        total[...] += nt(source(m), flat(weights[seg, m]))

    half_loop(weights.shape[1], one)


def feed_up(normed_two, weights, which, m, active, slope):
    hidden = nn(normed_two[...], flat(weights[UPS[which], m]))
    bell = 0.5 + 0.5 * lax.erf(hidden * (0.5**0.5))
    active[which, m] = (hidden * bell).astype(BF)
    density = jnp.exp(-0.5 * hidden * hidden) * 0.3989422804014327
    slope[which, m] = bell + hidden * density


def turn(source, target):
    def block(rows, _):
        target[:, rows] = source[rows, :].T

    row_loop(source.shape[0], block)


def weight_grad(turned, right, target, seg):
    def one(m):
        product = nn(turned[...], right(m)).astype(BF)
        target[seg, m] = product.reshape(target.shape[2:])

    half_loop(target.shape[1], one)


class Place:
    def __init__(self, shape):
        self.nz, self.nx, self.ny = shape
        index = lax.axis_index("dp")
        self.core = lax.rem(index, 2)
        chip = lax.div(index, 2)
        self.at = {"z": lax.div(chip, self.nx), "x": lax.rem(chip, self.nx), "y": lax.axis_index("mp")}
        self.count = {"z": self.nz, "x": self.nx, "y": self.ny}

    def device(self, core=None, **moved):
        at = {**self.at, **moved}
        core = self.core if core is None else core
        return ((at["z"] * self.nx + at["x"]) * 2 + core, at["y"])

    def partner(self):
        return self.device(core=1 - self.core)

    def neighbour(self, dim, step):
        return self.device(**{dim: self.at[dim] + step})

    def barrier(self, dims):
        semaphore = pltpu.get_barrier_semaphore()
        pl.semaphore_signal(semaphore, inc=1, device_id=self.partner(), device_id_type=MESH)
        peers = 1
        for dim in dims:
            for step in (1, -1):
                there = self.at[dim] + step
                valid = (there >= 0) & (there < self.count[dim])
                peers = peers + valid.astype(jnp.int32)

                @pl.when(valid)
                def _(dim=dim, step=step):
                    other = self.neighbour(dim, step)
                    pl.semaphore_signal(semaphore, inc=1, device_id=other, device_id_type=MESH)

        pl.semaphore_wait(semaphore, peers)


def link_slots(count, dims):
    return sum(2 * (count[dim] - 1) for dim in dims)


class Gather:
    def __init__(self, place, buffer, axes, order, sems):
        self.place, self.buffer, self.axes, self.order = place, buffer, axes, order
        self.send, self.recv, self.pass_send, self.pass_recv = sems
        self.rounds = [(dim, t) for dim in order for t in range(place.count[dim] - 1)]
        self.slots = {}
        for dim, t in self.rounds:
            for way in (1, -1):
                self.slots[dim, t, way] = len(self.slots)

    def block(self, dim, position, core):
        done = self.order[: self.order.index(dim)] if dim else ""
        index = []
        for axis in self.axes:
            if axis == dim:
                index.append(position)
            elif axis in done:
                index.append(pl.ds(0, self.place.count[axis]))
            else:
                index.append(self.place.at[axis])
        return self.buffer.at[tuple(index) + (core,)]

    def link(self, dim, t, way, position, device):
        block = self.block(dim, position, self.place.core)
        slot = self.slots[dim, t, way]
        return pltpu.make_async_remote_copy(
            block, block, self.send.at[slot], self.recv.at[slot], device_id=device, device_id_type=MESH
        )

    def hand(self, slot, dim, position, core):
        block = self.block(dim, position, core)
        return pltpu.make_async_remote_copy(
            block,
            block,
            self.pass_send.at[slot],
            self.pass_recv.at[slot],
            device_id=self.place.partner(),
            device_id_type=MESH,
        )

    def sends(self, dim, t):
        here, count = self.place.at[dim], self.place.count[dim]
        yield 1, here - t, (here - t >= 0) & (here < count - 1)
        yield -1, here + t, (here + t < count) & (here > 0)

    def arrivals(self, dim, t):
        here, count = self.place.at[dim], self.place.count[dim]
        yield 1, here - 1 - t, here - 1 - t >= 0
        yield -1, here + 1 + t, here + 1 + t < count

    def start(self):
        self.hand(len(self.slots), "", None, self.place.core).start()
        self.send_round(0)

    def send_round(self, number):
        dim, t = self.rounds[number]
        for way, position, valid in self.sends(dim, t):

            @pl.when(valid)
            def _(way=way, position=position):
                self.link(dim, t, way, position, self.place.neighbour(dim, way)).start()

    def advance(self, number):
        dim, t = self.rounds[number - 1]
        for way, position, valid in self.arrivals(dim, t):

            @pl.when(valid)
            def _(way=way, position=position):
                self.link(dim, t, way, position, self.place.partner()).wait_recv()
                self.hand(self.slots[dim, t, way], dim, position, self.place.core).start()

        if number < len(self.rounds):
            self.send_round(number)

    def steps(self):
        return [self.start] + [functools.partial(self.advance, n + 1) for n in range(len(self.rounds))]

    def finish(self):
        other = 1 - self.place.core
        self.hand(len(self.slots), "", None, other).wait_recv()
        for dim, t in self.rounds:
            for way, position, valid in self.arrivals(dim, t):

                @pl.when(valid)
                def _(dim=dim, t=t, way=way, position=position):
                    self.hand(self.slots[dim, t, way], dim, position, other).wait_recv()

    def drain(self):
        self.hand(len(self.slots), "", None, self.place.core).wait_send()
        for dim, t in self.rounds:
            for way, position, valid in self.sends(dim, t):

                @pl.when(valid)
                def _(dim=dim, t=t, way=way, position=position):
                    self.link(dim, t, way, position, self.place.partner()).wait_send()

            for way, position, valid in self.arrivals(dim, t):

                @pl.when(valid)
                def _(dim=dim, t=t, way=way, position=position):
                    self.hand(self.slots[dim, t, way], dim, position, self.place.core).wait_send()


class Scatter:
    def __init__(self, place, mine, axes, order, inbox, hand_box, sems, both=False):
        self.place, self.mine, self.axes, self.order, self.both = place, mine, axes, order, both
        self.inbox, self.hand_box = inbox, hand_box
        self.send, self.recv = sems
        self.rounds = [(dim, t) for dim in order for t in range(place.count[dim] - 1)]
        self.slots = {}
        for dim, t in self.rounds:
            for way in (1, -1):
                self.slots[dim, t, way] = len(self.slots) + 1

    def own(self, index):
        return index + ((() if self.both else (self.place.core,)))

    def hand(self):
        whole = tuple(pl.ds(0, self.place.count[axis]) for axis in self.axes)
        source = self.mine.at[whole] if self.both else self.mine.at[whole + (1 - self.place.core,)]
        return pltpu.make_async_remote_copy(
            source, self.hand_box, self.send.at[0], self.recv.at[0], device_id=self.place.partner(), device_id_type=MESH
        )

    def start(self):
        self.hand().start()

    def take_hand(self):
        self.hand().wait_recv()
        first = self.place.count[self.axes[0]]
        rest = tuple(pl.ds(0, self.place.count[axis]) for axis in self.axes[1:])
        if self.both:
            self.hand().wait_send()
            self.mine[...] = self.mine[...] + self.hand_box[...]
        else:
            for p in range(first):
                for r in range(self.place.count[self.axes[1]]):
                    index = (p, r) + rest[1:]
                    here = self.mine[index + (self.place.core,)].astype(F32)
                    there = self.hand_box[index].astype(F32)
                    self.mine[index + (self.place.core,)] = (here + there).astype(self.mine.dtype)
        self.send_round(0)

    def block(self, dim, position):
        done = self.order[: self.order.index(dim)]
        index = []
        for axis in self.axes:
            if axis == dim:
                index.append(position)
            elif axis in done:
                index.append(self.place.at[axis])
            else:
                index.append(pl.ds(0, self.place.count[axis]))
        return self.own(tuple(index))

    def link(self, dim, t, way, position, device):
        slot = self.slots[dim, t, way]
        return pltpu.make_async_remote_copy(
            self.mine.at[self.block(dim, position)],
            self.inbox[slot],
            self.send.at[slot],
            self.recv.at[slot],
            device_id=device,
            device_id_type=MESH,
        )

    def sends(self, dim, t):
        here, count = self.place.at[dim], self.place.count[dim]
        yield 1, count - 1 - t + here, (t >= here) & (here < count - 1)
        back = count - 1 - here
        yield -1, t - back, (t >= back) & (here > 0)

    def arrivals(self, dim, t):
        here, count = self.place.at[dim], self.place.count[dim]
        yield 1, count - 2 - t + here, (t >= here - 1) & (here > 0)
        back = count - 1 - here
        yield -1, t + 1 - back, (t >= back - 1) & (here < count - 1)

    def send_round(self, number):
        dim, t = self.rounds[number]
        for way, position, valid in self.sends(dim, t):

            @pl.when(valid)
            def _(way=way, position=position):
                self.link(dim, t, way, position, self.place.neighbour(dim, way)).start()

    def advance(self, number):
        dim, t = self.rounds[number - 1]
        for way, position, valid in self.arrivals(dim, t):

            @pl.when(valid)
            def _(way=way, position=position):
                self.link(dim, t, way, position, self.place.partner()).wait_recv()
                index = self.block(dim, position)
                total = self.mine[index].astype(F32) + self.inbox[self.slots[dim, t, way]][...].astype(F32)
                self.mine[index] = total.astype(self.mine.dtype)

        if number < len(self.rounds):
            self.send_round(number)

    def steps(self):
        later = [functools.partial(self.advance, n + 1) for n in range(len(self.rounds))]
        return [self.start, self.take_hand] + later

    def result(self):
        return self.mine[self.own(tuple(self.place.at[axis] for axis in self.axes))]

    def drain(self):
        if not self.both:
            self.hand().wait_send()
        for dim, t in self.rounds:
            for way, position, valid in self.sends(dim, t):

                @pl.when(valid)
                def _(dim=dim, t=t, way=way, position=position):
                    self.link(dim, t, way, position, self.place.partner()).wait_send()


def inbox_shapes(count, axes, order, block):
    shapes, slots, left = [], {}, dict(count)
    for dim in order:
        left.pop(dim)
        for t in range(count[dim] - 1):
            for way in (1, -1):
                if way == 1 or count[dim] > 2:
                    shapes.append(tuple(count[axis] for axis in axes if axis in left) + block)
                slots[dim, t, way] = len(shapes) - 1
    return shapes, slots


def open_inbox(run, count, axes, order, block, boxes):
    shapes, slots = inbox_shapes(count, axes, order, block)
    for key, slot in run.slots.items():
        run.inbox[slot] = boxes[slots[key]]
    del boxes[: len(shapes)]


def play(plan, comm, pieces):
    plan = list(plan)
    while plan:
        token = plan.pop(0)
        if token >= 0:
            if comm:
                comm[token].pop(0)()
        elif callable(pieces[0]):
            pieces.pop(0)()
        else:
            count, piece = pieces.pop(0)
            between = [[] for _ in range(count - 1)]
            for spot in range(count - 1):
                while plan[0] >= 0:
                    token = plan.pop(0)
                    if comm:
                        between[spot].append(comm[token].pop(0))
                plan.pop(0)

            def once(index, carry, piece=piece, between=between):
                piece(index)
                for spot, steps in enumerate(between):
                    if steps:

                        @pl.when(index == spot)
                        def _(steps=steps):
                            for step in steps:
                                step()

                return carry

            lax.fori_loop(0, count, once, 0)
    assert not pieces and not any(comm.values())


class Mover:
    def __init__(self, sems):
        self.sems, self.used, self.open = sems, 0, []

    def start(self, source, target):
        copy = pltpu.make_async_copy(source, target, self.sems.at[self.used])
        self.used += 1
        copy.start()
        return copy

    def save(self, source, target):
        self.open.append(self.start(source, target))

    def close(self):
        for copy in self.open:
            copy.wait()


def read_vectors(vectors, tiles):
    nz, nx = tiles.shape[:2]
    pieces = [tiles[z, x, 0] + tiles[z, x, 1] for z in range(nz) for x in range(nx)]
    vectors[...] = jnp.concatenate(pieces, axis=1)


def column_parts(weights):
    wq, wk, wv, wo, wu, wd = weights
    left, right = pl.ds(0, SEG), pl.ds(SEG, SEG)
    return [wq, wk, wv, wo, wu.at[:, left], wu.at[:, right], wd.at[:, left], wd.at[:, right]]


def fill_tile(place, tiles, norms):
    tile = (place.at["z"], place.at["x"], place.core)
    tiles[tile] = jnp.zeros(tiles.shape[3:], F32)
    share = norms[0].shape[1]
    for line, norm in enumerate(norms):
        value = norm[...].astype(F32)
        for core in range(2):

            @pl.when(place.core == core)
            def _(line=line, value=value, core=core):
                tiles[tile + (slice(line, line + 1), slice(core * share, (core + 1) * share))] = value


FWD_OUT = (
    "x", "q", "k", "v", "probs", "mix", "res", "nrm2", "active", "slope", "out", "cot", "gl", "glt", "weight",
    "nrmt",
)
KEPT = len(FWD_OUT)


def forward_kernel(shape, micro, tokens, cotangent, ids, counts, *refs):
    if shape:
        weights, norms, g_out, refs = refs[:6], refs[6:10], refs[10], refs[11:]
    else:
        g_in, vectors_in, refs = refs[0], refs[1], refs[2:]
    if shape:
        vectors, refs = refs[0], refs[1:]
    else:
        vectors = vectors_in
    saved = dict(zip(FWD_OUT, refs[:KEPT]))
    here = dict(zip(FWD_OUT, refs[KEPT : 2 * KEPT]))
    refs = refs[2 * KEPT :]
    raw, nrm, low, total, g, sems = refs[:6]
    mover = Mover(sems)
    y = lax.axis_index("mp")
    take = mover.start(tokens.at[pl.ds(y * micro, micro)], raw)
    x, q, k, v, probs, mix, res, nrm2, active, slope, out, cot, gl, glt, weight, nrmt = (
        here[name] for name in FWD_OUT
    )

    def keep(*names):
        for name in names:
            mover.save(here[name], saved[name])

    comm = {}
    if shape:
        tiles, send, recv, pass_send, pass_recv = refs[6:]
        place = Place(shape)
        spot = (place.at["y"], place.at["z"], place.at["x"], place.core)
        mine = [mover.start(part, g.at[(seg,) + spot]) for seg, part in enumerate(column_parts(weights))]
        fill_tile(place, tiles, norms)
        place.barrier("zxy")
        pick = lambda seg: tuple(sem.at[seg] for sem in (send, recv, pass_send, pass_recv))
        runs = [Gather(place, g.at[seg], "yzx", ORDERS[seg], pick(seg)) for seg in range(8)]
        runs.append(Gather(place, tiles, "zx", "zx", pick(8)))
        comm = {seg: run.steps() for seg, run in enumerate(runs)}
        for seg in range(8):
            comm[seg][0] = lambda seg=seg: (mine[seg].wait(), runs[seg].start())

        def have(seg):
            runs[seg].finish()
            if seg < 8:
                mover.save(g.at[seg], g_out.at[seg])
            else:
                read_vectors(vectors, tiles)

    else:
        loads = [mover.start(g_in.at[seg], g.at[seg]) for seg in range(8)]

        def have(seg):
            if seg < 8:
                loads[seg].wait()

    def spread():
        take.wait()
        to_rows(raw, x)
        keep("x")
        loads_cot.append(mover.start(cotangent.at[pl.ds(y * micro, micro)], raw))
        row_weights(ids, counts, y, micro, weight)

    loads_cot = []

    def weigh():
        loads_cot[0].wait()
        to_rows(raw, cot)

        def block(rows, _):
            gl[rows, :] = (cot[rows, :].astype(F32) * weight[rows, :]).astype(BF)

        row_loop(cot.shape[0], block)
        turn(gl, glt)
        keep("cot", "gl", "glt", "weight")

    def norm_one():
        have(8)
        norm_in(x, nrm, vectors[0:1, :], vectors[1:2, :])
        turn(nrm, nrmt)
        keep("nrmt")

    def head_part(seg, target, name):
        have(seg)
        project(nrm, g, seg, target)
        keep(name)

    third = x.shape[0] // TILE // 3

    def mixing(part):
        attend(q, k, v, probs, mix, part * third, third)

    def project_out():
        keep("probs", "mix")
        have(O)
        res[...] = x[...].astype(F32)
        back_through(lambda m: mix[:, half(m)], g, O, res)
        keep("res")

    def norm_two():
        gain, shift = vectors[2:3, :], vectors[3:4, :]

        def block(rows, _):
            normal, _inv = norm_stats(res[rows, :])
            nrm2[rows, :] = (normal * gain + shift).astype(BF)

        row_loop(x.shape[0], block)
        keep("nrm2")

    def up(which, m):
        if m == 0:
            have(UPS[which])
        feed_up(nrm2, g, which, m, active, slope)
        mover.save(active.at[which, m], saved["active"].at[which, m])
        mover.save(slope.at[which, m], saved["slope"].at[which, m])

    def down(which):
        have(DOWNS[which])
        if which == 0:
            total[...] = res[...]
        back_through(lambda m: active[which, m], g, DOWNS[which], total)

    def last():
        low[...] = total[...].astype(BF)
        from_rows(low, out)
        keep("out")

    pieces = [spread, weigh, norm_one]
    pieces += [functools.partial(head_part, *args) for args in ((Q, q, "q"), (K, k, "k"), (V, v, "v"))]
    pieces += [(3, mixing), project_out, norm_two]
    pieces += [functools.partial(up, which, m) for which in range(2) for m in range(2)]
    pieces += [functools.partial(down, which) for which in range(2)] + [last]
    play(FORWARD_PLAN, comm, pieces)
    if shape:
        for run in runs:
            run.drain()
    mover.close()


def row_weights(ids, counts, y, micro, target):
    series = ids.shape[1]
    sums = counts[0]
    for kind in range(1, counts.shape[0]):
        sums = sums + counts[kind]
    mean = jnp.full((PAD, 1), sums.astype(F32), F32) / counts.shape[0]

    def one(index, carry):
        kind = ids[y * micro + lax.div(index, series), lax.rem(index, series)]
        count = counts[kind].astype(F32)
        target[pl.ds(pl.multiple_of(index * PAD, PAD), PAD), :] = 2.0 * mean / (mean + count)
        return carry

    lax.fori_loop(0, micro * series, one, 0)


class Swap:
    def __init__(self, place, mover, sems, ready, source, target):
        self.mover, self.source, self.ready = mover, source, ready
        y, (micro, patches) = place.at["y"], source.shape[:2]
        cut = patches // 2 + 1
        self.spots = [target.at[y * micro + part] for part in range(micro)]
        self.copies = []
        for part in range(micro):
            for piece in (pl.ds(0, cut), pl.ds(cut, patches - cut)):
                slot = 2 * len(self.copies)
                self.copies.append(
                    pltpu.make_async_remote_copy(
                        source.at[part, piece],
                        target.at[y * micro + part, piece],
                        sems.at[slot],
                        sems.at[slot + 1],
                        device_id=place.device(y=1 - y),
                        device_id_type=MESH,
                    )
                )

    def start(self, part):
        if part == 0:
            self.ready()
        self.copies[2 * part].start()
        self.mover.save(self.source.at[part], self.spots[part])

    def steps(self, part):
        return [functools.partial(self.start, part), self.copies[2 * part + 1].start]

    def wait(self):
        for copy in self.copies:
            copy.wait()


def feed_back_kernel(shape, vectors, g_in, active_in, slope_in, nrm2_in, res_in, out_in, cot_in, gl_in, glt_in, weight_in, mix_in, *refs):
    if shape:
        dw_out, gres_out, gm_out, vec, pair, grad_down, refs = refs[:6] + (refs[6:],)
    else:
        dw_out, gres_out, gm_out, vec, refs = refs[:4] + (refs[4:],)
    cot, weight, active, slope, nrm2, res, g, dw, gl, glt, gh, n2t, gn2, gres, mix, gm, sems = refs[:17]
    mover = Mover(sems)
    if shape:
        half_out, hands, send, recv, ysem = refs[17:22]
        boxes = list(refs[22:])
        side = mover.start(out_in, half_out)
    loads = {"glt": mover.start(glt_in, glt), ("active", 0): mover.start(active_in.at[0], active.at[0])}
    loads["gl"] = mover.start(gl_in, gl)
    for which in range(2):
        if which == 1:
            loads["active", which] = mover.start(active_in.at[which], active.at[which])
        loads["d", which] = mover.start(g_in.at[DOWNS[which]], g.at[2 + which])
        loads["slope", which] = mover.start(slope_in.at[which], slope.at[which])
    loads["nrm2"] = mover.start(nrm2_in, nrm2)
    for which in range(2):
        loads["u", which] = mover.start(g_in.at[UPS[which]], g.at[which])
    loads["res"] = mover.start(res_in, res)
    loads["cot"] = mover.start(cot_in, cot)
    loads["mix"] = mover.start(mix_in, mix)
    loads["o"] = mover.start(g_in.at[O], g.at[4])
    loads["weight"] = mover.start(weight_in, weight)
    comm = {}
    if shape:
        place = Place(shape)
        place.barrier("zxy")
        runs = []
        for which in range(2):
            order = BACK_ORDERS[DOWNS[which]]
            run = Scatter(
                place, dw.at[2 + which], "yzx", order, {}, hands.at[which], (send.at[which], recv.at[which])
            )
            open_inbox(run, place.count, "yzx", order, dw.shape[-2:], boxes)
            runs.append(run)
        swap = Swap(place, mover, ysem, side.wait, half_out, pair)
        comm = {0: runs[0].steps(), 1: runs[1].steps(), 2: swap.steps(0) + swap.steps(1)}

    def down_grad(which):
        if which == 0:
            loads["glt"].wait()
        loads["active", which].wait()
        weight_grad(glt, lambda m: active[which, m], dw, 2 + which)
        if not shape:
            mover.save(dw.at[2 + which], dw_out.at[2 + which])

    def hidden_grad(which):
        if which == 0:
            loads["gl"].wait()
        loads["d", which].wait()
        loads["slope", which].wait()

        def one(m):
            pulled = nn(gl[...], flat(g[2 + which, m]))
            gh[which, m] = (pulled * slope[which, m]).astype(BF)

        half_loop(g.shape[1], one)

    def turn_two():
        loads["nrm2"].wait()
        turn(nrm2, n2t)
        gn2[...] = jnp.zeros_like(gn2)

    def up_grad(which):
        weight_grad(n2t, lambda m: gh[which, m], dw, which)
        mover.save(dw.at[which], dw_out.at[which])

    def norm_grad(which):
        loads["u", which].wait()
        back_through(lambda m: gh[which, m], g, which, gn2)

    def last():
        for name in ("res", "cot", "weight"):
            loads[name].wait()
        gain = vectors[2:3, :]
        vec[...] = jnp.zeros_like(vec)

        def block(rows, _):
            grad = gn2[rows, :]
            pulled, normal = norm_pull(grad, res[rows, :], gain)
            vec[0] += fold_rows(grad * normal)
            vec[1] += fold_rows(grad)
            total = cot[rows, :].astype(F32) * weight[rows, :] + pulled
            gres[rows, :] = total
            gl[rows, :] = total.astype(BF)

        row_loop(cot.shape[0], block)
        mover.save(gres, gres_out)

    def mix_grad():
        loads["o"].wait()
        project(gl, g, 4, gm)
        mover.save(gm, gm_out)

    def out_grad():
        loads["mix"].wait()
        weight_grad(glt, lambda m: mix[:, half(m)], dw, 4)
        mover.save(dw.at[4], dw_out.at[4])

    pieces = []
    for which in range(2):
        pieces += [functools.partial(down_grad, which), functools.partial(hidden_grad, which)]
    pieces.append(turn_two)
    for which in range(2):
        pieces += [functools.partial(up_grad, which), functools.partial(norm_grad, which)]
    pieces += [last, mix_grad, lambda: turn(gl, glt), out_grad]
    play(FEED_PLAN, comm, pieces)
    if shape:
        for which in range(2):
            grad_down[:, which * SEG : (which + 1) * SEG] = runs[which].result().astype(F32)
            runs[which].drain()
        swap.wait()
    mover.close()


def vector_tiles(tiles, vec_a, vec_f):
    tiles[...] = jnp.zeros_like(tiles)
    nz, nx = tiles.shape[:2]
    for line, (source, part) in enumerate(((vec_a, 0), (vec_a, 1), (vec_f, 0), (vec_f, 1))):
        row = jnp.sum(source[part], axis=0, keepdims=True)
        for z in range(nz):
            for x in range(nx):
                chip = z * nx + x
                tiles[z, x, line : line + 1, :] = row[:, chip * 128 : (chip + 1) * 128]


BACK_IN = ("gm", "q", "k", "v", "probs", "nrmt", "gres", "x")
SHARED = (U0, U1, O, Q, K, V)
KEPT_GRADS = (0, 1, 4)


def attn_back_kernel(shape, vectors, vec_f, g_in, dw_in, *refs):
    given = dict(zip(BACK_IN, refs[:8]))
    refs = refs[8:]
    if shape:
        pair, grads, vec_out, refs = refs[0], refs[1:6], refs[6], refs[7:]
    else:
        dw_out, out, vec, refs = refs[0], refs[1], refs[2], refs[3:]
    here = dict(zip(BACK_IN, refs[:8]))
    g, dw, gal, pulls, raw, sems = refs[8:14]
    mover = Mover(sems)
    loads, comm = {}, {}
    if shape:
        held, tiles, hands, vec_hand, ybox, vec, send, recv, ysem = refs[14:23]
        boxes = list(refs[23:])

    def fetch_held(*spots):
        for spot in spots:
            if shape:
                loads["dw", spot] = mover.start(dw_in.at[KEPT_GRADS[spot]], held.at[spot])

    fetch_held(0)
    for name in BACK_IN[:5]:
        loads[name] = mover.start(given[name], here[name])
    fetch_held(1, 2)
    for name in BACK_IN[5:]:
        loads[name] = mover.start(given[name], here[name])
    for seg in (Q, K, V):
        loads[seg] = mover.start(g_in.at[seg], g.at[seg])
    gm, q, k, v, probs, nrmt, gres, x = (here[name] for name in BACK_IN)
    gn = probs
    if shape:
        place = Place(shape)
        place.barrier("zxy")
        runs = []
        for spot, seg in enumerate(SHARED):
            source = held.at[spot] if spot < 3 else dw.at[seg]
            order = BACK_ORDERS[seg]
            run = Scatter(place, source, "yzx", order, {}, hands.at[spot], (send.at[spot], recv.at[spot]))
            open_inbox(run, place.count, "yzx", order, dw.shape[-2:], boxes)
            runs.append(run)
        run = Scatter(place, tiles, "zx", "zx", {}, vec_hand, (send.at[6], recv.at[6]), both=True)
        open_inbox(run, {"z": place.nz, "x": place.nx}, "zx", "zx", (8, 128), boxes)
        runs.append(run)
        swap = Swap(place, mover, ysem, lambda: None, raw, pair)
        comm = {spot: run.steps() for spot, run in enumerate(runs)}
        comm[7], comm[8] = swap.steps(0), swap.steps(1)
        for spot in range(3):
            comm[spot][0] = lambda spot=spot: (loads["dw", spot].wait(), runs[spot].start())

    third = gal.shape[0] // TILE // 3
    micro = raw.shape[0]
    share = gal.shape[0] // micro

    def ready():
        for name in BACK_IN[:5]:
            loads[name].wait()
        vec[...] = jnp.zeros_like(vec)

    def mixing(part):
        attend_back(q, k, v, probs, gm, pulls.at[0], pulls.at[1], pulls.at[2], part * third, third)

    def head_grad(seg):
        weight_grad(nrmt, lambda m: pulls[seg, :, half(m)], dw, seg)

    def token_grad(part):
        rows_of = pl.ds(part * share, share)
        gn[rows_of, :] = jnp.zeros((share, gn.shape[1]), F32)
        if part == 0:
            for name in (Q, K, V, "gres", "x"):
                loads[name].wait()

        def one(index, carry):
            seg, m = lax.div(index, 2), lax.rem(index, 2)
            gn[rows_of, :] += nt(pulls[seg, rows_of, half(m)], flat(g[seg, m]))
            return carry

        lax.fori_loop(0, 6, one, 0)
        gain = vectors[0:1, :]

        def block(rows, _):
            grad = gn[rows, :]
            pulled, normal = norm_pull(grad, x[rows, :].astype(F32), gain)
            vec[0] += fold_rows(grad * normal)
            vec[1] += fold_rows(grad)
            gal[rows, :] = (gres[rows, :] + pulled).astype(BF)

        row_loop(share, block, part * share // TILE)
        patches, series, width = raw.shape[1:]
        turned = nn(gather_rows(patches, series), gal[rows_of, :]).astype(raw.dtype)
        raw[part] = turned.reshape(patches, series, width)

    def spread_vectors():
        if shape:
            vector_tiles(tiles, vec, vec_f)

    def before_heads():
        loads["nrmt"].wait()

    pieces = [ready, (3, mixing), before_heads]
    parts = [functools.partial(token_grad, part) for part in range(micro)]
    heads = [(3, head_grad)]
    pieces += heads + parts if GRADS_FIRST else parts + heads
    pieces.insert(len(pieces) - (0 if GRADS_FIRST else 1), spread_vectors)
    play(ATTN_PLAN, comm, pieces)
    if not shape:
        mover.save(raw, out)
        for seg in (Q, K, V):
            mover.save(dw.at[seg], dw_out.at[seg])
    if shape:
        here_tile = tiles.at[place.at["z"], place.at["x"]]
        copy = pltpu.make_async_remote_copy(
            here_tile, ybox, ysem.at[8], ysem.at[9], device_id=place.device(y=1 - place.at["y"]), device_id_type=MESH
        )
        copy.start()
        for spot, seg in enumerate(SHARED[2:]):
            grads[(3, 0, 1, 2)[spot]][...] = runs[2 + spot].result().astype(F32)
        for which in range(2):
            grads[4][:, which * SEG : (which + 1) * SEG] = runs[which].result().astype(F32)
        for run in runs:
            run.drain()
        copy.wait()
        vec_out[...] = tiles[place.at["z"], place.at["x"]] + ybox[...]
        swap.wait()
    mover.close()


def shape_of(shape, dtype):
    return jax.ShapeDtypeStruct(shape, dtype)


IN_VMEM = pl.BlockSpec(memory_space=pltpu.VMEM)
IN_SMEM = pl.BlockSpec(memory_space=pltpu.SMEM)
ANYWHERE = pl.BlockSpec(memory_space=pl.ANY)
DMA = pltpu.SemaphoreType.DMA


def call(body, outs, ins, out_specs, scratch, name, collective=None):
    params = {"vmem_limit_bytes": VMEM_LIMIT}
    if collective is not None:
        params.update(collective_id=collective, has_side_effects=True)
    return pl.pallas_call(
        body,
        out_shape=outs,
        in_specs=ins,
        out_specs=out_specs,
        scratch_shapes=scratch,
        compiler_params=pltpu.CompilerParams(**params),
        name=name,
    )


def vmem(like):
    return pltpu.VMEM(like.shape, like.dtype)


def forward(shape, micro, tokens, cotangent, ids, counts, weights, norms, g_in=None, vectors_in=None):
    _, patches, series, width = tokens.shape
    rows = micro * series * PAD
    full = g_in.shape if shape is None else (8, shape[2], shape[0], shape[1], 2, weights[0].shape[0], SEG)
    low, high = shape_of((rows, width), BF), shape_of((rows, width), F32)
    wide = (2, full[1], rows, SEG)
    raw = shape_of((micro, patches, series, width), BF)
    kinds = {name: low for name in FWD_OUT}
    kinds.update(
        probs=high,
        res=high,
        active=shape_of(wide, BF),
        slope=shape_of(wide, F32),
        out=raw,
        glt=shape_of((width, rows), BF),
        nrmt=shape_of((width, rows), BF),
        weight=shape_of((rows, 1), F32),
    )
    saved = tuple(kinds[name] for name in FWD_OUT)
    scratch = [vmem(kind) for kind in saved] + [vmem(raw), vmem(low), vmem(low), vmem(high), pltpu.VMEM(full, BF), DMA((64,))]
    if shape is None:
        results = call(
            functools.partial(forward_kernel, None, micro),
            saved,
            [ANYWHERE, ANYWHERE, IN_SMEM, IN_SMEM, ANYWHERE, IN_VMEM],
            (ANYWHERE,) * KEPT,
            scratch,
            "forward",
        )(tokens, cotangent, ids, counts, g_in, vectors_in)
        return g_in, vectors_in, dict(zip(FWD_OUT, results))
    count = dict(zip("zxy", shape))
    slots = link_slots(count, "zxy")
    scratch += [pltpu.VMEM(shape[:2] + (2, 8, 128), F32)]
    scratch += [DMA((9, slots)), DMA((9, slots)), DMA((9, slots + 1)), DMA((9, slots + 1))]
    results = call(
        functools.partial(forward_kernel, shape, micro),
        (shape_of(full, BF), shape_of((8, width), F32)) + saved,
        [ANYWHERE, ANYWHERE, IN_SMEM, IN_SMEM] + [ANYWHERE] * 6 + [IN_VMEM] * 4,
        (ANYWHERE, IN_VMEM) + (ANYWHERE,) * KEPT,
        scratch,
        "forward",
        0,
    )(tokens, cotangent, ids, counts, *weights, *norms)
    return results[0], results[1], dict(zip(FWD_OUT, results[2:]))


def scatter_scratch(segs, part, count, orders):
    rows, cols = part.shape[-2:]
    slots = link_slots(count, "zxy") + 1
    boxes = []
    for order in orders:
        boxes += [pltpu.VMEM(s, BF) for s in inbox_shapes(count, "yzx", order, (rows, cols))[0]]
    hands = pltpu.VMEM((len(orders),) + part.shape[1:4] + (rows, cols), BF)
    return hands, [DMA((segs, slots)), DMA((segs, slots))], boxes


def pair_of(raw, ny):
    return shape_of((ny * raw.shape[0],) + raw.shape[1:], BF)


def feed_back(shape, vectors, g, kept):
    low, high, raw = kept["x"], kept["res"], kept["out"]
    rows, width = low.shape
    part = shape_of((5,) + g.shape[1:], BF)
    turned = pltpu.VMEM((width, rows), BF)
    scratch = [
        vmem(low),
        pltpu.VMEM((rows, 1), F32),
        vmem(kept["active"]),
        vmem(kept["slope"]),
        vmem(low),
        vmem(high),
        vmem(part),
        vmem(part),
        vmem(low),
        turned,
        vmem(kept["active"]),
        turned,
        vmem(high),
        vmem(high),
        vmem(low),
        vmem(low),
        DMA((32,)),
    ]
    given = [g] + [kept[name] for name in ("active", "slope", "nrm2", "res", "out", "cot", "gl", "glt", "weight", "mix")]
    outs = [part, shape_of(high.shape, F32), shape_of(low.shape, BF), shape_of((2, 8, width), F32)]
    specs = [ANYWHERE, ANYWHERE, ANYWHERE, IN_VMEM]
    if shape:
        count = dict(zip("zxy", shape))
        hands, sems, boxes = scatter_scratch(2, part, count, [BACK_ORDERS[seg] for seg in DOWNS])
        scratch += [vmem(raw), hands] + sems + [DMA((8,))] + boxes
        outs += [pair_of(raw, shape[2]), shape_of((part.shape[-2], 2 * SEG), F32)]
        specs += [ANYWHERE, IN_VMEM]
    return call(
        functools.partial(feed_back_kernel, shape),
        tuple(outs),
        [IN_VMEM] + [ANYWHERE] * 11,
        tuple(specs),
        scratch,
        "feed_back",
        1 if shape else None,
    )(vectors, *given)


def attn_back(shape, vectors, vec_f, g, dw_in, kept):
    low, raw = kept["x"], kept["out"]
    width = low.shape[1]
    part = shape_of((3,) + g.shape[1:], BF)
    scratch = [vmem(kept[name]) for name in BACK_IN]
    scratch += [vmem(part), vmem(part), vmem(low), pltpu.VMEM((3,) + low.shape, BF), vmem(raw), DMA((32,))]
    vec = shape_of((2, 8, width), F32)
    if shape:
        nz, nx, ny = shape
        count = dict(zip("zxy", shape))
        share = part.shape[-2]
        small, large = shape_of((share, SEG), F32), shape_of((share, 2 * SEG), F32)
        outs = [pair_of(raw, ny)] + [small] * 4 + [large, shape_of((8, 128), F32)]
        specs = [ANYWHERE] + [IN_VMEM] * 6
        hands, sems, boxes = scatter_scratch(7, part, count, [BACK_ORDERS[seg] for seg in SHARED])
        tiles = pltpu.VMEM((nz, nx, 8, 128), F32)
        scratch += [vmem(part), tiles, hands, tiles, pltpu.VMEM((8, 128), F32), vmem(vec)]
        scratch += sems + [DMA((10,))] + boxes
        scratch += [pltpu.VMEM(s, F32) for s in inbox_shapes({"z": nz, "x": nx}, "zx", "zx", (8, 128))[0]]
    else:
        outs, specs = [part, raw, vec], [ANYWHERE, ANYWHERE, IN_VMEM]
        outs[1] = shape_of(raw.shape, BF)
    return call(
        functools.partial(attn_back_kernel, shape),
        tuple(outs),
        [IN_VMEM] * 2 + [ANYWHERE] * 10,
        tuple(specs),
        scratch,
        "attn_back",
        2 if shape else None,
    )(vectors, vec_f, g, dw_in, *(kept[name] for name in BACK_IN))


def chip_grid(chips):
    nx = 1
    while (nx * 2) ** 2 <= chips:
        nx *= 2
    return chips // nx, nx


def body(counts_of, tokens, cotangent, domain_ids, domain_counts, *params):
    weights, norms = params[:6], params[6:]
    n_dp, n_mp = counts_of
    micro = tokens.shape[0] // n_mp
    width = tokens.shape[3]
    share = width // n_dp
    y = lax.axis_index("mp")
    linked = n_mp == 2 and share * 2 == TILE
    flip = lambda array: jnp.transpose(array, (0, 2, 1, 3))
    x, cot = flip(tokens), flip(cotangent)
    if linked:
        shape = chip_grid(n_dp // 2) + (n_mp,)
        g, vectors, kept = forward(shape, micro, x, cot, domain_ids, domain_counts, weights, [norm.reshape(1, -1) for norm in norms])
    else:
        shards = jnp.stack(
            weights[:4] + tuple(w[:, i * SEG : (i + 1) * SEG] for w in weights[4:] for i in range(2))
        )
        g = lax.all_gather(lax.all_gather(shards, "dp", axis=1, tiled=True), "mp", axis=1)
        vectors = lax.all_gather(jnp.stack(norms), "dp", axis=1, tiled=True).astype(F32)
        vectors = jnp.pad(vectors, ((0, 4), (0, 0)))
        g, vectors, kept = forward(None, micro, x, cot, domain_ids, domain_counts, None, None, g, vectors)
    shape = shape if linked else None
    results = feed_back(shape, vectors, g, kept)
    dw_f, gres, gm, vec_f = results[:4]
    kept = {**kept, "gres": gres, "gm": gm}
    if linked:
        out, grad_down = results[4:]
        grad_tokens, *grads, vec = attn_back(shape, vectors, vec_f, g, dw_f, kept)
        grads.append(grad_down)
        core = lax.rem(lax.axis_index("dp"), 2)
        vec = lax.dynamic_slice(vec, (0, core * share), (4, share))
    else:
        dw_a, low_tokens, vec_a = attn_back(shape, vectors, vec_f, g, dw_f, kept)
        dw = jnp.concatenate((dw_a, dw_f[4:], dw_f[:4])).astype(F32)
        dw = lax.psum_scatter(lax.psum_scatter(dw, "mp", scatter_dimension=1), "dp", scatter_dimension=1, tiled=True)
        grads = [dw[0], dw[1], dw[2], dw[3]]
        grads += [jnp.concatenate((dw[a], dw[b]), axis=1) for a, b in (UPS, DOWNS)]
        vec = jnp.concatenate((jnp.sum(vec_a, axis=1), jnp.sum(vec_f, axis=1)))
        vec = lax.psum_scatter(lax.psum(vec, "mp"), "dp", scatter_dimension=1, tiled=True)
        out = lax.all_gather(kept["out"], "mp", axis=0, tiled=True)
        grad_tokens = lax.all_gather(low_tokens, "mp", axis=0, tiled=True)
    return (flip(out), flip(grad_tokens.astype(F32)), *grads, vec[0], vec[1], vec[2], vec[3])


def solution(mesh):
    rows, matrix, vector = P(None, "dp", None, None), P("dp", "mp"), P("dp")
    in_specs = (rows, rows, P(None, "dp"), P()) + (matrix,) * 6 + (vector,) * 4
    out_specs = (rows, rows) + (matrix,) * 6 + (vector,) * 4
    run = functools.partial(body, (mesh.shape["dp"], mesh.shape["mp"]))
    return jax.shard_map(run, mesh=mesh, in_specs=in_specs, out_specs=out_specs, check_vma=False)
```

```python
import functools

import jax
import jax.numpy as jnp
from jax import lax
from jax.experimental import pallas as pl
from jax.experimental.pallas import tpu as pltpu
from jax.sharding import PartitionSpec as P

BF = jnp.bfloat16
F32 = jnp.float32
HD = 128
SEG = 512
TILE = 128
PAD = 16
EPS = 1e-05
MESH = pl.DeviceIdType.MESH
VMEM_LIMIT = 62 * 1024 * 1024

Q, K, V, O, U0, U1, D0, D1 = range(8)
UPS = (U0, U1)
DOWNS = (D0, D1)
ORDERS = ("zxy", "zxy", "zyx", "zyx", "zxy", "zyx", "yzx", "zxy", "yxz", "zxy", "zyx", "yxz", "xzy", "zxy", "xyz", "yzx")
BACK_ORDERS = ("yxz", "xzy", "xzy", "zxy", "xzy", "yxz")
FEED_ORDERS = ("xzy", "zxy", "zxy", "xzy")

FORWARD_PLAN = (
    3, 14, 7, 6, 5, 11, -1, 8, 15, 3, 7, 14, 11, 0, 10, 8, 12, 3, 3, 7, 5, 7, 0, 5,
    0, 16, 4, 5, 1, 9, 0, 13, 16, 3, 7, 4, 1, 16, 16, 2, 6, 0, 1, 4, 13, 2, 13, 10,
    1, 9, 4, 2, 15, 9, 16, 12, 6, 2, 1, 5, 7, 8, -1, -1, 3, 12, 2, 10, 6, 15, 4, 11,
    0, 12, 5, 10, 9, 1, 8, 6, 13, -1, 2, 12, 4, 9, 11, -1, 14, -1, 10, -1, 6, 8, 15, -1,
    12, -1, 11, 14, 13, -1, 15, 8, 9, -1, 11, 10, -1, -1, 14, -1, 13, -1, 15, 14, -1, -1, -1,
)
FEED_PLAN = (
    4, -1, 1, -1, 1, 0, -1, 3, 4, 0, 4, 1, 2, -1, 2, 3, -1, 1, -1, 0, 2, -1, 1, 0,
    -1, 3, 1, 4, 2, -1, 3, 1, -1, 0, 2, 3, -1, 0, -1, 2, 3, -1, 0, 2, 3,
)
ATTN_PLAN = (
    0, 1, -1, 1, 0, -1, 2, -1, -1, -1, -1, 3, 2, -1, 4, 3, -1, 2, 4, 0, 5, -1, 7, 0,
    5, 1, 0, 7, 3, 2, 4, -1, 8, -1, 0, 4, 5, 5, 8, 6, 6, 1, 4, 6, 5, 2, 6, 4,
    3, 1, 5, 6, 3, 1, 2, 6, 3, 5, 1, 4, 0, 3, 2,
)
GRADS_FIRST = 1


def nn(a, b):
    return lax.dot_general(a, b, (((1,), (0,)), ((), ())), preferred_element_type=F32)


def nt(a, b):
    return lax.dot_general(a, b, (((1,), (1,)), ((), ())), preferred_element_type=F32)


def flat(value):
    return value.reshape(-1, value.shape[-1])


def norm_stats(values):
    mean = jnp.mean(values, axis=-1, keepdims=True)
    center = values - mean
    inverse = lax.rsqrt(jnp.mean(center * center, axis=-1, keepdims=True) + EPS)
    return center * inverse, inverse


def norm_pull(grad, values, gain):
    normal, inverse = norm_stats(values)
    scaled = grad * gain
    first = jnp.mean(scaled, axis=-1, keepdims=True)
    second = jnp.mean(scaled * normal, axis=-1, keepdims=True)
    return inverse * (scaled - first - normal * second), normal


def fold_rows(values):
    rows, width = values.shape
    return jnp.sum(values.reshape(rows // 8, 8, width), axis=0)


def score_mask():
    key = lax.broadcasted_iota(jnp.int32, (TILE, TILE), 0)
    query = lax.broadcasted_iota(jnp.int32, (TILE, TILE), 1)
    return (query // PAD == key // PAD) & (key <= query)


def row_loop(rows, body, first=0):
    def once(index, carry):
        index = first + index
        body(pl.ds(pl.multiple_of(index * TILE, TILE), TILE), index)
        return carry

    lax.fori_loop(0, rows // TILE, once, 0)


def half_loop(count, body):
    def once(index, carry):
        body(index)
        return carry

    lax.fori_loop(0, count, once, 0)


def half(index):
    return pl.ds(pl.multiple_of(index * SEG, SEG), SEG)


def spread_rows(patches, series):
    row = lax.broadcasted_iota(jnp.int32, (series * PAD, patches * series), 0)
    col = lax.broadcasted_iota(jnp.int32, (series * PAD, patches * series), 1)
    hit = (lax.rem(row, PAD) * series + lax.div(row, PAD) == col) & (lax.rem(row, PAD) < patches)
    return jnp.where(hit, 1.0, 0.0).astype(BF)


def gather_rows(patches, series):
    row = lax.broadcasted_iota(jnp.int32, (patches * series, series * PAD), 0)
    col = lax.broadcasted_iota(jnp.int32, (patches * series, series * PAD), 1)
    return jnp.where(lax.rem(row, series) * PAD + lax.div(row, series) == col, 1.0, 0.0).astype(BF)


def to_rows(raw, target):
    micro, patches, series, _ = raw.shape
    matrix = spread_rows(patches, series)
    for part in range(micro):
        target[part * series * PAD : (part + 1) * series * PAD, :] = nn(matrix, flat(raw[part])).astype(BF)


def from_rows(source, raw):
    micro, patches, series, width = raw.shape
    matrix = gather_rows(patches, series)
    for part in range(micro):
        rows = source[part * series * PAD : (part + 1) * series * PAD, :]
        raw[part] = nn(matrix, rows).astype(raw.dtype).reshape(patches, series, width)


def norm_in(x, normed, gain, shift):
    def block(rows, _):
        normal, _inv = norm_stats(x[rows, :].astype(F32))
        normed[rows, :] = (normal * gain + shift).astype(BF)

    row_loop(x.shape[0], block)


def project(source, weights, seg, target):
    def one(m):
        target[:, half(m)] = nn(source[...], flat(weights[seg, m])).astype(BF)

    half_loop(weights.shape[1], one)


def attend(queries, keys, values, probs, mixture, first, count):
    mask = score_mask()
    scale = HD ** (-0.5)
    columns = [slice(at, at + HD) for at in range(0, queries.shape[1], HD)]

    def group(rows, _):
        scores = [nt(keys[rows, cols], queries[rows, cols]) * scale for cols in columns]
        scores = [jnp.where(mask, score, -1e30) for score in scores]
        peaks = [jnp.max(score, axis=0, keepdims=True) for score in scores]
        powers = [jnp.exp(score - peak) for score, peak in zip(scores, peaks)]
        inverses = [1.0 / jnp.sum(power, axis=0, keepdims=True) for power in powers]
        shares = [power * inverse for power, inverse in zip(powers, inverses)]
        for cols, share in zip(columns, shares):
            probs[rows, cols] = share
        mixed = [nn(share.astype(BF).T, values[rows, cols]) for share, cols in zip(shares, columns)]
        for cols, part in zip(columns, mixed):
            mixture[rows, cols] = part.astype(BF)

    row_loop(count * TILE, group, first)


def attend_back(queries, keys, values, probs, grad_mix, grad_q, grad_k, grad_v, first, count):
    scale = HD ** (-0.5)
    columns = [slice(at, at + HD) for at in range(0, queries.shape[1], HD)]

    def group(rows, _):
        shares = [probs[rows, cols] for cols in columns]
        grads = [grad_mix[rows, cols] for cols in columns]
        pulls = [nt(values[rows, cols], grad) for cols, grad in zip(columns, grads)]
        back_v = [nn(share.astype(BF), grad) for share, grad in zip(shares, grads)]
        inner = [jnp.sum(pull * share, axis=0, keepdims=True) for pull, share in zip(pulls, shares)]
        lows = [(share * (pull - mean)).astype(BF) for share, pull, mean in zip(shares, pulls, inner)]
        back_k = [nn(low, queries[rows, cols]) * scale for low, cols in zip(lows, columns)]
        back_q = [nn(low.T, keys[rows, cols]) * scale for low, cols in zip(lows, columns)]
        for cols, one, two, three in zip(columns, back_q, back_k, back_v):
            grad_q[rows, cols] = one.astype(BF)
            grad_k[rows, cols] = two.astype(BF)
            grad_v[rows, cols] = three.astype(BF)

    row_loop(count * TILE, group, first)


def back_through(source, weights, seg, total):
    def one(m):
        total[...] += nt(source(m), flat(weights[seg, m]))

    half_loop(weights.shape[1], one)


def feed_up(normed_two, weights, which, m, active, slope):
    hidden = nn(normed_two[...], flat(weights[UPS[which], m]))
    bell = 0.5 + 0.5 * lax.erf(hidden * (0.5**0.5))
    active[which, m] = (hidden * bell).astype(BF)
    density = jnp.exp(-0.5 * hidden * hidden) * 0.3989422804014327
    slope[which, m] = bell + hidden * density


def turn(source, target):
    def block(rows, _):
        target[:, rows] = source[rows, :].T

    row_loop(source.shape[0], block)


def weight_grad(turned, right, target, seg):
    def one(m):
        product = nn(turned[...], right(m)).astype(BF)
        target[seg, m] = product.reshape(target.shape[2:])

    half_loop(target.shape[1], one)


class Place:
    def __init__(self, shape):
        self.nz, self.nx, self.ny = shape
        index = lax.axis_index("dp")
        self.core = lax.rem(index, 2)
        chip = lax.div(index, 2)
        self.at = {"z": lax.div(chip, self.nx), "x": lax.rem(chip, self.nx), "y": lax.axis_index("mp")}
        self.count = {"z": self.nz, "x": self.nx, "y": self.ny}

    def device(self, core=None, **moved):
        at = {**self.at, **moved}
        core = self.core if core is None else core
        return ((at["z"] * self.nx + at["x"]) * 2 + core, at["y"])

    def partner(self):
        return self.device(core=1 - self.core)

    def neighbour(self, dim, step):
        return self.device(**{dim: self.at[dim] + step})

    def barrier(self, dims):
        semaphore = pltpu.get_barrier_semaphore()
        pl.semaphore_signal(semaphore, inc=1, device_id=self.partner(), device_id_type=MESH)
        peers = 1
        for dim in dims:
            for step in (1, -1):
                there = self.at[dim] + step
                valid = (there >= 0) & (there < self.count[dim])
                peers = peers + valid.astype(jnp.int32)

                @pl.when(valid)
                def _(dim=dim, step=step):
                    other = self.neighbour(dim, step)
                    pl.semaphore_signal(semaphore, inc=1, device_id=other, device_id_type=MESH)

        pl.semaphore_wait(semaphore, peers)


def link_slots(count, dims):
    return sum(2 * (count[dim] - 1) for dim in dims)


class Gather:
    def __init__(self, place, buffer, axes, order, sems):
        self.place, self.buffer, self.axes, self.order = place, buffer, axes, order
        self.send, self.recv, self.pass_send, self.pass_recv = sems
        self.rounds = [(dim, t) for dim in order for t in range(place.count[dim] - 1)]
        self.slots = {}
        for dim, t in self.rounds:
            for way in (1, -1):
                self.slots[dim, t, way] = len(self.slots)

    def block(self, dim, position, core):
        done = self.order[: self.order.index(dim)] if dim else ""
        index = []
        for axis in self.axes:
            if axis == dim:
                index.append(position)
            elif axis in done:
                index.append(pl.ds(0, self.place.count[axis]))
            else:
                index.append(self.place.at[axis])
        return self.buffer.at[tuple(index) + (core,)]

    def link(self, dim, t, way, position, device):
        block = self.block(dim, position, self.place.core)
        slot = self.slots[dim, t, way]
        return pltpu.make_async_remote_copy(
            block, block, self.send.at[slot], self.recv.at[slot], device_id=device, device_id_type=MESH
        )

    def hand(self, slot, dim, position, core):
        block = self.block(dim, position, core)
        return pltpu.make_async_remote_copy(
            block,
            block,
            self.pass_send.at[slot],
            self.pass_recv.at[slot],
            device_id=self.place.partner(),
            device_id_type=MESH,
        )

    def sends(self, dim, t):
        here, count = self.place.at[dim], self.place.count[dim]
        yield 1, here - t, (here - t >= 0) & (here < count - 1)
        yield -1, here + t, (here + t < count) & (here > 0)

    def arrivals(self, dim, t):
        here, count = self.place.at[dim], self.place.count[dim]
        yield 1, here - 1 - t, here - 1 - t >= 0
        yield -1, here + 1 + t, here + 1 + t < count

    def start(self):
        self.hand(len(self.slots), "", None, self.place.core).start()
        self.send_round(0)

    def send_round(self, number):
        dim, t = self.rounds[number]
        for way, position, valid in self.sends(dim, t):

            @pl.when(valid)
            def _(way=way, position=position):
                self.link(dim, t, way, position, self.place.neighbour(dim, way)).start()

    def advance(self, number):
        dim, t = self.rounds[number - 1]
        for way, position, valid in self.arrivals(dim, t):

            @pl.when(valid)
            def _(way=way, position=position):
                self.link(dim, t, way, position, self.place.partner()).wait_recv()
                self.hand(self.slots[dim, t, way], dim, position, self.place.core).start()

        if number < len(self.rounds):
            self.send_round(number)

    def steps(self):
        return [self.start] + [functools.partial(self.advance, n + 1) for n in range(len(self.rounds))]

    def finish(self):
        other = 1 - self.place.core
        self.hand(len(self.slots), "", None, other).wait_recv()
        for dim, t in self.rounds:
            for way, position, valid in self.arrivals(dim, t):

                @pl.when(valid)
                def _(dim=dim, t=t, way=way, position=position):
                    self.hand(self.slots[dim, t, way], dim, position, other).wait_recv()

    def drain(self):
        self.hand(len(self.slots), "", None, self.place.core).wait_send()
        for dim, t in self.rounds:
            for way, position, valid in self.sends(dim, t):

                @pl.when(valid)
                def _(dim=dim, t=t, way=way, position=position):
                    self.link(dim, t, way, position, self.place.partner()).wait_send()

            for way, position, valid in self.arrivals(dim, t):

                @pl.when(valid)
                def _(dim=dim, t=t, way=way, position=position):
                    self.hand(self.slots[dim, t, way], dim, position, self.place.core).wait_send()


class Scatter:
    def __init__(self, place, mine, axes, order, inbox, hand_box, sems, both=False):
        self.place, self.mine, self.axes, self.order, self.both = place, mine, axes, order, both
        self.inbox, self.hand_box = inbox, hand_box
        self.send, self.recv = sems
        self.rounds = [(dim, t) for dim in order for t in range(place.count[dim] - 1)]
        self.slots = {}
        for dim, t in self.rounds:
            for way in (1, -1):
                self.slots[dim, t, way] = len(self.slots) + 1

    def own(self, index):
        return index + ((() if self.both else (self.place.core,)))

    def hand(self):
        whole = tuple(pl.ds(0, self.place.count[axis]) for axis in self.axes)
        source = self.mine.at[whole] if self.both else self.mine.at[whole + (1 - self.place.core,)]
        return pltpu.make_async_remote_copy(
            source, self.hand_box, self.send.at[0], self.recv.at[0], device_id=self.place.partner(), device_id_type=MESH
        )

    def start(self):
        self.hand().start()

    def take_hand(self):
        self.hand().wait_recv()
        first = self.place.count[self.axes[0]]
        rest = tuple(pl.ds(0, self.place.count[axis]) for axis in self.axes[1:])
        if self.both:
            self.hand().wait_send()
            self.mine[...] = self.mine[...] + self.hand_box[...]
        else:
            for p in range(first):
                for r in range(self.place.count[self.axes[1]]):
                    index = (p, r) + rest[1:]
                    here = self.mine[index + (self.place.core,)].astype(F32)
                    there = self.hand_box[index].astype(F32)
                    self.mine[index + (self.place.core,)] = (here + there).astype(self.mine.dtype)
        self.send_round(0)

    def block(self, dim, position):
        done = self.order[: self.order.index(dim)]
        index = []
        for axis in self.axes:
            if axis == dim:
                index.append(position)
            elif axis in done:
                index.append(self.place.at[axis])
            else:
                index.append(pl.ds(0, self.place.count[axis]))
        return self.own(tuple(index))

    def link(self, dim, t, way, position, device):
        slot = self.slots[dim, t, way]
        return pltpu.make_async_remote_copy(
            self.mine.at[self.block(dim, position)],
            self.inbox[slot],
            self.send.at[slot],
            self.recv.at[slot],
            device_id=device,
            device_id_type=MESH,
        )

    def sends(self, dim, t):
        here, count = self.place.at[dim], self.place.count[dim]
        yield 1, count - 1 - t + here, (t >= here) & (here < count - 1)
        back = count - 1 - here
        yield -1, t - back, (t >= back) & (here > 0)

    def arrivals(self, dim, t):
        here, count = self.place.at[dim], self.place.count[dim]
        yield 1, count - 2 - t + here, (t >= here - 1) & (here > 0)
        back = count - 1 - here
        yield -1, t + 1 - back, (t >= back - 1) & (here < count - 1)

    def send_round(self, number):
        dim, t = self.rounds[number]
        for way, position, valid in self.sends(dim, t):

            @pl.when(valid)
            def _(way=way, position=position):
                self.link(dim, t, way, position, self.place.neighbour(dim, way)).start()

    def advance(self, number):
        dim, t = self.rounds[number - 1]
        for way, position, valid in self.arrivals(dim, t):

            @pl.when(valid)
            def _(way=way, position=position):
                self.link(dim, t, way, position, self.place.partner()).wait_recv()
                index = self.block(dim, position)
                total = self.mine[index].astype(F32) + self.inbox[self.slots[dim, t, way]][...].astype(F32)
                self.mine[index] = total.astype(self.mine.dtype)

        if number < len(self.rounds):
            self.send_round(number)

    def steps(self):
        later = [functools.partial(self.advance, n + 1) for n in range(len(self.rounds))]
        return [self.start, self.take_hand] + later

    def result(self):
        return self.mine[self.own(tuple(self.place.at[axis] for axis in self.axes))]

    def drain(self):
        if not self.both:
            self.hand().wait_send()
        for dim, t in self.rounds:
            for way, position, valid in self.sends(dim, t):

                @pl.when(valid)
                def _(dim=dim, t=t, way=way, position=position):
                    self.link(dim, t, way, position, self.place.partner()).wait_send()


def inbox_shapes(count, axes, order, block):
    shapes, slots, left = [], {}, dict(count)
    for dim in order:
        left.pop(dim)
        for t in range(count[dim] - 1):
            for way in (1, -1):
                if way == 1 or count[dim] > 2:
                    shapes.append(tuple(count[axis] for axis in axes if axis in left) + block)
                slots[dim, t, way] = len(shapes) - 1
    return shapes, slots


def open_inbox(run, count, axes, order, block, boxes):
    shapes, slots = inbox_shapes(count, axes, order, block)
    for key, slot in run.slots.items():
        run.inbox[slot] = boxes[slots[key]]
    del boxes[: len(shapes)]


def play(plan, comm, pieces):
    plan = list(plan)
    while plan:
        token = plan.pop(0)
        if token >= 0:
            if comm:
                comm[token].pop(0)()
        elif callable(pieces[0]):
            pieces.pop(0)()
        else:
            count, piece, before, after = pieces.pop(0)
            if before:
                before()
            between = [[] for _ in range(count - 1)]
            for spot in range(count - 1):
                while plan[0] >= 0:
                    token = plan.pop(0)
                    if comm:
                        between[spot].append(comm[token].pop(0))
                plan.pop(0)

            def once(index, carry, piece=piece, between=between):
                piece(index)
                for spot, steps in enumerate(between):
                    if steps:

                        @pl.when(index == spot)
                        def _(steps=steps):
                            for step in steps:
                                step()

                return carry

            lax.fori_loop(0, count, once, 0)
            if after:
                after()
    assert not pieces and not any(comm.values())


class Mover:
    def __init__(self, sems):
        self.sems, self.used, self.open = sems, 0, []

    def start(self, source, target):
        copy = pltpu.make_async_copy(source, target, self.sems.at[self.used])
        self.used += 1
        copy.start()
        return copy

    def save(self, source, target):
        self.open.append(self.start(source, target))

    def close(self):
        for copy in self.open:
            copy.wait()


def read_vectors(vectors, tiles):
    nz, nx = tiles.shape[:2]
    pieces = [tiles[z, x, 0] + tiles[z, x, 1] for z in range(nz) for x in range(nx)]
    vectors[...] = jnp.concatenate(pieces, axis=1)


def column_parts(weights):
    wq, wk, wv, wo, wu, wd = weights
    left, right = pl.ds(0, SEG), pl.ds(SEG, SEG)
    return [wq, wk, wv, wo, wu.at[:, left], wu.at[:, right], wd.at[:, left], wd.at[:, right]]


def fill_tile(place, tiles, norms):
    tile = (place.at["z"], place.at["x"], place.core)
    tiles[tile] = jnp.zeros(tiles.shape[3:], F32)
    share = norms[0].shape[1]
    for line, norm in enumerate(norms):
        value = norm[...].astype(F32)
        for core in range(2):

            @pl.when(place.core == core)
            def _(line=line, value=value, core=core):
                tiles[tile + (slice(line, line + 1), slice(core * share, (core + 1) * share))] = value


FWD_OUT = (
    "x", "q", "k", "v", "probs", "mix", "res", "nrm2", "active", "slope", "out", "cot", "gl", "glt", "weight",
    "nrmt",
)
KEPT = len(FWD_OUT)


def forward_kernel(shape, micro, tokens, cotangent, ids, counts, *refs):
    if shape:
        weights, norms, g_out, refs = refs[:6], refs[6:10], refs[10], refs[11:]
    else:
        g_in, vectors_in, refs = refs[0], refs[1], refs[2:]
    if shape:
        vectors, refs = refs[0], refs[1:]
    else:
        vectors = vectors_in
    saved = dict(zip(FWD_OUT, refs[:KEPT]))
    here = dict(zip(FWD_OUT, refs[KEPT : 2 * KEPT]))
    refs = refs[2 * KEPT :]
    raw, nrm, low, total, g, sems = refs[:6]
    mover = Mover(sems)
    y = lax.axis_index("mp")
    take = mover.start(tokens.at[pl.ds(y * micro, micro)], raw)
    x, q, k, v, probs, mix, res, nrm2, active, slope, out, cot, gl, glt, weight, nrmt = (
        here[name] for name in FWD_OUT
    )

    def keep(*names):
        for name in names:
            mover.save(here[name], saved[name])

    comm = {}
    if shape:
        tiles, send, recv, pass_send, pass_recv = refs[6:]
        place = Place(shape)
        spot = (place.at["y"], place.at["z"], place.at["x"], place.core)
        mine = [mover.start(part, g.at[(seg,) + spot]) for seg, part in enumerate(column_parts(weights))]
        fill_tile(place, tiles, norms)
        place.barrier("zxy")
        pick = lambda seg: tuple(sem.at[seg] for sem in (send, recv, pass_send, pass_recv))
        runs, cut = [], len(ORDERS) // 8
        for spot, order in enumerate(ORDERS):
            columns = pl.ds(spot % cut * (SEG // cut), SEG // cut)
            runs.append(Gather(place, g.at[spot // cut, :, :, :, :, :, columns], "yzx", order, pick(spot)))
        runs.append(Gather(place, tiles, "zx", "zx", pick(len(ORDERS))))
        comm = {spot: run.steps() for spot, run in enumerate(runs)}
        waiting = list(mine)

        def begin(spot):
            if waiting[spot // cut] is not None:
                waiting[spot // cut].wait()
                waiting[spot // cut] = None
            runs[spot].start()

        for spot in range(len(ORDERS)):
            comm[spot][0] = functools.partial(begin, spot)

        def have(seg):
            if seg < 8:
                for run in runs[seg * cut : (seg + 1) * cut]:
                    run.finish()
                mover.save(g.at[seg], g_out.at[seg])
            else:
                runs[-1].finish()
                read_vectors(vectors, tiles)

    else:
        loads = [mover.start(g_in.at[seg], g.at[seg]) for seg in range(8)]

        def have(seg):
            if seg < 8:
                loads[seg].wait()

    def spread():
        take.wait()
        to_rows(raw, x)
        keep("x")
        loads_cot.append(mover.start(cotangent.at[pl.ds(y * micro, micro)], raw))
        row_weights(ids, counts, y, micro, weight)

    loads_cot = []

    def weigh():
        loads_cot[0].wait()
        to_rows(raw, cot)

        def block(rows, _):
            gl[rows, :] = (cot[rows, :].astype(F32) * weight[rows, :]).astype(BF)

        row_loop(cot.shape[0], block)
        turn(gl, glt)
        keep("cot", "gl", "glt", "weight")

    def norm_one():
        have(8)
        norm_in(x, nrm, vectors[0:1, :], vectors[1:2, :])
        turn(nrm, nrmt)
        keep("nrmt")

    def head_part(seg, target, name):
        have(seg)
        project(nrm, g, seg, target)
        keep(name)

    third = x.shape[0] // TILE // 3

    def mixing(part):
        attend(q, k, v, probs, mix, part * third, third)

    def project_out():
        keep("probs", "mix")
        have(O)
        res[...] = x[...].astype(F32)
        back_through(lambda m: mix[:, half(m)], g, O, res)
        keep("res")

    def norm_two():
        gain, shift = vectors[2:3, :], vectors[3:4, :]

        def block(rows, _):
            normal, _inv = norm_stats(res[rows, :])
            nrm2[rows, :] = (normal * gain + shift).astype(BF)

        row_loop(x.shape[0], block)
        keep("nrm2")

    def up(which, m):
        feed_up(nrm2, g, which, m, active, slope)

    def keep_up(which):
        mover.save(active.at[which], saved["active"].at[which])
        mover.save(slope.at[which], saved["slope"].at[which])

    def down(which):
        have(DOWNS[which])
        if which == 0:
            total[...] = res[...]
        back_through(lambda m: active[which, m], g, DOWNS[which], total)

    def last():
        low[...] = total[...].astype(BF)
        from_rows(low, out)
        keep("out")

    pieces = [spread, weigh, norm_one]
    pieces += [functools.partial(head_part, *args) for args in ((Q, q, "q"), (K, k, "k"), (V, v, "v"))]
    pieces += [(3, mixing, None, None), project_out, norm_two]
    for which in range(2):
        before, after = functools.partial(have, UPS[which]), functools.partial(keep_up, which)
        pieces.append((2, functools.partial(up, which), before, after))
    pieces += [functools.partial(down, which) for which in range(2)] + [last]
    play(FORWARD_PLAN, comm, pieces)
    if shape:
        for run in runs:
            run.drain()
    mover.close()


def row_weights(ids, counts, y, micro, target):
    series = ids.shape[1]
    sums = counts[0]
    for kind in range(1, counts.shape[0]):
        sums = sums + counts[kind]
    mean = jnp.full((PAD, 1), sums.astype(F32), F32) / counts.shape[0]

    def one(index, carry):
        kind = ids[y * micro + lax.div(index, series), lax.rem(index, series)]
        count = counts[kind].astype(F32)
        target[pl.ds(pl.multiple_of(index * PAD, PAD), PAD), :] = 2.0 * mean / (mean + count)
        return carry

    lax.fori_loop(0, micro * series, one, 0)


class Swap:
    def __init__(self, place, mover, sems, ready, source, target):
        self.mover, self.source, self.ready = mover, source, ready
        y, (micro, patches) = place.at["y"], source.shape[:2]
        cut = patches // 2 + 1
        self.spots = [target.at[y * micro + part] for part in range(micro)]
        self.copies = []
        for part in range(micro):
            for piece in (pl.ds(0, cut), pl.ds(cut, patches - cut)):
                slot = 2 * len(self.copies)
                self.copies.append(
                    pltpu.make_async_remote_copy(
                        source.at[part, piece],
                        target.at[y * micro + part, piece],
                        sems.at[slot],
                        sems.at[slot + 1],
                        device_id=place.device(y=1 - y),
                        device_id_type=MESH,
                    )
                )

    def start(self, part):
        if part == 0:
            self.ready()
        self.copies[2 * part].start()
        self.mover.save(self.source.at[part], self.spots[part])

    def steps(self, part):
        return [functools.partial(self.start, part), self.copies[2 * part + 1].start]

    def wait(self):
        for copy in self.copies:
            copy.wait()


def feed_back_kernel(shape, vectors, g_in, active_in, slope_in, nrm2_in, res_in, out_in, cot_in, gl_in, glt_in, weight_in, mix_in, *refs):
    if shape:
        dw_out, gres_out, gm_out, vec, pair, grad_down, refs = refs[:6] + (refs[6:],)
    else:
        dw_out, gres_out, gm_out, vec, refs = refs[:4] + (refs[4:],)
    cot, weight, active, slope, nrm2, res, g, dw, gl, glt, gh, n2t, gn2, gres, mix, gm, sems = refs[:17]
    mover = Mover(sems)
    if shape:
        half_out, hands, send, recv, ysem = refs[17:22]
        boxes = list(refs[22:])
        side = mover.start(out_in, half_out)
    loads = {"glt": mover.start(glt_in, glt), ("active", 0): mover.start(active_in.at[0], active.at[0])}
    loads["gl"] = mover.start(gl_in, gl)
    for which in range(2):
        if which == 1:
            loads["active", which] = mover.start(active_in.at[which], active.at[which])
        loads["d", which] = mover.start(g_in.at[DOWNS[which]], g.at[2 + which])
        loads["slope", which] = mover.start(slope_in.at[which], slope.at[which])
    loads["nrm2"] = mover.start(nrm2_in, nrm2)
    for which in range(2):
        loads["u", which] = mover.start(g_in.at[UPS[which]], g.at[which])
    loads["res"] = mover.start(res_in, res)
    loads["cot"] = mover.start(cot_in, cot)
    loads["mix"] = mover.start(mix_in, mix)
    loads["o"] = mover.start(g_in.at[O], g.at[4])
    loads["weight"] = mover.start(weight_in, weight)
    comm = {}
    if shape:
        place = Place(shape)
        place.barrier("zxy")
        runs = []
        block = (dw.shape[-2], SEG // 2)
        for spot, order in enumerate(FEED_ORDERS):
            columns = pl.ds(spot % 2 * block[1], block[1])
            source = dw.at[2 + spot // 2, :, :, :, :, :, columns]
            run = Scatter(place, source, "yzx", order, {}, hands.at[spot], (send.at[spot], recv.at[spot]))
            open_inbox(run, place.count, "yzx", order, block, boxes)
            runs.append(run)
        swap = Swap(place, mover, ysem, side.wait, half_out, pair)
        comm = {spot: run.steps() for spot, run in enumerate(runs)}
        comm[len(runs)] = swap.steps(0) + swap.steps(1)

    def down_grad(which):
        if which == 0:
            loads["glt"].wait()
        loads["active", which].wait()
        weight_grad(glt, lambda m: active[which, m], dw, 2 + which)
        if not shape:
            mover.save(dw.at[2 + which], dw_out.at[2 + which])

    def hidden_grad(which):
        if which == 0:
            loads["gl"].wait()
        loads["d", which].wait()
        loads["slope", which].wait()

        def one(m):
            pulled = nn(gl[...], flat(g[2 + which, m]))
            gh[which, m] = (pulled * slope[which, m]).astype(BF)

        half_loop(g.shape[1], one)

    def turn_two():
        loads["nrm2"].wait()
        turn(nrm2, n2t)
        gn2[...] = jnp.zeros_like(gn2)

    def up_grad(which):
        weight_grad(n2t, lambda m: gh[which, m], dw, which)
        mover.save(dw.at[which], dw_out.at[which])

    def norm_grad(which):
        loads["u", which].wait()
        back_through(lambda m: gh[which, m], g, which, gn2)

    def last():
        for name in ("res", "cot", "weight"):
            loads[name].wait()
        gain = vectors[2:3, :]
        vec[...] = jnp.zeros_like(vec)

        def block(rows, _):
            grad = gn2[rows, :]
            pulled, normal = norm_pull(grad, res[rows, :], gain)
            vec[0] += fold_rows(grad * normal)
            vec[1] += fold_rows(grad)
            total = cot[rows, :].astype(F32) * weight[rows, :] + pulled
            gres[rows, :] = total
            gl[rows, :] = total.astype(BF)

        row_loop(cot.shape[0], block)
        mover.save(gres, gres_out)

    def mix_grad():
        loads["o"].wait()
        project(gl, g, 4, gm)
        mover.save(gm, gm_out)

    def out_grad():
        loads["mix"].wait()
        weight_grad(glt, lambda m: mix[:, half(m)], dw, 4)
        mover.save(dw.at[4], dw_out.at[4])

    pieces = []
    for which in range(2):
        pieces += [functools.partial(down_grad, which), functools.partial(hidden_grad, which)]
    pieces.append(turn_two)
    for which in range(2):
        pieces += [functools.partial(up_grad, which), functools.partial(norm_grad, which)]
    pieces += [last, mix_grad, lambda: turn(gl, glt), out_grad]
    play(FEED_PLAN, comm, pieces)
    if shape:
        for spot, run in enumerate(runs):
            grad_down[:, spot * block[1] : (spot + 1) * block[1]] = run.result().astype(F32)
            run.drain()
        swap.wait()
    mover.close()


def vector_tiles(tiles, vec_a, vec_f):
    tiles[...] = jnp.zeros_like(tiles)
    nz, nx = tiles.shape[:2]
    for line, (source, part) in enumerate(((vec_a, 0), (vec_a, 1), (vec_f, 0), (vec_f, 1))):
        row = jnp.sum(source[part], axis=0, keepdims=True)
        for z in range(nz):
            for x in range(nx):
                chip = z * nx + x
                tiles[z, x, line : line + 1, :] = row[:, chip * 128 : (chip + 1) * 128]


BACK_IN = ("gm", "q", "k", "v", "probs", "nrmt", "gres", "x")
SHARED = (U0, U1, O, Q, K, V)
KEPT_GRADS = (0, 1, 4)


def attn_back_kernel(shape, vectors, vec_f, g_in, dw_in, *refs):
    given = dict(zip(BACK_IN, refs[:8]))
    refs = refs[8:]
    if shape:
        pair, grads, vec_out, refs = refs[0], refs[1:6], refs[6], refs[7:]
    else:
        dw_out, out, vec, refs = refs[0], refs[1], refs[2], refs[3:]
    here = dict(zip(BACK_IN, refs[:8]))
    g, dw, gal, pulls, raw, sems = refs[8:14]
    mover = Mover(sems)
    loads, comm = {}, {}
    if shape:
        held, tiles, hands, vec_hand, ybox, vec, send, recv, ysem = refs[14:23]
        boxes = list(refs[23:])

    def fetch_held(*spots):
        for spot in spots:
            if shape:
                loads["dw", spot] = mover.start(dw_in.at[KEPT_GRADS[spot]], held.at[spot])

    fetch_held(0)
    for name in BACK_IN[:5]:
        loads[name] = mover.start(given[name], here[name])
    fetch_held(1, 2)
    for name in BACK_IN[5:]:
        loads[name] = mover.start(given[name], here[name])
    for seg in (Q, K, V):
        loads[seg] = mover.start(g_in.at[seg], g.at[seg])
    gm, q, k, v, probs, nrmt, gres, x = (here[name] for name in BACK_IN)
    gn = probs
    if shape:
        place = Place(shape)
        place.barrier("zxy")
        runs = []
        for spot, seg in enumerate(SHARED):
            source = held.at[spot] if spot < 3 else dw.at[seg]
            order = BACK_ORDERS[seg]
            run = Scatter(place, source, "yzx", order, {}, hands.at[spot], (send.at[spot], recv.at[spot]))
            open_inbox(run, place.count, "yzx", order, dw.shape[-2:], boxes)
            runs.append(run)
        run = Scatter(place, tiles, "zx", "zx", {}, vec_hand, (send.at[6], recv.at[6]), both=True)
        open_inbox(run, {"z": place.nz, "x": place.nx}, "zx", "zx", (8, 128), boxes)
        runs.append(run)
        swap = Swap(place, mover, ysem, lambda: None, raw, pair)
        comm = {spot: run.steps() for spot, run in enumerate(runs)}
        comm[7], comm[8] = swap.steps(0), swap.steps(1)
        for spot in range(3):
            comm[spot][0] = lambda spot=spot: (loads["dw", spot].wait(), runs[spot].start())

    third = gal.shape[0] // TILE // 3
    micro = raw.shape[0]
    share = gal.shape[0] // micro

    def ready():
        for name in BACK_IN[:5]:
            loads[name].wait()
        vec[...] = jnp.zeros_like(vec)

    def mixing(part):
        attend_back(q, k, v, probs, gm, pulls.at[0], pulls.at[1], pulls.at[2], part * third, third)

    def head_grad(seg):
        weight_grad(nrmt, lambda m: pulls[seg, :, half(m)], dw, seg)

    def token_grad(part):
        rows_of = pl.ds(part * share, share)
        gn[rows_of, :] = jnp.zeros((share, gn.shape[1]), F32)
        if part == 0:
            for name in (Q, K, V, "gres", "x"):
                loads[name].wait()

        def one(index, carry):
            seg, m = lax.div(index, 2), lax.rem(index, 2)
            gn[rows_of, :] += nt(pulls[seg, rows_of, half(m)], flat(g[seg, m]))
            return carry

        lax.fori_loop(0, 6, one, 0)
        gain = vectors[0:1, :]

        def block(rows, _):
            grad = gn[rows, :]
            pulled, normal = norm_pull(grad, x[rows, :].astype(F32), gain)
            vec[0] += fold_rows(grad * normal)
            vec[1] += fold_rows(grad)
            gal[rows, :] = (gres[rows, :] + pulled).astype(BF)

        row_loop(share, block, part * share // TILE)
        patches, series, width = raw.shape[1:]
        turned = nn(gather_rows(patches, series), gal[rows_of, :]).astype(raw.dtype)
        raw[part] = turned.reshape(patches, series, width)

    def spread_vectors():
        if shape:
            vector_tiles(tiles, vec, vec_f)

    def before_heads():
        loads["nrmt"].wait()

    pieces = [ready, (3, mixing, None, None), before_heads]
    parts = [functools.partial(token_grad, part) for part in range(micro)]
    heads = [(3, head_grad, None, None)]
    pieces += heads + parts if GRADS_FIRST else parts + heads
    pieces.insert(len(pieces) - (0 if GRADS_FIRST else 1), spread_vectors)
    play(ATTN_PLAN, comm, pieces)
    if not shape:
        mover.save(raw, out)
        for seg in (Q, K, V):
            mover.save(dw.at[seg], dw_out.at[seg])
    if shape:
        here_tile = tiles.at[place.at["z"], place.at["x"]]
        copy = pltpu.make_async_remote_copy(
            here_tile, ybox, ysem.at[8], ysem.at[9], device_id=place.device(y=1 - place.at["y"]), device_id_type=MESH
        )
        copy.start()
        for spot, seg in enumerate(SHARED[2:]):
            grads[(3, 0, 1, 2)[spot]][...] = runs[2 + spot].result().astype(F32)
        for which in range(2):
            grads[4][:, which * SEG : (which + 1) * SEG] = runs[which].result().astype(F32)
        for run in runs:
            run.drain()
        copy.wait()
        vec_out[...] = tiles[place.at["z"], place.at["x"]] + ybox[...]
        swap.wait()
    mover.close()


def finish_kernel(low, *refs):
    grads, tokens, outs = refs[:6], refs[6], refs[7:]
    tokens[...] = low[...].astype(F32)

    @pl.when((pl.program_id(0) == 0) & (pl.program_id(1) == 0))
    def _():
        for grad, out in zip(grads, outs):
            out[...] = grad[...]


def shape_of(shape, dtype):
    return jax.ShapeDtypeStruct(shape, dtype)


IN_VMEM = pl.BlockSpec(memory_space=pltpu.VMEM)
IN_SMEM = pl.BlockSpec(memory_space=pltpu.SMEM)
ANYWHERE = pl.BlockSpec(memory_space=pl.ANY)
DMA = pltpu.SemaphoreType.DMA


def call(body, outs, ins, out_specs, scratch, name, collective=None):
    params = {"vmem_limit_bytes": VMEM_LIMIT}
    if collective is not None:
        params.update(collective_id=collective, has_side_effects=True)
    return pl.pallas_call(
        body,
        out_shape=outs,
        in_specs=ins,
        out_specs=out_specs,
        scratch_shapes=scratch,
        compiler_params=pltpu.CompilerParams(**params),
        name=name,
    )


def vmem(like):
    return pltpu.VMEM(like.shape, like.dtype)


def forward(shape, micro, tokens, cotangent, ids, counts, weights, norms, g_in=None, vectors_in=None):
    _, patches, series, width = tokens.shape
    rows = micro * series * PAD
    full = g_in.shape if shape is None else (8, shape[2], shape[0], shape[1], 2, weights[0].shape[0], SEG)
    low, high = shape_of((rows, width), BF), shape_of((rows, width), F32)
    wide = (2, full[1], rows, SEG)
    raw = shape_of((micro, patches, series, width), BF)
    kinds = {name: low for name in FWD_OUT}
    kinds.update(
        probs=high,
        res=high,
        active=shape_of(wide, BF),
        slope=shape_of(wide, F32),
        out=raw,
        glt=shape_of((width, rows), BF),
        nrmt=shape_of((width, rows), BF),
        weight=shape_of((rows, 1), F32),
    )
    saved = tuple(kinds[name] for name in FWD_OUT)
    scratch = [vmem(kind) for kind in saved] + [vmem(raw), vmem(low), vmem(low), vmem(high), pltpu.VMEM(full, BF), DMA((64,))]
    if shape is None:
        results = call(
            functools.partial(forward_kernel, None, micro),
            saved,
            [ANYWHERE, ANYWHERE, IN_SMEM, IN_SMEM, ANYWHERE, IN_VMEM],
            (ANYWHERE,) * KEPT,
            scratch,
            "forward",
        )(tokens, cotangent, ids, counts, g_in, vectors_in)
        return g_in, vectors_in, dict(zip(FWD_OUT, results))
    count = dict(zip("zxy", shape))
    slots = link_slots(count, "zxy")
    scratch += [pltpu.VMEM(shape[:2] + (2, 8, 128), F32)]
    runs = len(ORDERS) + 1
    scratch += [DMA((runs, slots)), DMA((runs, slots)), DMA((runs, slots + 1)), DMA((runs, slots + 1))]
    results = call(
        functools.partial(forward_kernel, shape, micro),
        (shape_of(full, BF), shape_of((8, width), F32)) + saved,
        [ANYWHERE, ANYWHERE, IN_SMEM, IN_SMEM] + [ANYWHERE] * 6 + [IN_VMEM] * 4,
        (ANYWHERE, IN_VMEM) + (ANYWHERE,) * KEPT,
        scratch,
        "forward",
        0,
    )(tokens, cotangent, ids, counts, *weights, *norms)
    return results[0], results[1], dict(zip(FWD_OUT, results[2:]))


def scatter_scratch(segs, part, count, orders, cols=SEG):
    rows = part.shape[-2]
    slots = link_slots(count, "zxy") + 1
    boxes = []
    for order in orders:
        boxes += [pltpu.VMEM(s, BF) for s in inbox_shapes(count, "yzx", order, (rows, cols))[0]]
    hands = pltpu.VMEM((len(orders),) + part.shape[1:4] + (rows, cols), BF)
    return hands, [DMA((segs, slots)), DMA((segs, slots))], boxes


def pair_of(raw, ny):
    return shape_of((ny * raw.shape[0],) + raw.shape[1:], BF)


def feed_back(shape, vectors, g, kept):
    low, high, raw = kept["x"], kept["res"], kept["out"]
    rows, width = low.shape
    part = shape_of((5,) + g.shape[1:], BF)
    turned = pltpu.VMEM((width, rows), BF)
    scratch = [
        vmem(low),
        pltpu.VMEM((rows, 1), F32),
        vmem(kept["active"]),
        vmem(kept["slope"]),
        vmem(low),
        vmem(high),
        vmem(part),
        vmem(part),
        vmem(low),
        turned,
        vmem(kept["active"]),
        turned,
        vmem(high),
        vmem(high),
        vmem(low),
        vmem(low),
        DMA((32,)),
    ]
    given = [g] + [kept[name] for name in ("active", "slope", "nrm2", "res", "out", "cot", "gl", "glt", "weight", "mix")]
    outs = [part, shape_of(high.shape, F32), shape_of(low.shape, BF), shape_of((2, 8, width), F32)]
    specs = [ANYWHERE, ANYWHERE, ANYWHERE, IN_VMEM]
    if shape:
        count = dict(zip("zxy", shape))
        hands, sems, boxes = scatter_scratch(len(FEED_ORDERS), part, count, FEED_ORDERS, SEG // 2)
        scratch += [vmem(raw), hands] + sems + [DMA((8,))] + boxes
        outs += [pair_of(raw, shape[2]), shape_of((part.shape[-2], 2 * SEG), F32)]
        specs += [ANYWHERE, IN_VMEM]
    return call(
        functools.partial(feed_back_kernel, shape),
        tuple(outs),
        [IN_VMEM] + [ANYWHERE] * 11,
        tuple(specs),
        scratch,
        "feed_back",
        1 if shape else None,
    )(vectors, *given)


def attn_back(shape, vectors, vec_f, g, dw_in, kept):
    low, raw = kept["x"], kept["out"]
    width = low.shape[1]
    part = shape_of((3,) + g.shape[1:], BF)
    scratch = [vmem(kept[name]) for name in BACK_IN]
    scratch += [vmem(part), vmem(part), vmem(low), pltpu.VMEM((3,) + low.shape, BF), vmem(raw), DMA((32,))]
    vec = shape_of((2, 8, width), F32)
    if shape:
        nz, nx, ny = shape
        count = dict(zip("zxy", shape))
        share = part.shape[-2]
        small, large = shape_of((share, SEG), F32), shape_of((share, 2 * SEG), F32)
        outs = [pair_of(raw, ny)] + [small] * 4 + [large, shape_of((8, 128), F32)]
        specs = [ANYWHERE] + [IN_VMEM] * 6
        hands, sems, boxes = scatter_scratch(7, part, count, [BACK_ORDERS[seg] for seg in SHARED])
        tiles = pltpu.VMEM((nz, nx, 8, 128), F32)
        scratch += [vmem(part), tiles, hands, tiles, pltpu.VMEM((8, 128), F32), vmem(vec)]
        scratch += sems + [DMA((10,))] + boxes
        scratch += [pltpu.VMEM(s, F32) for s in inbox_shapes({"z": nz, "x": nx}, "zx", "zx", (8, 128))[0]]
    else:
        outs, specs = [part, raw, vec], [ANYWHERE, ANYWHERE, IN_VMEM]
        outs[1] = shape_of(raw.shape, BF)
    return call(
        functools.partial(attn_back_kernel, shape),
        tuple(outs),
        [IN_VMEM] * 2 + [ANYWHERE] * 10,
        tuple(specs),
        scratch,
        "attn_back",
        2 if shape else None,
    )(vectors, vec_f, g, dw_in, *(kept[name] for name in BACK_IN))


def finish(low, grads):
    parts, patches, series, width = low.shape
    cuts = 3 if patches % 3 == 0 else 1
    block = pl.BlockSpec((1, patches // cuts, series, width), lambda part, cut: (part, cut, 0, 0))
    whole = [pl.BlockSpec(grad.shape, lambda part, cut: (0, 0)) for grad in grads]
    return pl.pallas_call(
        finish_kernel,
        grid=(parts, cuts),
        out_shape=[shape_of(low.shape, F32)] + [shape_of(grad.shape, F32) for grad in grads],
        in_specs=[block] + whole,
        out_specs=[block] + whole,
        compiler_params=pltpu.CompilerParams(vmem_limit_bytes=VMEM_LIMIT),
        name="finish",
    )(low, *grads)


def chip_grid(chips):
    nx = 1
    while (nx * 2) ** 2 <= chips:
        nx *= 2
    return chips // nx, nx


def body(counts_of, tokens, cotangent, domain_ids, domain_counts, *params):
    weights, norms = params[:6], params[6:]
    n_dp, n_mp = counts_of
    micro = tokens.shape[0] // n_mp
    width = tokens.shape[3]
    share = width // n_dp
    y = lax.axis_index("mp")
    linked = n_mp == 2 and share * 2 == TILE
    flip = lambda array: jnp.transpose(array, (0, 2, 1, 3))
    x, cot = flip(tokens), flip(cotangent)
    if linked:
        shape = chip_grid(n_dp // 2) + (n_mp,)
        g, vectors, kept = forward(shape, micro, x, cot, domain_ids, domain_counts, weights, [norm.reshape(1, -1) for norm in norms])
    else:
        shards = jnp.stack(
            weights[:4] + tuple(w[:, i * SEG : (i + 1) * SEG] for w in weights[4:] for i in range(2))
        )
        g = lax.all_gather(lax.all_gather(shards, "dp", axis=1, tiled=True), "mp", axis=1)
        vectors = lax.all_gather(jnp.stack(norms), "dp", axis=1, tiled=True).astype(F32)
        vectors = jnp.pad(vectors, ((0, 4), (0, 0)))
        g, vectors, kept = forward(None, micro, x, cot, domain_ids, domain_counts, None, None, g, vectors)
    shape = shape if linked else None
    results = feed_back(shape, vectors, g, kept)
    dw_f, gres, gm, vec_f = results[:4]
    kept = {**kept, "gres": gres, "gm": gm}
    if linked:
        out, grad_down = results[4:]
        grad_tokens, *grads, vec = attn_back(shape, vectors, vec_f, g, dw_f, kept)
        grad_tokens, *grads = finish(grad_tokens, grads + [grad_down])
        core = lax.rem(lax.axis_index("dp"), 2)
        vec = lax.dynamic_slice(vec, (0, core * share), (4, share))
    else:
        dw_a, low_tokens, vec_a = attn_back(shape, vectors, vec_f, g, dw_f, kept)
        dw = jnp.concatenate((dw_a, dw_f[4:], dw_f[:4])).astype(F32)
        dw = lax.psum_scatter(lax.psum_scatter(dw, "mp", scatter_dimension=1), "dp", scatter_dimension=1, tiled=True)
        grads = [dw[0], dw[1], dw[2], dw[3]]
        grads += [jnp.concatenate((dw[a], dw[b]), axis=1) for a, b in (UPS, DOWNS)]
        vec = jnp.concatenate((jnp.sum(vec_a, axis=1), jnp.sum(vec_f, axis=1)))
        vec = lax.psum_scatter(lax.psum(vec, "mp"), "dp", scatter_dimension=1, tiled=True)
        out = lax.all_gather(kept["out"], "mp", axis=0, tiled=True)
        grad_tokens = lax.all_gather(low_tokens, "mp", axis=0, tiled=True)
    return (flip(out), flip(grad_tokens.astype(F32)), *grads, vec[0], vec[1], vec[2], vec[3])


def solution(mesh):
    rows, matrix, vector = P(None, "dp", None, None), P("dp", "mp"), P("dp")
    in_specs = (rows, rows, P(None, "dp"), P()) + (matrix,) * 6 + (vector,) * 4
    out_specs = (rows, rows) + (matrix,) * 6 + (vector,) * 4
    run = functools.partial(body, (mesh.shape["dp"], mesh.shape["mp"]))
    return jax.shard_map(run, mesh=mesh, in_specs=in_specs, out_specs=out_specs, check_vma=False)
```

```python
import functools

import jax
import jax.numpy as jnp
from jax import lax
from jax.experimental import pallas as pl
from jax.experimental.pallas import tpu as pltpu
from jax.sharding import PartitionSpec as P

BF = jnp.bfloat16
F32 = jnp.float32
HD = 128
SEG = 512
TILE = 128
PAD = 16
EPS = 1e-05
MESH = pl.DeviceIdType.MESH
VMEM_LIMIT = 62 * 1024 * 1024

Q, K, V, O, U0, U1, D0, D1 = range(8)
UPS = (U0, U1)
DOWNS = (D0, D1)
ORDERS = ("zyx", "zxy", "zxy", "yzx", "xyz", "zxy", "zyx", "xyz")
BACK_ORDERS = ("yxz", "xzy", "xzy", "zxy", "xzy", "yxz")
FEED_ORDERS = ("xzy", "zxy", "zxy", "xzy")

FORWARD_PLAN = (
    2, 1, 8, 4, 0, 3, 4, 2, 7, 8, -1, 0, 2, 7, 8, 1, 2, 0, 6, 0, 1, 5, 3, 1,
    2, 8, 5, 4, 0, 5, 8, 6, -1, 6, 3, 1, 5, 3, 3, 0, 4, -1, 2, 6, -1, 4, 1, 5,
    7, -1, -1, 6, -1, 4, 3, -1, 7, -1, -1, -1, -1, 5, 7, -1, -1, 6, -1, 7, -1, -1, -1,
)
FEED_PLAN = (
    4, -1, 1, -1, 1, 0, -1, 3, 4, 0, 4, 1, 2, -1, 2, 3, -1, 1, -1, 0, 2, -1, 1, 0,
    -1, 3, 1, 4, 2, -1, 3, 1, -1, 0, 2, 3, -1, 0, -1, 2, 3, -1, 0, 2, 3,
)
ATTN_PLAN = (
    0, 1, -1, 1, 0, -1, 2, -1, -1, -1, -1, 3, 2, -1, 4, 3, -1, 2, 4, 0, 5, -1, 7, 0,
    5, 1, 0, 7, 3, 2, 4, -1, 8, -1, 0, 4, 5, 5, 8, 6, 6, 1, 4, 6, 5, 2, 6, 4,
    3, 1, 5, 6, 3, 1, 2, 6, 3, 5, 1, 4, 0, 3, 2,
)
GRADS_FIRST = 1


def nn(a, b):
    return lax.dot_general(a, b, (((1,), (0,)), ((), ())), preferred_element_type=F32)


def nt(a, b):
    return lax.dot_general(a, b, (((1,), (1,)), ((), ())), preferred_element_type=F32)


def flat(value):
    return value.reshape(-1, value.shape[-1])


def norm_stats(values):
    mean = jnp.mean(values, axis=-1, keepdims=True)
    center = values - mean
    inverse = lax.rsqrt(jnp.mean(center * center, axis=-1, keepdims=True) + EPS)
    return center * inverse, inverse


def norm_pull(grad, values, gain):
    normal, inverse = norm_stats(values)
    scaled = grad * gain
    first = jnp.mean(scaled, axis=-1, keepdims=True)
    second = jnp.mean(scaled * normal, axis=-1, keepdims=True)
    return inverse * (scaled - first - normal * second), normal


def fold_rows(values):
    rows, width = values.shape
    return jnp.sum(values.reshape(rows // 8, 8, width), axis=0)


def score_mask():
    key = lax.broadcasted_iota(jnp.int32, (TILE, TILE), 0)
    query = lax.broadcasted_iota(jnp.int32, (TILE, TILE), 1)
    return (query // PAD == key // PAD) & (key <= query)


def row_loop(rows, body, first=0):
    def once(index, carry):
        index = first + index
        body(pl.ds(pl.multiple_of(index * TILE, TILE), TILE), index)
        return carry

    lax.fori_loop(0, rows // TILE, once, 0)


def half_loop(count, body):
    def once(index, carry):
        body(index)
        return carry

    lax.fori_loop(0, count, once, 0)


def half(index):
    return pl.ds(pl.multiple_of(index * SEG, SEG), SEG)


def spread_rows(patches, series):
    row = lax.broadcasted_iota(jnp.int32, (series * PAD, patches * series), 0)
    col = lax.broadcasted_iota(jnp.int32, (series * PAD, patches * series), 1)
    hit = (lax.rem(row, PAD) * series + lax.div(row, PAD) == col) & (lax.rem(row, PAD) < patches)
    return jnp.where(hit, 1.0, 0.0).astype(BF)


def gather_rows(patches, series):
    row = lax.broadcasted_iota(jnp.int32, (patches * series, series * PAD), 0)
    col = lax.broadcasted_iota(jnp.int32, (patches * series, series * PAD), 1)
    return jnp.where(lax.rem(row, series) * PAD + lax.div(row, series) == col, 1.0, 0.0).astype(BF)


def to_rows(raw, target):
    micro, patches, series, _ = raw.shape
    matrix = spread_rows(patches, series)
    for part in range(micro):
        target[part * series * PAD : (part + 1) * series * PAD, :] = nn(matrix, flat(raw[part])).astype(BF)


def from_rows(source, raw):
    micro, patches, series, width = raw.shape
    matrix = gather_rows(patches, series)
    for part in range(micro):
        rows = source[part * series * PAD : (part + 1) * series * PAD, :]
        raw[part] = nn(matrix, rows).astype(raw.dtype).reshape(patches, series, width)


def norm_in(x, normed, gain, shift):
    def block(rows, _):
        normal, _inv = norm_stats(x[rows, :].astype(F32))
        normed[rows, :] = (normal * gain + shift).astype(BF)

    row_loop(x.shape[0], block)


def project(source, weights, seg, target):
    def one(m):
        target[:, half(m)] = nn(source[...], flat(weights[seg, m])).astype(BF)

    half_loop(weights.shape[1], one)


def attend(queries, keys, values, probs, mixture, first, count):
    mask = score_mask()
    scale = HD ** (-0.5)
    columns = [slice(at, at + HD) for at in range(0, queries.shape[1], HD)]

    def group(rows, _):
        scores = [nt(keys[rows, cols], queries[rows, cols]) * scale for cols in columns]
        scores = [jnp.where(mask, score, -1e30) for score in scores]
        peaks = [jnp.max(score, axis=0, keepdims=True) for score in scores]
        powers = [jnp.exp(score - peak) for score, peak in zip(scores, peaks)]
        inverses = [1.0 / jnp.sum(power, axis=0, keepdims=True) for power in powers]
        shares = [power * inverse for power, inverse in zip(powers, inverses)]
        for cols, share in zip(columns, shares):
            probs[rows, cols] = share
        mixed = [nn(share.astype(BF).T, values[rows, cols]) for share, cols in zip(shares, columns)]
        for cols, part in zip(columns, mixed):
            mixture[rows, cols] = part.astype(BF)

    row_loop(count * TILE, group, first)


def attend_back(queries, keys, values, probs, grad_mix, grad_q, grad_k, grad_v, first, count):
    scale = HD ** (-0.5)
    columns = [slice(at, at + HD) for at in range(0, queries.shape[1], HD)]

    def group(rows, _):
        shares = [probs[rows, cols] for cols in columns]
        grads = [grad_mix[rows, cols] for cols in columns]
        pulls = [nt(values[rows, cols], grad) for cols, grad in zip(columns, grads)]
        back_v = [nn(share.astype(BF), grad) for share, grad in zip(shares, grads)]
        inner = [jnp.sum(pull * share, axis=0, keepdims=True) for pull, share in zip(pulls, shares)]
        lows = [(share * (pull - mean)).astype(BF) for share, pull, mean in zip(shares, pulls, inner)]
        back_k = [nn(low, queries[rows, cols]) * scale for low, cols in zip(lows, columns)]
        back_q = [nn(low.T, keys[rows, cols]) * scale for low, cols in zip(lows, columns)]
        for cols, one, two, three in zip(columns, back_q, back_k, back_v):
            grad_q[rows, cols] = one.astype(BF)
            grad_k[rows, cols] = two.astype(BF)
            grad_v[rows, cols] = three.astype(BF)

    row_loop(count * TILE, group, first)


def back_through(source, weights, seg, total):
    def one(m):
        total[...] += nt(source(m), flat(weights[seg, m]))

    half_loop(weights.shape[1], one)


def feed_up(normed_two, weights, which, m, active, slope):
    hidden = nn(normed_two[...], flat(weights[UPS[which], m]))
    bell = 0.5 + 0.5 * lax.erf(hidden * (0.5**0.5))
    active[which, m] = (hidden * bell).astype(BF)
    density = jnp.exp(-0.5 * hidden * hidden) * 0.3989422804014327
    slope[which, m] = bell + hidden * density


def turn(source, target):
    def block(rows, _):
        target[:, rows] = source[rows, :].T

    row_loop(source.shape[0], block)


def weight_grad(turned, right, target, seg):
    def one(m):
        product = nn(turned[...], right(m)).astype(BF)
        target[seg, m] = product.reshape(target.shape[2:])

    half_loop(target.shape[1], one)


class Place:
    def __init__(self, shape):
        self.nz, self.nx, self.ny = shape
        index = lax.axis_index("dp")
        self.core = lax.rem(index, 2)
        chip = lax.div(index, 2)
        self.at = {"z": lax.div(chip, self.nx), "x": lax.rem(chip, self.nx), "y": lax.axis_index("mp")}
        self.count = {"z": self.nz, "x": self.nx, "y": self.ny}

    def device(self, core=None, **moved):
        at = {**self.at, **moved}
        core = self.core if core is None else core
        return ((at["z"] * self.nx + at["x"]) * 2 + core, at["y"])

    def partner(self):
        return self.device(core=1 - self.core)

    def neighbour(self, dim, step):
        return self.device(**{dim: self.at[dim] + step})

    def barrier(self, dims):
        semaphore = pltpu.get_barrier_semaphore()
        pl.semaphore_signal(semaphore, inc=1, device_id=self.partner(), device_id_type=MESH)
        peers = 1
        for dim in dims:
            for step in (1, -1):
                there = self.at[dim] + step
                valid = (there >= 0) & (there < self.count[dim])
                peers = peers + valid.astype(jnp.int32)

                @pl.when(valid)
                def _(dim=dim, step=step):
                    other = self.neighbour(dim, step)
                    pl.semaphore_signal(semaphore, inc=1, device_id=other, device_id_type=MESH)

        pl.semaphore_wait(semaphore, peers)


def link_slots(count, dims):
    return sum(2 * (count[dim] - 1) for dim in dims)


class Gather:
    def __init__(self, place, buffer, axes, order, sems):
        self.place, self.buffer, self.axes, self.order = place, buffer, axes, order
        self.send, self.recv, self.pass_send, self.pass_recv = sems
        self.rounds = [(dim, t) for dim in order for t in range(place.count[dim] - 1)]
        self.slots = {}
        for dim, t in self.rounds:
            for way in (1, -1):
                self.slots[dim, t, way] = len(self.slots)

    def block(self, dim, position, core):
        done = self.order[: self.order.index(dim)] if dim else ""
        index = []
        for axis in self.axes:
            if axis == dim:
                index.append(position)
            elif axis in done:
                index.append(pl.ds(0, self.place.count[axis]))
            else:
                index.append(self.place.at[axis])
        return self.buffer.at[tuple(index) + (core,)]

    def link(self, dim, t, way, position, device):
        block = self.block(dim, position, self.place.core)
        slot = self.slots[dim, t, way]
        return pltpu.make_async_remote_copy(
            block, block, self.send.at[slot], self.recv.at[slot], device_id=device, device_id_type=MESH
        )

    def hand(self, slot, dim, position, core):
        block = self.block(dim, position, core)
        return pltpu.make_async_remote_copy(
            block,
            block,
            self.pass_send.at[slot],
            self.pass_recv.at[slot],
            device_id=self.place.partner(),
            device_id_type=MESH,
        )

    def sends(self, dim, t):
        here, count = self.place.at[dim], self.place.count[dim]
        yield 1, here - t, (here - t >= 0) & (here < count - 1)
        yield -1, here + t, (here + t < count) & (here > 0)

    def arrivals(self, dim, t):
        here, count = self.place.at[dim], self.place.count[dim]
        yield 1, here - 1 - t, here - 1 - t >= 0
        yield -1, here + 1 + t, here + 1 + t < count

    def start(self):
        self.hand(len(self.slots), "", None, self.place.core).start()
        self.send_round(0)

    def send_round(self, number):
        dim, t = self.rounds[number]
        for way, position, valid in self.sends(dim, t):

            @pl.when(valid)
            def _(way=way, position=position):
                self.link(dim, t, way, position, self.place.neighbour(dim, way)).start()

    def advance(self, number):
        dim, t = self.rounds[number - 1]
        for way, position, valid in self.arrivals(dim, t):

            @pl.when(valid)
            def _(way=way, position=position):
                self.link(dim, t, way, position, self.place.partner()).wait_recv()
                self.hand(self.slots[dim, t, way], dim, position, self.place.core).start()

        if number < len(self.rounds):
            self.send_round(number)

    def steps(self):
        return [self.start] + [functools.partial(self.advance, n + 1) for n in range(len(self.rounds))]

    def finish(self):
        other = 1 - self.place.core
        self.hand(len(self.slots), "", None, other).wait_recv()
        for dim, t in self.rounds:
            for way, position, valid in self.arrivals(dim, t):

                @pl.when(valid)
                def _(dim=dim, t=t, way=way, position=position):
                    self.hand(self.slots[dim, t, way], dim, position, other).wait_recv()

    def drain_hand(self):
        self.hand(len(self.slots), "", None, self.place.core).wait_send()

    def sent(self, dim, t):
        for way, position, valid in self.sends(dim, t):
            yield valid, self.link(dim, t, way, position, self.place.partner())
        for way, position, valid in self.arrivals(dim, t):
            yield valid, self.hand(self.slots[dim, t, way], dim, position, self.place.core)


class Scatter:
    def __init__(self, place, mine, axes, order, inbox, hand_box, sems, both=False):
        self.place, self.mine, self.axes, self.order, self.both = place, mine, axes, order, both
        self.inbox, self.hand_box = inbox, hand_box
        self.send, self.recv = sems
        self.rounds = [(dim, t) for dim in order for t in range(place.count[dim] - 1)]
        self.slots = {}
        for dim, t in self.rounds:
            for way in (1, -1):
                self.slots[dim, t, way] = len(self.slots) + 1

    def own(self, index):
        return index + ((() if self.both else (self.place.core,)))

    def hand(self):
        whole = tuple(pl.ds(0, self.place.count[axis]) for axis in self.axes)
        source = self.mine.at[whole] if self.both else self.mine.at[whole + (1 - self.place.core,)]
        return pltpu.make_async_remote_copy(
            source, self.hand_box, self.send.at[0], self.recv.at[0], device_id=self.place.partner(), device_id_type=MESH
        )

    def start(self):
        self.hand().start()

    def take_hand(self):
        self.hand().wait_recv()
        first = self.place.count[self.axes[0]]
        rest = tuple(pl.ds(0, self.place.count[axis]) for axis in self.axes[1:])
        if self.both:
            self.hand().wait_send()
            self.mine[...] = self.mine[...] + self.hand_box[...]
        else:
            for p in range(first):
                for r in range(self.place.count[self.axes[1]]):
                    index = (p, r) + rest[1:]
                    here = self.mine[index + (self.place.core,)].astype(F32)
                    there = self.hand_box[index].astype(F32)
                    self.mine[index + (self.place.core,)] = (here + there).astype(self.mine.dtype)
        self.send_round(0)

    def block(self, dim, position):
        done = self.order[: self.order.index(dim)]
        index = []
        for axis in self.axes:
            if axis == dim:
                index.append(position)
            elif axis in done:
                index.append(self.place.at[axis])
            else:
                index.append(pl.ds(0, self.place.count[axis]))
        return self.own(tuple(index))

    def link(self, dim, t, way, position, device):
        slot = self.slots[dim, t, way]
        return pltpu.make_async_remote_copy(
            self.mine.at[self.block(dim, position)],
            self.inbox[slot],
            self.send.at[slot],
            self.recv.at[slot],
            device_id=device,
            device_id_type=MESH,
        )

    def sends(self, dim, t):
        here, count = self.place.at[dim], self.place.count[dim]
        yield 1, count - 1 - t + here, (t >= here) & (here < count - 1)
        back = count - 1 - here
        yield -1, t - back, (t >= back) & (here > 0)

    def arrivals(self, dim, t):
        here, count = self.place.at[dim], self.place.count[dim]
        yield 1, count - 2 - t + here, (t >= here - 1) & (here > 0)
        back = count - 1 - here
        yield -1, t + 1 - back, (t >= back - 1) & (here < count - 1)

    def send_round(self, number):
        dim, t = self.rounds[number]
        for way, position, valid in self.sends(dim, t):

            @pl.when(valid)
            def _(way=way, position=position):
                self.link(dim, t, way, position, self.place.neighbour(dim, way)).start()

    def advance(self, number):
        dim, t = self.rounds[number - 1]
        for way, position, valid in self.arrivals(dim, t):

            @pl.when(valid)
            def _(way=way, position=position):
                self.link(dim, t, way, position, self.place.partner()).wait_recv()
                index = self.block(dim, position)
                total = self.mine[index].astype(F32) + self.inbox[self.slots[dim, t, way]][...].astype(F32)
                self.mine[index] = total.astype(self.mine.dtype)

        if number < len(self.rounds):
            self.send_round(number)

    def steps(self):
        later = [functools.partial(self.advance, n + 1) for n in range(len(self.rounds))]
        return [self.start, self.take_hand] + later

    def result(self):
        return self.mine[self.own(tuple(self.place.at[axis] for axis in self.axes))]

    def drain_hand(self):
        if not self.both:
            self.hand().wait_send()

    def sent(self, dim, t):
        for way, position, valid in self.sends(dim, t):
            yield valid, self.link(dim, t, way, position, self.place.partner())


def drain(runs):
    for run in runs:
        run.drain_hand()
    for dim, t in dict.fromkeys(key for run in runs for key in run.rounds):
        groups = [list(run.sent(dim, t)) for run in runs if (dim, t) in run.rounds]
        for same in zip(*groups):

            @pl.when(same[0][0])
            def _(same=same):
                for _valid, copy in same:
                    copy.wait_send()


def inbox_shapes(count, axes, order, block):
    shapes, slots, left = [], {}, dict(count)
    for dim in order:
        left.pop(dim)
        for t in range(count[dim] - 1):
            for way in (1, -1):
                if way == 1 or count[dim] > 2:
                    shapes.append(tuple(count[axis] for axis in axes if axis in left) + block)
                slots[dim, t, way] = len(shapes) - 1
    return shapes, slots


def open_inbox(run, count, axes, order, block, boxes):
    shapes, slots = inbox_shapes(count, axes, order, block)
    for key, slot in run.slots.items():
        run.inbox[slot] = boxes[slots[key]]
    del boxes[: len(shapes)]


def play(plan, comm, pieces):
    plan = list(plan)
    while plan:
        token = plan.pop(0)
        if token >= 0:
            if comm:
                comm[token].pop(0)()
        elif callable(pieces[0]):
            pieces.pop(0)()
        else:
            count, piece, before, after = pieces.pop(0)
            if before:
                before()
            between = [[] for _ in range(count - 1)]
            for spot in range(count - 1):
                while plan[0] >= 0:
                    token = plan.pop(0)
                    if comm:
                        between[spot].append(comm[token].pop(0))
                plan.pop(0)

            def once(index, carry, piece=piece, between=between):
                piece(index)
                for spot, steps in enumerate(between):
                    if steps:

                        @pl.when(index == spot)
                        def _(steps=steps):
                            for step in steps:
                                step()

                return carry

            lax.fori_loop(0, count, once, 0)
            if after:
                after()
    assert not pieces and not any(comm.values())


class Mover:
    def __init__(self, sems):
        self.sems, self.used, self.open = sems, 0, []

    def start(self, source, target):
        copy = pltpu.make_async_copy(source, target, self.sems.at[self.used])
        self.used += 1
        copy.start()
        return copy

    def save(self, source, target):
        self.open.append(self.start(source, target))

    def close(self):
        for copy in self.open:
            copy.wait()


def read_vectors(vectors, tiles):
    nz, nx = tiles.shape[:2]
    pieces = [tiles[z, x, 0] + tiles[z, x, 1] for z in range(nz) for x in range(nx)]
    vectors[...] = jnp.concatenate(pieces, axis=1)


def column_parts(weights):
    wq, wk, wv, wo, wu, wd = weights
    left, right = pl.ds(0, SEG), pl.ds(SEG, SEG)
    return [wq, wk, wv, wo, wu.at[:, left], wu.at[:, right], wd.at[:, left], wd.at[:, right]]


def fill_tile(place, tiles, norms):
    tile = (place.at["z"], place.at["x"], place.core)
    tiles[tile] = jnp.zeros(tiles.shape[3:], F32)
    share = norms[0].shape[1]
    for line, norm in enumerate(norms):
        value = norm[...].astype(F32)
        for core in range(2):

            @pl.when(place.core == core)
            def _(line=line, value=value, core=core):
                tiles[tile + (slice(line, line + 1), slice(core * share, (core + 1) * share))] = value


FWD_OUT = (
    "x", "q", "k", "v", "probs", "mix", "res", "nrm2", "active", "slope", "out", "cot", "gl", "glt", "weight",
    "nrmt",
)
KEPT = len(FWD_OUT)


def forward_kernel(shape, micro, tokens, cotangent, ids, counts, *refs):
    if shape:
        weights, norms, g_out, refs = refs[:6], refs[6:10], refs[10], refs[11:]
    else:
        g_in, vectors_in, refs = refs[0], refs[1], refs[2:]
    if shape:
        vectors, refs = refs[0], refs[1:]
    else:
        vectors = vectors_in
    saved = dict(zip(FWD_OUT, refs[:KEPT]))
    here = dict(zip(FWD_OUT, refs[KEPT : 2 * KEPT]))
    refs = refs[2 * KEPT :]
    raw, nrm, low, total, g, sems = refs[:6]
    mover = Mover(sems)
    y = lax.axis_index("mp")
    take = mover.start(tokens.at[pl.ds(y * micro, micro)], raw)
    x, q, k, v, probs, mix, res, nrm2, active, slope, out, cot, gl, glt, weight, nrmt = (
        here[name] for name in FWD_OUT
    )

    def keep(*names):
        for name in names:
            mover.save(here[name], saved[name])

    comm = {}
    if shape:
        tiles, send, recv, pass_send, pass_recv = refs[6:]
        place = Place(shape)
        spot = (place.at["y"], place.at["z"], place.at["x"], place.core)
        mine = [mover.start(part, g.at[(seg,) + spot]) for seg, part in enumerate(column_parts(weights))]
        fill_tile(place, tiles, norms)
        place.barrier("zxy")
        pick = lambda seg: tuple(sem.at[seg] for sem in (send, recv, pass_send, pass_recv))
        runs, cut = [], len(ORDERS) // 8
        for spot, order in enumerate(ORDERS):
            columns = pl.ds(spot % cut * (SEG // cut), SEG // cut)
            runs.append(Gather(place, g.at[spot // cut, :, :, :, :, :, columns], "yzx", order, pick(spot)))
        runs.append(Gather(place, tiles, "zx", "zx", pick(len(ORDERS))))
        comm = {spot: run.steps() for spot, run in enumerate(runs)}
        waiting = list(mine)

        def begin(spot):
            if waiting[spot // cut] is not None:
                waiting[spot // cut].wait()
                waiting[spot // cut] = None
            runs[spot].start()

        for spot in range(len(ORDERS)):
            comm[spot][0] = functools.partial(begin, spot)

        def have(seg):
            if seg < 8:
                for run in runs[seg * cut : (seg + 1) * cut]:
                    run.finish()
                mover.save(g.at[seg], g_out.at[seg])
            else:
                runs[-1].finish()
                read_vectors(vectors, tiles)

    else:
        loads = [mover.start(g_in.at[seg], g.at[seg]) for seg in range(8)]

        def have(seg):
            if seg < 8:
                loads[seg].wait()

    def spread():
        take.wait()
        to_rows(raw, x)
        keep("x")
        loads_cot.append(mover.start(cotangent.at[pl.ds(y * micro, micro)], raw))
        row_weights(ids, counts, y, micro, weight)

    loads_cot = []

    def weigh():
        loads_cot[0].wait()
        to_rows(raw, cot)

        def block(rows, _):
            gl[rows, :] = (cot[rows, :].astype(F32) * weight[rows, :]).astype(BF)

        row_loop(cot.shape[0], block)
        turn(gl, glt)
        keep("cot", "gl", "glt", "weight")

    def norm_one():
        have(8)
        norm_in(x, nrm, vectors[0:1, :], vectors[1:2, :])
        turn(nrm, nrmt)
        keep("nrmt")

    def head_part(seg, target, name):
        have(seg)
        project(nrm, g, seg, target)
        keep(name)

    third = x.shape[0] // TILE // 3

    def mixing(part):
        attend(q, k, v, probs, mix, part * third, third)

    def project_out():
        keep("probs", "mix")
        have(O)
        res[...] = x[...].astype(F32)
        back_through(lambda m: mix[:, half(m)], g, O, res)
        keep("res")

    def norm_two():
        gain, shift = vectors[2:3, :], vectors[3:4, :]

        def block(rows, _):
            normal, _inv = norm_stats(res[rows, :])
            nrm2[rows, :] = (normal * gain + shift).astype(BF)

        row_loop(x.shape[0], block)
        keep("nrm2")

    def up(which, m):
        feed_up(nrm2, g, which, m, active, slope)

    def keep_up(which):
        mover.save(active.at[which], saved["active"].at[which])
        mover.save(slope.at[which], saved["slope"].at[which])

    def down(which):
        have(DOWNS[which])
        if which == 0:
            total[...] = res[...]
        back_through(lambda m: active[which, m], g, DOWNS[which], total)

    def last():
        low[...] = total[...].astype(BF)
        from_rows(low, out)
        keep("out")

    pieces = [spread, weigh, norm_one]
    pieces += [functools.partial(head_part, *args) for args in ((Q, q, "q"), (K, k, "k"), (V, v, "v"))]
    pieces += [(3, mixing, None, None), project_out, norm_two]
    for which in range(2):
        before, after = functools.partial(have, UPS[which]), functools.partial(keep_up, which)
        pieces.append((2, functools.partial(up, which), before, after))
    pieces += [functools.partial(down, which) for which in range(2)] + [last]
    play(FORWARD_PLAN, comm, pieces)
    if shape:
        drain(runs)
    mover.close()


def row_weights(ids, counts, y, micro, target):
    series = ids.shape[1]
    sums = counts[0]
    for kind in range(1, counts.shape[0]):
        sums = sums + counts[kind]
    mean = jnp.full((PAD, 1), sums.astype(F32), F32) / counts.shape[0]

    def one(index, carry):
        kind = ids[y * micro + lax.div(index, series), lax.rem(index, series)]
        count = counts[kind].astype(F32)
        target[pl.ds(pl.multiple_of(index * PAD, PAD), PAD), :] = 2.0 * mean / (mean + count)
        return carry

    lax.fori_loop(0, micro * series, one, 0)


class Swap:
    def __init__(self, place, mover, sems, ready, source, target):
        self.mover, self.source, self.ready = mover, source, ready
        y, (micro, patches) = place.at["y"], source.shape[:2]
        cut = patches // 2 + 1
        self.spots = [target.at[y * micro + part] for part in range(micro)]
        self.copies = []
        for part in range(micro):
            for piece in (pl.ds(0, cut), pl.ds(cut, patches - cut)):
                slot = 2 * len(self.copies)
                self.copies.append(
                    pltpu.make_async_remote_copy(
                        source.at[part, piece],
                        target.at[y * micro + part, piece],
                        sems.at[slot],
                        sems.at[slot + 1],
                        device_id=place.device(y=1 - y),
                        device_id_type=MESH,
                    )
                )

    def start(self, part):
        if part == 0:
            self.ready()
        self.copies[2 * part].start()
        self.mover.save(self.source.at[part], self.spots[part])

    def steps(self, part):
        return [functools.partial(self.start, part), self.copies[2 * part + 1].start]

    def wait(self):
        for copy in self.copies:
            copy.wait()


def feed_back_kernel(shape, vectors, g_in, active_in, slope_in, nrm2_in, res_in, out_in, cot_in, gl_in, glt_in, weight_in, mix_in, *refs):
    if shape:
        dw_out, gres_out, gm_out, vec, pair, grad_down, refs = refs[:6] + (refs[6:],)
    else:
        dw_out, gres_out, gm_out, vec, refs = refs[:4] + (refs[4:],)
    cot, weight, active, slope, nrm2, res, g, dw, gl, glt, gh, n2t, gn2, gres, mix, gm, sems = refs[:17]
    mover = Mover(sems)
    if shape:
        half_out, hands, send, recv, ysem = refs[17:22]
        boxes = list(refs[22:])
        side = mover.start(out_in, half_out)
    loads = {"glt": mover.start(glt_in, glt), ("active", 0): mover.start(active_in.at[0], active.at[0])}
    loads["gl"] = mover.start(gl_in, gl)
    for which in range(2):
        if which == 1:
            loads["active", which] = mover.start(active_in.at[which], active.at[which])
        loads["d", which] = mover.start(g_in.at[DOWNS[which]], g.at[2 + which])
        loads["slope", which] = mover.start(slope_in.at[which], slope.at[which])
    loads["nrm2"] = mover.start(nrm2_in, nrm2)
    for which in range(2):
        loads["u", which] = mover.start(g_in.at[UPS[which]], g.at[which])
    loads["res"] = mover.start(res_in, res)
    loads["cot"] = mover.start(cot_in, cot)
    loads["mix"] = mover.start(mix_in, mix)
    loads["o"] = mover.start(g_in.at[O], g.at[4])
    loads["weight"] = mover.start(weight_in, weight)
    comm = {}
    if shape:
        place = Place(shape)
        place.barrier("zxy")
        runs = []
        block = (dw.shape[-2], SEG // 2)
        for spot, order in enumerate(FEED_ORDERS):
            columns = pl.ds(spot % 2 * block[1], block[1])
            source = dw.at[2 + spot // 2, :, :, :, :, :, columns]
            run = Scatter(place, source, "yzx", order, {}, hands.at[spot], (send.at[spot], recv.at[spot]))
            open_inbox(run, place.count, "yzx", order, block, boxes)
            runs.append(run)
        swap = Swap(place, mover, ysem, side.wait, half_out, pair)
        comm = {spot: run.steps() for spot, run in enumerate(runs)}
        comm[len(runs)] = swap.steps(0) + swap.steps(1)

    def down_grad(which):
        if which == 0:
            loads["glt"].wait()
        loads["active", which].wait()
        weight_grad(glt, lambda m: active[which, m], dw, 2 + which)
        if not shape:
            mover.save(dw.at[2 + which], dw_out.at[2 + which])

    def hidden_grad(which):
        if which == 0:
            loads["gl"].wait()
        loads["d", which].wait()
        loads["slope", which].wait()

        def one(m):
            pulled = nn(gl[...], flat(g[2 + which, m]))
            gh[which, m] = (pulled * slope[which, m]).astype(BF)

        half_loop(g.shape[1], one)

    def turn_two():
        loads["nrm2"].wait()
        turn(nrm2, n2t)
        gn2[...] = jnp.zeros_like(gn2)

    def up_grad(which):
        weight_grad(n2t, lambda m: gh[which, m], dw, which)
        mover.save(dw.at[which], dw_out.at[which])

    def norm_grad(which):
        loads["u", which].wait()
        back_through(lambda m: gh[which, m], g, which, gn2)

    def last():
        for name in ("res", "cot", "weight"):
            loads[name].wait()
        gain = vectors[2:3, :]
        vec[...] = jnp.zeros_like(vec)

        def block(rows, _):
            grad = gn2[rows, :]
            pulled, normal = norm_pull(grad, res[rows, :], gain)
            vec[0] += fold_rows(grad * normal)
            vec[1] += fold_rows(grad)
            total = cot[rows, :].astype(F32) * weight[rows, :] + pulled
            gres[rows, :] = total
            gl[rows, :] = total.astype(BF)

        row_loop(cot.shape[0], block)
        mover.save(gres, gres_out)

    def mix_grad():
        loads["o"].wait()
        project(gl, g, 4, gm)
        mover.save(gm, gm_out)

    def out_grad():
        loads["mix"].wait()
        weight_grad(glt, lambda m: mix[:, half(m)], dw, 4)
        mover.save(dw.at[4], dw_out.at[4])

    pieces = []
    for which in range(2):
        pieces += [functools.partial(down_grad, which), functools.partial(hidden_grad, which)]
    pieces.append(turn_two)
    for which in range(2):
        pieces += [functools.partial(up_grad, which), functools.partial(norm_grad, which)]
    pieces += [last, mix_grad, lambda: turn(gl, glt), out_grad]
    play(FEED_PLAN, comm, pieces)
    if shape:
        for spot, run in enumerate(runs):
            grad_down[:, spot * block[1] : (spot + 1) * block[1]] = run.result().astype(F32)
        drain(runs)
        swap.wait()
    mover.close()


def vector_tiles(tiles, vec_a, vec_f):
    tiles[...] = jnp.zeros_like(tiles)
    nz, nx = tiles.shape[:2]
    for line, (source, part) in enumerate(((vec_a, 0), (vec_a, 1), (vec_f, 0), (vec_f, 1))):
        row = jnp.sum(source[part], axis=0, keepdims=True)
        for z in range(nz):
            for x in range(nx):
                chip = z * nx + x
                tiles[z, x, line : line + 1, :] = row[:, chip * 128 : (chip + 1) * 128]


BACK_IN = ("gm", "q", "k", "v", "probs", "nrmt", "gres", "x")
SHARED = (U0, U1, O, Q, K, V)
KEPT_GRADS = (0, 1, 4)


def attn_back_kernel(shape, vectors, vec_f, g_in, dw_in, *refs):
    given = dict(zip(BACK_IN, refs[:8]))
    refs = refs[8:]
    if shape:
        grad_down, pair, packed, vec_out, refs = refs[:4] + (refs[4:],)
    else:
        dw_out, out, vec, refs = refs[0], refs[1], refs[2], refs[3:]
    here = dict(zip(BACK_IN, refs[:8]))
    g, dw, gal, pulls, raw, sems = refs[8:14]
    mover = Mover(sems)
    loads, comm = {}, {}
    if shape:
        held, tiles, hands, vec_hand, ybox, vec, send, recv, ysem = refs[14:23]
        boxes = list(refs[23:])

    def fetch_held(*spots):
        for spot in spots:
            if shape:
                loads["dw", spot] = mover.start(dw_in.at[KEPT_GRADS[spot]], held.at[spot])

    fetch_held(0)
    for name in BACK_IN[:5]:
        loads[name] = mover.start(given[name], here[name])
    fetch_held(1, 2)
    for name in BACK_IN[5:]:
        loads[name] = mover.start(given[name], here[name])
    for seg in (Q, K, V):
        loads[seg] = mover.start(g_in.at[seg], g.at[seg])
    gm, q, k, v, probs, nrmt, gres, x = (here[name] for name in BACK_IN)
    gn = probs
    if shape:
        place = Place(shape)
        place.barrier("zxy")
        runs = []
        for spot, seg in enumerate(SHARED):
            source = held.at[spot] if spot < 3 else dw.at[seg]
            order = BACK_ORDERS[seg]
            run = Scatter(place, source, "yzx", order, {}, hands.at[spot], (send.at[spot], recv.at[spot]))
            open_inbox(run, place.count, "yzx", order, dw.shape[-2:], boxes)
            runs.append(run)
        run = Scatter(place, tiles, "zx", "zx", {}, vec_hand, (send.at[6], recv.at[6]), both=True)
        open_inbox(run, {"z": place.nz, "x": place.nx}, "zx", "zx", (8, 128), boxes)
        runs.append(run)
        swap = Swap(place, mover, ysem, lambda: None, raw, pair)
        comm = {spot: run.steps() for spot, run in enumerate(runs)}
        comm[7], comm[8] = swap.steps(0), swap.steps(1)
        for spot in range(3):
            comm[spot][0] = lambda spot=spot: (loads["dw", spot].wait(), runs[spot].start())

    third = gal.shape[0] // TILE // 3
    micro = raw.shape[0]
    share = gal.shape[0] // micro

    def ready():
        for name in BACK_IN[:5]:
            loads[name].wait()
        vec[...] = jnp.zeros_like(vec)

    def mixing(part):
        attend_back(q, k, v, probs, gm, pulls.at[0], pulls.at[1], pulls.at[2], part * third, third)

    def head_grad(seg):
        weight_grad(nrmt, lambda m: pulls[seg, :, half(m)], dw, seg)

    def token_grad(part):
        rows_of = pl.ds(part * share, share)
        gn[rows_of, :] = jnp.zeros((share, gn.shape[1]), F32)
        if part == 0:
            for name in (Q, K, V, "gres", "x"):
                loads[name].wait()

        def one(index, carry):
            seg, m = lax.div(index, 2), lax.rem(index, 2)
            gn[rows_of, :] += nt(pulls[seg, rows_of, half(m)], flat(g[seg, m]))
            return carry

        lax.fori_loop(0, 6, one, 0)
        gain = vectors[0:1, :]

        def block(rows, _):
            grad = gn[rows, :]
            pulled, normal = norm_pull(grad, x[rows, :].astype(F32), gain)
            vec[0] += fold_rows(grad * normal)
            vec[1] += fold_rows(grad)
            gal[rows, :] = (gres[rows, :] + pulled).astype(BF)

        row_loop(share, block, part * share // TILE)
        patches, series, width = raw.shape[1:]
        turned = nn(gather_rows(patches, series), gal[rows_of, :]).astype(raw.dtype)
        raw[part] = turned.reshape(patches, series, width)

    def spread_vectors():
        if shape:
            vector_tiles(tiles, vec, vec_f)

    def before_heads():
        loads["nrmt"].wait()

    pieces = [ready, (3, mixing, None, None), before_heads]
    parts = [functools.partial(token_grad, part) for part in range(micro)]
    heads = [(3, head_grad, None, None)]
    pieces += heads + parts if GRADS_FIRST else parts + heads
    pieces.insert(len(pieces) - (0 if GRADS_FIRST else 1), spread_vectors)
    play(ATTN_PLAN, comm, pieces)
    if not shape:
        mover.save(raw, out)
        for seg in (Q, K, V):
            mover.save(dw.at[seg], dw_out.at[seg])
    if shape:
        here_tile = tiles.at[place.at["z"], place.at["x"]]
        copy = pltpu.make_async_remote_copy(
            here_tile, ybox, ysem.at[8], ysem.at[9], device_id=place.device(y=1 - place.at["y"]), device_id_type=MESH
        )
        copy.start()
        packed[:, 6 * SEG :] = grad_down[...]
        for spot, column in enumerate((4, 5, 3, 0, 1, 2)):
            packed[:, column * SEG : (column + 1) * SEG] = runs[spot].result().astype(F32)
        drain(runs)
        copy.wait()
        vec_out[...] = tiles[place.at["z"], place.at["x"]] + ybox[...]
        swap.wait()
    mover.close()


def shape_of(shape, dtype):
    return jax.ShapeDtypeStruct(shape, dtype)


IN_VMEM = pl.BlockSpec(memory_space=pltpu.VMEM)
IN_SMEM = pl.BlockSpec(memory_space=pltpu.SMEM)
ANYWHERE = pl.BlockSpec(memory_space=pl.ANY)
DMA = pltpu.SemaphoreType.DMA


def call(body, outs, ins, out_specs, scratch, name, collective=None):
    params = {"vmem_limit_bytes": VMEM_LIMIT}
    if collective is not None:
        params.update(collective_id=collective, has_side_effects=True)
    return pl.pallas_call(
        body,
        out_shape=outs,
        in_specs=ins,
        out_specs=out_specs,
        scratch_shapes=scratch,
        compiler_params=pltpu.CompilerParams(**params),
        name=name,
    )


def vmem(like):
    return pltpu.VMEM(like.shape, like.dtype)


def forward(shape, micro, tokens, cotangent, ids, counts, weights, norms, g_in=None, vectors_in=None):
    _, patches, series, width = tokens.shape
    rows = micro * series * PAD
    full = g_in.shape if shape is None else (8, shape[2], shape[0], shape[1], 2, weights[0].shape[0], SEG)
    low, high = shape_of((rows, width), BF), shape_of((rows, width), F32)
    wide = (2, full[1], rows, SEG)
    raw = shape_of((micro, patches, series, width), BF)
    kinds = {name: low for name in FWD_OUT}
    kinds.update(
        probs=high,
        res=high,
        active=shape_of(wide, BF),
        slope=shape_of(wide, F32),
        out=raw,
        glt=shape_of((width, rows), BF),
        nrmt=shape_of((width, rows), BF),
        weight=shape_of((rows, 1), F32),
    )
    saved = tuple(kinds[name] for name in FWD_OUT)
    scratch = [vmem(kind) for kind in saved] + [vmem(raw), vmem(low), vmem(low), vmem(high), pltpu.VMEM(full, BF), DMA((64,))]
    if shape is None:
        results = call(
            functools.partial(forward_kernel, None, micro),
            saved,
            [ANYWHERE, ANYWHERE, IN_SMEM, IN_SMEM, ANYWHERE, IN_VMEM],
            (ANYWHERE,) * KEPT,
            scratch,
            "forward",
        )(tokens, cotangent, ids, counts, g_in, vectors_in)
        return g_in, vectors_in, dict(zip(FWD_OUT, results))
    count = dict(zip("zxy", shape))
    slots = link_slots(count, "zxy")
    scratch += [pltpu.VMEM(shape[:2] + (2, 8, 128), F32)]
    runs = len(ORDERS) + 1
    scratch += [DMA((runs, slots)), DMA((runs, slots)), DMA((runs, slots + 1)), DMA((runs, slots + 1))]
    results = call(
        functools.partial(forward_kernel, shape, micro),
        (shape_of(full, BF), shape_of((8, width), F32)) + saved,
        [ANYWHERE, ANYWHERE, IN_SMEM, IN_SMEM] + [ANYWHERE] * 6 + [IN_VMEM] * 4,
        (ANYWHERE, IN_VMEM) + (ANYWHERE,) * KEPT,
        scratch,
        "forward",
        0,
    )(tokens, cotangent, ids, counts, *weights, *norms)
    return results[0], results[1], dict(zip(FWD_OUT, results[2:]))


def scatter_scratch(segs, part, count, orders, cols=SEG):
    rows = part.shape[-2]
    slots = link_slots(count, "zxy") + 1
    boxes = []
    for order in orders:
        boxes += [pltpu.VMEM(s, BF) for s in inbox_shapes(count, "yzx", order, (rows, cols))[0]]
    hands = pltpu.VMEM((len(orders),) + part.shape[1:4] + (rows, cols), BF)
    return hands, [DMA((segs, slots)), DMA((segs, slots))], boxes


def pair_of(raw, ny):
    return shape_of((ny * raw.shape[0],) + raw.shape[1:], BF)


def feed_back(shape, vectors, g, kept):
    low, high, raw = kept["x"], kept["res"], kept["out"]
    rows, width = low.shape
    part = shape_of((5,) + g.shape[1:], BF)
    turned = pltpu.VMEM((width, rows), BF)
    scratch = [
        vmem(low),
        pltpu.VMEM((rows, 1), F32),
        vmem(kept["active"]),
        vmem(kept["slope"]),
        vmem(low),
        vmem(high),
        vmem(part),
        vmem(part),
        vmem(low),
        turned,
        vmem(kept["active"]),
        turned,
        vmem(high),
        vmem(high),
        vmem(low),
        vmem(low),
        DMA((32,)),
    ]
    given = [g] + [kept[name] for name in ("active", "slope", "nrm2", "res", "out", "cot", "gl", "glt", "weight", "mix")]
    outs = [part, shape_of(high.shape, F32), shape_of(low.shape, BF), shape_of((2, 8, width), F32)]
    specs = [ANYWHERE, ANYWHERE, ANYWHERE, IN_VMEM]
    if shape:
        count = dict(zip("zxy", shape))
        hands, sems, boxes = scatter_scratch(len(FEED_ORDERS), part, count, FEED_ORDERS, SEG // 2)
        scratch += [vmem(raw), hands] + sems + [DMA((8,))] + boxes
        outs += [pair_of(raw, shape[2]), shape_of((part.shape[-2], 2 * SEG), F32)]
        specs += [ANYWHERE, IN_VMEM]
    return call(
        functools.partial(feed_back_kernel, shape),
        tuple(outs),
        [IN_VMEM] + [ANYWHERE] * 11,
        tuple(specs),
        scratch,
        "feed_back",
        1 if shape else None,
    )(vectors, *given)


def attn_back(shape, vectors, vec_f, g, dw_in, kept, grad_down=None):
    low, raw = kept["x"], kept["out"]
    width = low.shape[1]
    part = shape_of((3,) + g.shape[1:], BF)
    scratch = [vmem(kept[name]) for name in BACK_IN]
    scratch += [vmem(part), vmem(part), vmem(low), pltpu.VMEM((3,) + low.shape, BF), vmem(raw), DMA((32,))]
    vec = shape_of((2, 8, width), F32)
    if shape:
        nz, nx, ny = shape
        count = dict(zip("zxy", shape))
        share = part.shape[-2]
        outs = [pair_of(raw, ny), shape_of((share, 8 * SEG), F32), shape_of((8, 128), F32)]
        specs = [ANYWHERE] + [IN_VMEM] * 2
        hands, sems, boxes = scatter_scratch(7, part, count, [BACK_ORDERS[seg] for seg in SHARED])
        tiles = pltpu.VMEM((nz, nx, 8, 128), F32)
        scratch += [vmem(part), tiles, hands, tiles, pltpu.VMEM((8, 128), F32), vmem(vec)]
        scratch += sems + [DMA((10,))] + boxes
        scratch += [pltpu.VMEM(s, F32) for s in inbox_shapes({"z": nz, "x": nx}, "zx", "zx", (8, 128))[0]]
    else:
        outs, specs = [part, raw, vec], [ANYWHERE, ANYWHERE, IN_VMEM]
        outs[1] = shape_of(raw.shape, BF)
    return call(
        functools.partial(attn_back_kernel, shape),
        tuple(outs),
        [IN_VMEM] * 2 + [ANYWHERE] * 10 + ([IN_VMEM] if shape else []),
        tuple(specs),
        scratch,
        "attn_back",
        2 if shape else None,
    )(vectors, vec_f, g, dw_in, *(kept[name] for name in BACK_IN), *((grad_down,) if shape else ()))


def chip_grid(chips):
    nx = 1
    while (nx * 2) ** 2 <= chips:
        nx *= 2
    return chips // nx, nx


def body(counts_of, tokens, cotangent, domain_ids, domain_counts, *params):
    weights, norms = params[:6], params[6:]
    n_dp, n_mp = counts_of
    micro = tokens.shape[0] // n_mp
    width = tokens.shape[3]
    share = width // n_dp
    y = lax.axis_index("mp")
    linked = n_mp == 2 and share * 2 == TILE
    flip = lambda array: jnp.transpose(array, (0, 2, 1, 3))
    x, cot = flip(tokens), flip(cotangent)
    if linked:
        shape = chip_grid(n_dp // 2) + (n_mp,)
        g, vectors, kept = forward(shape, micro, x, cot, domain_ids, domain_counts, weights, [norm.reshape(1, -1) for norm in norms])
    else:
        shards = jnp.stack(
            weights[:4] + tuple(w[:, i * SEG : (i + 1) * SEG] for w in weights[4:] for i in range(2))
        )
        g = lax.all_gather(lax.all_gather(shards, "dp", axis=1, tiled=True), "mp", axis=1)
        vectors = lax.all_gather(jnp.stack(norms), "dp", axis=1, tiled=True).astype(F32)
        vectors = jnp.pad(vectors, ((0, 4), (0, 0)))
        g, vectors, kept = forward(None, micro, x, cot, domain_ids, domain_counts, None, None, g, vectors)
    shape = shape if linked else None
    results = feed_back(shape, vectors, g, kept)
    dw_f, gres, gm, vec_f = results[:4]
    kept = {**kept, "gres": gres, "gm": gm}
    if linked:
        out, grad_down = results[4:]
        grad_tokens, packed, vec = attn_back(shape, vectors, vec_f, g, dw_f, kept, grad_down)
        cuts = [0, SEG, 2 * SEG, 3 * SEG, 4 * SEG, 6 * SEG, 8 * SEG]
        grads = [packed[:, start:stop] for start, stop in zip(cuts, cuts[1:])]
        core = lax.rem(lax.axis_index("dp"), 2)
        vec = lax.dynamic_slice(vec, (0, core * share), (4, share))
    else:
        dw_a, low_tokens, vec_a = attn_back(shape, vectors, vec_f, g, dw_f, kept)
        dw = jnp.concatenate((dw_a, dw_f[4:], dw_f[:4])).astype(F32)
        dw = lax.psum_scatter(lax.psum_scatter(dw, "mp", scatter_dimension=1), "dp", scatter_dimension=1, tiled=True)
        grads = [dw[0], dw[1], dw[2], dw[3]]
        grads += [jnp.concatenate((dw[a], dw[b]), axis=1) for a, b in (UPS, DOWNS)]
        vec = jnp.concatenate((jnp.sum(vec_a, axis=1), jnp.sum(vec_f, axis=1)))
        vec = lax.psum_scatter(lax.psum(vec, "mp"), "dp", scatter_dimension=1, tiled=True)
        out = lax.all_gather(kept["out"], "mp", axis=0, tiled=True)
        grad_tokens = lax.all_gather(low_tokens, "mp", axis=0, tiled=True)
    return (flip(out), flip(grad_tokens.astype(F32)), *grads, vec[0], vec[1], vec[2], vec[3])


def solution(mesh):
    rows, matrix, vector = P(None, "dp", None, None), P("dp", "mp"), P("dp")
    in_specs = (rows, rows, P(None, "dp"), P()) + (matrix,) * 6 + (vector,) * 4
    out_specs = (rows, rows) + (matrix,) * 6 + (vector,) * 4
    run = functools.partial(body, (mesh.shape["dp"], mesh.shape["mp"]))
    return jax.shard_map(run, mesh=mesh, in_specs=in_specs, out_specs=out_specs, check_vma=False)
```

```python
import functools

import jax
import jax.numpy as jnp
from jax import lax
from jax.experimental import pallas as pl
from jax.experimental.pallas import tpu as pltpu
from jax.sharding import PartitionSpec as P

BF = jnp.bfloat16
F32 = jnp.float32
HD = 128
SEG = 512
TILE = 128
PAD = 16
EPS = 1e-05
MESH = pl.DeviceIdType.MESH
VMEM_LIMIT = 62 * 1024 * 1024

Q, K, V, O, U0, U1, D0, D1 = range(8)
UPS = (U0, U1)
DOWNS = (D0, D1)
ORDERS = ("zxy", "zyx", "zxy", "xyz", "yzx", "zxy", "zyx", "xyz")
BACK_ORDERS = ("zxy", "xzy", "yxz", "xyz", "xzy", "zxy", "yxz", "xzy", "xzy")
FEED_ORDERS = ("zxy", "xzy", "zxy", "xzy")

FORWARD_PLAN = (
    0, 1, 4, 3, 0, 8, 2, 7, 3, -1, 0, 1, 0, 8, 7, 1, 2, 1, 8, 8, 2, 2, 5, 6,
    0, 4, 1, 5, 2, 6, 5, 6, 4, 3, 5, -1, 6, 4, 8, 4, 0, 3, -1, 1, -1, 2, 5, 3,
    7, -1, -1, -1, 3, 6, -1, -1, -1, 7, -1, 4, -1, 5, -1, 7, -1, 6, -1, -1, 7, -1, -1,
)
FEED_PLAN = (
    4, -1, 0, 4, -1, 0, 1, -1, 0, 2, 1, 3, -1, 2, -1, 4, -1, 4, 3, 2, 0, -1, -1, 1,
    -1, 1, 0, 3, 2, -1, 3, -1, 1, 2, 3, 1, 0, -1, 2, 3, -1, 0, 2, 1, 3,
)
ATTN_PLAN = (
    2, 0, -1, -1, 2, 1, 0, -1, -1, 1, -1, -1, -1, 0, 4, 6, 5, -1, 8, 5, 6, -1, 10, 8,
    0, 7, 4, -1, -1, 1, 3, 3, 10, 1, 7, 2, 9, 9, 8, 9, 8, 11, 9, 1, 4, 3, 4, 5,
    8, 5, 1, 7, 6, 0, 11, 4, 3, 2, 9, 8, 6, 4, 7, 3, 2, 7, 5, 0, 6, 9, 2, 3,
    5, 6, 7, 1, 4, 8, 0, 5, 2, 3, 7, 6,
)
GRADS_FIRST = 1


def nn(a, b):
    return lax.dot_general(a, b, (((1,), (0,)), ((), ())), preferred_element_type=F32)


def nt(a, b):
    return lax.dot_general(a, b, (((1,), (1,)), ((), ())), preferred_element_type=F32)


def flat(value):
    return value.reshape(-1, value.shape[-1])


def norm_stats(values):
    mean = jnp.mean(values, axis=-1, keepdims=True)
    center = values - mean
    inverse = lax.rsqrt(jnp.mean(center * center, axis=-1, keepdims=True) + EPS)
    return center * inverse, inverse


def norm_pull(grad, values, gain):
    normal, inverse = norm_stats(values)
    scaled = grad * gain
    first = jnp.mean(scaled, axis=-1, keepdims=True)
    second = jnp.mean(scaled * normal, axis=-1, keepdims=True)
    return inverse * (scaled - first - normal * second), normal


def fold_rows(values):
    rows, width = values.shape
    return jnp.sum(values.reshape(rows // 8, 8, width), axis=0)


def score_mask():
    key = lax.broadcasted_iota(jnp.int32, (TILE, TILE), 0)
    query = lax.broadcasted_iota(jnp.int32, (TILE, TILE), 1)
    return (query // PAD == key // PAD) & (key <= query)


def row_loop(rows, body, first=0):
    def once(index, carry):
        index = first + index
        body(pl.ds(pl.multiple_of(index * TILE, TILE), TILE), index)
        return carry

    lax.fori_loop(0, rows // TILE, once, 0)


def half_loop(count, body):
    def once(index, carry):
        body(index)
        return carry

    lax.fori_loop(0, count, once, 0)


def half(index):
    return pl.ds(pl.multiple_of(index * SEG, SEG), SEG)


def spread_rows(patches, series):
    row = lax.broadcasted_iota(jnp.int32, (series * PAD, patches * series), 0)
    col = lax.broadcasted_iota(jnp.int32, (series * PAD, patches * series), 1)
    hit = (lax.rem(row, PAD) * series + lax.div(row, PAD) == col) & (lax.rem(row, PAD) < patches)
    return jnp.where(hit, 1.0, 0.0).astype(BF)


def gather_rows(patches, series):
    row = lax.broadcasted_iota(jnp.int32, (patches * series, series * PAD), 0)
    col = lax.broadcasted_iota(jnp.int32, (patches * series, series * PAD), 1)
    return jnp.where(lax.rem(row, series) * PAD + lax.div(row, series) == col, 1.0, 0.0).astype(BF)


def to_rows(raw, target):
    micro, patches, series, _ = raw.shape
    matrix = spread_rows(patches, series)
    for part in range(micro):
        target[part * series * PAD : (part + 1) * series * PAD, :] = nn(matrix, flat(raw[part])).astype(BF)


def from_rows(source, raw):
    micro, patches, series, width = raw.shape
    matrix = gather_rows(patches, series)
    for part in range(micro):
        rows = source[part * series * PAD : (part + 1) * series * PAD, :]
        raw[part] = nn(matrix, rows).astype(raw.dtype).reshape(patches, series, width)


def norm_in(x, normed, gain, shift):
    def block(rows, _):
        normal, _inv = norm_stats(x[rows, :].astype(F32))
        normed[rows, :] = (normal * gain + shift).astype(BF)

    row_loop(x.shape[0], block)


def project(source, weights, seg, target):
    def one(m):
        target[:, half(m)] = nn(source[...], flat(weights[seg, m])).astype(BF)

    half_loop(weights.shape[1], one)


def attend(queries, keys, values, probs, mixture, first, count):
    mask = score_mask()
    scale = HD ** (-0.5)
    columns = [slice(at, at + HD) for at in range(0, queries.shape[1], HD)]

    def group(rows, _):
        scores = [nt(keys[rows, cols], queries[rows, cols]) * scale for cols in columns]
        scores = [jnp.where(mask, score, -1e30) for score in scores]
        peaks = [jnp.max(score, axis=0, keepdims=True) for score in scores]
        powers = [jnp.exp(score - peak) for score, peak in zip(scores, peaks)]
        inverses = [1.0 / jnp.sum(power, axis=0, keepdims=True) for power in powers]
        shares = [power * inverse for power, inverse in zip(powers, inverses)]
        for cols, share in zip(columns, shares):
            probs[rows, cols] = share
        mixed = [nn(share.astype(BF).T, values[rows, cols]) for share, cols in zip(shares, columns)]
        for cols, part in zip(columns, mixed):
            mixture[rows, cols] = part.astype(BF)

    row_loop(count * TILE, group, first)


def attend_back(queries, keys, values, probs, grad_mix, grad_q, grad_k, grad_v, first, count):
    scale = HD ** (-0.5)
    columns = [slice(at, at + HD) for at in range(0, queries.shape[1], HD)]

    def group(rows, _):
        shares = [probs[rows, cols] for cols in columns]
        grads = [grad_mix[rows, cols] for cols in columns]
        pulls = [nt(values[rows, cols], grad) for cols, grad in zip(columns, grads)]
        back_v = [nn(share.astype(BF), grad) for share, grad in zip(shares, grads)]
        inner = [jnp.sum(pull * share, axis=0, keepdims=True) for pull, share in zip(pulls, shares)]
        lows = [(share * (pull - mean)).astype(BF) for share, pull, mean in zip(shares, pulls, inner)]
        back_k = [nn(low, queries[rows, cols]) * scale for low, cols in zip(lows, columns)]
        back_q = [nn(low.T, keys[rows, cols]) * scale for low, cols in zip(lows, columns)]
        for cols, one, two, three in zip(columns, back_q, back_k, back_v):
            grad_q[rows, cols] = one.astype(BF)
            grad_k[rows, cols] = two.astype(BF)
            grad_v[rows, cols] = three.astype(BF)

    row_loop(count * TILE, group, first)


def back_through(source, weights, seg, total):
    def one(m):
        total[...] += nt(source(m), flat(weights[seg, m]))

    half_loop(weights.shape[1], one)


def feed_up(normed_two, weights, which, m, active, slope):
    hidden = nn(normed_two[...], flat(weights[UPS[which], m]))
    bell = 0.5 + 0.5 * lax.erf(hidden * (0.5**0.5))
    active[which, m] = (hidden * bell).astype(BF)
    density = jnp.exp(-0.5 * hidden * hidden) * 0.3989422804014327
    slope[which, m] = bell + hidden * density


def turn(source, target):
    def block(rows, _):
        target[:, rows] = source[rows, :].T

    row_loop(source.shape[0], block)


def weight_grad(turned, right, target, seg):
    def one(m):
        product = nn(turned[...], right(m)).astype(BF)
        target[seg, m] = product.reshape(target.shape[2:])

    half_loop(target.shape[1], one)


class Place:
    def __init__(self, shape):
        self.nz, self.nx, self.ny = shape
        index = lax.axis_index("dp")
        self.core = lax.rem(index, 2)
        chip = lax.div(index, 2)
        self.at = {"z": lax.div(chip, self.nx), "x": lax.rem(chip, self.nx), "y": lax.axis_index("mp")}
        self.count = {"z": self.nz, "x": self.nx, "y": self.ny}

    def device(self, core=None, **moved):
        at = {**self.at, **moved}
        core = self.core if core is None else core
        return ((at["z"] * self.nx + at["x"]) * 2 + core, at["y"])

    def partner(self):
        return self.device(core=1 - self.core)

    def neighbour(self, dim, step):
        return self.device(**{dim: self.at[dim] + step})

    def barrier(self, dims):
        semaphore = pltpu.get_barrier_semaphore()
        pl.semaphore_signal(semaphore, inc=1, device_id=self.partner(), device_id_type=MESH)
        peers = 1
        for dim in dims:
            for step in (1, -1):
                there = self.at[dim] + step
                valid = (there >= 0) & (there < self.count[dim])
                peers = peers + valid.astype(jnp.int32)

                @pl.when(valid)
                def _(dim=dim, step=step):
                    other = self.neighbour(dim, step)
                    pl.semaphore_signal(semaphore, inc=1, device_id=other, device_id_type=MESH)

        pl.semaphore_wait(semaphore, peers)


def link_slots(count, dims):
    return sum(2 * (count[dim] - 1) for dim in dims)


class Gather:
    def __init__(self, place, buffer, axes, order, sems):
        self.place, self.buffer, self.axes, self.order = place, buffer, axes, order
        self.send, self.recv, self.pass_send, self.pass_recv = sems
        self.rounds = [(dim, t) for dim in order for t in range(place.count[dim] - 1)]
        self.slots = {}
        for dim, t in self.rounds:
            for way in (1, -1):
                self.slots[dim, t, way] = len(self.slots)

    def block(self, dim, position, core):
        done = self.order[: self.order.index(dim)] if dim else ""
        index = []
        for axis in self.axes:
            if axis == dim:
                index.append(position)
            elif axis in done:
                index.append(pl.ds(0, self.place.count[axis]))
            else:
                index.append(self.place.at[axis])
        return self.buffer.at[tuple(index) + (core,)]

    def link(self, dim, t, way, position, device):
        block = self.block(dim, position, self.place.core)
        slot = self.slots[dim, t, way]
        return pltpu.make_async_remote_copy(
            block, block, self.send.at[slot], self.recv.at[slot], device_id=device, device_id_type=MESH
        )

    def hand(self, slot, dim, position, core):
        block = self.block(dim, position, core)
        return pltpu.make_async_remote_copy(
            block,
            block,
            self.pass_send.at[slot],
            self.pass_recv.at[slot],
            device_id=self.place.partner(),
            device_id_type=MESH,
        )

    def sends(self, dim, t):
        here, count = self.place.at[dim], self.place.count[dim]
        yield 1, here - t, (here - t >= 0) & (here < count - 1)
        yield -1, here + t, (here + t < count) & (here > 0)

    def arrivals(self, dim, t):
        here, count = self.place.at[dim], self.place.count[dim]
        yield 1, here - 1 - t, here - 1 - t >= 0
        yield -1, here + 1 + t, here + 1 + t < count

    def start(self):
        self.hand(len(self.slots), "", None, self.place.core).start()
        self.send_round(0)

    def send_round(self, number):
        dim, t = self.rounds[number]
        for way, position, valid in self.sends(dim, t):

            @pl.when(valid)
            def _(way=way, position=position):
                self.link(dim, t, way, position, self.place.neighbour(dim, way)).start()

    def advance(self, number):
        dim, t = self.rounds[number - 1]
        for way, position, valid in self.arrivals(dim, t):

            @pl.when(valid)
            def _(way=way, position=position):
                self.link(dim, t, way, position, self.place.partner()).wait_recv()
                self.hand(self.slots[dim, t, way], dim, position, self.place.core).start()

        if number < len(self.rounds):
            self.send_round(number)

    def steps(self):
        return [self.start] + [functools.partial(self.advance, n + 1) for n in range(len(self.rounds))]

    def finish(self):
        other = 1 - self.place.core
        self.hand(len(self.slots), "", None, other).wait_recv()
        for dim, t in self.rounds:
            for way, position, valid in self.arrivals(dim, t):

                @pl.when(valid)
                def _(dim=dim, t=t, way=way, position=position):
                    self.hand(self.slots[dim, t, way], dim, position, other).wait_recv()

    def drain_hand(self):
        self.hand(len(self.slots), "", None, self.place.core).wait_send()

    def sent(self, dim, t):
        for way, position, valid in self.sends(dim, t):
            yield valid, self.link(dim, t, way, position, self.place.partner())
        for way, position, valid in self.arrivals(dim, t):
            yield valid, self.hand(self.slots[dim, t, way], dim, position, self.place.core)


class Scatter:
    def __init__(self, place, mine, axes, order, inbox, hand_box, sems, both=False):
        self.place, self.mine, self.axes, self.order, self.both = place, mine, axes, order, both
        self.inbox, self.hand_box = inbox, hand_box
        self.send, self.recv = sems
        self.rounds = [(dim, t) for dim in order for t in range(place.count[dim] - 1)]
        self.slots = {}
        for dim, t in self.rounds:
            for way in (1, -1):
                self.slots[dim, t, way] = len(self.slots) + 1

    def own(self, index):
        return index + ((() if self.both else (self.place.core,)))

    def hand(self):
        whole = tuple(pl.ds(0, self.place.count[axis]) for axis in self.axes)
        source = self.mine.at[whole] if self.both else self.mine.at[whole + (1 - self.place.core,)]
        return pltpu.make_async_remote_copy(
            source, self.hand_box, self.send.at[0], self.recv.at[0], device_id=self.place.partner(), device_id_type=MESH
        )

    def start(self):
        self.hand().start()

    def take_hand(self):
        self.hand().wait_recv()
        first = self.place.count[self.axes[0]]
        rest = tuple(pl.ds(0, self.place.count[axis]) for axis in self.axes[1:])
        if self.both:
            self.hand().wait_send()
            self.mine[...] = self.mine[...] + self.hand_box[...]
        else:
            for p in range(first):
                for r in range(self.place.count[self.axes[1]]):
                    index = (p, r) + rest[1:]
                    here = self.mine[index + (self.place.core,)].astype(F32)
                    there = self.hand_box[index].astype(F32)
                    self.mine[index + (self.place.core,)] = (here + there).astype(self.mine.dtype)
        self.send_round(0)

    def block(self, dim, position):
        done = self.order[: self.order.index(dim)]
        index = []
        for axis in self.axes:
            if axis == dim:
                index.append(position)
            elif axis in done:
                index.append(self.place.at[axis])
            else:
                index.append(pl.ds(0, self.place.count[axis]))
        return self.own(tuple(index))

    def link(self, dim, t, way, position, device):
        slot = self.slots[dim, t, way]
        return pltpu.make_async_remote_copy(
            self.mine.at[self.block(dim, position)],
            self.inbox[slot],
            self.send.at[slot],
            self.recv.at[slot],
            device_id=device,
            device_id_type=MESH,
        )

    def sends(self, dim, t):
        here, count = self.place.at[dim], self.place.count[dim]
        yield 1, count - 1 - t + here, (t >= here) & (here < count - 1)
        back = count - 1 - here
        yield -1, t - back, (t >= back) & (here > 0)

    def arrivals(self, dim, t):
        here, count = self.place.at[dim], self.place.count[dim]
        yield 1, count - 2 - t + here, (t >= here - 1) & (here > 0)
        back = count - 1 - here
        yield -1, t + 1 - back, (t >= back - 1) & (here < count - 1)

    def send_round(self, number):
        dim, t = self.rounds[number]
        for way, position, valid in self.sends(dim, t):

            @pl.when(valid)
            def _(way=way, position=position):
                self.link(dim, t, way, position, self.place.neighbour(dim, way)).start()

    def advance(self, number):
        dim, t = self.rounds[number - 1]
        for way, position, valid in self.arrivals(dim, t):

            @pl.when(valid)
            def _(way=way, position=position):
                self.link(dim, t, way, position, self.place.partner()).wait_recv()
                index = self.block(dim, position)
                total = self.mine[index].astype(F32) + self.inbox[self.slots[dim, t, way]][...].astype(F32)
                self.mine[index] = total.astype(self.mine.dtype)

        if number < len(self.rounds):
            self.send_round(number)

    def steps(self):
        later = [functools.partial(self.advance, n + 1) for n in range(len(self.rounds))]
        return [self.start, self.take_hand] + later

    def result(self):
        return self.mine[self.own(tuple(self.place.at[axis] for axis in self.axes))]

    def drain_hand(self):
        if not self.both:
            self.hand().wait_send()

    def sent(self, dim, t):
        for way, position, valid in self.sends(dim, t):
            yield valid, self.link(dim, t, way, position, self.place.partner())


def drain(runs):
    for run in runs:
        run.drain_hand()
    for dim, t in dict.fromkeys(key for run in runs for key in run.rounds):
        groups = [list(run.sent(dim, t)) for run in runs if (dim, t) in run.rounds]
        for same in zip(*groups):

            @pl.when(same[0][0])
            def _(same=same):
                for _valid, copy in same:
                    copy.wait_send()


def inbox_shapes(count, axes, order, block):
    shapes, slots, left = [], {}, dict(count)
    for dim in order:
        left.pop(dim)
        for t in range(count[dim] - 1):
            for way in (1, -1):
                if way == 1 or count[dim] > 2:
                    shapes.append(tuple(count[axis] for axis in axes if axis in left) + block)
                slots[dim, t, way] = len(shapes) - 1
    return shapes, slots


def open_inbox(run, count, axes, order, block, boxes):
    shapes, slots = inbox_shapes(count, axes, order, block)
    for key, slot in run.slots.items():
        run.inbox[slot] = boxes[slots[key]]
    del boxes[: len(shapes)]


def play(plan, comm, pieces):
    plan = list(plan)
    while plan:
        token = plan.pop(0)
        if token >= 0:
            if comm:
                comm[token].pop(0)()
        elif callable(pieces[0]):
            pieces.pop(0)()
        else:
            count, piece, before, after = pieces.pop(0)
            if before:
                before()
            between = [[] for _ in range(count - 1)]
            for spot in range(count - 1):
                while plan[0] >= 0:
                    token = plan.pop(0)
                    if comm:
                        between[spot].append(comm[token].pop(0))
                plan.pop(0)

            def once(index, carry, piece=piece, between=between):
                piece(index)
                for spot, steps in enumerate(between):
                    if steps:

                        @pl.when(index == spot)
                        def _(steps=steps):
                            for step in steps:
                                step()

                return carry

            lax.fori_loop(0, count, once, 0)
            if after:
                after()
    assert not pieces and not any(comm.values())


class Mover:
    def __init__(self, sems):
        self.sems, self.used, self.open = sems, 0, []

    def start(self, source, target):
        copy = pltpu.make_async_copy(source, target, self.sems.at[self.used])
        self.used += 1
        copy.start()
        return copy

    def save(self, source, target):
        self.open.append(self.start(source, target))

    def close(self):
        for copy in self.open:
            copy.wait()


def read_vectors(vectors, tiles):
    nz, nx = tiles.shape[:2]
    pieces = [tiles[z, x, 0] + tiles[z, x, 1] for z in range(nz) for x in range(nx)]
    vectors[...] = jnp.concatenate(pieces, axis=1)


def column_parts(weights):
    wq, wk, wv, wo, wu, wd = weights
    left, right = pl.ds(0, SEG), pl.ds(SEG, SEG)
    return [wq, wk, wv, wo, wu.at[:, left], wu.at[:, right], wd.at[:, left], wd.at[:, right]]


def fill_tile(place, tiles, norms):
    tile = (place.at["z"], place.at["x"], place.core)
    tiles[tile] = jnp.zeros(tiles.shape[3:], F32)
    share = norms[0].shape[1]
    for line, norm in enumerate(norms):
        value = norm[...].astype(F32)
        for core in range(2):

            @pl.when(place.core == core)
            def _(line=line, value=value, core=core):
                tiles[tile + (slice(line, line + 1), slice(core * share, (core + 1) * share))] = value


FWD_OUT = (
    "x", "q", "k", "v", "probs", "mix", "res", "nrm2", "active", "slope", "out", "cot", "gl", "glt", "weight",
    "nrmt",
)
KEPT = len(FWD_OUT)


def forward_kernel(shape, micro, tokens, cotangent, ids, counts, *refs):
    if shape:
        weights, norms, g_out, refs = refs[:6], refs[6:10], refs[10], refs[11:]
    else:
        g_in, vectors_in, refs = refs[0], refs[1], refs[2:]
    if shape:
        vectors, refs = refs[0], refs[1:]
    else:
        vectors = vectors_in
    saved = dict(zip(FWD_OUT, refs[:KEPT]))
    here = dict(zip(FWD_OUT, refs[KEPT : 2 * KEPT]))
    refs = refs[2 * KEPT :]
    raw, nrm, low, total, g, sems = refs[:6]
    mover = Mover(sems)
    y = lax.axis_index("mp")
    take = mover.start(tokens.at[pl.ds(y * micro, micro)], raw)
    x, q, k, v, probs, mix, res, nrm2, active, slope, out, cot, gl, glt, weight, nrmt = (
        here[name] for name in FWD_OUT
    )

    def keep(*names):
        for name in names:
            mover.save(here[name], saved[name])

    comm = {}
    if shape:
        tiles, send, recv, pass_send, pass_recv = refs[6:]
        place = Place(shape)
        spot = (place.at["y"], place.at["z"], place.at["x"], place.core)
        mine = [mover.start(part, g.at[(seg,) + spot]) for seg, part in enumerate(column_parts(weights))]
        fill_tile(place, tiles, norms)
        place.barrier("zxy")
        pick = lambda seg: tuple(sem.at[seg] for sem in (send, recv, pass_send, pass_recv))
        runs, cut = [], len(ORDERS) // 8
        for spot, order in enumerate(ORDERS):
            columns = pl.ds(spot % cut * (SEG // cut), SEG // cut)
            runs.append(Gather(place, g.at[spot // cut, :, :, :, :, :, columns], "yzx", order, pick(spot)))
        runs.append(Gather(place, tiles, "zx", "zx", pick(len(ORDERS))))
        comm = {spot: run.steps() for spot, run in enumerate(runs)}
        waiting = list(mine)

        def begin(spot):
            if waiting[spot // cut] is not None:
                waiting[spot // cut].wait()
                waiting[spot // cut] = None
            runs[spot].start()

        for spot in range(len(ORDERS)):
            comm[spot][0] = functools.partial(begin, spot)

        def have(seg):
            if seg < 8:
                for run in runs[seg * cut : (seg + 1) * cut]:
                    run.finish()
                mover.save(g.at[seg], g_out.at[seg])
            else:
                runs[-1].finish()
                read_vectors(vectors, tiles)

    else:
        loads = [mover.start(g_in.at[seg], g.at[seg]) for seg in range(8)]

        def have(seg):
            if seg < 8:
                loads[seg].wait()

    def spread():
        take.wait()
        to_rows(raw, x)
        keep("x")
        loads_cot.append(mover.start(cotangent.at[pl.ds(y * micro, micro)], raw))
        row_weights(ids, counts, y, micro, weight)

    loads_cot = []

    def weigh():
        loads_cot[0].wait()
        to_rows(raw, cot)

        def block(rows, _):
            gl[rows, :] = (cot[rows, :].astype(F32) * weight[rows, :]).astype(BF)

        row_loop(cot.shape[0], block)
        turn(gl, glt)
        keep("cot", "gl", "glt", "weight")

    def norm_one():
        have(8)
        norm_in(x, nrm, vectors[0:1, :], vectors[1:2, :])
        turn(nrm, nrmt)
        keep("nrmt")

    def head_part(seg, target, name):
        have(seg)
        project(nrm, g, seg, target)
        keep(name)

    third = x.shape[0] // TILE // 3

    def mixing(part):
        attend(q, k, v, probs, mix, part * third, third)

    def project_out():
        keep("probs", "mix")
        have(O)
        res[...] = x[...].astype(F32)
        back_through(lambda m: mix[:, half(m)], g, O, res)
        keep("res")

    def norm_two():
        gain, shift = vectors[2:3, :], vectors[3:4, :]

        def block(rows, _):
            normal, _inv = norm_stats(res[rows, :])
            nrm2[rows, :] = (normal * gain + shift).astype(BF)

        row_loop(x.shape[0], block)
        keep("nrm2")

    def up(which, m):
        feed_up(nrm2, g, which, m, active, slope)

    def keep_up(which):
        mover.save(active.at[which], saved["active"].at[which])
        mover.save(slope.at[which], saved["slope"].at[which])

    def down(which):
        have(DOWNS[which])
        if which == 0:
            total[...] = res[...]
        back_through(lambda m: active[which, m], g, DOWNS[which], total)

    def last():
        low[...] = total[...].astype(BF)
        from_rows(low, out)
        keep("out")

    pieces = [spread, weigh, norm_one]
    pieces += [functools.partial(head_part, *args) for args in ((Q, q, "q"), (K, k, "k"), (V, v, "v"))]
    pieces += [(3, mixing, None, None), project_out, norm_two]
    for which in range(2):
        before, after = functools.partial(have, UPS[which]), functools.partial(keep_up, which)
        pieces.append((2, functools.partial(up, which), before, after))
    pieces += [functools.partial(down, which) for which in range(2)] + [last]
    play(FORWARD_PLAN, comm, pieces)
    if shape:
        drain(runs)
    mover.close()


def row_weights(ids, counts, y, micro, target):
    series = ids.shape[1]
    sums = counts[0]
    for kind in range(1, counts.shape[0]):
        sums = sums + counts[kind]
    mean = jnp.full((PAD, 1), sums.astype(F32), F32) / counts.shape[0]

    def one(index, carry):
        kind = ids[y * micro + lax.div(index, series), lax.rem(index, series)]
        count = counts[kind].astype(F32)
        target[pl.ds(pl.multiple_of(index * PAD, PAD), PAD), :] = 2.0 * mean / (mean + count)
        return carry

    lax.fori_loop(0, micro * series, one, 0)


class Swap:
    def __init__(self, place, mover, sems, ready, source, target):
        self.mover, self.source, self.ready = mover, source, ready
        y, (micro, patches) = place.at["y"], source.shape[:2]
        cut = patches // 2 + 1
        self.spots = [target.at[y * micro + part] for part in range(micro)]
        self.copies = []
        for part in range(micro):
            for piece in (pl.ds(0, cut), pl.ds(cut, patches - cut)):
                slot = 2 * len(self.copies)
                self.copies.append(
                    pltpu.make_async_remote_copy(
                        source.at[part, piece],
                        target.at[y * micro + part, piece],
                        sems.at[slot],
                        sems.at[slot + 1],
                        device_id=place.device(y=1 - y),
                        device_id_type=MESH,
                    )
                )

    def start(self, part):
        if part == 0:
            self.ready()
        self.copies[2 * part].start()
        self.mover.save(self.source.at[part], self.spots[part])

    def steps(self, part):
        return [functools.partial(self.start, part), self.copies[2 * part + 1].start]

    def wait(self):
        for copy in self.copies:
            copy.wait()


def feed_back_kernel(shape, vectors, g_in, active_in, slope_in, nrm2_in, res_in, out_in, cot_in, gl_in, glt_in, weight_in, mix_in, *refs):
    if shape:
        dw_out, gres_out, gm_out, vec, pair, grad_down, refs = refs[:6] + (refs[6:],)
    else:
        dw_out, gres_out, gm_out, vec, refs = refs[:4] + (refs[4:],)
    cot, weight, active, slope, nrm2, res, g, dw, gl, glt, gh, n2t, gn2, gres, mix, gm, sems = refs[:17]
    mover = Mover(sems)
    if shape:
        half_out, hands, send, recv, ysem = refs[17:22]
        boxes = list(refs[22:])
        side = mover.start(out_in, half_out)
    loads = {"glt": mover.start(glt_in, glt), ("active", 0): mover.start(active_in.at[0], active.at[0])}
    loads["gl"] = mover.start(gl_in, gl)
    for which in range(2):
        if which == 1:
            loads["active", which] = mover.start(active_in.at[which], active.at[which])
        loads["d", which] = mover.start(g_in.at[DOWNS[which]], g.at[2 + which])
        loads["slope", which] = mover.start(slope_in.at[which], slope.at[which])
    loads["nrm2"] = mover.start(nrm2_in, nrm2)
    for which in range(2):
        loads["u", which] = mover.start(g_in.at[UPS[which]], g.at[which])
    loads["res"] = mover.start(res_in, res)
    loads["cot"] = mover.start(cot_in, cot)
    loads["mix"] = mover.start(mix_in, mix)
    loads["o"] = mover.start(g_in.at[O], g.at[4])
    loads["weight"] = mover.start(weight_in, weight)
    comm = {}
    if shape:
        place = Place(shape)
        place.barrier("zxy")
        runs = []
        block = (dw.shape[-2], SEG // 2)
        for spot, order in enumerate(FEED_ORDERS):
            columns = pl.ds(spot % 2 * block[1], block[1])
            source = dw.at[2 + spot // 2, :, :, :, :, :, columns]
            run = Scatter(place, source, "yzx", order, {}, hands.at[spot], (send.at[spot], recv.at[spot]))
            open_inbox(run, place.count, "yzx", order, block, boxes)
            runs.append(run)
        swap = Swap(place, mover, ysem, side.wait, half_out, pair)
        comm = {spot: run.steps() for spot, run in enumerate(runs)}
        comm[len(runs)] = swap.steps(0) + swap.steps(1)

    def down_grad(which):
        if which == 0:
            loads["glt"].wait()
        loads["active", which].wait()
        weight_grad(glt, lambda m: active[which, m], dw, 2 + which)
        if not shape:
            mover.save(dw.at[2 + which], dw_out.at[2 + which])

    def hidden_grad(which):
        if which == 0:
            loads["gl"].wait()
        loads["d", which].wait()
        loads["slope", which].wait()

        def one(m):
            pulled = nn(gl[...], flat(g[2 + which, m]))
            gh[which, m] = (pulled * slope[which, m]).astype(BF)

        half_loop(g.shape[1], one)

    def turn_two():
        loads["nrm2"].wait()
        turn(nrm2, n2t)
        gn2[...] = jnp.zeros_like(gn2)

    def up_grad(which):
        weight_grad(n2t, lambda m: gh[which, m], dw, which)
        mover.save(dw.at[which], dw_out.at[which])

    def norm_grad(which):
        loads["u", which].wait()
        back_through(lambda m: gh[which, m], g, which, gn2)

    def last():
        for name in ("res", "cot", "weight"):
            loads[name].wait()
        gain = vectors[2:3, :]
        vec[...] = jnp.zeros_like(vec)

        def block(rows, _):
            grad = gn2[rows, :]
            pulled, normal = norm_pull(grad, res[rows, :], gain)
            vec[0] += fold_rows(grad * normal)
            vec[1] += fold_rows(grad)
            total = cot[rows, :].astype(F32) * weight[rows, :] + pulled
            gres[rows, :] = total
            gl[rows, :] = total.astype(BF)

        row_loop(cot.shape[0], block)
        mover.save(gres, gres_out)

    def mix_grad():
        loads["o"].wait()
        project(gl, g, 4, gm)
        mover.save(gm, gm_out)

    def out_grad():
        loads["mix"].wait()
        weight_grad(glt, lambda m: mix[:, half(m)], dw, 4)
        mover.save(dw.at[4], dw_out.at[4])

    pieces = []
    for which in range(2):
        pieces += [functools.partial(down_grad, which), functools.partial(hidden_grad, which)]
    pieces.append(turn_two)
    for which in range(2):
        pieces += [functools.partial(up_grad, which), functools.partial(norm_grad, which)]
    pieces += [last, mix_grad, lambda: turn(gl, glt), out_grad]
    play(FEED_PLAN, comm, pieces)
    if shape:
        for spot, run in enumerate(runs):
            grad_down[:, spot * block[1] : (spot + 1) * block[1]] = run.result().astype(F32)
        drain(runs)
        swap.wait()
    mover.close()


def vector_tiles(tiles, vec_a, vec_f):
    tiles[...] = jnp.zeros_like(tiles)
    nz, nx = tiles.shape[:2]
    for line, (source, part) in enumerate(((vec_a, 0), (vec_a, 1), (vec_f, 0), (vec_f, 1))):
        row = jnp.sum(source[part], axis=0, keepdims=True)
        for z in range(nz):
            for x in range(nx):
                chip = z * nx + x
                tiles[z, x, line : line + 1, :] = row[:, chip * 128 : (chip + 1) * 128]


BACK_IN = ("gm", "q", "k", "v", "probs", "nrmt", "gres", "x")
KEPT_GRADS = (0, 1, 4)
HALF = SEG // 2
SPOTS = (4 * SEG, 5 * SEG, 3 * SEG, 0, HALF, SEG, SEG + HALF, 2 * SEG, 2 * SEG + HALF)


def attn_back_kernel(shape, vectors, vec_f, g_in, dw_in, *refs):
    given = dict(zip(BACK_IN, refs[:8]))
    refs = refs[8:]
    if shape:
        grad_down, pair, packed, vec_out, refs = refs[:4] + (refs[4:],)
    else:
        dw_out, out, vec, refs = refs[0], refs[1], refs[2], refs[3:]
    here = dict(zip(BACK_IN, refs[:8]))
    g, dw, gal, pulls, raw, sems = refs[8:14]
    mover = Mover(sems)
    loads, comm = {}, {}
    if shape:
        held, tiles, hands, half_hands, vec_hand, ybox, vec, send, recv, ysem = refs[14:24]
        boxes = list(refs[24:])

    def fetch_held(*spots):
        for spot in spots:
            if shape:
                loads["dw", spot] = mover.start(dw_in.at[KEPT_GRADS[spot]], held.at[spot])

    fetch_held(0)
    some = here["gm"].shape[0] // 3
    for part in range(3):
        rows = pl.ds(part * some, some)
        for name in BACK_IN[:5]:
            loads[name, part] = mover.start(given[name].at[rows], here[name].at[rows])
        if part == 0:
            fetch_held(1, 2)
    for name in BACK_IN[5:]:
        loads[name] = mover.start(given[name], here[name])
    for seg in (Q, K, V):
        loads[seg] = mover.start(g_in.at[seg], g.at[seg])
    gm, q, k, v, probs, nrmt, gres, x = (here[name] for name in BACK_IN)
    gn = probs
    if shape:
        place = Place(shape)
        place.barrier("zxy")
        runs = []
        for spot, order in enumerate(BACK_ORDERS):
            sems_of = (send.at[spot], recv.at[spot])
            if spot < 3:
                width, source, hand = SEG, held.at[spot], hands.at[spot]
            else:
                seg, side = (spot - 3) // 2, (spot - 3) % 2
                width, hand = HALF, half_hands.at[spot - 3]
                source = dw.at[seg, :, :, :, :, :, pl.ds(side * HALF, HALF)]
            run = Scatter(place, source, "yzx", order, {}, hand, sems_of)
            open_inbox(run, place.count, "yzx", order, (dw.shape[-2], width), boxes)
            runs.append(run)
        run = Scatter(place, tiles, "zx", "zx", {}, vec_hand, (send.at[9], recv.at[9]), both=True)
        open_inbox(run, {"z": place.nz, "x": place.nx}, "zx", "zx", (8, 128), boxes)
        runs.append(run)
        swap = Swap(place, mover, ysem, lambda: None, raw, pair)
        comm = {spot: run.steps() for spot, run in enumerate(runs)}
        comm[10], comm[11] = swap.steps(0), swap.steps(1)
        for spot in range(3):
            comm[spot][0] = lambda spot=spot: (loads["dw", spot].wait(), runs[spot].start())

    third = gal.shape[0] // TILE // 3
    micro = raw.shape[0]
    share = gal.shape[0] // micro

    def ready():
        vec[...] = jnp.zeros_like(vec)

    def mixing(part):
        for third_of in range(3):

            @pl.when(part == third_of)
            def _(third_of=third_of):
                for name in BACK_IN[:5]:
                    loads[name, third_of].wait()

        attend_back(q, k, v, probs, gm, pulls.at[0], pulls.at[1], pulls.at[2], part * third, third)

    def head_grad(seg):
        weight_grad(nrmt, lambda m: pulls[seg, :, half(m)], dw, seg)

    def token_grad(part):
        rows_of = pl.ds(part * share, share)
        gn[rows_of, :] = jnp.zeros((share, gn.shape[1]), F32)
        if part == 0:
            for name in (Q, K, V, "gres", "x"):
                loads[name].wait()

        def one(index, carry):
            seg, m = lax.div(index, 2), lax.rem(index, 2)
            gn[rows_of, :] += nt(pulls[seg, rows_of, half(m)], flat(g[seg, m]))
            return carry

        lax.fori_loop(0, 6, one, 0)
        gain = vectors[0:1, :]

        def block(rows, _):
            grad = gn[rows, :]
            pulled, normal = norm_pull(grad, x[rows, :].astype(F32), gain)
            vec[0] += fold_rows(grad * normal)
            vec[1] += fold_rows(grad)
            gal[rows, :] = (gres[rows, :] + pulled).astype(BF)

        row_loop(share, block, part * share // TILE)
        patches, series, width = raw.shape[1:]
        turned = nn(gather_rows(patches, series), gal[rows_of, :]).astype(raw.dtype)
        raw[part] = turned.reshape(patches, series, width)

    def spread_vectors():
        if shape:
            vector_tiles(tiles, vec, vec_f)

    def before_heads():
        loads["nrmt"].wait()

    pieces = [ready, (3, mixing, None, None), before_heads]
    parts = [functools.partial(token_grad, part) for part in range(micro)]
    heads = [(3, head_grad, None, None)]
    pieces += heads + parts if GRADS_FIRST else parts + heads
    pieces.insert(len(pieces) - (0 if GRADS_FIRST else 1), spread_vectors)
    play(ATTN_PLAN, comm, pieces)
    if not shape:
        mover.save(raw, out)
        for seg in (Q, K, V):
            mover.save(dw.at[seg], dw_out.at[seg])
    if shape:
        here_tile = tiles.at[place.at["z"], place.at["x"]]
        copy = pltpu.make_async_remote_copy(
            here_tile, ybox, ysem.at[8], ysem.at[9], device_id=place.device(y=1 - place.at["y"]), device_id_type=MESH
        )
        copy.start()
        packed[:, 6 * SEG :] = grad_down[...]
        for spot, column in enumerate(SPOTS):
            width = SEG if spot < 3 else HALF
            packed[:, column : column + width] = runs[spot].result().astype(F32)
        drain(runs)
        copy.wait()
        vec_out[...] = tiles[place.at["z"], place.at["x"]] + ybox[...]
        swap.wait()
    mover.close()


def shape_of(shape, dtype):
    return jax.ShapeDtypeStruct(shape, dtype)


IN_VMEM = pl.BlockSpec(memory_space=pltpu.VMEM)
IN_SMEM = pl.BlockSpec(memory_space=pltpu.SMEM)
ANYWHERE = pl.BlockSpec(memory_space=pl.ANY)
DMA = pltpu.SemaphoreType.DMA


def call(body, outs, ins, out_specs, scratch, name, collective=None):
    params = {"vmem_limit_bytes": VMEM_LIMIT}
    if collective is not None:
        params.update(collective_id=collective, has_side_effects=True)
    return pl.pallas_call(
        body,
        out_shape=outs,
        in_specs=ins,
        out_specs=out_specs,
        scratch_shapes=scratch,
        compiler_params=pltpu.CompilerParams(**params),
        name=name,
    )


def vmem(like):
    return pltpu.VMEM(like.shape, like.dtype)


def forward(shape, micro, tokens, cotangent, ids, counts, weights, norms, g_in=None, vectors_in=None):
    _, patches, series, width = tokens.shape
    rows = micro * series * PAD
    full = g_in.shape if shape is None else (8, shape[2], shape[0], shape[1], 2, weights[0].shape[0], SEG)
    low, high = shape_of((rows, width), BF), shape_of((rows, width), F32)
    wide = (2, full[1], rows, SEG)
    raw = shape_of((micro, patches, series, width), BF)
    kinds = {name: low for name in FWD_OUT}
    kinds.update(
        probs=high,
        res=high,
        active=shape_of(wide, BF),
        slope=shape_of(wide, F32),
        out=raw,
        glt=shape_of((width, rows), BF),
        nrmt=shape_of((width, rows), BF),
        weight=shape_of((rows, 1), F32),
    )
    saved = tuple(kinds[name] for name in FWD_OUT)
    scratch = [vmem(kind) for kind in saved] + [vmem(raw), vmem(low), vmem(low), vmem(high), pltpu.VMEM(full, BF), DMA((64,))]
    if shape is None:
        results = call(
            functools.partial(forward_kernel, None, micro),
            saved,
            [ANYWHERE, ANYWHERE, IN_SMEM, IN_SMEM, ANYWHERE, IN_VMEM],
            (ANYWHERE,) * KEPT,
            scratch,
            "forward",
        )(tokens, cotangent, ids, counts, g_in, vectors_in)
        return g_in, vectors_in, dict(zip(FWD_OUT, results))
    count = dict(zip("zxy", shape))
    slots = link_slots(count, "zxy")
    scratch += [pltpu.VMEM(shape[:2] + (2, 8, 128), F32)]
    runs = len(ORDERS) + 1
    scratch += [DMA((runs, slots)), DMA((runs, slots)), DMA((runs, slots + 1)), DMA((runs, slots + 1))]
    results = call(
        functools.partial(forward_kernel, shape, micro),
        (shape_of(full, BF), shape_of((8, width), F32)) + saved,
        [ANYWHERE, ANYWHERE, IN_SMEM, IN_SMEM] + [ANYWHERE] * 6 + [IN_VMEM] * 4,
        (ANYWHERE, IN_VMEM) + (ANYWHERE,) * KEPT,
        scratch,
        "forward",
        0,
    )(tokens, cotangent, ids, counts, *weights, *norms)
    return results[0], results[1], dict(zip(FWD_OUT, results[2:]))


def scatter_scratch(segs, part, count, orders, cols=SEG):
    rows = part.shape[-2]
    slots = link_slots(count, "zxy") + 1
    boxes = []
    for order in orders:
        boxes += [pltpu.VMEM(s, BF) for s in inbox_shapes(count, "yzx", order, (rows, cols))[0]]
    hands = pltpu.VMEM((len(orders),) + part.shape[1:4] + (rows, cols), BF)
    return hands, [DMA((segs, slots)), DMA((segs, slots))], boxes


def pair_of(raw, ny):
    return shape_of((ny * raw.shape[0],) + raw.shape[1:], BF)


def feed_back(shape, vectors, g, kept):
    low, high, raw = kept["x"], kept["res"], kept["out"]
    rows, width = low.shape
    part = shape_of((5,) + g.shape[1:], BF)
    turned = pltpu.VMEM((width, rows), BF)
    scratch = [
        vmem(low),
        pltpu.VMEM((rows, 1), F32),
        vmem(kept["active"]),
        vmem(kept["slope"]),
        vmem(low),
        vmem(high),
        vmem(part),
        vmem(part),
        vmem(low),
        turned,
        vmem(kept["active"]),
        turned,
        vmem(high),
        vmem(high),
        vmem(low),
        vmem(low),
        DMA((32,)),
    ]
    given = [g] + [kept[name] for name in ("active", "slope", "nrm2", "res", "out", "cot", "gl", "glt", "weight", "mix")]
    outs = [part, shape_of(high.shape, F32), shape_of(low.shape, BF), shape_of((2, 8, width), F32)]
    specs = [ANYWHERE, ANYWHERE, ANYWHERE, IN_VMEM]
    if shape:
        count = dict(zip("zxy", shape))
        hands, sems, boxes = scatter_scratch(len(FEED_ORDERS), part, count, FEED_ORDERS, SEG // 2)
        scratch += [vmem(raw), hands] + sems + [DMA((8,))] + boxes
        outs += [pair_of(raw, shape[2]), shape_of((part.shape[-2], 2 * SEG), F32)]
        specs += [ANYWHERE, IN_VMEM]
    return call(
        functools.partial(feed_back_kernel, shape),
        tuple(outs),
        [IN_VMEM] + [ANYWHERE] * 11,
        tuple(specs),
        scratch,
        "feed_back",
        1 if shape else None,
    )(vectors, *given)


def attn_back(shape, vectors, vec_f, g, dw_in, kept, grad_down=None):
    low, raw = kept["x"], kept["out"]
    width = low.shape[1]
    part = shape_of((3,) + g.shape[1:], BF)
    scratch = [vmem(kept[name]) for name in BACK_IN]
    scratch += [vmem(part), vmem(part), vmem(low), pltpu.VMEM((3,) + low.shape, BF), vmem(raw), DMA((32,))]
    vec = shape_of((2, 8, width), F32)
    if shape:
        nz, nx, ny = shape
        count = dict(zip("zxy", shape))
        share = part.shape[-2]
        outs = [pair_of(raw, ny), shape_of((share, 8 * SEG), F32), shape_of((8, 128), F32)]
        specs = [ANYWHERE] + [IN_VMEM] * 2
        hands, sems, boxes = scatter_scratch(10, part, count, BACK_ORDERS[:3])
        half_hands, _, more = scatter_scratch(10, part, count, BACK_ORDERS[3:], HALF)
        boxes += more
        tiles = pltpu.VMEM((nz, nx, 8, 128), F32)
        scratch += [vmem(part), tiles, hands, half_hands, tiles, pltpu.VMEM((8, 128), F32), vmem(vec)]
        scratch += sems + [DMA((10,))] + boxes
        scratch += [pltpu.VMEM(s, F32) for s in inbox_shapes({"z": nz, "x": nx}, "zx", "zx", (8, 128))[0]]
    else:
        outs, specs = [part, raw, vec], [ANYWHERE, ANYWHERE, IN_VMEM]
        outs[1] = shape_of(raw.shape, BF)
    return call(
        functools.partial(attn_back_kernel, shape),
        tuple(outs),
        [IN_VMEM] * 2 + [ANYWHERE] * 10 + ([IN_VMEM] if shape else []),
        tuple(specs),
        scratch,
        "attn_back",
        2 if shape else None,
    )(vectors, vec_f, g, dw_in, *(kept[name] for name in BACK_IN), *((grad_down,) if shape else ()))


def chip_grid(chips):
    nx = 1
    while (nx * 2) ** 2 <= chips:
        nx *= 2
    return chips // nx, nx


def body(counts_of, tokens, cotangent, domain_ids, domain_counts, *params):
    weights, norms = params[:6], params[6:]
    n_dp, n_mp = counts_of
    micro = tokens.shape[0] // n_mp
    width = tokens.shape[3]
    share = width // n_dp
    y = lax.axis_index("mp")
    linked = n_mp == 2 and share * 2 == TILE
    flip = lambda array: jnp.transpose(array, (0, 2, 1, 3))
    x, cot = flip(tokens), flip(cotangent)
    if linked:
        shape = chip_grid(n_dp // 2) + (n_mp,)
        g, vectors, kept = forward(shape, micro, x, cot, domain_ids, domain_counts, weights, [norm.reshape(1, -1) for norm in norms])
    else:
        shards = jnp.stack(
            weights[:4] + tuple(w[:, i * SEG : (i + 1) * SEG] for w in weights[4:] for i in range(2))
        )
        g = lax.all_gather(lax.all_gather(shards, "dp", axis=1, tiled=True), "mp", axis=1)
        vectors = lax.all_gather(jnp.stack(norms), "dp", axis=1, tiled=True).astype(F32)
        vectors = jnp.pad(vectors, ((0, 4), (0, 0)))
        g, vectors, kept = forward(None, micro, x, cot, domain_ids, domain_counts, None, None, g, vectors)
    shape = shape if linked else None
    results = feed_back(shape, vectors, g, kept)
    dw_f, gres, gm, vec_f = results[:4]
    kept = {**kept, "gres": gres, "gm": gm}
    if linked:
        out, grad_down = results[4:]
        grad_tokens, packed, vec = attn_back(shape, vectors, vec_f, g, dw_f, kept, grad_down)
        cuts = [0, SEG, 2 * SEG, 3 * SEG, 4 * SEG, 6 * SEG, 8 * SEG]
        grads = [packed[:, start:stop] for start, stop in zip(cuts, cuts[1:])]
        core = lax.rem(lax.axis_index("dp"), 2)
        vec = lax.dynamic_slice(vec, (0, core * share), (4, share))
    else:
        dw_a, low_tokens, vec_a = attn_back(shape, vectors, vec_f, g, dw_f, kept)
        dw = jnp.concatenate((dw_a, dw_f[4:], dw_f[:4])).astype(F32)
        dw = lax.psum_scatter(lax.psum_scatter(dw, "mp", scatter_dimension=1), "dp", scatter_dimension=1, tiled=True)
        grads = [dw[0], dw[1], dw[2], dw[3]]
        grads += [jnp.concatenate((dw[a], dw[b]), axis=1) for a, b in (UPS, DOWNS)]
        vec = jnp.concatenate((jnp.sum(vec_a, axis=1), jnp.sum(vec_f, axis=1)))
        vec = lax.psum_scatter(lax.psum(vec, "mp"), "dp", scatter_dimension=1, tiled=True)
        out = lax.all_gather(kept["out"], "mp", axis=0, tiled=True)
        grad_tokens = lax.all_gather(low_tokens, "mp", axis=0, tiled=True)
    return (flip(out), flip(grad_tokens.astype(F32)), *grads, vec[0], vec[1], vec[2], vec[3])


def solution(mesh):
    rows, matrix, vector = P(None, "dp", None, None), P("dp", "mp"), P("dp")
    in_specs = (rows, rows, P(None, "dp"), P()) + (matrix,) * 6 + (vector,) * 4
    out_specs = (rows, rows) + (matrix,) * 6 + (vector,) * 4
    run = functools.partial(body, (mesh.shape["dp"], mesh.shape["mp"]))
    return jax.shard_map(run, mesh=mesh, in_specs=in_specs, out_specs=out_specs, check_vma=False)
```

```python
import functools

import jax
import jax.numpy as jnp
from jax import lax
from jax.experimental import pallas as pl
from jax.experimental.pallas import tpu as pltpu
from jax.sharding import PartitionSpec as P

BF = jnp.bfloat16
F32 = jnp.float32
HD = 128
SEG = 512
TILE = 128
PAD = 16
EPS = 1e-05
MESH = pl.DeviceIdType.MESH
VMEM_LIMIT = 62 * 1024 * 1024

Q, K, V, O, U0, U1, D0, D1 = range(8)
UPS = (U0, U1)
DOWNS = (D0, D1)
ORDERS = ("zxy", "zyx", "yxz", "zxy", "zyx", "zxy", "yzx", "xyz")
BACK_ORDERS = ("zxy", "xzy", "yxz", "xzy", "xyz", "xzy", "yxz", "xzy", "xzy")
FEED_ORDERS = ("zxy", "zxy", "xzy", "xzy")

FORWARD_PLAN = (
    0, 1, 2, 3, 7, 0, 8, 6, 1, 2, -1, 0, 8, 0, 3, 7, 1, 4, 8, 3, 1, 8, 6, 5,
    4, 2, 3, 0, 4, 1, 5, -1, 5, 6, 2, 8, 4, 0, 5, 3, -1, 4, 2, -1, 6, 1, 7, 2,
    -1, 5, -1, 3, 6, -1, -1, 4, 7, -1, -1, -1, -1, 7, 5, -1, -1, 6, -1, 7, -1, -1, -1,
)
FEED_PLAN = (
    4, 4, -1, 0, -1, 1, 0, 4, -1, 2, 3, 4, 1, 3, 0, -1, 2, -1, 1, -1, 0, -1, 3, 1,
    -1, -1, 2, 0, 3, -1, 1, 0, 2, -1, 3, -1, 2, 1, -1, 3, 2, 1, 3, 0, 2,
)
ATTN_PLAN = (
    2, 0, 1, -1, 2, 1, -1, 0, -1, -1, -1, -1, -1, 4, 6, -1, 6, 0, 4, 8, -1, 10, 1, 8,
    5, 0, 7, 4, 5, 1, -1, 3, 8, 11, 3, 4, 1, 7, 11, 4, 6, 8, 2, -1, 5, 1, 9, 3,
    9, 9, 10, 9, 5, 3, 7, 7, 5, 6, 6, 8, 0, 1, 5, 3, 2, 7, 9, 2, 8, 3, 0, 4,
    7, 6, 5, 2, 4, 9, 6, 8, 3, 0, 7, 2,
)
GRADS_FIRST = 1


def nn(a, b):
    return lax.dot_general(a, b, (((1,), (0,)), ((), ())), preferred_element_type=F32)


def nt(a, b):
    return lax.dot_general(a, b, (((1,), (1,)), ((), ())), preferred_element_type=F32)


def flat(value):
    return value.reshape(-1, value.shape[-1])


def norm_stats(values):
    mean = jnp.mean(values, axis=-1, keepdims=True)
    center = values - mean
    inverse = lax.rsqrt(jnp.mean(center * center, axis=-1, keepdims=True) + EPS)
    return center * inverse, inverse


def norm_pull(grad, values, gain):
    normal, inverse = norm_stats(values)
    scaled = grad * gain
    first = jnp.mean(scaled, axis=-1, keepdims=True)
    second = jnp.mean(scaled * normal, axis=-1, keepdims=True)
    return inverse * (scaled - first - normal * second), normal


def fold_rows(values):
    rows, width = values.shape
    return jnp.sum(values.reshape(rows // 8, 8, width), axis=0)


def score_mask():
    key = lax.broadcasted_iota(jnp.int32, (TILE, TILE), 0)
    query = lax.broadcasted_iota(jnp.int32, (TILE, TILE), 1)
    return (query // PAD == key // PAD) & (key <= query)


def row_loop(rows, body, first=0):
    def once(index, carry):
        index = first + index
        body(pl.ds(pl.multiple_of(index * TILE, TILE), TILE), index)
        return carry

    lax.fori_loop(0, rows // TILE, once, 0)


def half_loop(count, body):
    def once(index, carry):
        body(index)
        return carry

    lax.fori_loop(0, count, once, 0)


def half(index):
    return pl.ds(pl.multiple_of(index * SEG, SEG), SEG)


def spread_rows(patches, series):
    row = lax.broadcasted_iota(jnp.int32, (series * PAD, patches * series), 0)
    col = lax.broadcasted_iota(jnp.int32, (series * PAD, patches * series), 1)
    hit = (lax.rem(row, PAD) * series + lax.div(row, PAD) == col) & (lax.rem(row, PAD) < patches)
    return jnp.where(hit, 1.0, 0.0).astype(BF)


def gather_rows(patches, series):
    row = lax.broadcasted_iota(jnp.int32, (patches * series, series * PAD), 0)
    col = lax.broadcasted_iota(jnp.int32, (patches * series, series * PAD), 1)
    return jnp.where(lax.rem(row, series) * PAD + lax.div(row, series) == col, 1.0, 0.0).astype(BF)


def to_rows(raw, target):
    micro, patches, series, _ = raw.shape
    matrix = spread_rows(patches, series)
    for part in range(micro):
        target[part * series * PAD : (part + 1) * series * PAD, :] = nn(matrix, flat(raw[part])).astype(BF)


def from_rows(source, raw):
    micro, patches, series, width = raw.shape
    matrix = gather_rows(patches, series)
    for part in range(micro):
        rows = source[part * series * PAD : (part + 1) * series * PAD, :]
        raw[part] = nn(matrix, rows).astype(raw.dtype).reshape(patches, series, width)


def norm_in(x, normed, gain, shift):
    def block(rows, _):
        normal, _inv = norm_stats(x[rows, :].astype(F32))
        normed[rows, :] = (normal * gain + shift).astype(BF)

    row_loop(x.shape[0], block)


def project(source, weights, seg, target):
    def one(m):
        target[:, half(m)] = nn(source[...], flat(weights[seg, m])).astype(BF)

    half_loop(weights.shape[1], one)


def attend(queries, keys, values, probs, mixture, first, count):
    mask = score_mask()
    scale = HD ** (-0.5)
    columns = [slice(at, at + HD) for at in range(0, queries.shape[1], HD)]

    def group(rows, _):
        scores = [nt(keys[rows, cols], queries[rows, cols]) * scale for cols in columns]
        scores = [jnp.where(mask, score, -1e30) for score in scores]
        peaks = [jnp.max(score, axis=0, keepdims=True) for score in scores]
        powers = [jnp.exp(score - peak) for score, peak in zip(scores, peaks)]
        inverses = [1.0 / jnp.sum(power, axis=0, keepdims=True) for power in powers]
        shares = [power * inverse for power, inverse in zip(powers, inverses)]
        for cols, share in zip(columns, shares):
            probs[rows, cols] = share
        mixed = [nn(share.astype(BF).T, values[rows, cols]) for share, cols in zip(shares, columns)]
        for cols, part in zip(columns, mixed):
            mixture[rows, cols] = part.astype(BF)

    row_loop(count * TILE, group, first)


def attend_back(queries, keys, values, probs, grad_mix, grad_q, grad_k, grad_v, first, count):
    scale = HD ** (-0.5)
    columns = [slice(at, at + HD) for at in range(0, queries.shape[1], HD)]

    def group(rows, _):
        shares = [probs[rows, cols] for cols in columns]
        grads = [grad_mix[rows, cols] for cols in columns]
        pulls = [nt(values[rows, cols], grad) for cols, grad in zip(columns, grads)]
        back_v = [nn(share.astype(BF), grad) for share, grad in zip(shares, grads)]
        inner = [jnp.sum(pull * share, axis=0, keepdims=True) for pull, share in zip(pulls, shares)]
        lows = [(share * (pull - mean)).astype(BF) for share, pull, mean in zip(shares, pulls, inner)]
        back_k = [nn(low, queries[rows, cols]) * scale for low, cols in zip(lows, columns)]
        back_q = [nn(low.T, keys[rows, cols]) * scale for low, cols in zip(lows, columns)]
        for cols, one, two, three in zip(columns, back_q, back_k, back_v):
            grad_q[rows, cols] = one.astype(BF)
            grad_k[rows, cols] = two.astype(BF)
            grad_v[rows, cols] = three.astype(BF)

    row_loop(count * TILE, group, first)


def back_through(source, weights, seg, total):
    def one(m):
        total[...] += nt(source(m), flat(weights[seg, m]))

    half_loop(weights.shape[1], one)


def feed_up(normed_two, weights, which, m, active, slope):
    hidden = nn(normed_two[...], flat(weights[UPS[which], m]))
    bell = 0.5 + 0.5 * lax.erf(hidden * (0.5**0.5))
    active[which, m] = (hidden * bell).astype(BF)
    density = jnp.exp(-0.5 * hidden * hidden) * 0.3989422804014327
    slope[which, m] = bell + hidden * density


def turn(source, target):
    def block(rows, _):
        target[:, rows] = source[rows, :].T

    row_loop(source.shape[0], block)


def weight_grad(turned, right, target, seg):
    def one(m):
        product = nn(turned[...], right(m)).astype(BF)
        target[seg, m] = product.reshape(target.shape[2:])

    half_loop(target.shape[1], one)


class Place:
    def __init__(self, shape):
        self.nz, self.nx, self.ny = shape
        index = lax.axis_index("dp")
        self.core = lax.rem(index, 2)
        chip = lax.div(index, 2)
        self.at = {"z": lax.div(chip, self.nx), "x": lax.rem(chip, self.nx), "y": lax.axis_index("mp")}
        self.count = {"z": self.nz, "x": self.nx, "y": self.ny}

    def device(self, core=None, **moved):
        at = {**self.at, **moved}
        core = self.core if core is None else core
        return ((at["z"] * self.nx + at["x"]) * 2 + core, at["y"])

    def partner(self):
        return self.device(core=1 - self.core)

    def neighbour(self, dim, step):
        return self.device(**{dim: self.at[dim] + step})

    def barrier(self, dims):
        semaphore = pltpu.get_barrier_semaphore()
        pl.semaphore_signal(semaphore, inc=1, device_id=self.partner(), device_id_type=MESH)
        peers = 1
        for dim in dims:
            for step in (1, -1):
                there = self.at[dim] + step
                valid = (there >= 0) & (there < self.count[dim])
                peers = peers + valid.astype(jnp.int32)

                @pl.when(valid)
                def _(dim=dim, step=step):
                    other = self.neighbour(dim, step)
                    pl.semaphore_signal(semaphore, inc=1, device_id=other, device_id_type=MESH)

        pl.semaphore_wait(semaphore, peers)


def link_slots(count, dims):
    return sum(2 * (count[dim] - 1) for dim in dims)


class Gather:
    def __init__(self, place, buffer, axes, order, sems):
        self.place, self.buffer, self.axes, self.order = place, buffer, axes, order
        self.send, self.recv, self.pass_send, self.pass_recv = sems
        self.rounds = [(dim, t) for dim in order for t in range(place.count[dim] - 1)]
        self.slots = {}
        for dim, t in self.rounds:
            for way in (1, -1):
                self.slots[dim, t, way] = len(self.slots)

    def block(self, dim, position, core):
        done = self.order[: self.order.index(dim)] if dim else ""
        index = []
        for axis in self.axes:
            if axis == dim:
                index.append(position)
            elif axis in done:
                index.append(pl.ds(0, self.place.count[axis]))
            else:
                index.append(self.place.at[axis])
        return self.buffer.at[tuple(index) + (core,)]

    def link(self, dim, t, way, position, device):
        block = self.block(dim, position, self.place.core)
        slot = self.slots[dim, t, way]
        return pltpu.make_async_remote_copy(
            block, block, self.send.at[slot], self.recv.at[slot], device_id=device, device_id_type=MESH
        )

    def hand(self, slot, dim, position, core):
        block = self.block(dim, position, core)
        return pltpu.make_async_remote_copy(
            block,
            block,
            self.pass_send.at[slot],
            self.pass_recv.at[slot],
            device_id=self.place.partner(),
            device_id_type=MESH,
        )

    def sends(self, dim, t):
        here, count = self.place.at[dim], self.place.count[dim]
        yield 1, here - t, (here - t >= 0) & (here < count - 1)
        yield -1, here + t, (here + t < count) & (here > 0)

    def arrivals(self, dim, t):
        here, count = self.place.at[dim], self.place.count[dim]
        yield 1, here - 1 - t, here - 1 - t >= 0
        yield -1, here + 1 + t, here + 1 + t < count

    def start(self):
        self.hand(len(self.slots), "", None, self.place.core).start()
        self.send_round(0)

    def send_round(self, number):
        dim, t = self.rounds[number]
        for way, position, valid in self.sends(dim, t):

            @pl.when(valid)
            def _(way=way, position=position):
                self.link(dim, t, way, position, self.place.neighbour(dim, way)).start()

    def advance(self, number):
        dim, t = self.rounds[number - 1]
        for way, position, valid in self.arrivals(dim, t):

            @pl.when(valid)
            def _(way=way, position=position):
                self.link(dim, t, way, position, self.place.partner()).wait_recv()
                self.hand(self.slots[dim, t, way], dim, position, self.place.core).start()

        if number < len(self.rounds):
            self.send_round(number)

    def steps(self):
        return [self.start] + [functools.partial(self.advance, n + 1) for n in range(len(self.rounds))]

    def finish(self):
        other = 1 - self.place.core
        self.hand(len(self.slots), "", None, other).wait_recv()
        for dim, t in self.rounds:
            for way, position, valid in self.arrivals(dim, t):

                @pl.when(valid)
                def _(dim=dim, t=t, way=way, position=position):
                    self.hand(self.slots[dim, t, way], dim, position, other).wait_recv()

    def drain_hand(self):
        self.hand(len(self.slots), "", None, self.place.core).wait_send()

    def sent(self, dim, t):
        for way, position, valid in self.sends(dim, t):
            yield valid, self.link(dim, t, way, position, self.place.partner())
        for way, position, valid in self.arrivals(dim, t):
            yield valid, self.hand(self.slots[dim, t, way], dim, position, self.place.core)


class Scatter:
    def __init__(self, place, mine, axes, order, inbox, hand_box, sems, both=False):
        self.place, self.mine, self.axes, self.order, self.both = place, mine, axes, order, both
        self.inbox, self.hand_box = inbox, hand_box
        self.send, self.recv = sems
        self.rounds = [(dim, t) for dim in order for t in range(place.count[dim] - 1)]
        self.slots = {}
        for dim, t in self.rounds:
            for way in (1, -1):
                self.slots[dim, t, way] = len(self.slots) + 1

    def own(self, index):
        return index + ((() if self.both else (self.place.core,)))

    def hand(self):
        whole = tuple(pl.ds(0, self.place.count[axis]) for axis in self.axes)
        source = self.mine.at[whole] if self.both else self.mine.at[whole + (1 - self.place.core,)]
        return pltpu.make_async_remote_copy(
            source, self.hand_box, self.send.at[0], self.recv.at[0], device_id=self.place.partner(), device_id_type=MESH
        )

    def start(self):
        self.hand().start()

    def take_hand(self):
        self.hand().wait_recv()
        first = self.place.count[self.axes[0]]
        rest = tuple(pl.ds(0, self.place.count[axis]) for axis in self.axes[1:])
        if self.both:
            self.hand().wait_send()
            self.mine[...] = self.mine[...] + self.hand_box[...]
        else:
            for p in range(first):
                for r in range(self.place.count[self.axes[1]]):
                    index = (p, r) + rest[1:]
                    here = self.mine[index + (self.place.core,)].astype(F32)
                    there = self.hand_box[index].astype(F32)
                    self.mine[index + (self.place.core,)] = (here + there).astype(self.mine.dtype)
        self.send_round(0)

    def block(self, dim, position):
        done = self.order[: self.order.index(dim)]
        index = []
        for axis in self.axes:
            if axis == dim:
                index.append(position)
            elif axis in done:
                index.append(self.place.at[axis])
            else:
                index.append(pl.ds(0, self.place.count[axis]))
        return self.own(tuple(index))

    def link(self, dim, t, way, position, device):
        slot = self.slots[dim, t, way]
        return pltpu.make_async_remote_copy(
            self.mine.at[self.block(dim, position)],
            self.inbox[slot],
            self.send.at[slot],
            self.recv.at[slot],
            device_id=device,
            device_id_type=MESH,
        )

    def sends(self, dim, t):
        here, count = self.place.at[dim], self.place.count[dim]
        yield 1, count - 1 - t + here, (t >= here) & (here < count - 1)
        back = count - 1 - here
        yield -1, t - back, (t >= back) & (here > 0)

    def arrivals(self, dim, t):
        here, count = self.place.at[dim], self.place.count[dim]
        yield 1, count - 2 - t + here, (t >= here - 1) & (here > 0)
        back = count - 1 - here
        yield -1, t + 1 - back, (t >= back - 1) & (here < count - 1)

    def send_round(self, number):
        dim, t = self.rounds[number]
        for way, position, valid in self.sends(dim, t):

            @pl.when(valid)
            def _(way=way, position=position):
                self.link(dim, t, way, position, self.place.neighbour(dim, way)).start()

    def advance(self, number):
        dim, t = self.rounds[number - 1]
        for way, position, valid in self.arrivals(dim, t):

            @pl.when(valid)
            def _(way=way, position=position):
                self.link(dim, t, way, position, self.place.partner()).wait_recv()
                index = self.block(dim, position)
                total = self.mine[index].astype(F32) + self.inbox[self.slots[dim, t, way]][...].astype(F32)
                self.mine[index] = total.astype(self.mine.dtype)

        if number < len(self.rounds):
            self.send_round(number)

    def steps(self):
        later = [functools.partial(self.advance, n + 1) for n in range(len(self.rounds))]
        return [self.start, self.take_hand] + later

    def result(self):
        return self.mine[self.own(tuple(self.place.at[axis] for axis in self.axes))]

    def drain_hand(self):
        if not self.both:
            self.hand().wait_send()

    def sent(self, dim, t):
        for way, position, valid in self.sends(dim, t):
            yield valid, self.link(dim, t, way, position, self.place.partner())


def drain(runs):
    for run in runs:
        run.drain_hand()
    for dim, t in dict.fromkeys(key for run in runs for key in run.rounds):
        groups = [list(run.sent(dim, t)) for run in runs if (dim, t) in run.rounds]
        for same in zip(*groups):

            @pl.when(same[0][0])
            def _(same=same):
                for _valid, copy in same:
                    copy.wait_send()


def inbox_shapes(count, axes, order, block):
    shapes, slots, left = [], {}, dict(count)
    for dim in order:
        left.pop(dim)
        for t in range(count[dim] - 1):
            for way in (1, -1):
                if way == 1 or count[dim] > 2:
                    shapes.append(tuple(count[axis] for axis in axes if axis in left) + block)
                slots[dim, t, way] = len(shapes) - 1
    return shapes, slots


def open_inbox(run, count, axes, order, block, boxes):
    shapes, slots = inbox_shapes(count, axes, order, block)
    for key, slot in run.slots.items():
        run.inbox[slot] = boxes[slots[key]]
    del boxes[: len(shapes)]


def play(plan, comm, pieces):
    plan = list(plan)
    while plan:
        token = plan.pop(0)
        if token >= 0:
            if comm:
                comm[token].pop(0)()
        elif callable(pieces[0]):
            pieces.pop(0)()
        else:
            count, piece, before, after = pieces.pop(0)
            if before:
                before()
            between = [[] for _ in range(count - 1)]
            for spot in range(count - 1):
                while plan[0] >= 0:
                    token = plan.pop(0)
                    if comm:
                        between[spot].append(comm[token].pop(0))
                plan.pop(0)

            def once(index, carry, piece=piece, between=between):
                piece(index)
                for spot, steps in enumerate(between):
                    if steps:

                        @pl.when(index == spot)
                        def _(steps=steps):
                            for step in steps:
                                step()

                return carry

            lax.fori_loop(0, count, once, 0)
            if after:
                after()
    assert not pieces and not any(comm.values())


class Mover:
    def __init__(self, sems):
        self.sems, self.used, self.open = sems, 0, []

    def start(self, source, target):
        copy = pltpu.make_async_copy(source, target, self.sems.at[self.used])
        self.used += 1
        copy.start()
        return copy

    def save(self, source, target):
        self.open.append(self.start(source, target))

    def close(self):
        for copy in self.open:
            copy.wait()


def read_vectors(vectors, tiles):
    nz, nx = tiles.shape[:2]
    pieces = [tiles[z, x, 0] + tiles[z, x, 1] for z in range(nz) for x in range(nx)]
    vectors[...] = jnp.concatenate(pieces, axis=1)


def column_parts(weights):
    wq, wk, wv, wo, wu, wd = weights
    left, right = pl.ds(0, SEG), pl.ds(SEG, SEG)
    return [wq, wk, wv, wo, wu.at[:, left], wu.at[:, right], wd.at[:, left], wd.at[:, right]]


def fill_tile(place, tiles, norms):
    tile = (place.at["z"], place.at["x"], place.core)
    tiles[tile] = jnp.zeros(tiles.shape[3:], F32)
    share = norms[0].shape[1]
    for line, norm in enumerate(norms):
        value = norm[...].astype(F32)
        for core in range(2):

            @pl.when(place.core == core)
            def _(line=line, value=value, core=core):
                tiles[tile + (slice(line, line + 1), slice(core * share, (core + 1) * share))] = value


FWD_OUT = (
    "x", "q", "k", "v", "probs", "mix", "res", "nrm2", "active", "slope", "out", "cot", "gl", "glt", "weight",
    "nrmt",
)
KEPT = len(FWD_OUT)


def forward_kernel(shape, micro, tokens, cotangent, ids, counts, *refs):
    if shape:
        weights, norms, g_out, refs = refs[:6], refs[6:10], refs[10], refs[11:]
    else:
        g_in, vectors_in, refs = refs[0], refs[1], refs[2:]
    if shape:
        vectors, refs = refs[0], refs[1:]
    else:
        vectors = vectors_in
    saved = dict(zip(FWD_OUT, refs[:KEPT]))
    here = dict(zip(FWD_OUT, refs[KEPT : 2 * KEPT]))
    refs = refs[2 * KEPT :]
    raw, nrm, low, total, g, sems = refs[:6]
    mover = Mover(sems)
    y = lax.axis_index("mp")
    take = mover.start(tokens.at[pl.ds(y * micro, micro)], raw)
    x, q, k, v, probs, mix, res, nrm2, active, slope, out, cot, gl, glt, weight, nrmt = (
        here[name] for name in FWD_OUT
    )

    def keep(*names):
        for name in names:
            mover.save(here[name], saved[name])

    comm = {}
    if shape:
        tiles, send, recv, pass_send, pass_recv = refs[6:]
        place = Place(shape)
        spot = (place.at["y"], place.at["z"], place.at["x"], place.core)
        mine = [mover.start(part, g.at[(seg,) + spot]) for seg, part in enumerate(column_parts(weights))]
        fill_tile(place, tiles, norms)
        place.barrier("zxy")
        pick = lambda seg: tuple(sem.at[seg] for sem in (send, recv, pass_send, pass_recv))
        runs, cut = [], len(ORDERS) // 8
        for spot, order in enumerate(ORDERS):
            columns = pl.ds(spot % cut * (SEG // cut), SEG // cut)
            runs.append(Gather(place, g.at[spot // cut, :, :, :, :, :, columns], "yzx", order, pick(spot)))
        runs.append(Gather(place, tiles, "zx", "zx", pick(len(ORDERS))))
        comm = {spot: run.steps() for spot, run in enumerate(runs)}
        waiting = list(mine)

        def begin(spot):
            if waiting[spot // cut] is not None:
                waiting[spot // cut].wait()
                waiting[spot // cut] = None
            runs[spot].start()

        for spot in range(len(ORDERS)):
            comm[spot][0] = functools.partial(begin, spot)

        def have(seg):
            if seg < 8:
                for run in runs[seg * cut : (seg + 1) * cut]:
                    run.finish()
                mover.save(g.at[seg], g_out.at[seg])
            else:
                runs[-1].finish()
                read_vectors(vectors, tiles)

    else:
        loads = [mover.start(g_in.at[seg], g.at[seg]) for seg in range(8)]

        def have(seg):
            if seg < 8:
                loads[seg].wait()

    def spread():
        take.wait()
        to_rows(raw, x)
        keep("x")
        loads_cot.append(mover.start(cotangent.at[pl.ds(y * micro, micro)], raw))
        row_weights(ids, counts, y, micro, weight)

    loads_cot = []

    def weigh():
        loads_cot[0].wait()
        to_rows(raw, cot)

        def block(rows, _):
            gl[rows, :] = (cot[rows, :].astype(F32) * weight[rows, :]).astype(BF)

        row_loop(cot.shape[0], block)
        turn(gl, glt)
        keep("cot", "gl", "glt", "weight")

    def norm_one():
        have(8)
        norm_in(x, nrm, vectors[0:1, :], vectors[1:2, :])
        turn(nrm, nrmt)
        keep("nrmt")

    def head_part(seg, target, name):
        have(seg)
        project(nrm, g, seg, target)
        keep(name)

    third = x.shape[0] // TILE // 3

    def mixing(part):
        attend(q, k, v, probs, mix, part * third, third)

    def project_out():
        keep("probs", "mix")
        have(O)
        res[...] = x[...].astype(F32)
        back_through(lambda m: mix[:, half(m)], g, O, res)
        keep("res")

    def norm_two():
        gain, shift = vectors[2:3, :], vectors[3:4, :]

        def block(rows, _):
            normal, _inv = norm_stats(res[rows, :])
            nrm2[rows, :] = (normal * gain + shift).astype(BF)

        row_loop(x.shape[0], block)
        keep("nrm2")

    def up(which, m):
        feed_up(nrm2, g, which, m, active, slope)

    def keep_up(which):
        mover.save(active.at[which], saved["active"].at[which])
        mover.save(slope.at[which], saved["slope"].at[which])

    def down(which):
        have(DOWNS[which])
        if which == 0:
            total[...] = res[...]
        back_through(lambda m: active[which, m], g, DOWNS[which], total)

    def last():
        low[...] = total[...].astype(BF)
        from_rows(low, out)
        keep("out")

    pieces = [spread, weigh, norm_one]
    pieces += [functools.partial(head_part, *args) for args in ((Q, q, "q"), (K, k, "k"), (V, v, "v"))]
    pieces += [(3, mixing, None, None), project_out, norm_two]
    for which in range(2):
        before, after = functools.partial(have, UPS[which]), functools.partial(keep_up, which)
        pieces.append((2, functools.partial(up, which), before, after))
    pieces += [functools.partial(down, which) for which in range(2)] + [last]
    play(FORWARD_PLAN, comm, pieces)
    if shape:
        drain(runs)
    mover.close()


def row_weights(ids, counts, y, micro, target):
    series = ids.shape[1]
    sums = counts[0]
    for kind in range(1, counts.shape[0]):
        sums = sums + counts[kind]
    mean = jnp.full((PAD, 1), sums.astype(F32), F32) / counts.shape[0]

    def one(index, carry):
        kind = ids[y * micro + lax.div(index, series), lax.rem(index, series)]
        count = counts[kind].astype(F32)
        target[pl.ds(pl.multiple_of(index * PAD, PAD), PAD), :] = 2.0 * mean / (mean + count)
        return carry

    lax.fori_loop(0, micro * series, one, 0)


class Swap:
    def __init__(self, place, mover, sems, ready, source, target):
        self.mover, self.source, self.ready = mover, source, ready
        y, (micro, patches) = place.at["y"], source.shape[:2]
        cut = patches // 2 + 1
        self.spots = [target.at[y * micro + part] for part in range(micro)]
        self.copies = []
        for part in range(micro):
            for piece in (pl.ds(0, cut), pl.ds(cut, patches - cut)):
                slot = 2 * len(self.copies)
                self.copies.append(
                    pltpu.make_async_remote_copy(
                        source.at[part, piece],
                        target.at[y * micro + part, piece],
                        sems.at[slot],
                        sems.at[slot + 1],
                        device_id=place.device(y=1 - y),
                        device_id_type=MESH,
                    )
                )

    def start(self, part):
        if part == 0:
            self.ready()
        self.copies[2 * part].start()
        self.mover.save(self.source.at[part], self.spots[part])

    def steps(self, part):
        return [functools.partial(self.start, part), self.copies[2 * part + 1].start]

    def wait(self):
        for copy in self.copies:
            copy.wait()


def feed_back_kernel(shape, vectors, g_in, active_in, slope_in, nrm2_in, res_in, out_in, cot_in, gl_in, glt_in, weight_in, mix_in, *refs):
    if shape:
        dw_out, gres_out, gm_out, vec, pair, grad_down, refs = refs[:6] + (refs[6:],)
    else:
        dw_out, gres_out, gm_out, vec, refs = refs[:4] + (refs[4:],)
    cot, weight, active, slope, nrm2, res, g, dw, gl, glt, gh, n2t, gn2, gres, mix, gm, sems = refs[:17]
    mover = Mover(sems)
    if shape:
        half_out, hands, send, recv, ysem = refs[17:22]
        boxes = list(refs[22:])
        side = mover.start(out_in, half_out)
    loads = {"glt": mover.start(glt_in, glt), ("active", 0): mover.start(active_in.at[0], active.at[0])}
    loads["gl"] = mover.start(gl_in, gl)
    for which in range(2):
        if which == 1:
            loads["active", which] = mover.start(active_in.at[which], active.at[which])
        loads["d", which] = mover.start(g_in.at[DOWNS[which]], g.at[2 + which])
        loads["slope", which] = mover.start(slope_in.at[which], slope.at[which])
    loads["nrm2"] = mover.start(nrm2_in, nrm2)
    for which in range(2):
        loads["u", which] = mover.start(g_in.at[UPS[which]], g.at[which])
    loads["res"] = mover.start(res_in, res)
    loads["cot"] = mover.start(cot_in, cot)
    loads["mix"] = mover.start(mix_in, mix)
    loads["o"] = mover.start(g_in.at[O], g.at[4])
    loads["weight"] = mover.start(weight_in, weight)
    comm = {}
    if shape:
        place = Place(shape)
        place.barrier("zxy")
        runs = []
        block = (dw.shape[-2], SEG // 2)
        for spot, order in enumerate(FEED_ORDERS):
            columns = pl.ds(spot % 2 * block[1], block[1])
            source = dw.at[2 + spot // 2, :, :, :, :, :, columns]
            run = Scatter(place, source, "yzx", order, {}, hands.at[spot], (send.at[spot], recv.at[spot]))
            open_inbox(run, place.count, "yzx", order, block, boxes)
            runs.append(run)
        swap = Swap(place, mover, ysem, side.wait, half_out, pair)
        comm = {spot: run.steps() for spot, run in enumerate(runs)}
        comm[len(runs)] = swap.steps(0) + swap.steps(1)

    def down_grad(which):
        if which == 0:
            loads["glt"].wait()
        loads["active", which].wait()
        weight_grad(glt, lambda m: active[which, m], dw, 2 + which)
        if not shape:
            mover.save(dw.at[2 + which], dw_out.at[2 + which])

    def hidden_grad(which):
        if which == 0:
            loads["gl"].wait()
        loads["d", which].wait()
        loads["slope", which].wait()

        def one(m):
            pulled = nn(gl[...], flat(g[2 + which, m]))
            gh[which, m] = (pulled * slope[which, m]).astype(BF)

        half_loop(g.shape[1], one)

    def turn_two():
        loads["nrm2"].wait()
        turn(nrm2, n2t)
        gn2[...] = jnp.zeros_like(gn2)

    def up_grad(which):
        weight_grad(n2t, lambda m: gh[which, m], dw, which)
        mover.save(dw.at[which], dw_out.at[which])

    def norm_grad(which):
        loads["u", which].wait()
        back_through(lambda m: gh[which, m], g, which, gn2)

    def last():
        for name in ("res", "cot", "weight"):
            loads[name].wait()
        gain = vectors[2:3, :]
        vec[...] = jnp.zeros_like(vec)

        def block(rows, _):
            grad = gn2[rows, :]
            pulled, normal = norm_pull(grad, res[rows, :], gain)
            vec[0] += fold_rows(grad * normal)
            vec[1] += fold_rows(grad)
            total = cot[rows, :].astype(F32) * weight[rows, :] + pulled
            gres[rows, :] = total
            gl[rows, :] = total.astype(BF)

        row_loop(cot.shape[0], block)
        mover.save(gres, gres_out)

    def mix_grad():
        loads["o"].wait()
        project(gl, g, 4, gm)
        mover.save(gm, gm_out)

    def out_grad():
        loads["mix"].wait()
        weight_grad(glt, lambda m: mix[:, half(m)], dw, 4)
        mover.save(dw.at[4], dw_out.at[4])

    pieces = []
    for which in range(2):
        pieces += [functools.partial(down_grad, which), functools.partial(hidden_grad, which)]
    pieces.append(turn_two)
    for which in range(2):
        pieces += [functools.partial(up_grad, which), functools.partial(norm_grad, which)]
    pieces += [last, mix_grad, lambda: turn(gl, glt), out_grad]
    play(FEED_PLAN, comm, pieces)
    if shape:
        for spot, run in enumerate(runs):
            grad_down[:, spot * block[1] : (spot + 1) * block[1]] = run.result().astype(F32)
        drain(runs)
        swap.wait()
    mover.close()


def vector_tiles(tiles, vec_a, vec_f):
    tiles[...] = jnp.zeros_like(tiles)
    nz, nx = tiles.shape[:2]
    for line, (source, part) in enumerate(((vec_a, 0), (vec_a, 1), (vec_f, 0), (vec_f, 1))):
        row = jnp.sum(source[part], axis=0, keepdims=True)
        for z in range(nz):
            for x in range(nx):
                chip = z * nx + x
                tiles[z, x, line : line + 1, :] = row[:, chip * 128 : (chip + 1) * 128]


BACK_IN = ("gm", "q", "k", "v", "probs", "nrmt", "gres", "x")
KEPT_GRADS = (0, 1, 4)
HALF = SEG // 2
SPOTS = (4 * SEG, 5 * SEG, 3 * SEG, 0, HALF, SEG, SEG + HALF, 2 * SEG, 2 * SEG + HALF)


def attn_back_kernel(shape, vectors, vec_f, g_in, dw_in, *refs):
    given = dict(zip(BACK_IN, refs[:8]))
    refs = refs[8:]
    if shape:
        grad_down, pair, packed, vec_out, refs = refs[:4] + (refs[4:],)
    else:
        dw_out, out, vec, refs = refs[0], refs[1], refs[2], refs[3:]
    here = dict(zip(BACK_IN, refs[:8]))
    g, dw, gal, pulls, raw, sems = refs[8:14]
    mover = Mover(sems)
    loads, comm = {}, {}
    if shape:
        held, tiles, hands, half_hands, vec_hand, ybox, vec, send, recv, ysem = refs[14:24]
        boxes = list(refs[24:])

    def fetch_held(*spots):
        for spot in spots:
            if shape:
                loads["dw", spot] = mover.start(dw_in.at[KEPT_GRADS[spot]], held.at[spot])

    fetch_held(0)
    some = here["gm"].shape[0] // 3
    for part in range(3):
        rows = pl.ds(part * some, some)
        for name in BACK_IN[:5]:
            loads[name, part] = mover.start(given[name].at[rows], here[name].at[rows])
        if part == 0:
            fetch_held(1, 2)
    for name in BACK_IN[5:]:
        loads[name] = mover.start(given[name], here[name])
    for seg in (Q, K, V):
        loads[seg] = mover.start(g_in.at[seg], g.at[seg])
    gm, q, k, v, probs, nrmt, gres, x = (here[name] for name in BACK_IN)
    gn = probs
    if shape:
        place = Place(shape)
        place.barrier("zxy")
        runs = []
        for spot, order in enumerate(BACK_ORDERS):
            sems_of = (send.at[spot], recv.at[spot])
            if spot < 3:
                width, source, hand = SEG, held.at[spot], hands.at[spot]
            else:
                seg, side = (spot - 3) // 2, (spot - 3) % 2
                width, hand = HALF, half_hands.at[spot - 3]
                source = dw.at[seg, :, :, :, :, :, pl.ds(side * HALF, HALF)]
            run = Scatter(place, source, "yzx", order, {}, hand, sems_of)
            open_inbox(run, place.count, "yzx", order, (dw.shape[-2], width), boxes)
            runs.append(run)
        run = Scatter(place, tiles, "zx", "zx", {}, vec_hand, (send.at[9], recv.at[9]), both=True)
        open_inbox(run, {"z": place.nz, "x": place.nx}, "zx", "zx", (8, 128), boxes)
        runs.append(run)
        swap = Swap(place, mover, ysem, lambda: None, raw, pair)
        comm = {spot: run.steps() for spot, run in enumerate(runs)}
        comm[10], comm[11] = swap.steps(0), swap.steps(1)
        for spot in range(3):
            comm[spot][0] = lambda spot=spot: (loads["dw", spot].wait(), runs[spot].start())

    third = gal.shape[0] // TILE // 3
    micro = raw.shape[0]
    share = gal.shape[0] // micro

    def ready():
        vec[...] = jnp.zeros_like(vec)

    def mixing(part):
        for third_of in range(3):

            @pl.when(part == third_of)
            def _(third_of=third_of):
                for name in BACK_IN[:5]:
                    loads[name, third_of].wait()

        attend_back(q, k, v, probs, gm, pulls.at[0], pulls.at[1], pulls.at[2], part * third, third)

    def head_grad(seg):
        weight_grad(nrmt, lambda m: pulls[seg, :, half(m)], dw, seg)

    def token_grad(part):
        rows_of = pl.ds(part * share, share)
        gn[rows_of, :] = jnp.zeros((share, gn.shape[1]), F32)
        if part == 0:
            for name in (Q, K, V, "gres", "x"):
                loads[name].wait()

        def one(index, carry):
            seg, m = lax.div(index, 2), lax.rem(index, 2)
            gn[rows_of, :] += nt(pulls[seg, rows_of, half(m)], flat(g[seg, m]))
            return carry

        lax.fori_loop(0, 6, one, 0)
        gain = vectors[0:1, :]

        def block(rows, _):
            grad = gn[rows, :]
            pulled, normal = norm_pull(grad, x[rows, :].astype(F32), gain)
            vec[0] += fold_rows(grad * normal)
            vec[1] += fold_rows(grad)
            gal[rows, :] = (gres[rows, :] + pulled).astype(BF)

        row_loop(share, block, part * share // TILE)
        patches, series, width = raw.shape[1:]
        turned = nn(gather_rows(patches, series), gal[rows_of, :]).astype(raw.dtype)
        raw[part] = turned.reshape(patches, series, width)

    def spread_vectors():
        if shape:
            vector_tiles(tiles, vec, vec_f)

    def before_heads():
        loads["nrmt"].wait()

    pieces = [ready, (3, mixing, None, None), before_heads]
    parts = [functools.partial(token_grad, part) for part in range(micro)]
    heads = [(3, head_grad, None, None)]
    pieces += heads + parts if GRADS_FIRST else parts + heads
    pieces.insert(len(pieces) - (0 if GRADS_FIRST else 1), spread_vectors)
    play(ATTN_PLAN, comm, pieces)
    if not shape:
        mover.save(raw, out)
        for seg in (Q, K, V):
            mover.save(dw.at[seg], dw_out.at[seg])
    if shape:
        here_tile = tiles.at[place.at["z"], place.at["x"]]
        copy = pltpu.make_async_remote_copy(
            here_tile, ybox, ysem.at[8], ysem.at[9], device_id=place.device(y=1 - place.at["y"]), device_id_type=MESH
        )
        copy.start()
        packed[:, 6 * SEG :] = grad_down[...]
        for spot, column in enumerate(SPOTS):
            width = SEG if spot < 3 else HALF
            packed[:, column : column + width] = runs[spot].result().astype(F32)
        drain(runs)
        copy.wait()
        vec_out[...] = tiles[place.at["z"], place.at["x"]] + ybox[...]
        swap.wait()
    mover.close()


def shape_of(shape, dtype):
    return jax.ShapeDtypeStruct(shape, dtype)


IN_VMEM = pl.BlockSpec(memory_space=pltpu.VMEM)
IN_SMEM = pl.BlockSpec(memory_space=pltpu.SMEM)
ANYWHERE = pl.BlockSpec(memory_space=pl.ANY)
DMA = pltpu.SemaphoreType.DMA


def call(body, outs, ins, out_specs, scratch, name, collective=None):
    params = {"vmem_limit_bytes": VMEM_LIMIT}
    if collective is not None:
        params.update(collective_id=collective, has_side_effects=True)
    return pl.pallas_call(
        body,
        out_shape=outs,
        in_specs=ins,
        out_specs=out_specs,
        scratch_shapes=scratch,
        compiler_params=pltpu.CompilerParams(**params),
        name=name,
    )


def vmem(like):
    return pltpu.VMEM(like.shape, like.dtype)


def forward(shape, micro, tokens, cotangent, ids, counts, weights, norms, g_in=None, vectors_in=None):
    _, patches, series, width = tokens.shape
    rows = micro * series * PAD
    full = g_in.shape if shape is None else (8, shape[2], shape[0], shape[1], 2, weights[0].shape[0], SEG)
    low, high = shape_of((rows, width), BF), shape_of((rows, width), F32)
    wide = (2, full[1], rows, SEG)
    raw = shape_of((micro, patches, series, width), BF)
    kinds = {name: low for name in FWD_OUT}
    kinds.update(
        probs=high,
        res=high,
        active=shape_of(wide, BF),
        slope=shape_of(wide, F32),
        out=raw,
        glt=shape_of((width, rows), BF),
        nrmt=shape_of((width, rows), BF),
        weight=shape_of((rows, 1), F32),
    )
    saved = tuple(kinds[name] for name in FWD_OUT)
    scratch = [vmem(kind) for kind in saved] + [vmem(raw), vmem(low), vmem(low), vmem(high), pltpu.VMEM(full, BF), DMA((64,))]
    if shape is None:
        results = call(
            functools.partial(forward_kernel, None, micro),
            saved,
            [ANYWHERE, ANYWHERE, IN_SMEM, IN_SMEM, ANYWHERE, IN_VMEM],
            (ANYWHERE,) * KEPT,
            scratch,
            "forward",
        )(tokens, cotangent, ids, counts, g_in, vectors_in)
        return g_in, vectors_in, dict(zip(FWD_OUT, results))
    count = dict(zip("zxy", shape))
    slots = link_slots(count, "zxy")
    scratch += [pltpu.VMEM(shape[:2] + (2, 8, 128), F32)]
    runs = len(ORDERS) + 1
    scratch += [DMA((runs, slots)), DMA((runs, slots)), DMA((runs, slots + 1)), DMA((runs, slots + 1))]
    results = call(
        functools.partial(forward_kernel, shape, micro),
        (shape_of(full, BF), shape_of((8, width), F32)) + saved,
        [ANYWHERE, ANYWHERE, IN_SMEM, IN_SMEM] + [ANYWHERE] * 6 + [IN_VMEM] * 4,
        (ANYWHERE, IN_VMEM) + (ANYWHERE,) * KEPT,
        scratch,
        "forward",
        0,
    )(tokens, cotangent, ids, counts, *weights, *norms)
    return results[0], results[1], dict(zip(FWD_OUT, results[2:]))


def scatter_scratch(segs, part, count, orders, cols=SEG):
    rows = part.shape[-2]
    slots = link_slots(count, "zxy") + 1
    boxes = []
    for order in orders:
        boxes += [pltpu.VMEM(s, BF) for s in inbox_shapes(count, "yzx", order, (rows, cols))[0]]
    hands = pltpu.VMEM((len(orders),) + part.shape[1:4] + (rows, cols), BF)
    return hands, [DMA((segs, slots)), DMA((segs, slots))], boxes


def pair_of(raw, ny):
    return shape_of((ny * raw.shape[0],) + raw.shape[1:], BF)


def feed_back(shape, vectors, g, kept):
    low, high, raw = kept["x"], kept["res"], kept["out"]
    rows, width = low.shape
    part = shape_of((5,) + g.shape[1:], BF)
    turned = pltpu.VMEM((width, rows), BF)
    scratch = [
        vmem(low),
        pltpu.VMEM((rows, 1), F32),
        vmem(kept["active"]),
        vmem(kept["slope"]),
        vmem(low),
        vmem(high),
        vmem(part),
        vmem(part),
        vmem(low),
        turned,
        vmem(kept["active"]),
        turned,
        vmem(high),
        vmem(high),
        vmem(low),
        vmem(low),
        DMA((32,)),
    ]
    given = [g] + [kept[name] for name in ("active", "slope", "nrm2", "res", "out", "cot", "gl", "glt", "weight", "mix")]
    outs = [part, shape_of(high.shape, F32), shape_of(low.shape, BF), shape_of((2, 8, width), F32)]
    specs = [ANYWHERE, ANYWHERE, ANYWHERE, IN_VMEM]
    if shape:
        count = dict(zip("zxy", shape))
        hands, sems, boxes = scatter_scratch(len(FEED_ORDERS), part, count, FEED_ORDERS, SEG // 2)
        scratch += [vmem(raw), hands] + sems + [DMA((8,))] + boxes
        outs += [pair_of(raw, shape[2]), shape_of((part.shape[-2], 2 * SEG), F32)]
        specs += [ANYWHERE, IN_VMEM]
    return call(
        functools.partial(feed_back_kernel, shape),
        tuple(outs),
        [IN_VMEM] + [ANYWHERE] * 11,
        tuple(specs),
        scratch,
        "feed_back",
        1 if shape else None,
    )(vectors, *given)


def attn_back(shape, vectors, vec_f, g, dw_in, kept, grad_down=None):
    low, raw = kept["x"], kept["out"]
    width = low.shape[1]
    part = shape_of((3,) + g.shape[1:], BF)
    scratch = [vmem(kept[name]) for name in BACK_IN]
    scratch += [vmem(part), vmem(part), vmem(low), pltpu.VMEM((3,) + low.shape, BF), vmem(raw), DMA((32,))]
    vec = shape_of((2, 8, width), F32)
    if shape:
        nz, nx, ny = shape
        count = dict(zip("zxy", shape))
        share = part.shape[-2]
        outs = [pair_of(raw, ny), shape_of((share, 8 * SEG), F32), shape_of((8, 128), F32)]
        specs = [ANYWHERE] + [IN_VMEM] * 2
        hands, sems, boxes = scatter_scratch(10, part, count, BACK_ORDERS[:3])
        half_hands, _, more = scatter_scratch(10, part, count, BACK_ORDERS[3:], HALF)
        boxes += more
        tiles = pltpu.VMEM((nz, nx, 8, 128), F32)
        scratch += [vmem(part), tiles, hands, half_hands, tiles, pltpu.VMEM((8, 128), F32), vmem(vec)]
        scratch += sems + [DMA((10,))] + boxes
        scratch += [pltpu.VMEM(s, F32) for s in inbox_shapes({"z": nz, "x": nx}, "zx", "zx", (8, 128))[0]]
    else:
        outs, specs = [part, raw, vec], [ANYWHERE, ANYWHERE, IN_VMEM]
        outs[1] = shape_of(raw.shape, BF)
    return call(
        functools.partial(attn_back_kernel, shape),
        tuple(outs),
        [IN_VMEM] * 2 + [ANYWHERE] * 10 + ([IN_VMEM] if shape else []),
        tuple(specs),
        scratch,
        "attn_back",
        2 if shape else None,
    )(vectors, vec_f, g, dw_in, *(kept[name] for name in BACK_IN), *((grad_down,) if shape else ()))


def chip_grid(chips):
    nx = 1
    while (nx * 2) ** 2 <= chips:
        nx *= 2
    return chips // nx, nx


def body(counts_of, tokens, cotangent, domain_ids, domain_counts, *params):
    weights, norms = params[:6], params[6:]
    n_dp, n_mp = counts_of
    micro = tokens.shape[0] // n_mp
    width = tokens.shape[3]
    share = width // n_dp
    y = lax.axis_index("mp")
    linked = n_mp == 2 and share * 2 == TILE
    flip = lambda array: jnp.transpose(array, (0, 2, 1, 3))
    x, cot = flip(tokens), flip(cotangent)
    if linked:
        shape = chip_grid(n_dp // 2) + (n_mp,)
        g, vectors, kept = forward(shape, micro, x, cot, domain_ids, domain_counts, weights, [norm.reshape(1, -1) for norm in norms])
    else:
        shards = jnp.stack(
            weights[:4] + tuple(w[:, i * SEG : (i + 1) * SEG] for w in weights[4:] for i in range(2))
        )
        g = lax.all_gather(lax.all_gather(shards, "dp", axis=1, tiled=True), "mp", axis=1)
        vectors = lax.all_gather(jnp.stack(norms), "dp", axis=1, tiled=True).astype(F32)
        vectors = jnp.pad(vectors, ((0, 4), (0, 0)))
        g, vectors, kept = forward(None, micro, x, cot, domain_ids, domain_counts, None, None, g, vectors)
    shape = shape if linked else None
    results = feed_back(shape, vectors, g, kept)
    dw_f, gres, gm, vec_f = results[:4]
    kept = {**kept, "gres": gres, "gm": gm}
    if linked:
        out, grad_down = results[4:]
        grad_tokens, packed, vec = attn_back(shape, vectors, vec_f, g, dw_f, kept, grad_down)
        cuts = [0, SEG, 2 * SEG, 3 * SEG, 4 * SEG, 6 * SEG, 8 * SEG]
        grads = [packed[:, start:stop] for start, stop in zip(cuts, cuts[1:])]
        core = lax.rem(lax.axis_index("dp"), 2)
        vec = lax.dynamic_slice(vec, (0, core * share), (4, share))
    else:
        dw_a, low_tokens, vec_a = attn_back(shape, vectors, vec_f, g, dw_f, kept)
        dw = jnp.concatenate((dw_a, dw_f[4:], dw_f[:4])).astype(F32)
        dw = lax.psum_scatter(lax.psum_scatter(dw, "mp", scatter_dimension=1), "dp", scatter_dimension=1, tiled=True)
        grads = [dw[0], dw[1], dw[2], dw[3]]
        grads += [jnp.concatenate((dw[a], dw[b]), axis=1) for a, b in (UPS, DOWNS)]
        vec = jnp.concatenate((jnp.sum(vec_a, axis=1), jnp.sum(vec_f, axis=1)))
        vec = lax.psum_scatter(lax.psum(vec, "mp"), "dp", scatter_dimension=1, tiled=True)
        out = lax.all_gather(kept["out"], "mp", axis=0, tiled=True)
        grad_tokens = lax.all_gather(low_tokens, "mp", axis=0, tiled=True)
    return (flip(out), flip(grad_tokens.astype(F32)), *grads, vec[0], vec[1], vec[2], vec[3])


def solution(mesh):
    rows, matrix, vector = P(None, "dp", None, None), P("dp", "mp"), P("dp")
    in_specs = (rows, rows, P(None, "dp"), P()) + (matrix,) * 6 + (vector,) * 4
    out_specs = (rows, rows) + (matrix,) * 6 + (vector,) * 4
    run = functools.partial(body, (mesh.shape["dp"], mesh.shape["mp"]))
    return jax.shard_map(run, mesh=mesh, in_specs=in_specs, out_specs=out_specs, check_vma=False)
```

```python
import functools

import jax
import jax.numpy as jnp
from jax import lax
from jax.experimental import pallas as pl
from jax.experimental.pallas import tpu as pltpu
from jax.sharding import PartitionSpec as P

BF = jnp.bfloat16
F32 = jnp.float32
HD = 128
SEG = 512
TILE = 128
PAD = 16
EPS = 1e-05
MESH = pl.DeviceIdType.MESH
VMEM_LIMIT = 62 * 1024 * 1024

Q, K, V, O, U0, U1, D0, D1 = range(8)
UPS = (U0, U1)
DOWNS = (D0, D1)
ORDERS = ("zxy", "zyx", "yxz", "zxy", "zyx", "zxy", "yzx", "xyz")
BACK_ORDERS = ("zxy", "xzy", "yxz", "xyz", "xzy", "zxy", "yxz", "xzy", "xzy")
FEED_ORDERS = ("zxy", "zxy", "xzy", "xzy")

FORWARD_PLAN = (
    0, 1, 2, 3, 7, 0, 8, 6, 1, 2, -1, 0, 8, 0, 3, 7, 1, 4, 8, 3, 1, 8, 6, 5,
    4, 2, 3, 0, 4, 1, 5, -1, 5, 6, 2, 8, 4, 0, 5, 3, -1, 4, 2, -1, 6, 1, 7, 2,
    -1, 5, -1, 3, 6, -1, -1, 4, 7, -1, -1, -1, -1, 7, 5, -1, -1, 6, -1, 7, -1, -1, -1,
)
FEED_PLAN = (
    4, 4, -1, 0, -1, 1, 0, 4, -1, 2, 3, 4, 1, 3, 0, -1, 2, -1, 1, -1, 0, -1, 3, 1,
    -1, -1, 2, 0, 3, -1, 1, 0, 2, -1, 3, -1, 2, 1, -1, 3, 2, 1, 3, 0, 2,
)
ATTN_PLAN = (
    2, 0, -1, -1, 2, 1, 0, -1, -1, 1, -1, -1, -1, 0, 4, 6, 5, -1, 8, 5, 6, -1, 10, 8,
    0, 7, 4, -1, -1, 1, 3, 3, 10, 1, 7, 2, 9, 9, 8, 9, 8, 11, 9, 1, 4, 3, 4, 5,
    8, 5, 1, 7, 6, 0, 11, 4, 3, 2, 9, 8, 6, 4, 7, 3, 2, 7, 5, 0, 6, 9, 2, 3,
    5, 6, 7, 1, 4, 8, 0, 5, 2, 3, 7, 6,
)
GRADS_FIRST = 1


def nn(a, b):
    return lax.dot_general(a, b, (((1,), (0,)), ((), ())), preferred_element_type=F32)


def nt(a, b):
    return lax.dot_general(a, b, (((1,), (1,)), ((), ())), preferred_element_type=F32)


def flat(value):
    return value.reshape(-1, value.shape[-1])


def norm_stats(values):
    mean = jnp.mean(values, axis=-1, keepdims=True)
    center = values - mean
    inverse = lax.rsqrt(jnp.mean(center * center, axis=-1, keepdims=True) + EPS)
    return center * inverse, inverse


def norm_pull(grad, values, gain):
    normal, inverse = norm_stats(values)
    scaled = grad * gain
    first = jnp.mean(scaled, axis=-1, keepdims=True)
    second = jnp.mean(scaled * normal, axis=-1, keepdims=True)
    return inverse * (scaled - first - normal * second), normal


def fold_rows(values):
    rows, width = values.shape
    return jnp.sum(values.reshape(rows // 8, 8, width), axis=0)


def score_mask():
    key = lax.broadcasted_iota(jnp.int32, (TILE, TILE), 0)
    query = lax.broadcasted_iota(jnp.int32, (TILE, TILE), 1)
    return (query // PAD == key // PAD) & (key <= query)


def row_loop(rows, body, first=0):
    def once(index, carry):
        index = first + index
        body(pl.ds(pl.multiple_of(index * TILE, TILE), TILE), index)
        return carry

    lax.fori_loop(0, rows // TILE, once, 0)


def half_loop(count, body):
    def once(index, carry):
        body(index)
        return carry

    lax.fori_loop(0, count, once, 0)


def half(index):
    return pl.ds(pl.multiple_of(index * SEG, SEG), SEG)


def spread_rows(patches, series):
    row = lax.broadcasted_iota(jnp.int32, (series * PAD, patches * series), 0)
    col = lax.broadcasted_iota(jnp.int32, (series * PAD, patches * series), 1)
    hit = (lax.rem(row, PAD) * series + lax.div(row, PAD) == col) & (lax.rem(row, PAD) < patches)
    return jnp.where(hit, 1.0, 0.0).astype(BF)


def gather_rows(patches, series):
    row = lax.broadcasted_iota(jnp.int32, (patches * series, series * PAD), 0)
    col = lax.broadcasted_iota(jnp.int32, (patches * series, series * PAD), 1)
    return jnp.where(lax.rem(row, series) * PAD + lax.div(row, series) == col, 1.0, 0.0).astype(BF)


def to_rows(raw, target):
    micro, patches, series, _ = raw.shape
    matrix = spread_rows(patches, series)
    for part in range(micro):
        target[part * series * PAD : (part + 1) * series * PAD, :] = nn(matrix, flat(raw[part])).astype(BF)


def from_rows(source, raw):
    micro, patches, series, width = raw.shape
    matrix = gather_rows(patches, series)
    for part in range(micro):
        rows = source[part * series * PAD : (part + 1) * series * PAD, :]
        raw[part] = nn(matrix, rows).astype(raw.dtype).reshape(patches, series, width)


def norm_in(x, normed, gain, shift):
    def block(rows, _):
        normal, _inv = norm_stats(x[rows, :].astype(F32))
        normed[rows, :] = (normal * gain + shift).astype(BF)

    row_loop(x.shape[0], block)


def project(source, weights, seg, target):
    def one(m):
        target[:, half(m)] = nn(source[...], flat(weights[seg, m])).astype(BF)

    half_loop(weights.shape[1], one)


def attend(queries, keys, values, probs, mixture, first, count):
    mask = score_mask()
    scale = HD ** (-0.5)
    columns = [slice(at, at + HD) for at in range(0, queries.shape[1], HD)]

    def group(rows, _):
        scores = [nt(keys[rows, cols], queries[rows, cols]) * scale for cols in columns]
        scores = [jnp.where(mask, score, -1e30) for score in scores]
        peaks = [jnp.max(score, axis=0, keepdims=True) for score in scores]
        powers = [jnp.exp(score - peak) for score, peak in zip(scores, peaks)]
        inverses = [1.0 / jnp.sum(power, axis=0, keepdims=True) for power in powers]
        shares = [power * inverse for power, inverse in zip(powers, inverses)]
        for cols, share in zip(columns, shares):
            probs[rows, cols] = share
        mixed = [nn(share.astype(BF).T, values[rows, cols]) for share, cols in zip(shares, columns)]
        for cols, part in zip(columns, mixed):
            mixture[rows, cols] = part.astype(BF)

    row_loop(count * TILE, group, first)


def attend_back(queries, keys, values, probs, grad_mix, grad_q, grad_k, grad_v, first, count):
    scale = HD ** (-0.5)
    columns = [slice(at, at + HD) for at in range(0, queries.shape[1], HD)]

    def group(rows, _):
        shares = [probs[rows, cols] for cols in columns]
        grads = [grad_mix[rows, cols] for cols in columns]
        pulls = [nt(values[rows, cols], grad) for cols, grad in zip(columns, grads)]
        back_v = [nn(share.astype(BF), grad) for share, grad in zip(shares, grads)]
        inner = [jnp.sum(pull * share, axis=0, keepdims=True) for pull, share in zip(pulls, shares)]
        lows = [(share * (pull - mean)).astype(BF) for share, pull, mean in zip(shares, pulls, inner)]
        back_k = [nn(low, queries[rows, cols]) * scale for low, cols in zip(lows, columns)]
        back_q = [nn(low.T, keys[rows, cols]) * scale for low, cols in zip(lows, columns)]
        for cols, one, two, three in zip(columns, back_q, back_k, back_v):
            grad_q[rows, cols] = one.astype(BF)
            grad_k[rows, cols] = two.astype(BF)
            grad_v[rows, cols] = three.astype(BF)

    row_loop(count * TILE, group, first)


def back_through(source, weights, seg, total):
    def one(m):
        total[...] += nt(source(m), flat(weights[seg, m]))

    half_loop(weights.shape[1], one)


def feed_up(normed_two, weights, which, m, active, slope):
    hidden = nn(normed_two[...], flat(weights[UPS[which], m]))
    bell = 0.5 + 0.5 * lax.erf(hidden * (0.5**0.5))
    active[which, m] = (hidden * bell).astype(BF)
    density = jnp.exp(-0.5 * hidden * hidden) * 0.3989422804014327
    slope[which, m] = bell + hidden * density


def turn(source, target):
    def block(rows, _):
        target[:, rows] = source[rows, :].T

    row_loop(source.shape[0], block)


def weight_grad(turned, right, target, seg):
    def one(m):
        product = nn(turned[...], right(m)).astype(BF)
        target[seg, m] = product.reshape(target.shape[2:])

    half_loop(target.shape[1], one)


class Place:
    def __init__(self, shape):
        self.nz, self.nx, self.ny = shape
        index = lax.axis_index("dp")
        self.core = lax.rem(index, 2)
        chip = lax.div(index, 2)
        self.at = {"z": lax.div(chip, self.nx), "x": lax.rem(chip, self.nx), "y": lax.axis_index("mp")}
        self.count = {"z": self.nz, "x": self.nx, "y": self.ny}

    def device(self, core=None, **moved):
        at = {**self.at, **moved}
        core = self.core if core is None else core
        return ((at["z"] * self.nx + at["x"]) * 2 + core, at["y"])

    def partner(self):
        return self.device(core=1 - self.core)

    def neighbour(self, dim, step):
        return self.device(**{dim: self.at[dim] + step})

    def barrier(self, dims):
        semaphore = pltpu.get_barrier_semaphore()
        pl.semaphore_signal(semaphore, inc=1, device_id=self.partner(), device_id_type=MESH)
        peers = 1
        for dim in dims:
            for step in (1, -1):
                there = self.at[dim] + step
                valid = (there >= 0) & (there < self.count[dim])
                peers = peers + valid.astype(jnp.int32)

                @pl.when(valid)
                def _(dim=dim, step=step):
                    other = self.neighbour(dim, step)
                    pl.semaphore_signal(semaphore, inc=1, device_id=other, device_id_type=MESH)

        pl.semaphore_wait(semaphore, peers)


def link_slots(count, dims):
    return sum(2 * (count[dim] - 1) for dim in dims)


class Gather:
    def __init__(self, place, buffer, axes, order, sems):
        self.place, self.buffer, self.axes, self.order = place, buffer, axes, order
        self.send, self.recv, self.pass_send, self.pass_recv = sems
        self.rounds = [(dim, t) for dim in order for t in range(place.count[dim] - 1)]
        self.slots = {}
        for dim, t in self.rounds:
            for way in (1, -1):
                self.slots[dim, t, way] = len(self.slots)

    def block(self, dim, position, core):
        done = self.order[: self.order.index(dim)] if dim else ""
        index = []
        for axis in self.axes:
            if axis == dim:
                index.append(position)
            elif axis in done:
                index.append(pl.ds(0, self.place.count[axis]))
            else:
                index.append(self.place.at[axis])
        return self.buffer.at[tuple(index) + (core,)]

    def link(self, dim, t, way, position, device):
        block = self.block(dim, position, self.place.core)
        slot = self.slots[dim, t, way]
        return pltpu.make_async_remote_copy(
            block, block, self.send.at[slot], self.recv.at[slot], device_id=device, device_id_type=MESH
        )

    def hand(self, slot, dim, position, core):
        block = self.block(dim, position, core)
        return pltpu.make_async_remote_copy(
            block,
            block,
            self.pass_send.at[slot],
            self.pass_recv.at[slot],
            device_id=self.place.partner(),
            device_id_type=MESH,
        )

    def sends(self, dim, t):
        here, count = self.place.at[dim], self.place.count[dim]
        yield 1, here - t, (here - t >= 0) & (here < count - 1)
        yield -1, here + t, (here + t < count) & (here > 0)

    def arrivals(self, dim, t):
        here, count = self.place.at[dim], self.place.count[dim]
        yield 1, here - 1 - t, here - 1 - t >= 0
        yield -1, here + 1 + t, here + 1 + t < count

    def start(self):
        self.hand(len(self.slots), "", None, self.place.core).start()
        self.send_round(0)

    def send_round(self, number):
        dim, t = self.rounds[number]
        for way, position, valid in self.sends(dim, t):

            @pl.when(valid)
            def _(way=way, position=position):
                self.link(dim, t, way, position, self.place.neighbour(dim, way)).start()

    def advance(self, number):
        dim, t = self.rounds[number - 1]
        for way, position, valid in self.arrivals(dim, t):

            @pl.when(valid)
            def _(way=way, position=position):
                self.link(dim, t, way, position, self.place.partner()).wait_recv()
                self.hand(self.slots[dim, t, way], dim, position, self.place.core).start()

        if number < len(self.rounds):
            self.send_round(number)

    def steps(self):
        return [self.start] + [functools.partial(self.advance, n + 1) for n in range(len(self.rounds))]

    def finish(self):
        other = 1 - self.place.core
        self.hand(len(self.slots), "", None, other).wait_recv()
        for dim, t in self.rounds:
            for way, position, valid in self.arrivals(dim, t):

                @pl.when(valid)
                def _(dim=dim, t=t, way=way, position=position):
                    self.hand(self.slots[dim, t, way], dim, position, other).wait_recv()

    def drain_hand(self):
        self.hand(len(self.slots), "", None, self.place.core).wait_send()

    def sent(self, dim, t):
        for way, position, valid in self.sends(dim, t):
            yield valid, self.link(dim, t, way, position, self.place.partner())
        for way, position, valid in self.arrivals(dim, t):
            yield valid, self.hand(self.slots[dim, t, way], dim, position, self.place.core)


class Scatter:
    def __init__(self, place, mine, axes, order, inbox, hand_box, sems, both=False):
        self.place, self.mine, self.axes, self.order, self.both = place, mine, axes, order, both
        self.inbox, self.hand_box = inbox, hand_box
        self.send, self.recv = sems
        self.rounds = [(dim, t) for dim in order for t in range(place.count[dim] - 1)]
        self.slots = {}
        for dim, t in self.rounds:
            for way in (1, -1):
                self.slots[dim, t, way] = len(self.slots) + 1

    def own(self, index):
        return index + ((() if self.both else (self.place.core,)))

    def hand(self):
        whole = tuple(pl.ds(0, self.place.count[axis]) for axis in self.axes)
        source = self.mine.at[whole] if self.both else self.mine.at[whole + (1 - self.place.core,)]
        return pltpu.make_async_remote_copy(
            source, self.hand_box, self.send.at[0], self.recv.at[0], device_id=self.place.partner(), device_id_type=MESH
        )

    def start(self):
        self.hand().start()

    def take_hand(self):
        self.hand().wait_recv()
        first = self.place.count[self.axes[0]]
        rest = tuple(pl.ds(0, self.place.count[axis]) for axis in self.axes[1:])
        if self.both:
            self.hand().wait_send()
            self.mine[...] = self.mine[...] + self.hand_box[...]
        else:
            for p in range(first):
                for r in range(self.place.count[self.axes[1]]):
                    index = (p, r) + rest[1:]
                    here = self.mine[index + (self.place.core,)].astype(F32)
                    there = self.hand_box[index].astype(F32)
                    self.mine[index + (self.place.core,)] = (here + there).astype(self.mine.dtype)
        self.send_round(0)

    def block(self, dim, position):
        done = self.order[: self.order.index(dim)]
        index = []
        for axis in self.axes:
            if axis == dim:
                index.append(position)
            elif axis in done:
                index.append(self.place.at[axis])
            else:
                index.append(pl.ds(0, self.place.count[axis]))
        return self.own(tuple(index))

    def link(self, dim, t, way, position, device):
        slot = self.slots[dim, t, way]
        return pltpu.make_async_remote_copy(
            self.mine.at[self.block(dim, position)],
            self.inbox[slot],
            self.send.at[slot],
            self.recv.at[slot],
            device_id=device,
            device_id_type=MESH,
        )

    def sends(self, dim, t):
        here, count = self.place.at[dim], self.place.count[dim]
        yield 1, count - 1 - t + here, (t >= here) & (here < count - 1)
        back = count - 1 - here
        yield -1, t - back, (t >= back) & (here > 0)

    def arrivals(self, dim, t):
        here, count = self.place.at[dim], self.place.count[dim]
        yield 1, count - 2 - t + here, (t >= here - 1) & (here > 0)
        back = count - 1 - here
        yield -1, t + 1 - back, (t >= back - 1) & (here < count - 1)

    def send_round(self, number):
        dim, t = self.rounds[number]
        for way, position, valid in self.sends(dim, t):

            @pl.when(valid)
            def _(way=way, position=position):
                self.link(dim, t, way, position, self.place.neighbour(dim, way)).start()

    def advance(self, number):
        dim, t = self.rounds[number - 1]
        for way, position, valid in self.arrivals(dim, t):

            @pl.when(valid)
            def _(way=way, position=position):
                self.link(dim, t, way, position, self.place.partner()).wait_recv()
                index = self.block(dim, position)
                total = self.mine[index].astype(F32) + self.inbox[self.slots[dim, t, way]][...].astype(F32)
                self.mine[index] = total.astype(self.mine.dtype)

        if number < len(self.rounds):
            self.send_round(number)

    def steps(self):
        later = [functools.partial(self.advance, n + 1) for n in range(len(self.rounds))]
        return [self.start, self.take_hand] + later

    def result(self):
        return self.mine[self.own(tuple(self.place.at[axis] for axis in self.axes))]

    def drain_hand(self):
        if not self.both:
            self.hand().wait_send()

    def sent(self, dim, t):
        for way, position, valid in self.sends(dim, t):
            yield valid, self.link(dim, t, way, position, self.place.partner())


def drain(runs):
    for run in runs:
        run.drain_hand()
    for dim, t in dict.fromkeys(key for run in runs for key in run.rounds):
        groups = [list(run.sent(dim, t)) for run in runs if (dim, t) in run.rounds]
        for same in zip(*groups):

            @pl.when(same[0][0])
            def _(same=same):
                for _valid, copy in same:
                    copy.wait_send()


def inbox_shapes(count, axes, order, block):
    shapes, slots, left = [], {}, dict(count)
    for dim in order:
        left.pop(dim)
        for t in range(count[dim] - 1):
            for way in (1, -1):
                if way == 1 or count[dim] > 2:
                    shapes.append(tuple(count[axis] for axis in axes if axis in left) + block)
                slots[dim, t, way] = len(shapes) - 1
    return shapes, slots


def open_inbox(run, count, axes, order, block, boxes):
    shapes, slots = inbox_shapes(count, axes, order, block)
    for key, slot in run.slots.items():
        run.inbox[slot] = boxes[slots[key]]
    del boxes[: len(shapes)]


def play(plan, comm, pieces):
    plan = list(plan)
    while plan:
        token = plan.pop(0)
        if token >= 0:
            if comm:
                comm[token].pop(0)()
        elif callable(pieces[0]):
            pieces.pop(0)()
        else:
            count, piece, before, after = pieces.pop(0)
            if before:
                before()
            between = [[] for _ in range(count - 1)]
            for spot in range(count - 1):
                while plan[0] >= 0:
                    token = plan.pop(0)
                    if comm:
                        between[spot].append(comm[token].pop(0))
                plan.pop(0)

            def once(index, carry, piece=piece, between=between):
                piece(index)
                for spot, steps in enumerate(between):
                    if steps:

                        @pl.when(index == spot)
                        def _(steps=steps):
                            for step in steps:
                                step()

                return carry

            lax.fori_loop(0, count, once, 0)
            if after:
                after()
    assert not pieces and not any(comm.values())


class Mover:
    def __init__(self, sems):
        self.sems, self.used, self.open = sems, 0, []

    def start(self, source, target):
        copy = pltpu.make_async_copy(source, target, self.sems.at[self.used])
        self.used += 1
        copy.start()
        return copy

    def save(self, source, target):
        self.open.append(self.start(source, target))

    def close(self):
        for copy in self.open:
            copy.wait()


def read_vectors(vectors, tiles):
    nz, nx = tiles.shape[:2]
    pieces = [tiles[z, x, 0] + tiles[z, x, 1] for z in range(nz) for x in range(nx)]
    vectors[...] = jnp.concatenate(pieces, axis=1)


def column_parts(weights):
    wq, wk, wv, wo, wu, wd = weights
    left, right = pl.ds(0, SEG), pl.ds(SEG, SEG)
    return [wq, wk, wv, wo, wu.at[:, left], wu.at[:, right], wd.at[:, left], wd.at[:, right]]


def fill_tile(place, tiles, norms):
    tile = (place.at["z"], place.at["x"], place.core)
    tiles[tile] = jnp.zeros(tiles.shape[3:], F32)
    share = norms[0].shape[1]
    for line, norm in enumerate(norms):
        value = norm[...].astype(F32)
        for core in range(2):

            @pl.when(place.core == core)
            def _(line=line, value=value, core=core):
                tiles[tile + (slice(line, line + 1), slice(core * share, (core + 1) * share))] = value


FWD_OUT = (
    "x", "q", "k", "v", "probs", "mix", "res", "nrm2", "active", "slope", "out", "cot", "gl", "glt", "weight",
    "nrmt",
)
KEPT = len(FWD_OUT)


def forward_kernel(shape, micro, tokens, cotangent, ids, counts, *refs):
    if shape:
        weights, norms, g_out, refs = refs[:6], refs[6:10], refs[10], refs[11:]
    else:
        g_in, vectors_in, refs = refs[0], refs[1], refs[2:]
    if shape:
        vectors, refs = refs[0], refs[1:]
    else:
        vectors = vectors_in
    saved = dict(zip(FWD_OUT, refs[:KEPT]))
    here = dict(zip(FWD_OUT, refs[KEPT : 2 * KEPT]))
    refs = refs[2 * KEPT :]
    raw, nrm, low, total, g, sems = refs[:6]
    mover = Mover(sems)
    y = lax.axis_index("mp")
    take = mover.start(tokens.at[pl.ds(y * micro, micro)], raw)
    x, q, k, v, probs, mix, res, nrm2, active, slope, out, cot, gl, glt, weight, nrmt = (
        here[name] for name in FWD_OUT
    )

    def keep(*names):
        for name in names:
            mover.save(here[name], saved[name])

    comm = {}
    if shape:
        tiles, send, recv, pass_send, pass_recv = refs[6:]
        place = Place(shape)
        spot = (place.at["y"], place.at["z"], place.at["x"], place.core)
        mine = [mover.start(part, g.at[(seg,) + spot]) for seg, part in enumerate(column_parts(weights))]
        fill_tile(place, tiles, norms)
        place.barrier("zxy")
        pick = lambda seg: tuple(sem.at[seg] for sem in (send, recv, pass_send, pass_recv))
        runs, cut = [], len(ORDERS) // 8
        for spot, order in enumerate(ORDERS):
            columns = pl.ds(spot % cut * (SEG // cut), SEG // cut)
            runs.append(Gather(place, g.at[spot // cut, :, :, :, :, :, columns], "yzx", order, pick(spot)))
        runs.append(Gather(place, tiles, "zx", "zx", pick(len(ORDERS))))
        comm = {spot: run.steps() for spot, run in enumerate(runs)}
        waiting = list(mine)

        def begin(spot):
            if waiting[spot // cut] is not None:
                waiting[spot // cut].wait()
                waiting[spot // cut] = None
            runs[spot].start()

        for spot in range(len(ORDERS)):
            comm[spot][0] = functools.partial(begin, spot)

        def have(seg):
            if seg < 8:
                for run in runs[seg * cut : (seg + 1) * cut]:
                    run.finish()
                mover.save(g.at[seg], g_out.at[seg])
            else:
                runs[-1].finish()
                read_vectors(vectors, tiles)

    else:
        loads = [mover.start(g_in.at[seg], g.at[seg]) for seg in range(8)]

        def have(seg):
            if seg < 8:
                loads[seg].wait()

    def spread():
        take.wait()
        to_rows(raw, x)
        keep("x")
        loads_cot.append(mover.start(cotangent.at[pl.ds(y * micro, micro)], raw))
        row_weights(ids, counts, y, micro, weight)

    loads_cot = []

    def weigh():
        loads_cot[0].wait()
        to_rows(raw, cot)

        def block(rows, _):
            gl[rows, :] = (cot[rows, :].astype(F32) * weight[rows, :]).astype(BF)

        row_loop(cot.shape[0], block)
        turn(gl, glt)
        keep("cot", "gl", "glt", "weight")

    def norm_one():
        have(8)
        norm_in(x, nrm, vectors[0:1, :], vectors[1:2, :])
        turn(nrm, nrmt)
        keep("nrmt")

    def head_part(seg, target, name):
        have(seg)
        project(nrm, g, seg, target)
        keep(name)

    third = x.shape[0] // TILE // 3

    def mixing(part):
        attend(q, k, v, probs, mix, part * third, third)

    def project_out():
        keep("probs", "mix")
        have(O)
        res[...] = x[...].astype(F32)
        back_through(lambda m: mix[:, half(m)], g, O, res)
        keep("res")

    def norm_two():
        gain, shift = vectors[2:3, :], vectors[3:4, :]

        def block(rows, _):
            normal, _inv = norm_stats(res[rows, :])
            nrm2[rows, :] = (normal * gain + shift).astype(BF)

        row_loop(x.shape[0], block)
        keep("nrm2")

    def up(which, m):
        feed_up(nrm2, g, which, m, active, slope)

    def keep_up(which):
        mover.save(active.at[which], saved["active"].at[which])
        mover.save(slope.at[which], saved["slope"].at[which])

    def down(which):
        have(DOWNS[which])
        if which == 0:
            total[...] = res[...]
        back_through(lambda m: active[which, m], g, DOWNS[which], total)

    def last():
        low[...] = total[...].astype(BF)
        from_rows(low, out)
        keep("out")

    pieces = [spread, weigh, norm_one]
    pieces += [functools.partial(head_part, *args) for args in ((Q, q, "q"), (K, k, "k"), (V, v, "v"))]
    pieces += [(3, mixing, None, None), project_out, norm_two]
    for which in range(2):
        before, after = functools.partial(have, UPS[which]), functools.partial(keep_up, which)
        pieces.append((2, functools.partial(up, which), before, after))
    pieces += [functools.partial(down, which) for which in range(2)] + [last]
    play(FORWARD_PLAN, comm, pieces)
    if shape:
        drain(runs)
    mover.close()


def row_weights(ids, counts, y, micro, target):
    series = ids.shape[1]
    sums = counts[0]
    for kind in range(1, counts.shape[0]):
        sums = sums + counts[kind]
    mean = jnp.full((PAD, 1), sums.astype(F32), F32) / counts.shape[0]

    def one(index, carry):
        kind = ids[y * micro + lax.div(index, series), lax.rem(index, series)]
        count = counts[kind].astype(F32)
        target[pl.ds(pl.multiple_of(index * PAD, PAD), PAD), :] = 2.0 * mean / (mean + count)
        return carry

    lax.fori_loop(0, micro * series, one, 0)


class Swap:
    def __init__(self, place, mover, sems, ready, source, target):
        self.mover, self.source, self.ready = mover, source, ready
        y, (micro, patches) = place.at["y"], source.shape[:2]
        cut = patches // 2 + 1
        self.spots = [target.at[y * micro + part] for part in range(micro)]
        self.copies = []
        for part in range(micro):
            for piece in (pl.ds(0, cut), pl.ds(cut, patches - cut)):
                slot = 2 * len(self.copies)
                self.copies.append(
                    pltpu.make_async_remote_copy(
                        source.at[part, piece],
                        target.at[y * micro + part, piece],
                        sems.at[slot],
                        sems.at[slot + 1],
                        device_id=place.device(y=1 - y),
                        device_id_type=MESH,
                    )
                )

    def start(self, part):
        if part == 0:
            self.ready()
        self.copies[2 * part].start()
        self.mover.save(self.source.at[part], self.spots[part])

    def steps(self, part):
        return [functools.partial(self.start, part), self.copies[2 * part + 1].start]

    def wait(self):
        for copy in self.copies:
            copy.wait()


def feed_back_kernel(shape, vectors, g_in, active_in, slope_in, nrm2_in, res_in, out_in, cot_in, gl_in, glt_in, weight_in, mix_in, *refs):
    if shape:
        dw_out, gres_out, gm_out, vec, pair, grad_down, refs = refs[:6] + (refs[6:],)
    else:
        dw_out, gres_out, gm_out, vec, refs = refs[:4] + (refs[4:],)
    cot, weight, active, slope, nrm2, res, g, dw, gl, glt, gh, n2t, gn2, gres, mix, gm, sems = refs[:17]
    mover = Mover(sems)
    if shape:
        half_out, hands, send, recv, ysem = refs[17:22]
        boxes = list(refs[22:])
        side = mover.start(out_in, half_out)
    loads = {}

    def fetch(key, source, target):
        loads[key] = mover.start(source, target)

    def fetch_down(which):
        fetch(("active", which), active_in.at[which], active.at[which])
        fetch(("d", which), g_in.at[DOWNS[which]], g.at[2 + which])
        fetch(("slope", which), slope_in.at[which], slope.at[which])

    def fetch_up(which):
        fetch(("u", which), g_in.at[UPS[which]], g.at[which])

    fetch("glt", glt_in, glt)
    fetch("gl", gl_in, gl)
    fetch_down(0)
    comm = {}
    if shape:
        place = Place(shape)
        place.barrier("zxy")
        runs = []
        block = (dw.shape[-2], SEG // 2)
        for spot, order in enumerate(FEED_ORDERS):
            columns = pl.ds(spot % 2 * block[1], block[1])
            source = dw.at[2 + spot // 2, :, :, :, :, :, columns]
            run = Scatter(place, source, "yzx", order, {}, hands.at[spot], (send.at[spot], recv.at[spot]))
            open_inbox(run, place.count, "yzx", order, block, boxes)
            runs.append(run)
        swap = Swap(place, mover, ysem, side.wait, half_out, pair)
        comm = {spot: run.steps() for spot, run in enumerate(runs)}
        comm[len(runs)] = swap.steps(0) + swap.steps(1)

    def down_grad(which):
        if which == 0:
            fetch_down(1)
            loads["glt"].wait()
        else:
            fetch_up(1)
            fetch("res", res_in, res)
        loads["active", which].wait()
        weight_grad(glt, lambda m: active[which, m], dw, 2 + which)
        if not shape:
            mover.save(dw.at[2 + which], dw_out.at[2 + which])

    def hidden_grad(which):
        if which == 0:
            fetch("nrm2", nrm2_in, nrm2)
            fetch_up(0)
            loads["gl"].wait()
        else:
            fetch("cot", cot_in, cot)
            fetch("weight", weight_in, weight)
            fetch("o", g_in.at[O], g.at[4])
            fetch("mix", mix_in, mix)
        loads["d", which].wait()
        loads["slope", which].wait()

        def one(m):
            pulled = nn(gl[...], flat(g[2 + which, m]))
            gh[which, m] = (pulled * slope[which, m]).astype(BF)

        half_loop(g.shape[1], one)

    def turn_two():
        loads["nrm2"].wait()
        turn(nrm2, n2t)
        gn2[...] = jnp.zeros_like(gn2)

    def up_grad(which):
        weight_grad(n2t, lambda m: gh[which, m], dw, which)
        mover.save(dw.at[which], dw_out.at[which])

    def norm_grad(which):
        loads["u", which].wait()
        back_through(lambda m: gh[which, m], g, which, gn2)

    def last():
        for name in ("res", "cot", "weight"):
            loads[name].wait()
        gain = vectors[2:3, :]
        vec[...] = jnp.zeros_like(vec)

        def block(rows, _):
            grad = gn2[rows, :]
            pulled, normal = norm_pull(grad, res[rows, :], gain)
            vec[0] += fold_rows(grad * normal)
            vec[1] += fold_rows(grad)
            total = cot[rows, :].astype(F32) * weight[rows, :] + pulled
            gres[rows, :] = total
            gl[rows, :] = total.astype(BF)

        row_loop(cot.shape[0], block)
        mover.save(gres, gres_out)

    def mix_grad():
        loads["o"].wait()
        project(gl, g, 4, gm)
        mover.save(gm, gm_out)

    def out_grad():
        loads["mix"].wait()
        weight_grad(glt, lambda m: mix[:, half(m)], dw, 4)
        mover.save(dw.at[4], dw_out.at[4])

    pieces = []
    for which in range(2):
        pieces += [functools.partial(down_grad, which), functools.partial(hidden_grad, which)]
    pieces.append(turn_two)
    for which in range(2):
        pieces += [functools.partial(up_grad, which), functools.partial(norm_grad, which)]
    pieces += [last, mix_grad, lambda: turn(gl, glt), out_grad]
    play(FEED_PLAN, comm, pieces)
    if shape:
        for spot, run in enumerate(runs):
            grad_down[:, spot * block[1] : (spot + 1) * block[1]] = run.result().astype(F32)
        drain(runs)
        swap.wait()
    mover.close()


def vector_tiles(tiles, vec_a, vec_f):
    tiles[...] = jnp.zeros_like(tiles)
    nz, nx = tiles.shape[:2]
    for line, (source, part) in enumerate(((vec_a, 0), (vec_a, 1), (vec_f, 0), (vec_f, 1))):
        row = jnp.sum(source[part], axis=0, keepdims=True)
        for z in range(nz):
            for x in range(nx):
                chip = z * nx + x
                tiles[z, x, line : line + 1, :] = row[:, chip * 128 : (chip + 1) * 128]


BACK_IN = ("gm", "q", "k", "v", "probs", "nrmt", "gres", "x")
KEPT_GRADS = (0, 1, 4)
HALF = SEG // 2
SPOTS = (4 * SEG, 5 * SEG, 3 * SEG, 0, HALF, SEG, SEG + HALF, 2 * SEG, 2 * SEG + HALF)


def attn_back_kernel(shape, vectors, vec_f, g_in, dw_in, *refs):
    given = dict(zip(BACK_IN, refs[:8]))
    refs = refs[8:]
    if shape:
        grad_down, pair, packed, vec_out, refs = refs[:4] + (refs[4:],)
    else:
        dw_out, out, vec, refs = refs[0], refs[1], refs[2], refs[3:]
    here = dict(zip(BACK_IN, refs[:8]))
    g, dw, gal, pulls, raw, sems = refs[8:14]
    mover = Mover(sems)
    loads, comm = {}, {}
    if shape:
        held, tiles, hands, half_hands, vec_hand, ybox, vec, send, recv, ysem = refs[14:24]
        boxes = list(refs[24:])

    def fetch_held(*spots):
        for spot in spots:
            if shape:
                loads["dw", spot] = mover.start(dw_in.at[KEPT_GRADS[spot]], held.at[spot])

    fetch_held(0)
    some = here["gm"].shape[0] // 3
    for part in range(3):
        rows = pl.ds(part * some, some)
        for name in BACK_IN[:5]:
            loads[name, part] = mover.start(given[name].at[rows], here[name].at[rows])
        if part == 0:
            fetch_held(1, 2)
    loads["nrmt"] = mover.start(given["nrmt"], here["nrmt"])
    gm, q, k, v, probs, nrmt, gres, x = (here[name] for name in BACK_IN)
    gn = probs
    if shape:
        place = Place(shape)
        place.barrier("zxy")
        runs = []
        for spot, order in enumerate(BACK_ORDERS):
            sems_of = (send.at[spot], recv.at[spot])
            if spot < 3:
                width, source, hand = SEG, held.at[spot], hands.at[spot]
            else:
                seg, side = (spot - 3) // 2, (spot - 3) % 2
                width, hand = HALF, half_hands.at[spot - 3]
                source = dw.at[seg, :, :, :, :, :, pl.ds(side * HALF, HALF)]
            run = Scatter(place, source, "yzx", order, {}, hand, sems_of)
            open_inbox(run, place.count, "yzx", order, (dw.shape[-2], width), boxes)
            runs.append(run)
        run = Scatter(place, tiles, "zx", "zx", {}, vec_hand, (send.at[9], recv.at[9]), both=True)
        open_inbox(run, {"z": place.nz, "x": place.nx}, "zx", "zx", (8, 128), boxes)
        runs.append(run)
        swap = Swap(place, mover, ysem, lambda: None, raw, pair)
        comm = {spot: run.steps() for spot, run in enumerate(runs)}
        comm[10], comm[11] = swap.steps(0), swap.steps(1)
        for spot in range(3):
            comm[spot][0] = lambda spot=spot: (loads["dw", spot].wait(), runs[spot].start())

    third = gal.shape[0] // TILE // 3
    micro = raw.shape[0]
    share = gal.shape[0] // micro

    def ready():
        vec[...] = jnp.zeros_like(vec)

    def mixing(part):
        for third_of in range(3):

            @pl.when(part == third_of)
            def _(third_of=third_of):
                for name in BACK_IN[:5]:
                    loads[name, third_of].wait()

        attend_back(q, k, v, probs, gm, pulls.at[0], pulls.at[1], pulls.at[2], part * third, third)

    def head_grad(seg):
        weight_grad(nrmt, lambda m: pulls[seg, :, half(m)], dw, seg)

    def token_grad(part):
        rows_of = pl.ds(part * share, share)
        gn[rows_of, :] = jnp.zeros((share, gn.shape[1]), F32)
        if part == 0:
            for name in (Q, K, V, "gres", "x"):
                loads[name].wait()

        def one(index, carry):
            seg, m = lax.div(index, 2), lax.rem(index, 2)
            gn[rows_of, :] += nt(pulls[seg, rows_of, half(m)], flat(g[seg, m]))
            return carry

        lax.fori_loop(0, 6, one, 0)
        gain = vectors[0:1, :]

        def block(rows, _):
            grad = gn[rows, :]
            pulled, normal = norm_pull(grad, x[rows, :].astype(F32), gain)
            vec[0] += fold_rows(grad * normal)
            vec[1] += fold_rows(grad)
            gal[rows, :] = (gres[rows, :] + pulled).astype(BF)

        row_loop(share, block, part * share // TILE)
        patches, series, width = raw.shape[1:]
        turned = nn(gather_rows(patches, series), gal[rows_of, :]).astype(raw.dtype)
        raw[part] = turned.reshape(patches, series, width)

    def spread_vectors():
        if shape:
            vector_tiles(tiles, vec, vec_f)

    def before_heads():
        for seg in (Q, K, V):
            loads[seg] = mover.start(g_in.at[seg], g.at[seg])
        for name in ("gres", "x"):
            loads[name] = mover.start(given[name], here[name])
        loads["nrmt"].wait()

    pieces = [ready, (3, mixing, None, None), before_heads]
    parts = [functools.partial(token_grad, part) for part in range(micro)]
    heads = [(3, head_grad, None, None)]
    pieces += heads + parts if GRADS_FIRST else parts + heads
    pieces.insert(len(pieces) - (0 if GRADS_FIRST else 1), spread_vectors)
    play(ATTN_PLAN, comm, pieces)
    if not shape:
        mover.save(raw, out)
        for seg in (Q, K, V):
            mover.save(dw.at[seg], dw_out.at[seg])
    if shape:
        here_tile = tiles.at[place.at["z"], place.at["x"]]
        copy = pltpu.make_async_remote_copy(
            here_tile, ybox, ysem.at[8], ysem.at[9], device_id=place.device(y=1 - place.at["y"]), device_id_type=MESH
        )
        copy.start()
        packed[:, 6 * SEG :] = grad_down[...]
        for spot, column in enumerate(SPOTS):
            width = SEG if spot < 3 else HALF
            packed[:, column : column + width] = runs[spot].result().astype(F32)
        drain(runs)
        copy.wait()
        vec_out[...] = tiles[place.at["z"], place.at["x"]] + ybox[...]
        swap.wait()
    mover.close()


def shape_of(shape, dtype):
    return jax.ShapeDtypeStruct(shape, dtype)


IN_VMEM = pl.BlockSpec(memory_space=pltpu.VMEM)
IN_SMEM = pl.BlockSpec(memory_space=pltpu.SMEM)
ANYWHERE = pl.BlockSpec(memory_space=pl.ANY)
DMA = pltpu.SemaphoreType.DMA


def call(body, outs, ins, out_specs, scratch, name, collective=None):
    params = {"vmem_limit_bytes": VMEM_LIMIT}
    if collective is not None:
        params.update(collective_id=collective, has_side_effects=True)
    return pl.pallas_call(
        body,
        out_shape=outs,
        in_specs=ins,
        out_specs=out_specs,
        scratch_shapes=scratch,
        compiler_params=pltpu.CompilerParams(**params),
        name=name,
    )


def vmem(like):
    return pltpu.VMEM(like.shape, like.dtype)


def forward(shape, micro, tokens, cotangent, ids, counts, weights, norms, g_in=None, vectors_in=None):
    _, patches, series, width = tokens.shape
    rows = micro * series * PAD
    full = g_in.shape if shape is None else (8, shape[2], shape[0], shape[1], 2, weights[0].shape[0], SEG)
    low, high = shape_of((rows, width), BF), shape_of((rows, width), F32)
    wide = (2, full[1], rows, SEG)
    raw = shape_of((micro, patches, series, width), BF)
    kinds = {name: low for name in FWD_OUT}
    kinds.update(
        probs=high,
        res=high,
        active=shape_of(wide, BF),
        slope=shape_of(wide, F32),
        out=raw,
        glt=shape_of((width, rows), BF),
        nrmt=shape_of((width, rows), BF),
        weight=shape_of((rows, 1), F32),
    )
    saved = tuple(kinds[name] for name in FWD_OUT)
    scratch = [vmem(kind) for kind in saved] + [vmem(raw), vmem(low), vmem(low), vmem(high), pltpu.VMEM(full, BF), DMA((64,))]
    if shape is None:
        results = call(
            functools.partial(forward_kernel, None, micro),
            saved,
            [ANYWHERE, ANYWHERE, IN_SMEM, IN_SMEM, ANYWHERE, IN_VMEM],
            (ANYWHERE,) * KEPT,
            scratch,
            "forward",
        )(tokens, cotangent, ids, counts, g_in, vectors_in)
        return g_in, vectors_in, dict(zip(FWD_OUT, results))
    count = dict(zip("zxy", shape))
    slots = link_slots(count, "zxy")
    scratch += [pltpu.VMEM(shape[:2] + (2, 8, 128), F32)]
    runs = len(ORDERS) + 1
    scratch += [DMA((runs, slots)), DMA((runs, slots)), DMA((runs, slots + 1)), DMA((runs, slots + 1))]
    results = call(
        functools.partial(forward_kernel, shape, micro),
        (shape_of(full, BF), shape_of((8, width), F32)) + saved,
        [ANYWHERE, ANYWHERE, IN_SMEM, IN_SMEM] + [ANYWHERE] * 6 + [IN_VMEM] * 4,
        (ANYWHERE, IN_VMEM) + (ANYWHERE,) * KEPT,
        scratch,
        "forward",
        0,
    )(tokens, cotangent, ids, counts, *weights, *norms)
    return results[0], results[1], dict(zip(FWD_OUT, results[2:]))


def scatter_scratch(segs, part, count, orders, cols=SEG):
    rows = part.shape[-2]
    slots = link_slots(count, "zxy") + 1
    boxes = []
    for order in orders:
        boxes += [pltpu.VMEM(s, BF) for s in inbox_shapes(count, "yzx", order, (rows, cols))[0]]
    hands = pltpu.VMEM((len(orders),) + part.shape[1:4] + (rows, cols), BF)
    return hands, [DMA((segs, slots)), DMA((segs, slots))], boxes


def pair_of(raw, ny):
    return shape_of((ny * raw.shape[0],) + raw.shape[1:], BF)


def feed_back(shape, vectors, g, kept):
    low, high, raw = kept["x"], kept["res"], kept["out"]
    rows, width = low.shape
    part = shape_of((5,) + g.shape[1:], BF)
    turned = pltpu.VMEM((width, rows), BF)
    scratch = [
        vmem(low),
        pltpu.VMEM((rows, 1), F32),
        vmem(kept["active"]),
        vmem(kept["slope"]),
        vmem(low),
        vmem(high),
        vmem(part),
        vmem(part),
        vmem(low),
        turned,
        vmem(kept["active"]),
        turned,
        vmem(high),
        vmem(high),
        vmem(low),
        vmem(low),
        DMA((32,)),
    ]
    given = [g] + [kept[name] for name in ("active", "slope", "nrm2", "res", "out", "cot", "gl", "glt", "weight", "mix")]
    outs = [part, shape_of(high.shape, F32), shape_of(low.shape, BF), shape_of((2, 8, width), F32)]
    specs = [ANYWHERE, ANYWHERE, ANYWHERE, IN_VMEM]
    if shape:
        count = dict(zip("zxy", shape))
        hands, sems, boxes = scatter_scratch(len(FEED_ORDERS), part, count, FEED_ORDERS, SEG // 2)
        scratch += [vmem(raw), hands] + sems + [DMA((8,))] + boxes
        outs += [pair_of(raw, shape[2]), shape_of((part.shape[-2], 2 * SEG), F32)]
        specs += [ANYWHERE, IN_VMEM]
    return call(
        functools.partial(feed_back_kernel, shape),
        tuple(outs),
        [IN_VMEM] + [ANYWHERE] * 11,
        tuple(specs),
        scratch,
        "feed_back",
        1 if shape else None,
    )(vectors, *given)


def attn_back(shape, vectors, vec_f, g, dw_in, kept, grad_down=None):
    low, raw = kept["x"], kept["out"]
    width = low.shape[1]
    part = shape_of((3,) + g.shape[1:], BF)
    scratch = [vmem(kept[name]) for name in BACK_IN]
    scratch += [vmem(part), vmem(part), vmem(low), pltpu.VMEM((3,) + low.shape, BF), vmem(raw), DMA((32,))]
    vec = shape_of((2, 8, width), F32)
    if shape:
        nz, nx, ny = shape
        count = dict(zip("zxy", shape))
        share = part.shape[-2]
        outs = [pair_of(raw, ny), shape_of((share, 8 * SEG), F32), shape_of((8, 128), F32)]
        specs = [ANYWHERE] + [IN_VMEM] * 2
        hands, sems, boxes = scatter_scratch(10, part, count, BACK_ORDERS[:3])
        half_hands, _, more = scatter_scratch(10, part, count, BACK_ORDERS[3:], HALF)
        boxes += more
        tiles = pltpu.VMEM((nz, nx, 8, 128), F32)
        scratch += [vmem(part), tiles, hands, half_hands, tiles, pltpu.VMEM((8, 128), F32), vmem(vec)]
        scratch += sems + [DMA((10,))] + boxes
        scratch += [pltpu.VMEM(s, F32) for s in inbox_shapes({"z": nz, "x": nx}, "zx", "zx", (8, 128))[0]]
    else:
        outs, specs = [part, raw, vec], [ANYWHERE, ANYWHERE, IN_VMEM]
        outs[1] = shape_of(raw.shape, BF)
    return call(
        functools.partial(attn_back_kernel, shape),
        tuple(outs),
        [IN_VMEM] * 2 + [ANYWHERE] * 10 + ([IN_VMEM] if shape else []),
        tuple(specs),
        scratch,
        "attn_back",
        2 if shape else None,
    )(vectors, vec_f, g, dw_in, *(kept[name] for name in BACK_IN), *((grad_down,) if shape else ()))


def chip_grid(chips):
    nx = 1
    while (nx * 2) ** 2 <= chips:
        nx *= 2
    return chips // nx, nx


def body(counts_of, tokens, cotangent, domain_ids, domain_counts, *params):
    weights, norms = params[:6], params[6:]
    n_dp, n_mp = counts_of
    micro = tokens.shape[0] // n_mp
    width = tokens.shape[3]
    share = width // n_dp
    y = lax.axis_index("mp")
    linked = n_mp == 2 and share * 2 == TILE
    flip = lambda array: jnp.transpose(array, (0, 2, 1, 3))
    x, cot = flip(tokens), flip(cotangent)
    if linked:
        shape = chip_grid(n_dp // 2) + (n_mp,)
        g, vectors, kept = forward(shape, micro, x, cot, domain_ids, domain_counts, weights, [norm.reshape(1, -1) for norm in norms])
    else:
        shards = jnp.stack(
            weights[:4] + tuple(w[:, i * SEG : (i + 1) * SEG] for w in weights[4:] for i in range(2))
        )
        g = lax.all_gather(lax.all_gather(shards, "dp", axis=1, tiled=True), "mp", axis=1)
        vectors = lax.all_gather(jnp.stack(norms), "dp", axis=1, tiled=True).astype(F32)
        vectors = jnp.pad(vectors, ((0, 4), (0, 0)))
        g, vectors, kept = forward(None, micro, x, cot, domain_ids, domain_counts, None, None, g, vectors)
    shape = shape if linked else None
    results = feed_back(shape, vectors, g, kept)
    dw_f, gres, gm, vec_f = results[:4]
    kept = {**kept, "gres": gres, "gm": gm}
    if linked:
        out, grad_down = results[4:]
        grad_tokens, packed, vec = attn_back(shape, vectors, vec_f, g, dw_f, kept, grad_down)
        cuts = [0, SEG, 2 * SEG, 3 * SEG, 4 * SEG, 6 * SEG, 8 * SEG]
        grads = [packed[:, start:stop] for start, stop in zip(cuts, cuts[1:])]
        core = lax.rem(lax.axis_index("dp"), 2)
        vec = lax.dynamic_slice(vec, (0, core * share), (4, share))
    else:
        dw_a, low_tokens, vec_a = attn_back(shape, vectors, vec_f, g, dw_f, kept)
        dw = jnp.concatenate((dw_a, dw_f[4:], dw_f[:4])).astype(F32)
        dw = lax.psum_scatter(lax.psum_scatter(dw, "mp", scatter_dimension=1), "dp", scatter_dimension=1, tiled=True)
        grads = [dw[0], dw[1], dw[2], dw[3]]
        grads += [jnp.concatenate((dw[a], dw[b]), axis=1) for a, b in (UPS, DOWNS)]
        vec = jnp.concatenate((jnp.sum(vec_a, axis=1), jnp.sum(vec_f, axis=1)))
        vec = lax.psum_scatter(lax.psum(vec, "mp"), "dp", scatter_dimension=1, tiled=True)
        out = lax.all_gather(kept["out"], "mp", axis=0, tiled=True)
        grad_tokens = lax.all_gather(low_tokens, "mp", axis=0, tiled=True)
    return (flip(out), flip(grad_tokens.astype(F32)), *grads, vec[0], vec[1], vec[2], vec[3])


def solution(mesh):
    rows, matrix, vector = P(None, "dp", None, None), P("dp", "mp"), P("dp")
    in_specs = (rows, rows, P(None, "dp"), P()) + (matrix,) * 6 + (vector,) * 4
    out_specs = (rows, rows) + (matrix,) * 6 + (vector,) * 4
    run = functools.partial(body, (mesh.shape["dp"], mesh.shape["mp"]))
    return jax.shard_map(run, mesh=mesh, in_specs=in_specs, out_specs=out_specs, check_vma=False)
```
